32 devices in a mesh: dp: 4 (over y, x), fsdp: 8 (over z, core).
Axes of the slice: x: 2, y: 2, z: 4, core: 2. Of those that a mesh axis runs over, the one named last changes fastest.
Arguments:
- tokens_in: bfloat16 [32, 256, 1024], P(('dp', 'fsdp')), may hold values from -6 to 6
- cotangent: bfloat16 [32, 256, 1024], P(('dp', 'fsdp')), may hold values from -6 to 6
- lengths: int32 [32], P(('dp', 'fsdp')), may hold values from 128 to 256
- qkv_master: float32 [1024, 3072], P('fsdp'), may hold values from -0.5625 to 0.5625
- out_master: float32 [1024, 1024], P('fsdp'), may hold values from -2.25 to 2.25
- up_master: float32 [1024, 4096], P('fsdp'), may hold values from -0.5625 to 0.5625
- down_master: float32 [4096, 1024], P('fsdp'), may hold values from -0.28125 to 0.28125
- small_master: float32 [13312], P('fsdp'), may hold values from -0.8 to 1.4
- qkv_first: float32 [1024, 3072], P('fsdp'), may hold values from -814.58701 to 814.58701
- out_first: float32 [1024, 1024], P('fsdp'), may hold values from -407.29351 to 407.29351
- up_first: float32 [1024, 4096], P('fsdp'), may hold values from -814.58701 to 814.58701
- down_first: float32 [4096, 1024], P('fsdp'), may hold values from -814.58701 to 814.58701
- small_first: float32 [13312], P('fsdp'), may hold values from -1629.17402 to 1629.17402
- qkv_second: float32 [1024, 3072], P('fsdp'), may hold values from 2048 to 8192
- out_second: float32 [1024, 1024], P('fsdp'), may hold values from 512 to 2048
- up_second: float32 [1024, 4096], P('fsdp'), may hold values from 2048 to 8192
- down_second: float32 [4096, 1024], P('fsdp'), may hold values from 2048 to 8192
- small_second: float32 [13312], P('fsdp'), may hold values from 8192 to 32768
Outputs:
- output: bfloat16 [32, 256, 1024], P(('dp', 'fsdp'))
- input_grad: bfloat16 [32, 256, 1024], P(('dp', 'fsdp'))
- qkv_new: float32 [1024, 3072], P('fsdp')
- out_new: float32 [1024, 1024], P('fsdp')
- up_new: float32 [1024, 4096], P('fsdp')
- down_new: float32 [4096, 1024], P('fsdp')
- small_new: float32 [13312], P('fsdp')
- qkv_first_new: float32 [1024, 3072], P('fsdp')
- out_first_new: float32 [1024, 1024], P('fsdp')
- up_first_new: float32 [1024, 4096], P('fsdp')
- down_first_new: float32 [4096, 1024], P('fsdp')
- small_first_new: float32 [13312], P('fsdp')
- qkv_second_new: float32 [1024, 3072], P('fsdp')
- out_second_new: float32 [1024, 1024], P('fsdp')
- up_second_new: float32 [1024, 4096], P('fsdp')
- down_second_new: float32 [4096, 1024], P('fsdp')
- small_second_new: float32 [13312], P('fsdp')
- lamb_norms: float32 [2, 5], replicated
The draws below stay inside these ranges and needn't reach their ends.
All inputs are finite; a program needn't handle non-finite values.
Results may differ from the reference program's by a relative error of at most 0.012.
The reference program's roundings to bfloat16 on the way count: a program that leaves them out, or rounds other values in their place, can miss the bound.
Values may be sent and summed in bfloat16 or wider, within the bound.
A program may use at most 256 MiB of HBM per device.

```python
import math
import jax
import jax.numpy as jnp
from jax import lax

D = 1024
HEADS = 16
HD = 64
FF = 4096
SEQ = 256
ROT = 16
SMALL = 13312
BATCH = 32
TOKENS = 8192


def shaped(key, row_count, col_count, entry_scale, rise_factor):
    key_entries, key_rows, key_cols = jax.random.split(key, 3)
    entries = jnp.clip(jax.random.normal(key_entries, (row_count, col_count), jnp.float32), -4.0, 4.0)
    place_rows = jnp.arange(row_count, dtype=jnp.float32) / max(row_count - 1, 1)
    row_trend = jnp.exp(math.log(rise_factor) * (place_rows - 0.5))
    row_scale = jnp.exp(jax.random.uniform(key_rows, (row_count,), jnp.float32, -0.35, 0.35))
    col_scale = jnp.exp(jax.random.uniform(key_cols, (col_count,), jnp.float32, -0.35, 0.35))
    return entries * (entry_scale * row_trend * row_scale)[:, None] * col_scale[None, :]


def draw_qkv_master(key, part):
    key = jax.random.fold_in(key, 101)
    return shaped(key, D, 3 * D, D ** (-0.5), 3.0)


def draw_out_master(key, part):
    key = jax.random.fold_in(key, 102)
    return shaped(key, D, D, (D // 16) ** (-0.5), 3.0)


def draw_up_master(key, part):
    key = jax.random.fold_in(key, 103)
    return shaped(key, D, FF, D ** (-0.5), 3.0)


def draw_down_master(key, part):
    key = jax.random.fold_in(key, 104)
    return shaped(key, FF, D, FF ** (-0.5), 3.0)


def draw_small_master(key, part):
    key = jax.random.fold_in(key, 105)
    position = jnp.arange(SMALL)
    is_gain = (position < D) | (position >= 2 * D) & (position < 3 * D)
    noise_draw = jnp.clip(jax.random.normal(key, (SMALL,), jnp.float32), -4.0, 4.0)
    return jnp.where(is_gain, 1.0 + 0.1 * noise_draw, 0.2 * noise_draw)


def draw_qkv_first(key, part):
    key = jax.random.fold_in(key, 201)
    return shaped(key, D, 3 * D, 0.5 * TOKENS ** 0.5, 3.0)


def draw_out_first(key, part):
    key = jax.random.fold_in(key, 202)
    return shaped(key, D, D, 0.25 * TOKENS ** 0.5, 3.0)


def draw_up_first(key, part):
    key = jax.random.fold_in(key, 203)
    return shaped(key, D, FF, 0.5 * TOKENS ** 0.5, 3.0)


def draw_down_first(key, part):
    key = jax.random.fold_in(key, 204)
    return shaped(key, FF, D, 0.5 * TOKENS ** 0.5, 3.0)


def draw_small_first(key, part):
    key = jax.random.fold_in(key, 205)
    return shaped(key, SMALL, 1, TOKENS ** 0.5, 3.0).reshape(SMALL)


def place_ends(values, stream_key, smallest, top_value):
    shape = values.shape
    spot = [jax.random.randint(jax.random.fold_in(stream_key, axis), (), 0, shape[axis]) for axis in range(len(shape))]
    values = values.at[tuple(spot)].set(smallest)
    longest = shape.index(max(shape))
    spot[longest] = (spot[longest] + 1) % shape[longest]
    return values.at[tuple(spot)].set(top_value)


def levels(own_key, shape, pieces, least, high):
    level, own = 1.0, jax.random.fold_in(own_key, 6)
    for dim, parts in pieces:
        draws = jnp.exp(jax.random.uniform(jax.random.fold_in(own, dim), (parts,), jnp.float32, least / len(pieces), high / len(pieces)))
        level = level * jnp.repeat(draws, shape[dim] // parts).reshape([-1 if axis == dim else 1 for axis in range(len(shape))])
    return level


def noise(stream_key, extent, scale, limit, shards=(), kind=jnp.bfloat16):
    values = scale * jax.random.normal(stream_key, extent, jnp.float32)
    if shards:
        values = values * levels(stream_key, extent, shards, -0.22, 0.18)
    return jnp.clip(values, -limit, limit).astype(kind)


def setup_inputs(seed: int = 0) -> dict:
    key_of = jax.random.split(jax.random.key(seed), 19)
    return {
        "tokens_in": noise(key_of[0], (BATCH, SEQ, D), 1.0, 6.0, ((0, 32),)),
        "cotangent": noise(key_of[1], (BATCH, SEQ, D), 1.0, 6.0, ((0, 32),)),
        "lengths": place_ends(jax.random.randint(key_of[2], (BATCH,), SEQ // 2, SEQ + 1), jax.random.fold_in(key_of[2], 1), SEQ // 2, SEQ).astype(jnp.int32),
        "qkv_master": draw_qkv_master(jax.random.fold_in(key_of[18], 71), 0),
        "out_master": draw_out_master(jax.random.fold_in(key_of[18], 71), 0),
        "up_master": draw_up_master(jax.random.fold_in(key_of[18], 71), 0),
        "down_master": draw_down_master(jax.random.fold_in(key_of[18], 71), 0),
        "small_master": draw_small_master(jax.random.fold_in(key_of[18], 71), 0),
        "qkv_first": draw_qkv_first(jax.random.fold_in(key_of[18], 71), 0),
        "out_first": draw_out_first(jax.random.fold_in(key_of[18], 71), 0),
        "up_first": draw_up_first(jax.random.fold_in(key_of[18], 71), 0),
        "down_first": draw_down_first(jax.random.fold_in(key_of[18], 71), 0),
        "small_first": draw_small_first(jax.random.fold_in(key_of[18], 71), 0),
        "qkv_second": jnp.clip(jnp.exp(math.log(8192.0) - 1.3862944 * jax.random.uniform(key_of[13], (D, 3 * D), jnp.float32) ** levels(key_of[13], (D, 3 * D), ((0, 8),), -0.2, 0.2)), 2048.0, 8192.0),
        "out_second": jnp.clip(jnp.exp(math.log(2048.0) - 1.3862944 * jax.random.uniform(key_of[14], (D, D), jnp.float32) ** levels(key_of[14], (D, D), ((0, 8),), -0.2, 0.2)), 512.0, 2048.0),
        "up_second": jnp.clip(jnp.exp(math.log(8192.0) - 1.3862944 * jax.random.uniform(key_of[15], (D, FF), jnp.float32) ** levels(key_of[15], (D, FF), ((0, 8),), -0.2, 0.2)), 2048.0, 8192.0),
        "down_second": jnp.clip(jnp.exp(math.log(8192.0) - 1.3862944 * jax.random.uniform(key_of[16], (FF, D), jnp.float32) ** levels(key_of[16], (FF, D), ((0, 8),), -0.2, 0.2)), 2048.0, 8192.0),
        "small_second": jnp.clip(jnp.exp(math.log(32768.0) - 1.3862944 * jax.random.uniform(key_of[17], (SMALL,), jnp.float32) ** levels(key_of[17], (SMALL,), ((0, 8),), -0.2, 0.2)), 8192.0, 32768.0),
    }


@jax.custom_vjp
def low(v):
    return lax.optimization_barrier(v.astype(jnp.bfloat16)).astype(jnp.float32)

@jax.custom_vjp
def low_back(v):
    return v

def low_keep(v):
    return (low(v), None)

def low_pass(kept, grad):
    return (grad,)

def back_keep(v):
    return (v, None)

def back_low(kept, grad):
    return (low(grad),)
low.defvjp(low_keep, low_pass)
low_back.defvjp(back_keep, back_low)
NORM_EPSILON = 1e-05
ADAM_EPSILON = 1e-06
ROPE_BASE = 10000.0
RATE = 0.5
DECAY = 0.01
BETA_ONE = 0.5
BETA_TWO = 0.5

def matmul(left, right):
    return jnp.dot(left, right, precision=lax.Precision.HIGHEST)

def layer_norm(values, gain_vec, shift_vec):
    average = lax.optimization_barrier(jnp.mean(values, axis=-1, keepdims=True))
    centred = values - average
    variance = lax.optimization_barrier(jnp.mean(centred * centred, axis=-1, keepdims=True))
    return centred * lax.rsqrt(variance + NORM_EPSILON) * gain_vec + shift_vec

def rotary_tables(length):
    half_dims = ROT // 2
    position = jnp.arange(length, dtype=jnp.float32)[:, None]
    number = jnp.arange(half_dims, dtype=jnp.float32)[None, :]
    angle = position * jnp.exp(number * (-2.0 * math.log(ROPE_BASE) / ROT))
    return (jnp.cos(angle), jnp.sin(angle))

def rotate(heads_in, cosine_table, sine_table):
    half_dims = ROT // 2
    first_half = heads_in[..., :half_dims]
    second_half = heads_in[..., half_dims:ROT]
    cosine_b = cosine_table[:, None, :]
    sine_b = sine_table[:, None, :]
    return jnp.concatenate([first_half * cosine_b - second_half * sine_b, second_half * cosine_b + first_half * sine_b, heads_in[..., ROT:]], axis=-1)

def forward(params, inputs, block_lengths):
    qkv_weight, out_weight, up_weight, down_weight, small_vector = [low(param) for param in params]
    gain_one = small_vector[0:D]
    shift_one = small_vector[D:2 * D]
    gain_two = small_vector[2 * D:3 * D]
    shift_two = small_vector[3 * D:4 * D]
    qkv_bias = small_vector[4 * D:7 * D]
    out_bias = small_vector[7 * D:8 * D]
    up_bias = small_vector[8 * D:8 * D + FF]
    down_bias = small_vector[8 * D + FF:9 * D + FF]
    groups = inputs.shape[0]
    length = inputs.shape[1]
    position = jnp.arange(length)
    live_rows = (position[None, :] < block_lengths[:, None]).astype(jnp.float32)[:, :, None]
    normed_one = low(layer_norm(inputs, gain_one, shift_one))
    projected = low_back(matmul(normed_one, qkv_weight) + qkv_bias)
    projected = projected.reshape(groups, length, 3, HEADS, HD)
    cosine_table, sine_table = rotary_tables(length)
    query_heads = low(rotate(projected[:, :, 0], cosine_table, sine_table))
    key_heads = low(rotate(projected[:, :, 1], cosine_table, sine_table))
    value_heads = low(projected[:, :, 2])
    scores = jnp.einsum('gqhd,gkhd->ghqk', query_heads, key_heads, precision=lax.Precision.HIGHEST) * HD ** (-0.5)
    causal = position[None, :] <= position[:, None]
    allowed = causal[None, None] & (position[None, None, None, :] < block_lengths[:, None, None, None])
    scores = low_back(jnp.where(allowed, scores, -1e+30))
    attend = jax.nn.softmax(scores, axis=-1)
    mixed_heads = jnp.einsum('ghqk,gkhd->gqhd', low(attend), value_heads, precision=lax.Precision.HIGHEST)
    mixed_heads = low(low_back(mixed_heads.reshape(groups, length, D)))
    attention = matmul(mixed_heads, out_weight) + out_bias
    normed_two = low(layer_norm(inputs, gain_two, shift_two))
    hidden = low_back(matmul(normed_two, up_weight) + up_bias)
    activated = low(jax.nn.gelu(hidden, approximate=False))
    feed_out = matmul(activated, down_weight) + down_bias
    return (inputs + attention + feed_out) * live_rows

def reference(tokens_in, cotangent, lengths, qkv_master, out_master, up_master, down_master, small_master, qkv_first, out_first, up_first, down_first, small_first, qkv_second, out_second, up_second, down_second, small_second):
    masters = (qkv_master, out_master, up_master, down_master, small_master)
    firsts = (qkv_first, out_first, up_first, down_first, small_first)
    seconds = (qkv_second, out_second, up_second, down_second, small_second)
    group_size = math.gcd(BATCH, max(1, 4096 // SEQ))
    blocks_count = BATCH // group_size
    inputs = tokens_in.astype(jnp.float32).reshape(blocks_count, group_size, SEQ, D)
    returned = cotangent.astype(jnp.float32).reshape(blocks_count, group_size, SEQ, D)
    length_rows = lengths.reshape(blocks_count, group_size)

    def one_block(totals, block_items):
        block_in, block_back, block_lengths = block_items

        def run_block(params, values):
            return forward(params, values, block_lengths)
        result, pull_back = jax.vjp(run_block, masters, block_in)
        param_grads, input_grads = pull_back(block_back)
        totals = jax.tree.map(jnp.add, totals, param_grads)
        return (totals, (result.astype(jnp.bfloat16), input_grads.astype(jnp.bfloat16)))
    zeros_start = jax.tree.map(jnp.zeros_like, masters)
    gradients, (outputs, input_grads) = lax.scan(one_block, zeros_start, (inputs, returned, length_rows))
    new_masters = []
    first_news = []
    second_news = []
    weight_list = []
    update_list = []
    for master, first_old, second_old, grad_sum in zip(masters, firsts, seconds, gradients):
        first_new = BETA_ONE * first_old + (1.0 - BETA_ONE) * grad_sum
        second_new = BETA_TWO * second_old + (1.0 - BETA_TWO) * grad_sum * grad_sum
        update = first_new / (jnp.sqrt(second_new) + ADAM_EPSILON) + DECAY * master
        weight_norm = jnp.sqrt(jnp.sum(master * master))
        update_norm = jnp.sqrt(jnp.sum(update * update))
        new_masters.append(master - RATE * (weight_norm / update_norm) * update)
        first_news.append(first_new)
        second_news.append(second_new)
        weight_list.append(weight_norm)
        update_list.append(update_norm)
    lamb_norms = jnp.stack([jnp.stack(weight_list), jnp.stack(update_list)])
    return (outputs.reshape(BATCH, SEQ, D), input_grads.reshape(BATCH, SEQ, D), new_masters[0], new_masters[1], new_masters[2], new_masters[3], new_masters[4], first_news[0], first_news[1], first_news[2], first_news[3], first_news[4], second_news[0], second_news[1], second_news[2], second_news[3], second_news[4], lamb_norms)
```

```python
import math

import jax
import jax.numpy as jnp
from jax import lax
from jax.sharding import PartitionSpec as P

D = 1024
HEADS = 16
HD = 64
FF = 4096
ROT = 16


NORM_EPSILON = 1e-05
ADAM_EPSILON = 1e-06
ROPE_BASE = 10000.0
RATE = 0.5
DECAY = 0.01
BETA_ONE = 0.5
BETA_TWO = 0.5


def shortened(shard):

    def short(part):
        return part.astype(jnp.bfloat16) if part.dtype == jnp.float32 else part

    return jax.tree.map(short, shard)


def split_small(small_vector):
    bounds = [0, D, 2 * D, 3 * D, 4 * D, 7 * D, 8 * D, 8 * D + FF, 9 * D + FF]
    return [small_vector[bounds[number] : bounds[number + 1]] for number in range(8)]


def normalize(values):
    average = jnp.mean(values, axis=-1, keepdims=True)
    centred = values - average
    variance = jnp.mean(centred * centred, axis=-1, keepdims=True)
    inverse = lax.rsqrt(variance + NORM_EPSILON)
    return (centred * inverse, inverse)


def norm_back(grad_out, normalized, inverse, gain_vec):
    scaled = grad_out * gain_vec
    return inverse * (
        scaled
        - jnp.mean(scaled, axis=-1, keepdims=True)
        - normalized * jnp.mean(scaled * normalized, axis=-1, keepdims=True)
    )


def rotary_tables(length):
    half_dims = ROT // 2
    position = jnp.arange(length, dtype=jnp.float32)[:, None]
    number = jnp.arange(half_dims, dtype=jnp.float32)[None, :]
    angle = position * jnp.exp(number * (-2.0 * math.log(ROPE_BASE) / ROT))
    return (jnp.cos(angle)[:, None, :], jnp.sin(angle)[:, None, :])


def rotate(heads_in, cosine_table, sine_table):
    half_dims = ROT // 2
    first_half = heads_in[..., :half_dims]
    second_half = heads_in[..., half_dims:ROT]
    return jnp.concatenate(
        [
            first_half * cosine_table - second_half * sine_table,
            second_half * cosine_table + first_half * sine_table,
            heads_in[..., ROT:],
        ],
        axis=-1,
    )


def rotate_back(grads_in, cosine_table, sine_table):
    half_dims = ROT // 2
    first_half = grads_in[..., :half_dims]
    second_half = grads_in[..., half_dims:ROT]
    return jnp.concatenate(
        [
            first_half * cosine_table + second_half * sine_table,
            second_half * cosine_table - first_half * sine_table,
            grads_in[..., ROT:],
        ],
        axis=-1,
    )


def gelu_slope(values):
    return 0.5 * (1.0 + lax.erf(values * 2.0 ** (-0.5))) + values * jnp.exp(
        -0.5 * values * values
    ) * (2.0 * math.pi) ** (-0.5)


def against(left, right):
    return lax.dot_general(
        left, right, (((1,), (1,)), ((), ())), preferred_element_type=jnp.float32
    )


def outer_sum(columns, right):
    return lax.dot_general(
        columns, right, (((0,), (0,)), ((), ())), preferred_element_type=jnp.float32
    )


def score_block(query_heads, key_heads, allowed):
    scores = jnp.einsum(
        "qhd,khd->hqk", query_heads, key_heads, preferred_element_type=jnp.float32
    ) * HD ** (-0.5)
    return jnp.where(allowed[None], scores, -1e30)


def row_terms(left, right):
    return outer_sum(left, right)


def local_squares(arrays):
    return jnp.stack([jnp.sum(array_in * array_in) for array_in in arrays])


def local_rows(
    tokens_in,
    cotangent,
    lengths,
    qkv_master,
    out_master,
    up_master,
    down_master,
    small_master,
    qkv_first,
    out_first,
    up_first,
    down_first,
    small_first,
    qkv_second,
    out_second,
    up_second,
    down_second,
    small_second,
):
    masters = (qkv_master, out_master, up_master, down_master, small_master)
    firsts = (qkv_first, out_first, up_first, down_first, small_first)
    seconds = (qkv_second, out_second, up_second, down_second, small_second)
    rounded = tuple((master.astype(jnp.bfloat16) for master in masters))
    gathered = jax.tree.map(
        lambda part, own: part.astype(own.dtype),
        lax.all_gather(shortened(rounded), "fsdp", axis=0, tiled=True),
        rounded,
    )
    qkv_weight, out_weight, up_weight, down_weight, small_low = gathered
    gain_one, shift_one, gain_two, shift_two, qkv_bias, out_bias, up_bias, down_bias = split_small(
        small_low.astype(jnp.float32)
    )
    inputs = tokens_in[0].astype(jnp.float32)
    length = inputs.shape[0]
    length_now = lengths[0]
    position = jnp.arange(length)
    live_rows = (position < length_now).astype(jnp.float32)[:, None]
    allowed = (position[None, :] <= position[:, None]) & (position[None, :] < length_now)
    unit_rows, inverse_rows = normalize(inputs)
    normed_one = (unit_rows * gain_one + shift_one).astype(jnp.bfloat16)
    normed_two = (unit_rows * gain_two + shift_two).astype(jnp.bfloat16)
    projected = jnp.dot(normed_one, qkv_weight, preferred_element_type=jnp.float32) + qkv_bias
    projected = projected.reshape(length, 3, HEADS, HD)
    cosine_table, sine_table = rotary_tables(length)
    query_heads = rotate(projected[:, 0], cosine_table, sine_table).astype(jnp.bfloat16)
    key_heads = rotate(projected[:, 1], cosine_table, sine_table).astype(jnp.bfloat16)
    value_heads = projected[:, 2].astype(jnp.bfloat16)
    scores = score_block(query_heads, key_heads, allowed)
    row_top = jnp.max(scores, axis=-1, keepdims=True)
    log_total = row_top + jnp.log(jnp.sum(jnp.exp(scores - row_top), axis=-1, keepdims=True))
    attend_low = jnp.exp(scores - log_total).astype(jnp.bfloat16)
    mixed_heads = jnp.einsum(
        "hqk,khd->qhd", attend_low, value_heads, preferred_element_type=jnp.float32
    )
    mixed_heads = mixed_heads.reshape(length, D).astype(jnp.bfloat16)
    attention = jnp.dot(mixed_heads, out_weight, preferred_element_type=jnp.float32) + out_bias
    hidden = jnp.dot(normed_two, up_weight, preferred_element_type=jnp.float32) + up_bias
    activated = jax.nn.gelu(hidden, approximate=False).astype(jnp.bfloat16)
    feed_out = jnp.dot(activated, down_weight, preferred_element_type=jnp.float32) + down_bias
    output = ((inputs + attention + feed_out) * live_rows).astype(jnp.bfloat16)
    back_weights = jax.tree.map(
        lambda part, own: part.astype(own.dtype),
        lax.all_gather(shortened(rounded), "fsdp", axis=0, tiled=True),
        rounded,
    )
    qkv_back, out_back, up_back, down_back, small_back = back_weights
    back_gains = split_small(small_back.astype(jnp.float32))
    back_rows = cotangent[0].astype(jnp.float32) * live_rows
    back_narrow = back_rows.astype(jnp.bfloat16)
    d_hidden = (against(back_narrow, down_back) * gelu_slope(hidden)).astype(jnp.bfloat16)
    d_mixed = against(back_narrow, out_back).astype(jnp.bfloat16).reshape(length, HEADS, HD)
    scores_again = score_block(query_heads, key_heads, allowed)
    attend_full = jnp.exp(scores_again - log_total)
    d_attend = jnp.einsum("qhd,khd->hqk", d_mixed, value_heads, preferred_element_type=jnp.float32)
    row_inner = jnp.sum(attend_full * d_attend, axis=-1, keepdims=True)
    d_scores = (attend_full * (d_attend - row_inner)).astype(jnp.bfloat16)
    d_queries = jnp.einsum(
        "hqk,khd->qhd", d_scores, key_heads, preferred_element_type=jnp.float32
    ) * HD ** (-0.5)
    d_keys = jnp.einsum(
        "hqk,qhd->khd", d_scores, query_heads, preferred_element_type=jnp.float32
    ) * HD ** (-0.5)
    d_values = jnp.einsum(
        "hqk,qhd->khd",
        attend_full.astype(jnp.bfloat16),
        d_mixed,
        preferred_element_type=jnp.float32,
    )
    d_projected = jnp.stack(
        [
            rotate_back(d_queries, cosine_table, sine_table),
            rotate_back(d_keys, cosine_table, sine_table),
            d_values,
        ],
        axis=1,
    )
    d_projected = d_projected.reshape(length, 3 * D).astype(jnp.bfloat16)
    d_normed_one = against(d_projected, qkv_back)
    d_normed_two = against(d_hidden, up_back)
    input_grad = (
        back_rows
        + norm_back(d_normed_one, unit_rows, inverse_rows, back_gains[0])
        + norm_back(d_normed_two, unit_rows, inverse_rows, back_gains[2])
    )
    back_total = jnp.sum(back_rows, axis=0)
    small_grad = jnp.concatenate(
        [
            jnp.sum(d_normed_one * unit_rows, axis=0),
            jnp.sum(d_normed_one, axis=0),
            jnp.sum(d_normed_two * unit_rows, axis=0),
            jnp.sum(d_normed_two, axis=0),
            jnp.sum(d_projected, axis=0, dtype=jnp.float32),
            back_total,
            jnp.sum(d_hidden, axis=0, dtype=jnp.float32),
            back_total,
        ]
    )
    qkv_grad = lax.psum_scatter(
        row_terms(normed_one, d_projected), "fsdp", scatter_dimension=0, tiled=True
    )
    out_grad = lax.psum_scatter(
        row_terms(mixed_heads, back_narrow), "fsdp", scatter_dimension=0, tiled=True
    )
    up_grad = lax.psum_scatter(
        row_terms(normed_two, d_hidden), "fsdp", scatter_dimension=0, tiled=True
    )
    down_grad = lax.psum_scatter(
        row_terms(activated, back_narrow), "fsdp", scatter_dimension=0, tiled=True
    )
    small_part = lax.psum_scatter(small_grad, "fsdp", scatter_dimension=0, tiled=True)
    reduced = lax.psum((qkv_grad, out_grad, up_grad, down_grad, small_part), "dp")
    return (output[None], input_grad.astype(jnp.bfloat16)[None]) + lamb(
        masters, firsts, seconds, reduced
    )


def local_split(
    tokens_in,
    cotangent,
    lengths,
    qkv_master,
    out_master,
    up_master,
    down_master,
    small_master,
    qkv_first,
    out_first,
    up_first,
    down_first,
    small_first,
    qkv_second,
    out_second,
    up_second,
    down_second,
    small_second,
):
    masters = (qkv_master, out_master, up_master, down_master, small_master)
    firsts = (qkv_first, out_first, up_first, down_first, small_first)
    seconds = (qkv_second, out_second, up_second, down_second, small_second)
    qkv_low, out_weight, up_low, down_weight, small_low = (
        master.astype(jnp.bfloat16) for master in masters
    )
    group = lax.axis_size("fsdp")
    me = lax.axis_index("fsdp")
    heads = HEADS // group
    head_cols = heads * HD
    ff_cols = FF // group
    rows = qkv_master.shape[0]
    length = tokens_in.shape[1]
    tokens = group * length

    inputs_all = lax.all_gather(tokens_in[0], "fsdp", axis=0, tiled=True)
    cotangent_all = lax.all_gather(cotangent[0], "fsdp", axis=0, tiled=True)
    lengths_all = lax.all_gather(lengths, "fsdp", axis=0, tiled=True)
    small_all = lax.all_gather(small_low, "fsdp", axis=0, tiled=True)
    qkv_weight = lax.all_to_all(
        qkv_low.reshape(rows, 3, D), "fsdp", split_axis=2, concat_axis=0, tiled=True
    ).reshape(D, 3 * head_cols)
    up_weight = lax.all_to_all(up_low, "fsdp", split_axis=1, concat_axis=0, tiled=True)
    gain_one, shift_one, gain_two, shift_two, qkv_bias, out_bias, up_bias, down_bias = split_small(
        small_all.astype(jnp.float32)
    )
    qkv_bias = lax.dynamic_slice_in_dim(
        qkv_bias.reshape(3, D), me * head_cols, head_cols, axis=1
    ).reshape(3 * head_cols)
    up_bias = lax.dynamic_slice_in_dim(up_bias, me * ff_cols, ff_cols)

    inputs = inputs_all.astype(jnp.float32)
    position = jnp.arange(length)
    live = (position[None, :] < lengths_all[:, None]).astype(jnp.float32).reshape(tokens, 1)
    allowed = (position[None, None, :] <= position[None, :, None]) & (
        position[None, None, :] < lengths_all[:, None, None]
    )
    unit_rows, _ = normalize(inputs)
    normed_one = (unit_rows * gain_one + shift_one).astype(jnp.bfloat16)
    normed_two = (unit_rows * gain_two + shift_two).astype(jnp.bfloat16)
    projected = jnp.dot(normed_one, qkv_weight, preferred_element_type=jnp.float32) + qkv_bias
    projected = projected.reshape(group, length, 3, heads, HD)
    cosine_table, sine_table = rotary_tables(length)
    query_heads = rotate(projected[:, :, 0], cosine_table, sine_table).astype(jnp.bfloat16)
    key_heads = rotate(projected[:, :, 1], cosine_table, sine_table).astype(jnp.bfloat16)
    value_heads = projected[:, :, 2].astype(jnp.bfloat16)
    scores = jnp.einsum(
        "gqhd,gkhd->ghqk", query_heads, key_heads, preferred_element_type=jnp.float32
    ) * HD ** (-0.5)
    scores = jnp.where(allowed[:, None], scores, -1e30)
    row_top = jnp.max(scores, axis=-1, keepdims=True)
    raised = jnp.exp(scores - row_top)
    attend = raised / jnp.sum(raised, axis=-1, keepdims=True)
    attend_low = attend.astype(jnp.bfloat16)
    mixed = jnp.einsum(
        "ghqk,gkhd->gqhd", attend_low, value_heads, preferred_element_type=jnp.float32
    )
    mixed = mixed.reshape(tokens, head_cols).astype(jnp.bfloat16)
    hidden = jnp.dot(normed_two, up_weight, preferred_element_type=jnp.float32) + up_bias
    activated = jax.nn.gelu(hidden, approximate=False).astype(jnp.bfloat16)
    out_part = jnp.dot(mixed, out_weight, preferred_element_type=jnp.float32) + jnp.dot(
        activated, down_weight, preferred_element_type=jnp.float32
    )
    out_sum = lax.psum_scatter(
        out_part.astype(jnp.bfloat16), "fsdp", scatter_dimension=0, tiled=True
    ).astype(jnp.float32)

    own_inputs = tokens_in[0].astype(jnp.float32)
    own_live = (position < lengths[0]).astype(jnp.float32)[:, None]
    own_back = cotangent[0].astype(jnp.float32) * own_live
    own_unit, own_inverse = normalize(own_inputs)
    output = ((own_inputs + out_sum + out_bias + down_bias) * own_live).astype(jnp.bfloat16)

    back = (cotangent_all.astype(jnp.float32) * live).astype(jnp.bfloat16)
    d_hidden = (against(back, down_weight) * gelu_slope(hidden)).astype(jnp.bfloat16)
    d_mixed = against(back, out_weight).astype(jnp.bfloat16).reshape(group, length, heads, HD)
    d_attend = jnp.einsum(
        "gqhd,gkhd->ghqk", d_mixed, value_heads, preferred_element_type=jnp.float32
    )
    row_inner = jnp.sum(attend * d_attend, axis=-1, keepdims=True)
    d_scores = (attend * (d_attend - row_inner)).astype(jnp.bfloat16)
    d_queries = jnp.einsum(
        "ghqk,gkhd->gqhd", d_scores, key_heads, preferred_element_type=jnp.float32
    ) * HD ** (-0.5)
    d_keys = jnp.einsum(
        "ghqk,gqhd->gkhd", d_scores, query_heads, preferred_element_type=jnp.float32
    ) * HD ** (-0.5)
    d_values = jnp.einsum(
        "ghqk,gqhd->gkhd", attend_low, d_mixed, preferred_element_type=jnp.float32
    )
    d_projected = jnp.stack(
        [
            rotate_back(d_queries, cosine_table, sine_table),
            rotate_back(d_keys, cosine_table, sine_table),
            d_values,
        ],
        axis=2,
    )
    d_projected = d_projected.reshape(tokens, 3 * head_cols).astype(jnp.bfloat16)
    d_normed_one = against(d_projected, qkv_weight)
    d_normed_two = against(d_hidden, up_weight)
    scaled_part = d_normed_one * gain_one + d_normed_two * gain_two
    scaled = lax.psum_scatter(
        scaled_part.astype(jnp.bfloat16), "fsdp", scatter_dimension=0, tiled=True
    ).astype(jnp.float32)
    input_grad = own_back + own_inverse * (
        scaled
        - jnp.mean(scaled, axis=-1, keepdims=True)
        - own_unit * jnp.mean(scaled * own_unit, axis=-1, keepdims=True)
    )

    back_total = jnp.sum(own_back, axis=0)
    d_qkv_bias = lax.dynamic_update_slice_in_dim(
        jnp.zeros((3, D), jnp.float32),
        jnp.sum(d_projected, axis=0, dtype=jnp.float32).reshape(3, head_cols),
        me * head_cols,
        axis=1,
    ).reshape(3 * D)
    d_up_bias = lax.dynamic_update_slice_in_dim(
        jnp.zeros((FF,), jnp.float32),
        jnp.sum(d_hidden, axis=0, dtype=jnp.float32),
        me * ff_cols,
        axis=0,
    )
    small_grad = jnp.concatenate(
        [
            jnp.sum(d_normed_one * unit_rows, axis=0),
            jnp.sum(d_normed_one, axis=0),
            jnp.sum(d_normed_two * unit_rows, axis=0),
            jnp.sum(d_normed_two, axis=0),
            d_qkv_bias,
            back_total,
            d_up_bias,
            back_total,
        ]
    )
    small_sum = lax.psum(small_grad, ("dp", "fsdp"))
    small_rows = small_master.shape[0]
    small_sum = lax.dynamic_slice_in_dim(small_sum, me * small_rows, small_rows)
    qkv_term = outer_sum(normed_one, d_projected).astype(jnp.bfloat16)
    qkv_term = lax.all_to_all(
        qkv_term.reshape(D, 3, head_cols), "fsdp", split_axis=0, concat_axis=2, tiled=True
    ).reshape(rows, 3 * D)
    up_term = outer_sum(normed_two, d_hidden).astype(jnp.bfloat16)
    up_term = lax.all_to_all(up_term, "fsdp", split_axis=0, concat_axis=1, tiled=True)
    out_term = outer_sum(mixed, back).astype(jnp.bfloat16)
    down_term = outer_sum(activated, back).astype(jnp.bfloat16)
    summed = lax.psum((qkv_term, out_term, up_term, down_term), "dp")
    reduced = tuple(part.astype(jnp.float32) for part in summed) + (small_sum,)
    return (output[None], input_grad.astype(jnp.bfloat16)[None]) + lamb(
        masters, firsts, seconds, reduced
    )


def lamb(masters, firsts, seconds, reduced):
    updates = []
    first_news = []
    second_news = []
    for first_old, second_old, master, grad_sum in zip(firsts, seconds, masters, reduced):
        first_new = BETA_ONE * first_old + (1.0 - BETA_ONE) * grad_sum
        second_new = BETA_TWO * second_old + (1.0 - BETA_TWO) * grad_sum * grad_sum
        updates.append(first_new / (jnp.sqrt(second_new) + ADAM_EPSILON) + DECAY * master)
        first_news.append(first_new)
        second_news.append(second_new)
    weight_squares, update_squares = lax.psum(
        (local_squares(masters), local_squares(updates)), "fsdp"
    )
    weight_norms = jnp.sqrt(weight_squares)
    update_norms = jnp.sqrt(update_squares)
    new_masters = [
        masters[number] - RATE * (weight_norms[number] / update_norms[number]) * updates[number]
        for number in range(5)
    ]
    lamb_norms = jnp.stack([weight_norms, update_norms])
    return tuple(new_masters) + tuple(first_news) + tuple(second_news) + (lamb_norms,)


def solution(mesh):
    in_specs = (
        P(("dp", "fsdp"), None, None),
        P(("dp", "fsdp"), None, None),
        P(("dp", "fsdp")),
        P("fsdp", None),
        P("fsdp", None),
        P("fsdp", None),
        P("fsdp", None),
        P("fsdp"),
        P("fsdp", None),
        P("fsdp", None),
        P("fsdp", None),
        P("fsdp", None),
        P("fsdp"),
        P("fsdp", None),
        P("fsdp", None),
        P("fsdp", None),
        P("fsdp", None),
        P("fsdp"),
    )
    out_specs = (
        P(("dp", "fsdp"), None, None),
        P(("dp", "fsdp"), None, None),
        P("fsdp", None),
        P("fsdp", None),
        P("fsdp", None),
        P("fsdp", None),
        P("fsdp"),
        P("fsdp", None),
        P("fsdp", None),
        P("fsdp", None),
        P("fsdp", None),
        P("fsdp"),
        P("fsdp", None),
        P("fsdp", None),
        P("fsdp", None),
        P("fsdp", None),
        P("fsdp"),
        P(),
    )
    local = local_split if HEADS % mesh.shape["fsdp"] == 0 else local_rows
    return jax.shard_map(local, mesh=mesh, in_specs=in_specs, out_specs=out_specs, check_vma=False)
```

```python
import math

import jax
import jax.numpy as jnp
from jax import lax
from jax.sharding import PartitionSpec as P

D = 1024
HEADS = 16
HD = 64
FF = 4096
ROT = 16


NORM_EPSILON = 1e-05
ADAM_EPSILON = 1e-06
ROPE_BASE = 10000.0
RATE = 0.5
DECAY = 0.01
BETA_ONE = 0.5
BETA_TWO = 0.5


def split_small(small_vector):
    bounds = [0, D, 2 * D, 3 * D, 4 * D, 7 * D, 8 * D, 8 * D + FF, 9 * D + FF]
    return [small_vector[bounds[number] : bounds[number + 1]] for number in range(8)]


def normalize(values):
    average = jnp.mean(values, axis=-1, keepdims=True)
    centred = values - average
    variance = jnp.mean(centred * centred, axis=-1, keepdims=True)
    inverse = lax.rsqrt(variance + NORM_EPSILON)
    return (centred * inverse, inverse)


def rotary_tables(length):
    half_dims = ROT // 2
    position = jnp.arange(length, dtype=jnp.float32)[:, None]
    number = jnp.arange(half_dims, dtype=jnp.float32)[None, :]
    angle = position * jnp.exp(number * (-2.0 * math.log(ROPE_BASE) / ROT))
    return (jnp.cos(angle)[:, None, :], jnp.sin(angle)[:, None, :])


def rotate(heads_in, cosine_table, sine_table):
    half_dims = ROT // 2
    first_half = heads_in[..., :half_dims]
    second_half = heads_in[..., half_dims:ROT]
    return jnp.concatenate(
        [
            first_half * cosine_table - second_half * sine_table,
            second_half * cosine_table + first_half * sine_table,
            heads_in[..., ROT:],
        ],
        axis=-1,
    )


def rotate_back(grads_in, cosine_table, sine_table):
    half_dims = ROT // 2
    first_half = grads_in[..., :half_dims]
    second_half = grads_in[..., half_dims:ROT]
    return jnp.concatenate(
        [
            first_half * cosine_table + second_half * sine_table,
            second_half * cosine_table - first_half * sine_table,
            grads_in[..., ROT:],
        ],
        axis=-1,
    )


def gelu_slope(values):
    return 0.5 * (1.0 + lax.erf(values * 2.0 ** (-0.5))) + values * jnp.exp(
        -0.5 * values * values
    ) * (2.0 * math.pi) ** (-0.5)


def against(left, right):
    return lax.dot_general(
        left, right, (((1,), (1,)), ((), ())), preferred_element_type=jnp.float32
    )


def outer_sum(columns, right):
    return lax.dot_general(
        columns, right, (((0,), (0,)), ((), ())), preferred_element_type=jnp.float32
    )


def local_squares(arrays):
    return jnp.stack([jnp.sum(array_in * array_in) for array_in in arrays])


def sliced(master, part, parts, pieces):
    rows, columns = master.shape
    width = columns // (pieces * parts)
    return lax.dynamic_index_in_dim(
        master.reshape(rows, pieces, parts, width), part, axis=2, keepdims=False
    ).reshape(rows, pieces * width)


def joined(slices, pieces):
    parts, rows, columns = slices.shape
    width = columns // pieces
    return (
        slices.reshape(parts, rows, pieces, width)
        .transpose(1, 2, 0, 3)
        .reshape(rows, pieces * parts * width)
    )


def layer(x_all, cotangent_all, lengths_all, weights, small_all, part):
    qkv_weight, out_weight, up_weight, down_weight = weights
    group, length, _ = x_all.shape
    tokens = group * length
    head_cols = out_weight.shape[0]
    heads = head_cols // HD
    gain_one, shift_one, gain_two, shift_two, qkv_bias, up_bias = small_all
    inputs = x_all.reshape(tokens, D).astype(jnp.float32)
    position = jnp.arange(length)
    live = (position[None, :] < lengths_all[:, None]).astype(jnp.float32).reshape(tokens, 1)
    allowed = (position[None, None, :] <= position[None, :, None]) & (
        position[None, None, :] < lengths_all[:, None, None]
    )
    unit_rows, _ = normalize(inputs)
    normed_one = (unit_rows * gain_one + shift_one).astype(jnp.bfloat16)
    normed_two = (unit_rows * gain_two + shift_two).astype(jnp.bfloat16)
    projected = jnp.dot(normed_one, qkv_weight, preferred_element_type=jnp.float32) + qkv_bias
    projected = projected.reshape(group, length, 3, heads, HD)
    cosine_table, sine_table = rotary_tables(length)
    query_heads = rotate(projected[:, :, 0], cosine_table, sine_table).astype(jnp.bfloat16)
    key_heads = rotate(projected[:, :, 1], cosine_table, sine_table).astype(jnp.bfloat16)
    value_heads = projected[:, :, 2].astype(jnp.bfloat16)
    scores = jnp.einsum(
        "gqhd,gkhd->ghqk", query_heads, key_heads, preferred_element_type=jnp.float32
    ) * HD ** (-0.5)
    scores = jnp.where(allowed[:, None], scores, -1e30)
    row_top = jnp.max(scores, axis=-1, keepdims=True)
    raised = jnp.exp(scores - row_top)
    attend = raised / jnp.sum(raised, axis=-1, keepdims=True)
    attend_low = attend.astype(jnp.bfloat16)
    mixed = jnp.einsum(
        "ghqk,gkhd->gqhd", attend_low, value_heads, preferred_element_type=jnp.float32
    )
    mixed = mixed.reshape(tokens, head_cols).astype(jnp.bfloat16)
    hidden = jnp.dot(normed_two, up_weight, preferred_element_type=jnp.float32) + up_bias
    activated = jax.nn.gelu(hidden, approximate=False).astype(jnp.bfloat16)
    out_part = jnp.dot(mixed, out_weight, preferred_element_type=jnp.float32) + jnp.dot(
        activated, down_weight, preferred_element_type=jnp.float32
    )

    back = (cotangent_all.reshape(tokens, D).astype(jnp.float32) * live).astype(jnp.bfloat16)
    d_hidden = (against(back, down_weight) * gelu_slope(hidden)).astype(jnp.bfloat16)
    d_mixed = against(back, out_weight).astype(jnp.bfloat16).reshape(group, length, heads, HD)
    d_attend = jnp.einsum(
        "gqhd,gkhd->ghqk", d_mixed, value_heads, preferred_element_type=jnp.float32
    )
    row_inner = jnp.sum(attend * d_attend, axis=-1, keepdims=True)
    d_scores = (attend * (d_attend - row_inner)).astype(jnp.bfloat16)
    d_queries = jnp.einsum(
        "ghqk,gkhd->gqhd", d_scores, key_heads, preferred_element_type=jnp.float32
    ) * HD ** (-0.5)
    d_keys = jnp.einsum(
        "ghqk,gqhd->gkhd", d_scores, query_heads, preferred_element_type=jnp.float32
    ) * HD ** (-0.5)
    d_values = jnp.einsum(
        "ghqk,gqhd->gkhd", attend_low, d_mixed, preferred_element_type=jnp.float32
    )
    d_projected = jnp.stack(
        [
            rotate_back(d_queries, cosine_table, sine_table),
            rotate_back(d_keys, cosine_table, sine_table),
            d_values,
        ],
        axis=2,
    )
    d_projected = d_projected.reshape(tokens, 3 * head_cols).astype(jnp.bfloat16)
    d_normed_one = against(d_projected, qkv_weight)
    d_normed_two = against(d_hidden, up_weight)
    scaled_part = d_normed_one * gain_one + d_normed_two * gain_two
    norm_sums = jnp.stack(
        [
            jnp.sum(d_normed_one * unit_rows, axis=0),
            jnp.sum(d_normed_one, axis=0),
            jnp.sum(d_normed_two * unit_rows, axis=0),
            jnp.sum(d_normed_two, axis=0),
        ]
    )
    d_qkv_bias = jnp.sum(d_projected, axis=0, dtype=jnp.float32)
    d_up_bias = jnp.sum(d_hidden, axis=0, dtype=jnp.float32)
    terms = (
        outer_sum(normed_one, d_projected),
        outer_sum(mixed, back),
        outer_sum(normed_two, d_hidden),
        outer_sum(activated, back),
    )
    return (
        out_part.astype(jnp.bfloat16),
        scaled_part.astype(jnp.bfloat16),
        tuple(term.astype(jnp.bfloat16) for term in terms),
        (norm_sums, d_qkv_bias, d_up_bias),
    )


def local_split(
    tokens_in,
    cotangent,
    lengths,
    qkv_master,
    out_master,
    up_master,
    down_master,
    small_master,
    qkv_first,
    out_first,
    up_first,
    down_first,
    small_first,
    qkv_second,
    out_second,
    up_second,
    down_second,
    small_second,
):
    masters = (qkv_master, out_master, up_master, down_master, small_master)
    firsts = (qkv_first, out_first, up_first, down_first, small_first)
    seconds = (qkv_second, out_second, up_second, down_second, small_second)
    parts, shards = lax.axis_size("dp"), lax.axis_size("fsdp")
    part, shard = lax.axis_index("dp"), lax.axis_index("fsdp")
    length = tokens_in.shape[1]
    head_cols = D // parts
    ff_cols = FF // parts
    ff_rows = down_master.shape[0] // parts

    qkv_own = sliced(qkv_master, part, parts, 3).astype(jnp.bfloat16)
    up_own = sliced(up_master, part, parts, shards).astype(jnp.bfloat16)
    down_own = lax.dynamic_slice_in_dim(down_master, part * ff_rows, ff_rows).astype(jnp.bfloat16)
    out_own = out_master.astype(jnp.bfloat16)
    small_own = small_master.astype(jnp.bfloat16)

    def over_shards(own):
        return lax.all_gather(own, "fsdp", axis=0, tiled=True)

    x_all = lax.all_gather(tokens_in, "dp", axis=0, tiled=True)
    cotangent_all = lax.all_gather(cotangent, "dp", axis=0, tiled=True)
    lengths_all = lax.all_gather(lengths, "dp", axis=0, tiled=True)
    qkv_weight, up_weight, down_weight = (over_shards(w) for w in (qkv_own, up_own, down_own))
    out_weight = lax.dynamic_slice_in_dim(over_shards(out_own), part * head_cols, head_cols)
    gain_one, shift_one, gain_two, shift_two, qkv_bias, out_bias, up_bias, down_bias = split_small(
        over_shards(small_own).astype(jnp.float32)
    )
    qkv_bias = sliced(qkv_bias[None], part, parts, 3)[0]
    up_bias = sliced(up_bias[None], part, parts, shards)[0]

    out_part, scaled_part, terms, sums = layer(
        x_all,
        cotangent_all,
        lengths_all,
        (qkv_weight, out_weight, up_weight, down_weight),
        (gain_one, shift_one, gain_two, shift_two, qkv_bias, up_bias),
        part,
    )
    out_sum = lax.psum_scatter(out_part, "dp", scatter_dimension=0, tiled=True)
    scaled = lax.psum_scatter(scaled_part, "dp", scatter_dimension=0, tiled=True)
    out_sum, scaled = out_sum.astype(jnp.float32), scaled.astype(jnp.float32)

    inputs = tokens_in[0].astype(jnp.float32)
    live = (jnp.arange(length) < lengths[0]).astype(jnp.float32)[:, None]
    back = cotangent[0].astype(jnp.float32) * live
    unit_rows, inverse_rows = normalize(inputs)
    output = ((inputs + out_sum + out_bias + down_bias) * live).astype(jnp.bfloat16)
    input_grad = back + inverse_rows * (
        scaled
        - jnp.mean(scaled, axis=-1, keepdims=True)
        - unit_rows * jnp.mean(scaled * unit_rows, axis=-1, keepdims=True)
    )

    norm_sums, d_qkv_bias, d_up_bias = sums
    back_total = jnp.sum(back, axis=0)

    def spread(values, pieces):
        wide = jnp.zeros((pieces, parts, values.shape[0] // pieces), jnp.float32)
        return lax.dynamic_update_index_in_dim(
            wide, values.reshape(pieces, -1), part, axis=1
        ).reshape(-1)

    small_grad = jnp.concatenate(
        [
            norm_sums.reshape(4 * D),
            spread(d_qkv_bias, 3),
            back_total,
            spread(d_up_bias, shards),
            back_total,
        ]
    )
    small_sum = lax.psum(small_grad, ("dp", "fsdp"))
    small_rows = small_master.shape[0]
    small_sum = lax.dynamic_slice_in_dim(small_sum, shard * small_rows, small_rows)

    qkv_term, out_term, up_term, down_term = terms
    out_wide = lax.dynamic_update_slice_in_dim(
        jnp.zeros((D, D), jnp.bfloat16), out_term, part * head_cols, axis=0
    )

    def to_owner(term):
        own = lax.psum_scatter(term, "fsdp", scatter_dimension=0, tiled=True)
        return lax.all_gather(own, "dp", axis=0, tiled=False).astype(jnp.float32)

    qkv_sum = joined(to_owner(qkv_term), 3)
    up_sum = joined(to_owner(up_term), shards)
    down_sum = to_owner(down_term).reshape(down_master.shape)
    out_sum_grad = lax.psum(
        lax.psum_scatter(out_wide, "fsdp", scatter_dimension=0, tiled=True), "dp"
    ).astype(jnp.float32)
    reduced = (qkv_sum, out_sum_grad, up_sum, down_sum, small_sum)
    return (output[None], input_grad.astype(jnp.bfloat16)[None]) + lamb(
        masters, firsts, seconds, reduced
    )


def lamb(masters, firsts, seconds, reduced):
    updates = []
    first_news = []
    second_news = []
    for first_old, second_old, master, grad_sum in zip(firsts, seconds, masters, reduced):
        first_new = BETA_ONE * first_old + (1.0 - BETA_ONE) * grad_sum
        second_new = BETA_TWO * second_old + (1.0 - BETA_TWO) * grad_sum * grad_sum
        updates.append(first_new / (jnp.sqrt(second_new) + ADAM_EPSILON) + DECAY * master)
        first_news.append(first_new)
        second_news.append(second_new)
    weight_squares, update_squares = lax.psum(
        (local_squares(masters), local_squares(updates)), "fsdp"
    )
    weight_norms = jnp.sqrt(weight_squares)
    update_norms = jnp.sqrt(update_squares)
    new_masters = [
        masters[number] - RATE * (weight_norms[number] / update_norms[number]) * updates[number]
        for number in range(5)
    ]
    lamb_norms = jnp.stack([weight_norms, update_norms])
    return tuple(new_masters) + tuple(first_news) + tuple(second_news) + (lamb_norms,)


def solution(mesh):
    in_specs = (
        P(("dp", "fsdp"), None, None),
        P(("dp", "fsdp"), None, None),
        P(("dp", "fsdp")),
        P("fsdp", None),
        P("fsdp", None),
        P("fsdp", None),
        P("fsdp", None),
        P("fsdp"),
        P("fsdp", None),
        P("fsdp", None),
        P("fsdp", None),
        P("fsdp", None),
        P("fsdp"),
        P("fsdp", None),
        P("fsdp", None),
        P("fsdp", None),
        P("fsdp", None),
        P("fsdp"),
    )
    out_specs = (
        P(("dp", "fsdp"), None, None),
        P(("dp", "fsdp"), None, None),
        P("fsdp", None),
        P("fsdp", None),
        P("fsdp", None),
        P("fsdp", None),
        P("fsdp"),
        P("fsdp", None),
        P("fsdp", None),
        P("fsdp", None),
        P("fsdp", None),
        P("fsdp"),
        P("fsdp", None),
        P("fsdp", None),
        P("fsdp", None),
        P("fsdp", None),
        P("fsdp"),
        P(),
    )
    return jax.shard_map(local_split, mesh=mesh, in_specs=in_specs, out_specs=out_specs, check_vma=False)
```

```python
import math

import jax
import jax.numpy as jnp
from jax import lax
from jax.experimental import pallas as pl
from jax.experimental.pallas import tpu as pltpu
from jax.sharding import PartitionSpec as P

D = 1024
HEADS = 16
HD = 64
FF = 4096
ROT = 16
SMALL = 13312


NORM_EPSILON = 1e-05
ADAM_EPSILON = 1e-06
ROPE_BASE = 10000.0
RATE = 0.5
DECAY = 0.01
BETA_ONE = 0.5
BETA_TWO = 0.5


def split_small(small_vector):
    bounds = [0, D, 2 * D, 3 * D, 4 * D, 7 * D, 8 * D, 8 * D + FF, 9 * D + FF]
    return [small_vector[bounds[number] : bounds[number + 1]] for number in range(8)]


def normalize(values):
    average = jnp.mean(values, axis=-1, keepdims=True)
    centred = values - average
    variance = jnp.mean(centred * centred, axis=-1, keepdims=True)
    inverse = lax.rsqrt(variance + NORM_EPSILON)
    return (centred * inverse, inverse)


def rotary_tables(length):
    half_dims = ROT // 2
    position = jnp.arange(length, dtype=jnp.float32)[:, None]
    number = jnp.arange(half_dims, dtype=jnp.float32)[None, :]
    angle = position * jnp.exp(number * (-2.0 * math.log(ROPE_BASE) / ROT))
    return (jnp.cos(angle)[:, None, :], jnp.sin(angle)[:, None, :])


def rotate(heads_in, cosine_table, sine_table):
    half_dims = ROT // 2
    first_half = heads_in[..., :half_dims]
    second_half = heads_in[..., half_dims:ROT]
    return jnp.concatenate(
        [
            first_half * cosine_table - second_half * sine_table,
            second_half * cosine_table + first_half * sine_table,
            heads_in[..., ROT:],
        ],
        axis=-1,
    )


def rotate_back(grads_in, cosine_table, sine_table):
    half_dims = ROT // 2
    first_half = grads_in[..., :half_dims]
    second_half = grads_in[..., half_dims:ROT]
    return jnp.concatenate(
        [
            first_half * cosine_table + second_half * sine_table,
            second_half * cosine_table - first_half * sine_table,
            grads_in[..., ROT:],
        ],
        axis=-1,
    )


def gelu_slope(values):
    return 0.5 * (1.0 + lax.erf(values * 2.0 ** (-0.5))) + values * jnp.exp(
        -0.5 * values * values
    ) * (2.0 * math.pi) ** (-0.5)


def against(left, right):
    return lax.dot_general(
        left, right, (((1,), (1,)), ((), ())), preferred_element_type=jnp.float32
    )


def outer_sum(columns, right):
    return lax.dot_general(
        columns, right, (((0,), (0,)), ((), ())), preferred_element_type=jnp.float32
    )


def local_squares(arrays):
    return jnp.stack([jnp.sum(array_in * array_in) for array_in in arrays])


def sliced(master, part, parts, pieces):
    rows, columns = master.shape
    width = columns // (pieces * parts)
    return lax.dynamic_index_in_dim(
        master.reshape(rows, pieces, parts, width), part, axis=2, keepdims=False
    ).reshape(rows, pieces * width)


def joined(slices, pieces):
    parts, rows, columns = slices.shape
    width = columns // pieces
    return (
        slices.reshape(parts, rows, pieces, width)
        .transpose(1, 2, 0, 3)
        .reshape(rows, pieces * parts * width)
    )


def layer(x_all, cotangent_all, lengths_all, weights, small_all, part):
    qkv_weight, out_weight, up_weight, down_weight = weights
    group, length, _ = x_all.shape
    tokens = group * length
    head_cols = out_weight.shape[0]
    heads = head_cols // HD
    gain_one, shift_one, gain_two, shift_two, qkv_bias, up_bias = small_all
    inputs = x_all.reshape(tokens, D).astype(jnp.float32)
    position = jnp.arange(length)
    live = (position[None, :] < lengths_all[:, None]).astype(jnp.float32).reshape(tokens, 1)
    allowed = (position[None, None, :] <= position[None, :, None]) & (
        position[None, None, :] < lengths_all[:, None, None]
    )
    unit_rows, _ = normalize(inputs)
    normed_one = (unit_rows * gain_one + shift_one).astype(jnp.bfloat16)
    normed_two = (unit_rows * gain_two + shift_two).astype(jnp.bfloat16)
    projected = jnp.dot(normed_one, qkv_weight, preferred_element_type=jnp.float32) + qkv_bias
    projected = projected.reshape(group, length, 3, heads, HD)
    cosine_table, sine_table = rotary_tables(length)
    query_heads = rotate(projected[:, :, 0], cosine_table, sine_table).astype(jnp.bfloat16)
    key_heads = rotate(projected[:, :, 1], cosine_table, sine_table).astype(jnp.bfloat16)
    value_heads = projected[:, :, 2].astype(jnp.bfloat16)
    scores = jnp.einsum(
        "gqhd,gkhd->ghqk", query_heads, key_heads, preferred_element_type=jnp.float32
    ) * HD ** (-0.5)
    scores = jnp.where(allowed[:, None], scores, -1e30)
    row_top = jnp.max(scores, axis=-1, keepdims=True)
    raised = jnp.exp(scores - row_top)
    attend = raised / jnp.sum(raised, axis=-1, keepdims=True)
    attend_low = attend.astype(jnp.bfloat16)
    mixed = jnp.einsum(
        "ghqk,gkhd->gqhd", attend_low, value_heads, preferred_element_type=jnp.float32
    )
    mixed = mixed.reshape(tokens, head_cols).astype(jnp.bfloat16)
    hidden = jnp.dot(normed_two, up_weight, preferred_element_type=jnp.float32) + up_bias
    activated = jax.nn.gelu(hidden, approximate=False).astype(jnp.bfloat16)
    out_part = jnp.dot(mixed, out_weight, preferred_element_type=jnp.float32) + jnp.dot(
        activated, down_weight, preferred_element_type=jnp.float32
    )

    back = (cotangent_all.reshape(tokens, D).astype(jnp.float32) * live).astype(jnp.bfloat16)
    d_hidden = (against(back, down_weight) * gelu_slope(hidden)).astype(jnp.bfloat16)
    d_mixed = against(back, out_weight).astype(jnp.bfloat16).reshape(group, length, heads, HD)
    d_attend = jnp.einsum(
        "gqhd,gkhd->ghqk", d_mixed, value_heads, preferred_element_type=jnp.float32
    )
    row_inner = jnp.sum(attend * d_attend, axis=-1, keepdims=True)
    d_scores = (attend * (d_attend - row_inner)).astype(jnp.bfloat16)
    d_queries = jnp.einsum(
        "ghqk,gkhd->gqhd", d_scores, key_heads, preferred_element_type=jnp.float32
    ) * HD ** (-0.5)
    d_keys = jnp.einsum(
        "ghqk,gqhd->gkhd", d_scores, query_heads, preferred_element_type=jnp.float32
    ) * HD ** (-0.5)
    d_values = jnp.einsum(
        "ghqk,gqhd->gkhd", attend_low, d_mixed, preferred_element_type=jnp.float32
    )
    d_projected = jnp.stack(
        [
            rotate_back(d_queries, cosine_table, sine_table),
            rotate_back(d_keys, cosine_table, sine_table),
            d_values,
        ],
        axis=2,
    )
    d_projected = d_projected.reshape(tokens, 3 * head_cols).astype(jnp.bfloat16)
    d_normed_one = against(d_projected, qkv_weight)
    d_normed_two = against(d_hidden, up_weight)
    scaled_part = d_normed_one * gain_one + d_normed_two * gain_two
    norm_sums = jnp.stack(
        [
            jnp.sum(d_normed_one * unit_rows, axis=0),
            jnp.sum(d_normed_one, axis=0),
            jnp.sum(d_normed_two * unit_rows, axis=0),
            jnp.sum(d_normed_two, axis=0),
        ]
    )
    d_qkv_bias = jnp.sum(d_projected, axis=0, dtype=jnp.float32)
    d_up_bias = jnp.sum(d_hidden, axis=0, dtype=jnp.float32)
    terms = (
        outer_sum(normed_one, d_projected),
        outer_sum(mixed, back),
        outer_sum(normed_two, d_hidden),
        outer_sum(activated, back),
    )
    return (
        out_part.astype(jnp.bfloat16),
        scaled_part.astype(jnp.bfloat16),
        tuple(term.astype(jnp.bfloat16) for term in terms),
        (norm_sums, d_qkv_bias, d_up_bias),
    )


MESH_ID = pl.DeviceIdType.MESH
HALF = 128


class Place:
    def __init__(self):
        self.part = lax.axis_index("dp")
        self.shard = lax.axis_index("fsdp")
        self.z = self.shard // 2
        self.core = self.shard % 2
        self.x_part = 2 * (self.part // 2) + 1 - self.part % 2
        self.y_part = (self.part + 2) % 4
        self.far_part = 3 - self.part
        self.across_x = (self.x_part, self.shard)
        self.across_y = (self.y_part, self.shard)
        self.across_far = (self.far_part, self.shard)
        self.other_core = (self.part, 2 * self.z + 1 - self.core)
        self.up = (self.part, jnp.minimum(self.shard + 2, 7))
        self.down = (self.part, jnp.maximum(self.shard - 2, 0))

    def shard_after(self, k):
        return (self.part, (self.shard + k) % 8)


def send(source, target, send_sem, recv_sem, device):
    return pltpu.make_async_remote_copy(
        src_ref=source,
        dst_ref=target,
        send_sem=send_sem,
        recv_sem=recv_sem,
        device_id=device,
        device_id_type=MESH_ID,
    )


def arrived(target, recv_sem, device):
    send(target, target, recv_sem, recv_sem, device).wait_recv()


def sent(source, send_sem, device):
    send(source, source, send_sem, send_sem, device).wait_send()


def greet(at):
    barrier = pltpu.get_barrier_semaphore()
    peers = [at.across_x, at.across_y, at.across_far] + [at.shard_after(k) for k in range(1, 8)]
    for peer in peers:
        pl.semaphore_signal(barrier, inc=1, device_id=peer, device_id_type=MESH_ID)
    pl.semaphore_wait(barrier, len(peers))


def gather_kernel(
    x_own,
    cot_own,
    len_own,
    w_own,
    out_own,
    small_own,
    x_all,
    cot_all,
    len_all,
    w_all,
    out_all,
    small_all,
    plane_send,
    plane_recv,
    len_send,
    len_recv,
    w_send,
    w_recv,
    out_send,
    out_recv,
    small_send,
    small_recv,
):
    at = Place()
    z, core, part, shard = at.z, at.core, at.part, at.shard
    greet(at)
    spans = ((0, 768), (768, 1792), (1792, 2816))

    def piece(ref, slot, n):
        return ref.at[slot, :, spans[n][0] : spans[n][1]]

    for n, (low, high) in enumerate(spans):
        own = w_own.at[:, low:high]
        target = piece(w_all, shard, n)

        @pl.when(z < 3)
        def _():
            send(own, target, w_send.at[0, n, z], w_recv.at[n, shard], at.up).start()

        @pl.when(z > 0)
        def _():
            send(own, target, w_send.at[1, n, z], w_recv.at[n, shard], at.down).start()

        send(own, target, w_send.at[2, n, z], w_recv.at[n, shard], at.other_core).start()

    @pl.when(z == part)
    def _():
        @pl.when(z < 3)
        def _():
            send(out_own, out_all.at[core], out_send.at[0], out_recv.at[core], at.up).start()

        @pl.when(z > 0)
        def _():
            send(out_own, out_all.at[core], out_send.at[1], out_recv.at[core], at.down).start()

        send(out_own, out_all.at[core], out_send.at[2], out_recv.at[core], at.other_core).start()
        out_all[core] = out_own[...]

    activations = ((x_own, x_all), (cot_own, cot_all))
    for n, (own, whole) in enumerate(activations):
        send(own, whole.at[part], plane_send.at[n, 0], plane_recv.at[n, 0], at.across_x).start()
        send(own, whole.at[part], plane_send.at[n, 1], plane_recv.at[n, 1], at.across_y).start()
    for n, peer in enumerate((at.across_x, at.across_y, at.across_far)):
        send(len_own, len_all.at[part], len_send.at[n], len_recv.at[n], peer).start()
    for k in range(1, 8):
        send(
            small_own,
            small_all.at[shard],
            small_send.at[k - 1],
            small_recv.at[k - 1],
            at.shard_after(k),
        ).start()
    x_all[part] = x_own[...]
    cot_all[part] = cot_own[...]
    len_all[part] = len_own[...]
    w_all[shard] = w_own[...]
    small_all[shard] = small_own[...]

    for n in range(3):
        for k in range(1, 4):

            @pl.when(z >= k)
            def _():
                source = 2 * (z - k) + core
                block = piece(w_all, source, n)
                arrived(block, w_recv.at[n, source], at.down)

                @pl.when(z < 3)
                def _():
                    send(block, block, w_send.at[0, n, z - k], w_recv.at[n, source], at.up).start()

                send(
                    block, block, w_send.at[2, n, z - k], w_recv.at[n, source], at.other_core
                ).start()

            @pl.when(z + k <= 3)
            def _():
                source = 2 * (z + k) + core
                block = piece(w_all, source, n)
                arrived(block, w_recv.at[n, source], at.up)

                @pl.when(z > 0)
                def _():
                    send(
                        block, block, w_send.at[1, n, z + k], w_recv.at[n, source], at.down
                    ).start()

                send(
                    block, block, w_send.at[2, n, z + k], w_recv.at[n, source], at.other_core
                ).start()

    @pl.when(z != part)
    def _():
        block = out_all.at[core]
        arrived(block, out_recv.at[core], at.up)

        @pl.when((z > part) & (z < 3))
        def _():
            send(block, block, out_send.at[0], out_recv.at[core], at.up).start()

        @pl.when((z < part) & (z > 0))
        def _():
            send(block, block, out_send.at[1], out_recv.at[core], at.down).start()

        send(block, block, out_send.at[2], out_recv.at[core], at.other_core).start()

    for n, (_, whole) in enumerate(activations):
        arrived(whole.at[at.x_part], plane_recv.at[n, 0], at.across_x)
        block = whole.at[at.x_part, 0:HALF]
        send(block, block, plane_send.at[n, 2], plane_recv.at[n, 2], at.across_y).start()
        arrived(whole.at[at.y_part], plane_recv.at[n, 1], at.across_y)
        block = whole.at[at.y_part, HALF : 2 * HALF]
        send(block, block, plane_send.at[n, 3], plane_recv.at[n, 3], at.across_x).start()

    for n, (own, whole) in enumerate(activations):
        arrived(whole.at[at.far_part, 0:HALF], plane_recv.at[n, 2], at.across_y)
        arrived(whole.at[at.far_part, HALF : 2 * HALF], plane_recv.at[n, 3], at.across_x)
        sent(own, plane_send.at[n, 0], at.across_x)
        sent(own, plane_send.at[n, 1], at.across_y)
        sent(whole.at[at.x_part, 0:HALF], plane_send.at[n, 2], at.across_y)
        sent(whole.at[at.y_part, HALF : 2 * HALF], plane_send.at[n, 3], at.across_x)
    for n, (peer, other) in enumerate(
        ((at.across_x, at.x_part), (at.across_y, at.y_part), (at.across_far, at.far_part))
    ):
        arrived(len_all.at[other], len_recv.at[n], peer)
        sent(len_own, len_send.at[n], peer)
    for k in range(1, 8):
        arrived(small_all.at[(shard + 8 - k) % 8], small_recv.at[k - 1], at.shard_after(8 - k))
        sent(small_own, small_send.at[k - 1], at.shard_after(k))
    for n in range(3):
        for other in range(4):
            block = piece(w_all, 2 * other + 1 - core, n)
            arrived(block, w_recv.at[n, 2 * other + 1 - core], at.other_core)
            sent(block, w_send.at[2, n, other], at.other_core)

            @pl.when((other <= z) & (z < 3))
            def _():
                sent(block, w_send.at[0, n, other], at.up)

            @pl.when((other >= z) & (z > 0))
            def _():
                sent(block, w_send.at[1, n, other], at.down)

    arrived(out_all.at[1 - core], out_recv.at[1 - core], at.other_core)
    sent(out_own, out_send.at[2], at.other_core)

    @pl.when((z >= part) & (z < 3))
    def _():
        sent(out_own, out_send.at[0], at.up)

    @pl.when((z <= part) & (z > 0))
    def _():
        sent(out_own, out_send.at[1], at.down)


VMEM_SPEC = pl.BlockSpec(memory_space=pltpu.VMEM)


def gather(x_own, cot_own, len_own, w_own, out_own, small_own):
    shape = jax.ShapeDtypeStruct
    dma = pltpu.SemaphoreType.DMA
    return pl.pallas_call(
        gather_kernel,
        out_shape=(
            shape((4,) + x_own.shape, jnp.bfloat16),
            shape((4,) + x_own.shape, jnp.bfloat16),
            shape((4,) + len_own.shape, jnp.float32),
            shape((8,) + w_own.shape, jnp.bfloat16),
            shape((2,) + out_own.shape, jnp.bfloat16),
            shape((8,) + small_own.shape, jnp.float32),
        ),
        in_specs=[VMEM_SPEC] * 6,
        out_specs=(VMEM_SPEC,) * 6,
        scratch_shapes=[
            dma((2, 4)),
            dma((2, 4)),
            dma((3,)),
            dma((3,)),
            dma((3, 3, 4)),
            dma((3, 8)),
            dma((3,)),
            dma((2,)),
            dma((7,)),
            dma((7,)),
        ],
        compiler_params=pltpu.CompilerParams(
            collective_id=0, has_side_effects=True, vmem_limit_bytes=60 << 20
        ),
        name="gather",
    )(x_own, cot_own, len_own, w_own, out_own, small_own)


def reduce_kernel(
    out_part,
    dx_part,
    terms,
    out_term,
    small_part,
    out_sum,
    dx_sum,
    terms_all,
    out_grad,
    small_sum,
    plane_one,
    plane_two,
    plane_turn,
    core_in,
    line_sum,
    line_in,
    out_core_in,
    out_line,
    out_line_in,
    small_in,
    small_own,
    small_plane,
    plane_send,
    plane_recv,
    core_send,
    core_recv,
    line_send,
    line_recv,
    out_send,
    out_recv,
    all_send,
    all_recv,
    small_send,
    small_recv,
):
    at = Place()
    z, core, part, shard = at.z, at.core, at.part, at.shard
    greet(at)
    spans = ((1792, 2816), (768, 1792), (0, 768))
    first, second = slice(0, HALF), slice(HALF, 2 * HALF)
    f32, bf16 = jnp.float32, jnp.bfloat16

    for n, (low, high) in enumerate(spans):
        for other in range(4):
            send(
                terms.at[2 * other + 1 - core, :, low:high],
                core_in.at[other, :, low:high],
                core_send.at[n, other],
                core_recv.at[n, other],
                at.other_core,
            ).start()
    send(out_term.at[1 - core], out_core_in, out_send.at[0], out_recv.at[0], at.other_core).start()
    for k in range(1, 8):
        send(
            small_part.at[(shard + k) % 8],
            small_in.at[k - 1],
            small_send.at[k - 1],
            small_recv.at[k - 1],
            at.shard_after(k),
        ).start()

    parts = (out_part, dx_part)
    routes = (
        (first, at.across_x, at.x_part, at.across_y, at.y_part),
        (second, at.across_y, at.y_part, at.across_x, at.x_part),
    )
    for n, term in enumerate(parts):
        for r, (rows, peer, peer_part, _, _) in enumerate(routes):
            for m, target in enumerate((at.far_part, peer_part)):
                send(
                    term.at[target, rows],
                    plane_one.at[n, r, m],
                    plane_send.at[n, r, m],
                    plane_recv.at[n, r, m],
                    peer,
                ).start()

    def forward(n, target):
        low, high = spans[n]
        block = line_sum.at[target, :, low:high]

        @pl.when(z < target)
        def _():
            @pl.when(z > 0)
            def _():
                arrived(line_in.at[target, :, low:high], line_recv.at[n, target], at.down)
                block[...] = (
                    block[...].astype(f32) + line_in[target, :, low:high].astype(f32)
                ).astype(bf16)

            send(
                block,
                line_in.at[target, :, low:high],
                line_send.at[n, target],
                line_recv.at[n, target],
                at.up,
            ).start()

        @pl.when(z > target)
        def _():
            @pl.when(z < 3)
            def _():
                arrived(line_in.at[target, :, low:high], line_recv.at[n, target], at.up)
                block[...] = (
                    block[...].astype(f32) + line_in[target, :, low:high].astype(f32)
                ).astype(bf16)

            @pl.when(z - 1 == target)
            def _():
                send(
                    block,
                    line_in.at[4, :, low:high],
                    line_send.at[n, target],
                    line_recv.at[n, 4],
                    at.down,
                ).start()

            @pl.when(z - 1 > target)
            def _():
                send(
                    block,
                    line_in.at[target, :, low:high],
                    line_send.at[n, target],
                    line_recv.at[n, target],
                    at.down,
                ).start()

    def own_line(n):
        low, high = spans[n]
        block = line_sum.at[z, :, low:high]

        @pl.when(z > 0)
        def _():
            arrived(line_in.at[z, :, low:high], line_recv.at[n, z], at.down)
            block[...] = (block[...].astype(f32) + line_in[z, :, low:high].astype(f32)).astype(bf16)

        @pl.when(z < 3)
        def _():
            arrived(line_in.at[4, :, low:high], line_recv.at[n, 4], at.up)
            block[...] = (block[...].astype(f32) + line_in[4, :, low:high].astype(f32)).astype(bf16)

        terms_all[part, :, low:high] = block[...]
        own = terms_all.at[part, :, low:high]
        send(own, own, all_send.at[n, 0], all_recv.at[n, 0], at.across_x).start()
        send(own, own, all_send.at[n, 1], all_recv.at[n, 1], at.across_y).start()

    for n, (low, high) in enumerate(spans):
        for other in (3, 0, 2, 1):
            arrived(core_in.at[other, :, low:high], core_recv.at[n, other], at.other_core)
            line_sum[other, :, low:high] = (
                terms[2 * other + core, :, low:high].astype(f32)
                + core_in[other, :, low:high].astype(f32)
            ).astype(bf16)
        for target in (3, 0, 2, 1):
            forward(n, target)

    arrived(out_core_in, out_recv.at[0], at.other_core)
    out_line[...] = (out_term[core].astype(f32) + out_core_in[...].astype(f32)).astype(bf16)

    @pl.when((z < part) & (z > 0))
    def _():
        arrived(out_line_in.at[0], out_recv.at[1], at.down)
        out_line[...] = (out_line[...].astype(f32) + out_line_in[0].astype(f32)).astype(bf16)

    @pl.when((z > part) & (z < 3))
    def _():
        arrived(out_line_in.at[1], out_recv.at[2], at.up)
        out_line[...] = (out_line[...].astype(f32) + out_line_in[1].astype(f32)).astype(bf16)

    @pl.when(z < part)
    def _():
        send(out_line, out_line_in.at[0], out_send.at[1], out_recv.at[1], at.up).start()

    @pl.when(z > part)
    def _():
        send(out_line, out_line_in.at[1], out_send.at[1], out_recv.at[2], at.down).start()

    for n, term in enumerate(parts):
        for r, (rows, peer, _, turn, turn_part) in enumerate(routes):
            arrived(plane_one.at[n, r, 0], plane_recv.at[n, r, 0], peer)
            plane_turn[n, r] = (
                term[turn_part, rows].astype(f32) + plane_one[n, r, 0].astype(f32)
            ).astype(bf16)
            send(
                plane_turn.at[n, r],
                plane_two.at[n, r],
                plane_send.at[n, r, 2],
                plane_recv.at[n, r, 2],
                turn,
            ).start()

    total = small_part[shard]
    for k in range(1, 8):
        arrived(small_in.at[k - 1], small_recv.at[k - 1], at.shard_after(8 - k))
        total = total + small_in[k - 1]
    small_own[...] = total
    plane_peers = (
        (at.across_x, at.x_part),
        (at.across_y, at.y_part),
        (at.across_far, at.far_part),
    )
    for n, (peer, _) in enumerate(plane_peers):
        send(
            small_own, small_plane.at[part], small_send.at[7 + n], small_recv.at[7 + n], peer
        ).start()
    small_plane[part] = total

    for n, (term, result) in enumerate(((out_part, out_sum), (dx_part, dx_sum))):
        for r, (rows, peer, _, turn, _) in enumerate(routes):
            arrived(plane_one.at[n, r, 1], plane_recv.at[n, r, 1], peer)
            arrived(plane_two.at[n, r], plane_recv.at[n, r, 2], turn)
            result[rows] = (
                term[part, rows].astype(f32)
                + plane_one[n, r, 1].astype(f32)
                + plane_two[n, r].astype(f32)
            )

    for n in range(3):
        own_line(n)

    @pl.when(z == part)
    def _():
        @pl.when(z > 0)
        def _():
            arrived(out_line_in.at[0], out_recv.at[1], at.down)
            out_line[...] = (out_line[...].astype(f32) + out_line_in[0].astype(f32)).astype(bf16)

        @pl.when(z < 3)
        def _():
            arrived(out_line_in.at[1], out_recv.at[2], at.up)
            out_line[...] = (out_line[...].astype(f32) + out_line_in[1].astype(f32)).astype(bf16)

        for n, (peer, _) in enumerate(plane_peers):
            send(out_line, out_grad, out_send.at[2 + n], out_recv.at[3], peer).start()
        out_grad[...] = out_line[...]

    @pl.when(z != part)
    def _():
        arrived(out_grad, out_recv.at[3], at.across_x)

    for n, (low, high) in enumerate(spans):
        arrived(terms_all.at[at.x_part, :, low:high], all_recv.at[n, 0], at.across_x)
        block = terms_all.at[at.x_part, 0:64, low:high]
        send(block, block, all_send.at[n, 2], all_recv.at[n, 2], at.across_y).start()
        arrived(terms_all.at[at.y_part, :, low:high], all_recv.at[n, 1], at.across_y)
        block = terms_all.at[at.y_part, 64:128, low:high]
        send(block, block, all_send.at[n, 3], all_recv.at[n, 3], at.across_x).start()

    for n, (peer, other) in enumerate(plane_peers):
        arrived(small_plane.at[other], small_recv.at[7 + n], peer)
    small_sum[...] = (small_plane[0] + small_plane[1]) + (small_plane[2] + small_plane[3])

    for n, (low, high) in enumerate(spans):
        arrived(terms_all.at[at.far_part, 0:64, low:high], all_recv.at[n, 2], at.across_y)
        arrived(terms_all.at[at.far_part, 64:128, low:high], all_recv.at[n, 3], at.across_x)
        whole = terms_all.at[part, :, low:high]
        sent(whole, all_send.at[n, 0], at.across_x)
        sent(whole, all_send.at[n, 1], at.across_y)
        sent(terms_all.at[part, 0:64, low:high], all_send.at[n, 2], at.across_y)
        sent(terms_all.at[part, 64:128, low:high], all_send.at[n, 3], at.across_x)
        for other in range(4):
            block = line_sum.at[other, :, low:high]
            sent(block, core_send.at[n, other], at.other_core)

            @pl.when(z != other)
            def _():
                sent(block, line_send.at[n, other], at.up)

    for n in range(2):
        for r in range(2):
            for m in range(3):
                sent(plane_turn.at[n, r], plane_send.at[n, r, m], at.across_x)
    sent(out_line, out_send.at[0], at.other_core)

    @pl.when(z != part)
    def _():
        sent(out_line, out_send.at[1], at.up)

    @pl.when(z == part)
    def _():
        for n, (peer, _) in enumerate(plane_peers):
            sent(out_line, out_send.at[2 + n], peer)

    for k in range(1, 8):
        sent(small_own, small_send.at[k - 1], at.shard_after(k))
    for n, (peer, _) in enumerate(plane_peers):
        sent(small_own, small_send.at[7 + n], peer)


def reduce(out_part, dx_part, terms, out_term, small_part):
    shape = jax.ShapeDtypeStruct
    dma = pltpu.SemaphoreType.DMA
    vmem = pltpu.VMEM
    _, length, width = out_part.shape
    _, rows, wide = terms.shape
    bf16, f32 = jnp.bfloat16, jnp.float32
    small = small_part.shape[1:]
    return pl.pallas_call(
        reduce_kernel,
        out_shape=(
            shape((length, width), f32),
            shape((length, width), f32),
            shape((4, rows, wide), bf16),
            shape((rows, width), bf16),
            shape(small, f32),
        ),
        in_specs=[VMEM_SPEC] * 5,
        out_specs=(VMEM_SPEC,) * 5,
        scratch_shapes=[
            vmem((2, 2, 2, HALF, width), bf16),
            vmem((2, 2, HALF, width), bf16),
            vmem((2, 2, HALF, width), bf16),
            vmem((4, rows, wide), bf16),
            vmem((4, rows, wide), bf16),
            vmem((5, rows, wide), bf16),
            vmem((rows, width), bf16),
            vmem((rows, width), bf16),
            vmem((2, rows, width), bf16),
            vmem((7,) + small, f32),
            vmem(small, f32),
            vmem((4,) + small, f32),
            dma((2, 2, 3)),
            dma((2, 2, 3)),
            dma((3, 4)),
            dma((3, 4)),
            dma((3, 4)),
            dma((3, 5)),
            dma((5,)),
            dma((4,)),
            dma((3, 4)),
            dma((3, 4)),
            dma((10,)),
            dma((10,)),
        ],
        compiler_params=pltpu.CompilerParams(
            collective_id=1, has_side_effects=True, vmem_limit_bytes=60 << 20
        ),
        name="reduce",
    )(out_part, dx_part, terms, out_term, small_part)


def nt(a,b): return lax.dot_general(a,b,(((1,),(1,)),((),())),preferred_element_type=jnp.float32)
def tn(a,b): return lax.dot_general(a,b,(((0,),(0,)),((),())),preferred_element_type=jnp.float32)
def nn(a,b): return jnp.dot(a,b,preferred_element_type=jnp.float32)
def flat(v): return v.reshape(v.shape[0]*v.shape[1], v.shape[2])

def compute_kernel(x_ref,cot_ref,len_ref,w_ref,wout_ref,gains_ref,qb_ref,ub_ref,tab_ref,
                   outp_ref,dxp_ref,g_ref,gout_ref,sums_ref,dqb_ref,dub_ref,
                   unit_s,n1_s,n2_s,back_s,mix_s,dp_s,act_s,dh_s,sc_s):
    group,length,_=x_ref.shape
    hc=wout_ref.shape[0]*wout_ref.shape[1]
    nh=hc//HD
    Q=3*hc; U=ub_ref.shape[1]
    RB=64
    sums_ref[...]=jnp.zeros_like(sums_ref); dqb_ref[...]=jnp.zeros_like(dqb_ref); dub_ref[...]=jnp.zeros_like(dub_ref)
    row=lax.broadcasted_iota(jnp.int32,(length,length),0)
    col=lax.broadcasted_iota(jnp.int32,(length,length),1)
    causal=col<=row
    lane=lax.broadcasted_iota(jnp.int32,(length,hc),1)
    def norm_rows(s):
        @pl.loop(0,length//RB)
        def _(i):
            r=pl.ds(pl.multiple_of(i*RB,RB),RB)
            x=x_ref[s,r,:].astype(jnp.float32)
            mean=jnp.mean(x,axis=-1,keepdims=True)
            c=x-mean
            var=jnp.mean(c*c,axis=-1,keepdims=True)
            u=c*lax.rsqrt(var+1e-5)
            unit_s[s,r,:]=u
            n1_s[s,r,:]=(u*gains_ref[0:1]+gains_ref[1:2]).astype(jnp.bfloat16)
            n2_s[s,r,:]=(u*gains_ref[2:3]+gains_ref[3:4]).astype(jnp.bfloat16)
            rows=lax.broadcasted_iota(jnp.int32,(RB,1),0)+i*RB
            live=rows.astype(jnp.float32)<len_ref[s][0:1,0:1]
            back_s[s,r,:]=jnp.where(live,cot_ref[s,r,:],jnp.zeros((),jnp.bfloat16))
    def attn(s):
        norm_rows(s)
        w=flat(w_ref[:,:,0:Q])
        wout=flat(wout_ref[...])
        p=nn(n1_s[s],w)+qb_ref[...]
        C=tab_ref[0];S1=tab_ref[1];S2=tab_ref[2]
        def rot(v): return v*C+pltpu.roll(v,hc-8,1)*S1+pltpu.roll(v,8,1)*S2
        def rotb(v): return v*C-pltpu.roll(v,hc-8,1)*S1-pltpu.roll(v,8,1)*S2
        q=rot(p[:,0:hc]).astype(jnp.bfloat16); k=rot(p[:,hc:2*hc]).astype(jnp.bfloat16); v=p[:,2*hc:].astype(jnp.bfloat16)
        back=back_s[s]
        dm=nt(back,wout).astype(jnp.bfloat16)
        allowed=causal&(col.astype(jnp.float32)<len_ref[s][0:1,0:1])
        zero=jnp.zeros((),jnp.bfloat16)
        mixed=jnp.zeros((length,hc),jnp.float32); dq=mixed; dk=mixed; dv=mixed
        for h in range(nh):
            m=(lane>=h*HD)&(lane<(h+1)*HD)
            qh=jnp.where(m,q,zero);kh=jnp.where(m,k,zero);vh=jnp.where(m,v,zero);dmh=jnp.where(m,dm,zero)
            sc=jnp.where(allowed,nt(qh,k)*HD**-0.5,-1e30)
            e=jnp.exp(sc-jnp.max(sc,axis=-1,keepdims=True))
            A=e*(1.0/jnp.sum(e,axis=-1,keepdims=True))
            Ab=A.astype(jnp.bfloat16)
            mixed=mixed+nn(Ab,vh)
            dA=nt(dmh,v)
            dS=(A*(dA-jnp.sum(A*dA,axis=-1,keepdims=True))).astype(jnp.bfloat16)
            dq=dq+nn(dS,kh); dk=dk+tn(dS,qh); dv=dv+tn(Ab,dmh)
        mix_s[s]=mixed.astype(jnp.bfloat16)
        dq=rotb(dq*HD**-0.5).astype(jnp.bfloat16); dk=rotb(dk*HD**-0.5).astype(jnp.bfloat16); dv=dv.astype(jnp.bfloat16)
        dp_s[s,:,0:hc]=dq; dp_s[s,:,hc:2*hc]=dk; dp_s[s,:,2*hc:]=dv
        for i,t in enumerate((dq,dk,dv)):
            dqb_ref[:,i*hc:(i+1)*hc]+=jnp.sum(t.astype(jnp.float32),axis=0,keepdims=True)
        dn=nt(dp_s[s],w)
        sums_ref[0:1]+=jnp.sum(dn*unit_s[s],axis=0,keepdims=True)
        sums_ref[1:2]+=jnp.sum(dn,axis=0,keepdims=True)
        sc_s[s]=dn*gains_ref[0:1]
    @pl.loop(0,group)
    def _(s): attn(s)
    def grads(lhs_s,rhs,lo,hi):
        @pl.loop(0,w_ref.shape[0])
        def _(f):
            c=pl.ds(pl.multiple_of(f*128,128),128)
            g_ref[f,:,lo:hi]=tn(flat(lhs_s[:,:,c]),rhs).astype(jnp.bfloat16)
    for i in range(wout_ref.shape[0]):
        gout_ref[i]=tn(flat(mix_s[:,:,i*128:(i+1)*128]),flat(back_s[...])).astype(jnp.bfloat16)
    grads(n1_s,flat(dp_s[...]),0,Q)
    def mlp(s):
        wup=flat(w_ref[:,:,Q:Q+U]); wdown=flat(w_ref[:,:,Q+U:])
        h=nn(n2_s[s],wup)+ub_ref[...]
        cdf=0.5*(1.0+lax.erf(h*2.0**-0.5))
        act=(h*cdf).astype(jnp.bfloat16)
        act_s[s]=act
        slope=cdf+h*jnp.exp(-0.5*h*h)*(2*math.pi)**-0.5
        outp_ref[s]=(nn(act,wdown)+nn(mix_s[s],flat(wout_ref[...]))).astype(jnp.bfloat16)
        dh=(nt(back_s[s],wdown)*slope).astype(jnp.bfloat16)
        dh_s[s]=dh
        dub_ref[...]+=jnp.sum(dh.astype(jnp.float32),axis=0,keepdims=True)
        dn=nt(dh,wup)
        sums_ref[2:3]+=jnp.sum(dn*unit_s[s],axis=0,keepdims=True)
        sums_ref[3:4]+=jnp.sum(dn,axis=0,keepdims=True)
        dxp_ref[s]=(sc_s[s]+dn*gains_ref[2:3]).astype(jnp.bfloat16)
    @pl.loop(0,group)
    def _(s): mlp(s)
    grads(n2_s,flat(dh_s[...]),Q,Q+U)
    grads(act_s,flat(back_s[...]),Q+U,Q+2*U)

def rope_tables(length, heads):
    cosine, sine = (table[:, 0] for table in rotary_tables(length))
    rest = (length, HD - ROT)
    none = jnp.zeros_like(sine)
    tables = (
        jnp.concatenate([cosine, cosine, jnp.ones(rest)], axis=1),
        jnp.concatenate([-sine, none, jnp.zeros(rest)], axis=1),
        jnp.concatenate([none, sine, jnp.zeros(rest)], axis=1),
    )
    return jnp.stack([jnp.tile(table, (1, heads)) for table in tables])


def compute(x_all,cot_all,lens,w_all,wout,gains,qb,ub,tab):
    group,length,_=x_all.shape
    Q=qb.shape[1];U=ub.shape[1];hc=Q//3
    V=pl.BlockSpec(memory_space=pltpu.VMEM)
    S=jax.ShapeDtypeStruct
    big=lambda w,t: pltpu.VMEM((group,length,w),t)
    return pl.pallas_call(compute_kernel,
        out_shape=(S((group,length,D),jnp.bfloat16),S((group,length,D),jnp.bfloat16),S(w_all.shape,jnp.bfloat16),S(wout.shape,jnp.bfloat16),S((4,D),jnp.float32),S((1,Q),jnp.float32),S((1,U),jnp.float32)),
        in_specs=[V]*9,out_specs=(V,)*7,
        scratch_shapes=[big(D,jnp.float32),big(D,jnp.bfloat16),big(D,jnp.bfloat16),big(D,jnp.bfloat16),big(hc,jnp.bfloat16),big(Q,jnp.bfloat16),big(U,jnp.bfloat16),big(U,jnp.bfloat16),big(D,jnp.float32)],
        compiler_params=pltpu.CompilerParams(vmem_limit_bytes=62<<20),name="compute")(x_all,cot_all,lens,w_all,wout,gains,qb,ub,tab)


def local_split(
    tokens_in,
    cotangent,
    lengths,
    qkv_master,
    out_master,
    up_master,
    down_master,
    small_master,
    qkv_first,
    out_first,
    up_first,
    down_first,
    small_first,
    qkv_second,
    out_second,
    up_second,
    down_second,
    small_second,
):
    masters = (qkv_master, out_master, up_master, down_master, small_master)
    firsts = (qkv_first, out_first, up_first, down_first, small_first)
    seconds = (qkv_second, out_second, up_second, down_second, small_second)
    parts, shards = lax.axis_size("dp"), lax.axis_size("fsdp")
    part, shard = lax.axis_index("dp"), lax.axis_index("fsdp")
    length = tokens_in.shape[1]
    head_cols = D // parts
    ff_cols = FF // parts
    ff_rows = down_master.shape[0] // parts

    qkv_own = sliced(qkv_master, part, parts, 3).astype(jnp.bfloat16)
    up_own = sliced(up_master, part, parts, shards).astype(jnp.bfloat16)
    down_own = lax.dynamic_slice_in_dim(down_master, part * ff_rows, ff_rows).astype(jnp.bfloat16)
    out_own = out_master.astype(jnp.bfloat16)
    small_own = small_master.astype(jnp.bfloat16)
    own = (parts, shards) == (4, 8)

    def small_vectors(small_all):
        vectors = split_small(small_all)
        vectors[4] = sliced(vectors[4][None], part, parts, 3)[0]
        vectors[6] = sliced(vectors[6][None], part, parts, shards)[0]
        return vectors

    if own:
        small_rows = small_master.shape[0]
        padded = jnp.pad(small_own.astype(jnp.float32), (0, 2048 - small_rows)).reshape(16, 128)
        x_all, cotangent_all, lengths_all, w_all, out_all, small_all = gather(
            tokens_in[0],
            cotangent[0],
            jnp.broadcast_to(lengths.astype(jnp.float32)[:, None], (8, 128)),
            jnp.concatenate([qkv_own, up_own, down_own], axis=1),
            out_own,
            padded,
        )
        small_all = small_all.reshape(shards, 2048)[:, :small_rows].reshape(SMALL)
        gain_one, shift_one, gain_two, shift_two, qkv_bias, out_bias, up_bias, down_bias = (
            small_vectors(small_all)
        )
        out_part, scaled_part, terms, out_term, norm_sums, d_qkv_bias, d_up_bias = compute(
            x_all,
            cotangent_all,
            lengths_all,
            w_all,
            out_all,
            jnp.stack([gain_one, shift_one, gain_two, shift_two]),
            qkv_bias[None],
            up_bias[None],
            rope_tables(length, head_cols // HD),
        )
        d_qkv_bias, d_up_bias = d_qkv_bias[0], d_up_bias[0]
    else:

        def over_shards(own):
            return lax.all_gather(own, "fsdp", axis=0, tiled=True)

        x_all = lax.all_gather(tokens_in, "dp", axis=0, tiled=True)
        cotangent_all = lax.all_gather(cotangent, "dp", axis=0, tiled=True)
        lengths_all = lax.all_gather(lengths, "dp", axis=0, tiled=True)
        qkv_weight, up_weight, down_weight = (over_shards(w) for w in (qkv_own, up_own, down_own))
        out_weight = lax.dynamic_slice_in_dim(over_shards(out_own), part * head_cols, head_cols)
        gain_one, shift_one, gain_two, shift_two, qkv_bias, out_bias, up_bias, down_bias = (
            small_vectors(over_shards(small_own).astype(jnp.float32))
        )
        out_part, scaled_part, terms, sums = layer(
            x_all,
            cotangent_all,
            lengths_all,
            (qkv_weight, out_weight, up_weight, down_weight),
            (gain_one, shift_one, gain_two, shift_two, qkv_bias, up_bias),
            part,
        )
        norm_sums, d_qkv_bias, d_up_bias = sums
        out_sum = lax.psum_scatter(out_part, "dp", scatter_dimension=0, tiled=True)
        scaled = lax.psum_scatter(scaled_part, "dp", scatter_dimension=0, tiled=True)
        out_sum, scaled = out_sum.astype(jnp.float32), scaled.astype(jnp.float32)

    inputs = tokens_in[0].astype(jnp.float32)
    live = (jnp.arange(length) < lengths[0]).astype(jnp.float32)[:, None]
    back = cotangent[0].astype(jnp.float32) * live
    back_total = jnp.sum(back, axis=0)

    def spread(values, pieces):
        wide = jnp.zeros((pieces, parts, values.shape[0] // pieces), jnp.float32)
        return lax.dynamic_update_index_in_dim(
            wide, values.reshape(pieces, -1), part, axis=1
        ).reshape(-1)

    small_grad = jnp.concatenate(
        [
            norm_sums.reshape(4 * D),
            spread(d_qkv_bias, 3),
            back_total,
            spread(d_up_bias, shards),
            back_total,
        ]
    )
    if own:
        padded = jnp.pad(small_grad.reshape(shards, small_rows), ((0, 0), (0, 2048 - small_rows)))
        out_sum, scaled, terms_all, out_grad, small_sum = reduce(
            out_part, scaled_part, terms, out_term, padded.reshape(shards, 16, 128)
        )
        small_sum = small_sum.reshape(2048)[:small_rows]
        terms_all = terms_all.astype(jnp.float32)
        qkv_width, up_width = 3 * head_cols, ff_cols
        reduced = (
            joined(terms_all[:, :, :qkv_width], 3),
            out_grad.astype(jnp.float32),
            joined(terms_all[:, :, qkv_width : qkv_width + up_width], shards),
            terms_all[:, :, qkv_width + up_width :].reshape(down_master.shape),
            small_sum,
        )
    else:
        small_sum = lax.psum(small_grad, ("dp", "fsdp"))
        small_rows = small_master.shape[0]
        small_sum = lax.dynamic_slice_in_dim(small_sum, shard * small_rows, small_rows)
        qkv_term, out_term, up_term, down_term = terms
        out_wide = lax.dynamic_update_slice_in_dim(
            jnp.zeros((D, D), jnp.bfloat16), out_term, part * head_cols, axis=0
        )

        def to_owner(term):
            own = lax.psum_scatter(term, "fsdp", scatter_dimension=0, tiled=True)
            return lax.all_gather(own, "dp", axis=0, tiled=False).astype(jnp.float32)

        reduced = (
            joined(to_owner(qkv_term), 3),
            lax.psum(
                lax.psum_scatter(out_wide, "fsdp", scatter_dimension=0, tiled=True), "dp"
            ).astype(jnp.float32),
            joined(to_owner(up_term), shards),
            to_owner(down_term).reshape(down_master.shape),
            small_sum,
        )

    unit_rows, inverse_rows = normalize(inputs)
    output = ((inputs + out_sum + out_bias + down_bias) * live).astype(jnp.bfloat16)
    input_grad = back + inverse_rows * (
        scaled
        - jnp.mean(scaled, axis=-1, keepdims=True)
        - unit_rows * jnp.mean(scaled * unit_rows, axis=-1, keepdims=True)
    )
    return (output[None], input_grad.astype(jnp.bfloat16)[None]) + lamb(
        masters, firsts, seconds, reduced
    )


def lamb(masters, firsts, seconds, reduced):
    updates = []
    first_news = []
    second_news = []
    for first_old, second_old, master, grad_sum in zip(firsts, seconds, masters, reduced):
        first_new = BETA_ONE * first_old + (1.0 - BETA_ONE) * grad_sum
        second_new = BETA_TWO * second_old + (1.0 - BETA_TWO) * grad_sum * grad_sum
        updates.append(first_new / (jnp.sqrt(second_new) + ADAM_EPSILON) + DECAY * master)
        first_news.append(first_new)
        second_news.append(second_new)
    weight_squares, update_squares = lax.psum(
        (local_squares(masters), local_squares(updates)), "fsdp"
    )
    weight_norms = jnp.sqrt(weight_squares)
    update_norms = jnp.sqrt(update_squares)
    new_masters = [
        masters[number] - RATE * (weight_norms[number] / update_norms[number]) * updates[number]
        for number in range(5)
    ]
    lamb_norms = jnp.stack([weight_norms, update_norms])
    return tuple(new_masters) + tuple(first_news) + tuple(second_news) + (lamb_norms,)


def solution(mesh):
    in_specs = (
        P(("dp", "fsdp"), None, None),
        P(("dp", "fsdp"), None, None),
        P(("dp", "fsdp")),
        P("fsdp", None),
        P("fsdp", None),
        P("fsdp", None),
        P("fsdp", None),
        P("fsdp"),
        P("fsdp", None),
        P("fsdp", None),
        P("fsdp", None),
        P("fsdp", None),
        P("fsdp"),
        P("fsdp", None),
        P("fsdp", None),
        P("fsdp", None),
        P("fsdp", None),
        P("fsdp"),
    )
    out_specs = (
        P(("dp", "fsdp"), None, None),
        P(("dp", "fsdp"), None, None),
        P("fsdp", None),
        P("fsdp", None),
        P("fsdp", None),
        P("fsdp", None),
        P("fsdp"),
        P("fsdp", None),
        P("fsdp", None),
        P("fsdp", None),
        P("fsdp", None),
        P("fsdp"),
        P("fsdp", None),
        P("fsdp", None),
        P("fsdp", None),
        P("fsdp", None),
        P("fsdp"),
        P(),
    )
    return jax.shard_map(local_split, mesh=mesh, in_specs=in_specs, out_specs=out_specs, check_vma=False)
```

```python
import math

import jax
import jax.numpy as jnp
from jax import lax
from jax.experimental import pallas as pl
from jax.experimental.pallas import tpu as pltpu
from jax.sharding import PartitionSpec as P

D = 1024
HEADS = 16
HD = 64
FF = 4096
ROT = 16
SMALL = 13312


NORM_EPSILON = 1e-05
ADAM_EPSILON = 1e-06
ROPE_BASE = 10000.0
RATE = 0.5
DECAY = 0.01
BETA_ONE = 0.5
BETA_TWO = 0.5


def split_small(small_vector):
    bounds = [0, D, 2 * D, 3 * D, 4 * D, 7 * D, 8 * D, 8 * D + FF, 9 * D + FF]
    return [small_vector[bounds[number] : bounds[number + 1]] for number in range(8)]


def normalize(values):
    average = jnp.mean(values, axis=-1, keepdims=True)
    centred = values - average
    variance = jnp.mean(centred * centred, axis=-1, keepdims=True)
    inverse = lax.rsqrt(variance + NORM_EPSILON)
    return (centred * inverse, inverse)


def rotary_tables(length):
    half_dims = ROT // 2
    position = jnp.arange(length, dtype=jnp.float32)[:, None]
    number = jnp.arange(half_dims, dtype=jnp.float32)[None, :]
    angle = position * jnp.exp(number * (-2.0 * math.log(ROPE_BASE) / ROT))
    return (jnp.cos(angle)[:, None, :], jnp.sin(angle)[:, None, :])


def rotate(heads_in, cosine_table, sine_table):
    half_dims = ROT // 2
    first_half = heads_in[..., :half_dims]
    second_half = heads_in[..., half_dims:ROT]
    return jnp.concatenate(
        [
            first_half * cosine_table - second_half * sine_table,
            second_half * cosine_table + first_half * sine_table,
            heads_in[..., ROT:],
        ],
        axis=-1,
    )


def rotate_back(grads_in, cosine_table, sine_table):
    half_dims = ROT // 2
    first_half = grads_in[..., :half_dims]
    second_half = grads_in[..., half_dims:ROT]
    return jnp.concatenate(
        [
            first_half * cosine_table + second_half * sine_table,
            second_half * cosine_table - first_half * sine_table,
            grads_in[..., ROT:],
        ],
        axis=-1,
    )


def gelu_slope(values):
    return 0.5 * (1.0 + lax.erf(values * 2.0 ** (-0.5))) + values * jnp.exp(
        -0.5 * values * values
    ) * (2.0 * math.pi) ** (-0.5)


def against(left, right):
    return lax.dot_general(
        left, right, (((1,), (1,)), ((), ())), preferred_element_type=jnp.float32
    )


def outer_sum(columns, right):
    return lax.dot_general(
        columns, right, (((0,), (0,)), ((), ())), preferred_element_type=jnp.float32
    )


def local_squares(arrays):
    return jnp.stack([jnp.sum(array_in * array_in) for array_in in arrays])


def sliced(master, part, parts, pieces):
    rows, columns = master.shape
    width = columns // (pieces * parts)
    return lax.dynamic_index_in_dim(
        master.reshape(rows, pieces, parts, width), part, axis=2, keepdims=False
    ).reshape(rows, pieces * width)


def joined(slices, pieces):
    parts, rows, columns = slices.shape
    width = columns // pieces
    return (
        slices.reshape(parts, rows, pieces, width)
        .transpose(1, 2, 0, 3)
        .reshape(rows, pieces * parts * width)
    )


def layer(x_all, cotangent_all, lengths_all, weights, small_all, part):
    qkv_weight, out_weight, up_weight, down_weight = weights
    group, length, _ = x_all.shape
    tokens = group * length
    head_cols = out_weight.shape[0]
    heads = head_cols // HD
    gain_one, shift_one, gain_two, shift_two, qkv_bias, up_bias = small_all
    inputs = x_all.reshape(tokens, D).astype(jnp.float32)
    position = jnp.arange(length)
    live = (position[None, :] < lengths_all[:, None]).astype(jnp.float32).reshape(tokens, 1)
    allowed = (position[None, None, :] <= position[None, :, None]) & (
        position[None, None, :] < lengths_all[:, None, None]
    )
    unit_rows, _ = normalize(inputs)
    normed_one = (unit_rows * gain_one + shift_one).astype(jnp.bfloat16)
    normed_two = (unit_rows * gain_two + shift_two).astype(jnp.bfloat16)
    projected = jnp.dot(normed_one, qkv_weight, preferred_element_type=jnp.float32) + qkv_bias
    projected = projected.reshape(group, length, 3, heads, HD)
    cosine_table, sine_table = rotary_tables(length)
    query_heads = rotate(projected[:, :, 0], cosine_table, sine_table).astype(jnp.bfloat16)
    key_heads = rotate(projected[:, :, 1], cosine_table, sine_table).astype(jnp.bfloat16)
    value_heads = projected[:, :, 2].astype(jnp.bfloat16)
    scores = jnp.einsum(
        "gqhd,gkhd->ghqk", query_heads, key_heads, preferred_element_type=jnp.float32
    ) * HD ** (-0.5)
    scores = jnp.where(allowed[:, None], scores, -1e30)
    row_top = jnp.max(scores, axis=-1, keepdims=True)
    raised = jnp.exp(scores - row_top)
    attend = raised / jnp.sum(raised, axis=-1, keepdims=True)
    attend_low = attend.astype(jnp.bfloat16)
    mixed = jnp.einsum(
        "ghqk,gkhd->gqhd", attend_low, value_heads, preferred_element_type=jnp.float32
    )
    mixed = mixed.reshape(tokens, head_cols).astype(jnp.bfloat16)
    hidden = jnp.dot(normed_two, up_weight, preferred_element_type=jnp.float32) + up_bias
    activated = jax.nn.gelu(hidden, approximate=False).astype(jnp.bfloat16)
    out_part = jnp.dot(mixed, out_weight, preferred_element_type=jnp.float32) + jnp.dot(
        activated, down_weight, preferred_element_type=jnp.float32
    )

    back = (cotangent_all.reshape(tokens, D).astype(jnp.float32) * live).astype(jnp.bfloat16)
    d_hidden = (against(back, down_weight) * gelu_slope(hidden)).astype(jnp.bfloat16)
    d_mixed = against(back, out_weight).astype(jnp.bfloat16).reshape(group, length, heads, HD)
    d_attend = jnp.einsum(
        "gqhd,gkhd->ghqk", d_mixed, value_heads, preferred_element_type=jnp.float32
    )
    row_inner = jnp.sum(attend * d_attend, axis=-1, keepdims=True)
    d_scores = (attend * (d_attend - row_inner)).astype(jnp.bfloat16)
    d_queries = jnp.einsum(
        "ghqk,gkhd->gqhd", d_scores, key_heads, preferred_element_type=jnp.float32
    ) * HD ** (-0.5)
    d_keys = jnp.einsum(
        "ghqk,gqhd->gkhd", d_scores, query_heads, preferred_element_type=jnp.float32
    ) * HD ** (-0.5)
    d_values = jnp.einsum(
        "ghqk,gqhd->gkhd", attend_low, d_mixed, preferred_element_type=jnp.float32
    )
    d_projected = jnp.stack(
        [
            rotate_back(d_queries, cosine_table, sine_table),
            rotate_back(d_keys, cosine_table, sine_table),
            d_values,
        ],
        axis=2,
    )
    d_projected = d_projected.reshape(tokens, 3 * head_cols).astype(jnp.bfloat16)
    d_normed_one = against(d_projected, qkv_weight)
    d_normed_two = against(d_hidden, up_weight)
    scaled_part = d_normed_one * gain_one + d_normed_two * gain_two
    norm_sums = jnp.stack(
        [
            jnp.sum(d_normed_one * unit_rows, axis=0),
            jnp.sum(d_normed_one, axis=0),
            jnp.sum(d_normed_two * unit_rows, axis=0),
            jnp.sum(d_normed_two, axis=0),
        ]
    )
    d_qkv_bias = jnp.sum(d_projected, axis=0, dtype=jnp.float32)
    d_up_bias = jnp.sum(d_hidden, axis=0, dtype=jnp.float32)
    terms = (
        outer_sum(normed_one, d_projected),
        outer_sum(mixed, back),
        outer_sum(normed_two, d_hidden),
        outer_sum(activated, back),
    )
    return (
        out_part.astype(jnp.bfloat16),
        scaled_part.astype(jnp.bfloat16),
        tuple(term.astype(jnp.bfloat16) for term in terms),
        (norm_sums, d_qkv_bias, d_up_bias),
    )


MESH_ID = pl.DeviceIdType.MESH
HALF = 128


class Place:
    def __init__(self):
        self.part = lax.axis_index("dp")
        self.shard = lax.axis_index("fsdp")
        self.z = self.shard // 2
        self.core = self.shard % 2
        self.x_part = 2 * (self.part // 2) + 1 - self.part % 2
        self.y_part = (self.part + 2) % 4
        self.far_part = 3 - self.part
        self.across_x = (self.x_part, self.shard)
        self.across_y = (self.y_part, self.shard)
        self.across_far = (self.far_part, self.shard)
        self.other_core = (self.part, 2 * self.z + 1 - self.core)
        self.up = (self.part, jnp.minimum(self.shard + 2, 7))
        self.down = (self.part, jnp.maximum(self.shard - 2, 0))

    def shard_after(self, k):
        return (self.part, (self.shard + k) % 8)


def send(source, target, send_sem, recv_sem, device):
    return pltpu.make_async_remote_copy(
        src_ref=source,
        dst_ref=target,
        send_sem=send_sem,
        recv_sem=recv_sem,
        device_id=device,
        device_id_type=MESH_ID,
    )


def arrived(target, recv_sem, device):
    send(target, target, recv_sem, recv_sem, device).wait_recv()


def sent(source, send_sem, device):
    send(source, source, send_sem, send_sem, device).wait_send()


def greet(at):
    barrier = pltpu.get_barrier_semaphore()
    peers = [at.across_x, at.across_y, at.across_far] + [at.shard_after(k) for k in range(1, 8)]
    for peer in peers:
        pl.semaphore_signal(barrier, inc=1, device_id=peer, device_id_type=MESH_ID)
    pl.semaphore_wait(barrier, len(peers))


def gather_kernel(
    x_own,
    cot_own,
    len_own,
    w_own,
    out_own,
    small_own,
    x_all,
    cot_all,
    len_all,
    w_all,
    out_all,
    small_all,
    plane_send,
    plane_recv,
    len_send,
    len_recv,
    w_send,
    w_recv,
    out_send,
    out_recv,
    small_send,
    small_recv,
):
    at = Place()
    z, core, part, shard = at.z, at.core, at.part, at.shard
    greet(at)
    spans = ((0, 768), (768, 1792), (1792, 2816))

    def piece(ref, slot, n):
        return ref.at[slot, :, spans[n][0] : spans[n][1]]

    for n, (low, high) in enumerate(spans):
        own = w_own.at[:, low:high]
        target = piece(w_all, shard, n)

        @pl.when(z < 3)
        def _():
            send(own, target, w_send.at[0, n, z], w_recv.at[n, shard], at.up).start()

        @pl.when(z > 0)
        def _():
            send(own, target, w_send.at[1, n, z], w_recv.at[n, shard], at.down).start()

        send(own, target, w_send.at[2, n, z], w_recv.at[n, shard], at.other_core).start()

    @pl.when(z == part)
    def _():
        @pl.when(z < 3)
        def _():
            send(out_own, out_all.at[core], out_send.at[0], out_recv.at[core], at.up).start()

        @pl.when(z > 0)
        def _():
            send(out_own, out_all.at[core], out_send.at[1], out_recv.at[core], at.down).start()

        send(out_own, out_all.at[core], out_send.at[2], out_recv.at[core], at.other_core).start()
        out_all[core] = out_own[...]

    activations = ((x_own, x_all), (cot_own, cot_all))
    for n, (own, whole) in enumerate(activations):
        send(own, whole.at[part], plane_send.at[n, 0], plane_recv.at[n, 0], at.across_x).start()
        send(own, whole.at[part], plane_send.at[n, 1], plane_recv.at[n, 1], at.across_y).start()
    for n, peer in enumerate((at.across_x, at.across_y, at.across_far)):
        send(len_own, len_all.at[part], len_send.at[n], len_recv.at[n], peer).start()
    for k in range(1, 8):
        send(
            small_own,
            small_all.at[shard],
            small_send.at[k - 1],
            small_recv.at[k - 1],
            at.shard_after(k),
        ).start()
    x_all[part] = x_own[...]
    cot_all[part] = cot_own[...]
    len_all[part] = len_own[...]
    w_all[shard] = w_own[...]
    small_all[shard] = small_own[...]

    def forward(k, n):
        @pl.when(z >= k)
        def _():
            source = 2 * (z - k) + core
            block = piece(w_all, source, n)
            arrived(block, w_recv.at[n, source], at.down)

            @pl.when(z < 3)
            def _():
                send(block, block, w_send.at[0, n, z - k], w_recv.at[n, source], at.up).start()

            send(
                block, block, w_send.at[2, n, z - k], w_recv.at[n, source], at.other_core
            ).start()

        @pl.when(z + k <= 3)
        def _():
            source = 2 * (z + k) + core
            block = piece(w_all, source, n)
            arrived(block, w_recv.at[n, source], at.up)

            @pl.when(z > 0)
            def _():
                send(block, block, w_send.at[1, n, z + k], w_recv.at[n, source], at.down).start()

            send(
                block, block, w_send.at[2, n, z + k], w_recv.at[n, source], at.other_core
            ).start()

    def forward_out(k):
        @pl.when((z - k == part) | (z + k == part))
        def _():
            block = out_all.at[core]
            arrived(block, out_recv.at[core], at.up)

            @pl.when((z > part) & (z < 3))
            def _():
                send(block, block, out_send.at[0], out_recv.at[core], at.up).start()

            @pl.when((z < part) & (z > 0))
            def _():
                send(block, block, out_send.at[1], out_recv.at[core], at.down).start()

            send(block, block, out_send.at[2], out_recv.at[core], at.other_core).start()

    def forward_plane(n):
        whole = activations[n][1]
        arrived(whole.at[at.x_part], plane_recv.at[n, 0], at.across_x)
        block = whole.at[at.x_part, 0:HALF]
        send(block, block, plane_send.at[n, 2], plane_recv.at[n, 2], at.across_y).start()
        arrived(whole.at[at.y_part], plane_recv.at[n, 1], at.across_y)
        block = whole.at[at.y_part, HALF : 2 * HALF]
        send(block, block, plane_send.at[n, 3], plane_recv.at[n, 3], at.across_x).start()

    forward(1, 0)
    forward(1, 1)
    forward_plane(0)
    forward(1, 2)
    forward_out(1)
    forward(2, 0)
    forward_plane(1)
    forward(2, 1)
    forward(2, 2)
    forward_out(2)
    for n in range(3):
        forward(3, n)
    forward_out(3)

    for n, (own, whole) in enumerate(activations):
        arrived(whole.at[at.far_part, 0:HALF], plane_recv.at[n, 2], at.across_y)
        arrived(whole.at[at.far_part, HALF : 2 * HALF], plane_recv.at[n, 3], at.across_x)
        sent(own, plane_send.at[n, 0], at.across_x)
        sent(own, plane_send.at[n, 1], at.across_y)
        sent(whole.at[at.x_part, 0:HALF], plane_send.at[n, 2], at.across_y)
        sent(whole.at[at.y_part, HALF : 2 * HALF], plane_send.at[n, 3], at.across_x)
    for n, (peer, other) in enumerate(
        ((at.across_x, at.x_part), (at.across_y, at.y_part), (at.across_far, at.far_part))
    ):
        arrived(len_all.at[other], len_recv.at[n], peer)
        sent(len_own, len_send.at[n], peer)
    for k in range(1, 8):
        arrived(small_all.at[(shard + 8 - k) % 8], small_recv.at[k - 1], at.shard_after(8 - k))
        sent(small_own, small_send.at[k - 1], at.shard_after(k))
    for n in range(3):
        for other in range(4):
            block = piece(w_all, 2 * other + 1 - core, n)
            arrived(block, w_recv.at[n, 2 * other + 1 - core], at.other_core)
            sent(block, w_send.at[2, n, other], at.other_core)

            @pl.when((other <= z) & (z < 3))
            def _():
                sent(block, w_send.at[0, n, other], at.up)

            @pl.when((other >= z) & (z > 0))
            def _():
                sent(block, w_send.at[1, n, other], at.down)

    arrived(out_all.at[1 - core], out_recv.at[1 - core], at.other_core)
    sent(out_own, out_send.at[2], at.other_core)

    @pl.when((z >= part) & (z < 3))
    def _():
        sent(out_own, out_send.at[0], at.up)

    @pl.when((z <= part) & (z > 0))
    def _():
        sent(out_own, out_send.at[1], at.down)


VMEM_SPEC = pl.BlockSpec(memory_space=pltpu.VMEM)


def gather(x_own, cot_own, len_own, w_own, out_own, small_own):
    shape = jax.ShapeDtypeStruct
    dma = pltpu.SemaphoreType.DMA
    return pl.pallas_call(
        gather_kernel,
        out_shape=(
            shape((4,) + x_own.shape, jnp.bfloat16),
            shape((4,) + x_own.shape, jnp.bfloat16),
            shape((4,) + len_own.shape, jnp.float32),
            shape((8,) + w_own.shape, jnp.bfloat16),
            shape((2,) + out_own.shape, jnp.bfloat16),
            shape((8,) + small_own.shape, jnp.float32),
        ),
        in_specs=[VMEM_SPEC] * 6,
        out_specs=(VMEM_SPEC,) * 6,
        scratch_shapes=[
            dma((2, 4)),
            dma((2, 4)),
            dma((3,)),
            dma((3,)),
            dma((3, 3, 4)),
            dma((3, 8)),
            dma((3,)),
            dma((2,)),
            dma((7,)),
            dma((7,)),
        ],
        compiler_params=pltpu.CompilerParams(
            collective_id=0, has_side_effects=True, vmem_limit_bytes=60 << 20
        ),
        name="gather",
    )(x_own, cot_own, len_own, w_own, out_own, small_own)


def reduce_kernel(
    out_part,
    dx_part,
    terms,
    out_term,
    small_part,
    out_sum,
    dx_sum,
    down_all,
    up_all,
    qkv_all,
    out_grad,
    small_sum,
    plane_one,
    plane_two,
    plane_turn,
    core_in,
    line_sum,
    line_in,
    out_core_in,
    out_line,
    out_line_in,
    small_in,
    small_own,
    small_plane,
    plane_send,
    plane_recv,
    core_send,
    core_recv,
    line_send,
    line_recv,
    out_send,
    out_recv,
    all_send,
    all_recv,
    small_send,
    small_recv,
):
    at = Place()
    z, core, part, shard = at.z, at.core, at.part, at.shard
    greet(at)
    spans = ((1792, 2816), (768, 1792), (0, 768))
    wholes = (down_all, up_all, qkv_all)
    first, second = slice(0, HALF), slice(HALF, 2 * HALF)
    f32, bf16 = jnp.float32, jnp.bfloat16

    for n, (low, high) in enumerate(spans):
        for other in range(4):
            send(
                terms.at[2 * other + 1 - core, :, low:high],
                core_in.at[other, :, low:high],
                core_send.at[n, other],
                core_recv.at[n, other],
                at.other_core,
            ).start()
    send(out_term.at[1 - core], out_core_in, out_send.at[0], out_recv.at[0], at.other_core).start()
    for k in range(1, 8):
        send(
            small_part.at[(shard + k) % 8],
            small_in.at[k - 1],
            small_send.at[k - 1],
            small_recv.at[k - 1],
            at.shard_after(k),
        ).start()

    parts = (out_part, dx_part)
    routes = (
        (first, at.across_x, at.x_part, at.across_y, at.y_part),
        (second, at.across_y, at.y_part, at.across_x, at.x_part),
    )
    for n, term in enumerate(parts):
        for r, (rows, peer, peer_part, _, _) in enumerate(routes):
            for m, target in enumerate((at.far_part, peer_part)):
                send(
                    term.at[target, rows],
                    plane_one.at[n, r, m],
                    plane_send.at[n, r, m],
                    plane_recv.at[n, r, m],
                    peer,
                ).start()

    def forward(n, target):
        low, high = spans[n]
        block = line_sum.at[target, :, low:high]

        @pl.when(z < target)
        def _():
            @pl.when(z > 0)
            def _():
                arrived(line_in.at[target, :, low:high], line_recv.at[n, target], at.down)
                block[...] = (
                    block[...].astype(f32) + line_in[target, :, low:high].astype(f32)
                ).astype(bf16)

            send(
                block,
                line_in.at[target, :, low:high],
                line_send.at[n, target],
                line_recv.at[n, target],
                at.up,
            ).start()

        @pl.when(z > target)
        def _():
            @pl.when(z < 3)
            def _():
                arrived(line_in.at[target, :, low:high], line_recv.at[n, target], at.up)
                block[...] = (
                    block[...].astype(f32) + line_in[target, :, low:high].astype(f32)
                ).astype(bf16)

            @pl.when(z - 1 == target)
            def _():
                send(
                    block,
                    line_in.at[4, :, low:high],
                    line_send.at[n, target],
                    line_recv.at[n, 4],
                    at.down,
                ).start()

            @pl.when(z - 1 > target)
            def _():
                send(
                    block,
                    line_in.at[target, :, low:high],
                    line_send.at[n, target],
                    line_recv.at[n, target],
                    at.down,
                ).start()

    def own_line(n):
        low, high = spans[n]
        block = line_sum.at[z, :, low:high]

        @pl.when(z > 0)
        def _():
            arrived(line_in.at[z, :, low:high], line_recv.at[n, z], at.down)
            block[...] = (block[...].astype(f32) + line_in[z, :, low:high].astype(f32)).astype(bf16)

        @pl.when(z < 3)
        def _():
            arrived(line_in.at[4, :, low:high], line_recv.at[n, 4], at.up)
            block[...] = (block[...].astype(f32) + line_in[4, :, low:high].astype(f32)).astype(bf16)

        wholes[n][part] = block[...]
        own = wholes[n].at[part]
        send(own, own, all_send.at[n, 0], all_recv.at[n, 0], at.across_x).start()
        send(own, own, all_send.at[n, 1], all_recv.at[n, 1], at.across_y).start()

    plane_peers = (
        (at.across_x, at.x_part),
        (at.across_y, at.y_part),
        (at.across_far, at.far_part),
    )

    def line(n):
        low, high = spans[n]
        for other in (3, 0, 2, 1):
            arrived(core_in.at[other, :, low:high], core_recv.at[n, other], at.other_core)
            line_sum[other, :, low:high] = (
                terms[2 * other + core, :, low:high].astype(f32)
                + core_in[other, :, low:high].astype(f32)
            ).astype(bf16)
        for target in (3, 0, 2, 1):
            forward(n, target)

    def plane_turns(n):
        term = parts[n]
        for r, (rows, peer, _, turn, turn_part) in enumerate(routes):
            arrived(plane_one.at[n, r, 0], plane_recv.at[n, r, 0], peer)
            plane_turn[n, r] = (
                term[turn_part, rows].astype(f32) + plane_one[n, r, 0].astype(f32)
            ).astype(bf16)
            send(
                plane_turn.at[n, r],
                plane_two.at[n, r],
                plane_send.at[n, r, 2],
                plane_recv.at[n, r, 2],
                turn,
            ).start()

    def plane_ends(n):
        term, result = parts[n], (out_sum, dx_sum)[n]
        for r, (rows, peer, _, turn, _) in enumerate(routes):
            arrived(plane_one.at[n, r, 1], plane_recv.at[n, r, 1], peer)
            arrived(plane_two.at[n, r], plane_recv.at[n, r, 2], turn)
            result[rows] = (
                term[part, rows].astype(f32)
                + plane_one[n, r, 1].astype(f32)
                + plane_two[n, r].astype(f32)
            )

    def out_travels():
        arrived(out_core_in, out_recv.at[0], at.other_core)
        out_line[...] = (out_term[core].astype(f32) + out_core_in[...].astype(f32)).astype(bf16)

        @pl.when((z < part) & (z > 0))
        def _():
            arrived(out_line_in.at[0], out_recv.at[1], at.down)
            out_line[...] = (out_line[...].astype(f32) + out_line_in[0].astype(f32)).astype(bf16)

        @pl.when((z > part) & (z < 3))
        def _():
            arrived(out_line_in.at[1], out_recv.at[2], at.up)
            out_line[...] = (out_line[...].astype(f32) + out_line_in[1].astype(f32)).astype(bf16)

        @pl.when(z < part)
        def _():
            send(out_line, out_line_in.at[0], out_send.at[1], out_recv.at[1], at.up).start()

        @pl.when(z > part)
        def _():
            send(out_line, out_line_in.at[1], out_send.at[1], out_recv.at[2], at.down).start()

    def out_ends():
        @pl.when(z == part)
        def _():
            @pl.when(z > 0)
            def _():
                arrived(out_line_in.at[0], out_recv.at[1], at.down)
                out_line[...] = (
                    out_line[...].astype(f32) + out_line_in[0].astype(f32)
                ).astype(bf16)

            @pl.when(z < 3)
            def _():
                arrived(out_line_in.at[1], out_recv.at[2], at.up)
                out_line[...] = (
                    out_line[...].astype(f32) + out_line_in[1].astype(f32)
                ).astype(bf16)

            for n, (peer, _) in enumerate(plane_peers):
                send(out_line, out_grad, out_send.at[2 + n], out_recv.at[3], peer).start()
            out_grad[...] = out_line[...]

        @pl.when(z != part)
        def _():
            arrived(out_grad, out_recv.at[3], at.across_x)

    def small_travels():
        total = small_part[shard]
        for k in range(1, 8):
            arrived(small_in.at[k - 1], small_recv.at[k - 1], at.shard_after(8 - k))
            total = total + small_in[k - 1]
        small_own[...] = total
        for n, (peer, _) in enumerate(plane_peers):
            send(
                small_own, small_plane.at[part], small_send.at[7 + n], small_recv.at[7 + n], peer
            ).start()
        small_plane[part] = total

    def share(n):
        whole = wholes[n]
        arrived(whole.at[at.x_part], all_recv.at[n, 0], at.across_x)
        block = whole.at[at.x_part, 0:64]
        send(block, block, all_send.at[n, 2], all_recv.at[n, 2], at.across_y).start()
        arrived(whole.at[at.y_part], all_recv.at[n, 1], at.across_y)
        block = whole.at[at.y_part, 64:128]
        send(block, block, all_send.at[n, 3], all_recv.at[n, 3], at.across_x).start()

    line(0)
    plane_turns(0)
    line(1)
    own_line(0)
    plane_turns(1)
    out_travels()
    line(2)
    small_travels()
    own_line(1)
    share(0)
    plane_ends(0)
    plane_ends(1)
    out_ends()
    own_line(2)
    share(1)
    share(2)
    for n, (peer, other) in enumerate(plane_peers):
        arrived(small_plane.at[other], small_recv.at[7 + n], peer)
    small_sum[...] = (small_plane[0] + small_plane[1]) + (small_plane[2] + small_plane[3])

    for n, (low, high) in enumerate(spans):
        whole = wholes[n]
        arrived(whole.at[at.far_part, 0:64], all_recv.at[n, 2], at.across_y)
        arrived(whole.at[at.far_part, 64:128], all_recv.at[n, 3], at.across_x)
        sent(whole.at[part], all_send.at[n, 0], at.across_x)
        sent(whole.at[part], all_send.at[n, 1], at.across_y)
        sent(whole.at[part, 0:64], all_send.at[n, 2], at.across_y)
        sent(whole.at[part, 64:128], all_send.at[n, 3], at.across_x)
        for other in range(4):
            block = line_sum.at[other, :, low:high]
            sent(block, core_send.at[n, other], at.other_core)

            @pl.when(z != other)
            def _():
                sent(block, line_send.at[n, other], at.up)

    for n in range(2):
        for r in range(2):
            for m in range(3):
                sent(plane_turn.at[n, r], plane_send.at[n, r, m], at.across_x)
    sent(out_line, out_send.at[0], at.other_core)

    @pl.when(z != part)
    def _():
        sent(out_line, out_send.at[1], at.up)

    @pl.when(z == part)
    def _():
        for n, (peer, _) in enumerate(plane_peers):
            sent(out_line, out_send.at[2 + n], peer)

    for k in range(1, 8):
        sent(small_own, small_send.at[k - 1], at.shard_after(k))
    for n, (peer, _) in enumerate(plane_peers):
        sent(small_own, small_send.at[7 + n], peer)


def reduce(out_part, dx_part, terms, out_term, small_part):
    shape = jax.ShapeDtypeStruct
    dma = pltpu.SemaphoreType.DMA
    vmem = pltpu.VMEM
    _, length, width = out_part.shape
    _, rows, wide = terms.shape
    bf16, f32 = jnp.bfloat16, jnp.float32
    small = small_part.shape[1:]
    return pl.pallas_call(
        reduce_kernel,
        out_shape=(
            shape((length, width), f32),
            shape((length, width), f32),
            shape((4, rows, 1024), bf16),
            shape((4, rows, 1024), bf16),
            shape((4, rows, 768), bf16),
            shape((rows, width), bf16),
            shape(small, f32),
        ),
        in_specs=[VMEM_SPEC] * 5,
        out_specs=(VMEM_SPEC,) * 7,
        scratch_shapes=[
            vmem((2, 2, 2, HALF, width), bf16),
            vmem((2, 2, HALF, width), bf16),
            vmem((2, 2, HALF, width), bf16),
            vmem((4, rows, wide), bf16),
            vmem((4, rows, wide), bf16),
            vmem((5, rows, wide), bf16),
            vmem((rows, width), bf16),
            vmem((rows, width), bf16),
            vmem((2, rows, width), bf16),
            vmem((7,) + small, f32),
            vmem(small, f32),
            vmem((4,) + small, f32),
            dma((2, 2, 3)),
            dma((2, 2, 3)),
            dma((3, 4)),
            dma((3, 4)),
            dma((3, 4)),
            dma((3, 5)),
            dma((5,)),
            dma((4,)),
            dma((3, 4)),
            dma((3, 4)),
            dma((10,)),
            dma((10,)),
        ],
        compiler_params=pltpu.CompilerParams(
            collective_id=1, has_side_effects=True, vmem_limit_bytes=60 << 20
        ),
        name="reduce",
    )(out_part, dx_part, terms, out_term, small_part)


def nt(a,b): return lax.dot_general(a,b,(((1,),(1,)),((),())),preferred_element_type=jnp.float32)
def tn(a,b): return lax.dot_general(a,b,(((0,),(0,)),((),())),preferred_element_type=jnp.float32)
def nn(a,b): return jnp.dot(a,b,preferred_element_type=jnp.float32)
def flat(v): return v.reshape(v.shape[0]*v.shape[1], v.shape[2])

def compute_kernel(x_ref,cot_ref,len_ref,w_ref,wout_ref,gains_ref,qb_ref,ub_ref,tab_ref,
                   outp_ref,dxp_ref,g_ref,gout_ref,sums_ref,dqb_ref,dub_ref,
                   unit_s,n1_s,n2_s,back_s,mix_s,dp_s,act_s,dh_s,sc_s):
    group,length,_=x_ref.shape
    hc=wout_ref.shape[0]*wout_ref.shape[1]
    nh=hc//HD
    Q=3*hc; U=ub_ref.shape[1]
    RB=64
    sums_ref[...]=jnp.zeros_like(sums_ref); dqb_ref[...]=jnp.zeros_like(dqb_ref); dub_ref[...]=jnp.zeros_like(dub_ref)
    row=lax.broadcasted_iota(jnp.int32,(length,length),0)
    col=lax.broadcasted_iota(jnp.int32,(length,length),1)
    causal=col<=row
    lane=lax.broadcasted_iota(jnp.int32,(length,hc),1)
    def norm_rows(s):
        @pl.loop(0,length//RB)
        def _(i):
            r=pl.ds(pl.multiple_of(i*RB,RB),RB)
            x=x_ref[s,r,:].astype(jnp.float32)
            mean=jnp.mean(x,axis=-1,keepdims=True)
            c=x-mean
            var=jnp.mean(c*c,axis=-1,keepdims=True)
            u=c*lax.rsqrt(var+1e-5)
            unit_s[s,r,:]=u
            n1_s[s,r,:]=(u*gains_ref[0:1]+gains_ref[1:2]).astype(jnp.bfloat16)
            n2_s[s,r,:]=(u*gains_ref[2:3]+gains_ref[3:4]).astype(jnp.bfloat16)
            rows=lax.broadcasted_iota(jnp.int32,(RB,1),0)+i*RB
            live=rows.astype(jnp.float32)<len_ref[s][0:1,0:1]
            back_s[s,r,:]=jnp.where(live,cot_ref[s,r,:],jnp.zeros((),jnp.bfloat16))
    def attn(s):
        norm_rows(s)
        w=flat(w_ref[:,:,0:Q])
        wout=flat(wout_ref[...])
        p=nn(n1_s[s],w)+qb_ref[...]
        C=tab_ref[0];S1=tab_ref[1];S2=tab_ref[2]
        def rot(v): return v*C+pltpu.roll(v,hc-8,1)*S1+pltpu.roll(v,8,1)*S2
        def rotb(v): return v*C-pltpu.roll(v,hc-8,1)*S1-pltpu.roll(v,8,1)*S2
        q=rot(p[:,0:hc]).astype(jnp.bfloat16); k=rot(p[:,hc:2*hc]).astype(jnp.bfloat16); v=p[:,2*hc:].astype(jnp.bfloat16)
        back=back_s[s]
        dm=nt(back,wout).astype(jnp.bfloat16)
        allowed=causal&(col.astype(jnp.float32)<len_ref[s][0:1,0:1])
        zero=jnp.zeros((),jnp.bfloat16)
        mixed=jnp.zeros((length,hc),jnp.float32); dq=mixed; dk=mixed; dv=mixed
        for h in range(nh):
            m=(lane>=h*HD)&(lane<(h+1)*HD)
            qh=jnp.where(m,q,zero);kh=jnp.where(m,k,zero);vh=jnp.where(m,v,zero);dmh=jnp.where(m,dm,zero)
            sc=jnp.where(allowed,nt(qh,k)*HD**-0.5,-1e30)
            e=jnp.exp(sc-jnp.max(sc,axis=-1,keepdims=True))
            A=e*(1.0/jnp.sum(e,axis=-1,keepdims=True))
            Ab=A.astype(jnp.bfloat16)
            mixed=mixed+nn(Ab,vh)
            dA=nt(dmh,v)
            dS=(A*(dA-jnp.sum(A*dA,axis=-1,keepdims=True))).astype(jnp.bfloat16)
            dq=dq+nn(dS,kh); dk=dk+tn(dS,qh); dv=dv+tn(Ab,dmh)
        mix_s[s]=mixed.astype(jnp.bfloat16)
        dq=rotb(dq*HD**-0.5).astype(jnp.bfloat16); dk=rotb(dk*HD**-0.5).astype(jnp.bfloat16); dv=dv.astype(jnp.bfloat16)
        dp_s[s,:,0:hc]=dq; dp_s[s,:,hc:2*hc]=dk; dp_s[s,:,2*hc:]=dv
        for i,t in enumerate((dq,dk,dv)):
            dqb_ref[:,i*hc:(i+1)*hc]+=jnp.sum(t.astype(jnp.float32),axis=0,keepdims=True)
        dn=nt(dp_s[s],w)
        sums_ref[0:1]+=jnp.sum(dn*unit_s[s],axis=0,keepdims=True)
        sums_ref[1:2]+=jnp.sum(dn,axis=0,keepdims=True)
        sc_s[s]=dn*gains_ref[0:1]
    @pl.loop(0,group)
    def _(s): attn(s)
    def grads(lhs_s,rhs,lo,hi):
        @pl.loop(0,w_ref.shape[0])
        def _(f):
            c=pl.ds(pl.multiple_of(f*128,128),128)
            g_ref[f,:,lo:hi]=tn(flat(lhs_s[:,:,c]),rhs).astype(jnp.bfloat16)
    for i in range(wout_ref.shape[0]):
        gout_ref[i]=tn(flat(mix_s[:,:,i*128:(i+1)*128]),flat(back_s[...])).astype(jnp.bfloat16)
    grads(n1_s,flat(dp_s[...]),0,Q)
    def mlp(s):
        wup=flat(w_ref[:,:,Q:Q+U]); wdown=flat(w_ref[:,:,Q+U:])
        h=nn(n2_s[s],wup)+ub_ref[...]
        cdf=0.5*(1.0+lax.erf(h*2.0**-0.5))
        act=(h*cdf).astype(jnp.bfloat16)
        act_s[s]=act
        slope=cdf+h*jnp.exp(-0.5*h*h)*(2*math.pi)**-0.5
        outp_ref[s]=(nn(act,wdown)+nn(mix_s[s],flat(wout_ref[...]))).astype(jnp.bfloat16)
        dh=(nt(back_s[s],wdown)*slope).astype(jnp.bfloat16)
        dh_s[s]=dh
        dub_ref[...]+=jnp.sum(dh.astype(jnp.float32),axis=0,keepdims=True)
        dn=nt(dh,wup)
        sums_ref[2:3]+=jnp.sum(dn*unit_s[s],axis=0,keepdims=True)
        sums_ref[3:4]+=jnp.sum(dn,axis=0,keepdims=True)
        dxp_ref[s]=(sc_s[s]+dn*gains_ref[2:3]).astype(jnp.bfloat16)
    @pl.loop(0,group)
    def _(s): mlp(s)
    grads(n2_s,flat(dh_s[...]),Q,Q+U)
    grads(act_s,flat(back_s[...]),Q+U,Q+2*U)

def rope_tables(length, heads):
    cosine, sine = (table[:, 0] for table in rotary_tables(length))
    rest = (length, HD - ROT)
    none = jnp.zeros_like(sine)
    tables = (
        jnp.concatenate([cosine, cosine, jnp.ones(rest)], axis=1),
        jnp.concatenate([-sine, none, jnp.zeros(rest)], axis=1),
        jnp.concatenate([none, sine, jnp.zeros(rest)], axis=1),
    )
    return jnp.stack([jnp.tile(table, (1, heads)) for table in tables])


def compute(x_all,cot_all,lens,w_all,wout,gains,qb,ub,tab):
    group,length,_=x_all.shape
    Q=qb.shape[1];U=ub.shape[1];hc=Q//3
    V=pl.BlockSpec(memory_space=pltpu.VMEM)
    S=jax.ShapeDtypeStruct
    big=lambda w,t: pltpu.VMEM((group,length,w),t)
    return pl.pallas_call(compute_kernel,
        out_shape=(S((group,length,D),jnp.bfloat16),S((group,length,D),jnp.bfloat16),S(w_all.shape,jnp.bfloat16),S(wout.shape,jnp.bfloat16),S((4,D),jnp.float32),S((1,Q),jnp.float32),S((1,U),jnp.float32)),
        in_specs=[V]*9,out_specs=(V,)*7,
        scratch_shapes=[big(D,jnp.float32),big(D,jnp.bfloat16),big(D,jnp.bfloat16),big(D,jnp.bfloat16),big(hc,jnp.bfloat16),big(Q,jnp.bfloat16),big(U,jnp.bfloat16),big(U,jnp.bfloat16),big(D,jnp.float32)],
        compiler_params=pltpu.CompilerParams(vmem_limit_bytes=62<<20),name="compute")(x_all,cot_all,lens,w_all,wout,gains,qb,ub,tab)


def local_split(
    tokens_in,
    cotangent,
    lengths,
    qkv_master,
    out_master,
    up_master,
    down_master,
    small_master,
    qkv_first,
    out_first,
    up_first,
    down_first,
    small_first,
    qkv_second,
    out_second,
    up_second,
    down_second,
    small_second,
):
    masters = (qkv_master, out_master, up_master, down_master, small_master)
    firsts = (qkv_first, out_first, up_first, down_first, small_first)
    seconds = (qkv_second, out_second, up_second, down_second, small_second)
    parts, shards = lax.axis_size("dp"), lax.axis_size("fsdp")
    part, shard = lax.axis_index("dp"), lax.axis_index("fsdp")
    length = tokens_in.shape[1]
    head_cols = D // parts
    ff_cols = FF // parts
    ff_rows = down_master.shape[0] // parts

    qkv_own = sliced(qkv_master, part, parts, 3).astype(jnp.bfloat16)
    up_own = sliced(up_master, part, parts, shards).astype(jnp.bfloat16)
    down_own = lax.dynamic_slice_in_dim(down_master, part * ff_rows, ff_rows).astype(jnp.bfloat16)
    out_own = out_master.astype(jnp.bfloat16)
    small_own = small_master.astype(jnp.bfloat16)
    own = (parts, shards) == (4, 8)

    def small_vectors(small_all):
        vectors = split_small(small_all)
        vectors[4] = sliced(vectors[4][None], part, parts, 3)[0]
        vectors[6] = sliced(vectors[6][None], part, parts, shards)[0]
        return vectors

    if own:
        small_rows = small_master.shape[0]
        padded = jnp.pad(small_own.astype(jnp.float32), (0, 2048 - small_rows)).reshape(16, 128)
        x_all, cotangent_all, lengths_all, w_all, out_all, small_all = gather(
            tokens_in[0],
            cotangent[0],
            jnp.broadcast_to(lengths.astype(jnp.float32)[:, None], (8, 128)),
            jnp.concatenate([qkv_own, up_own, down_own], axis=1),
            out_own,
            padded,
        )
        small_all = small_all.reshape(shards, 2048)[:, :small_rows].reshape(SMALL)
        gain_one, shift_one, gain_two, shift_two, qkv_bias, out_bias, up_bias, down_bias = (
            small_vectors(small_all)
        )
        out_part, scaled_part, terms, out_term, norm_sums, d_qkv_bias, d_up_bias = compute(
            x_all,
            cotangent_all,
            lengths_all,
            w_all,
            out_all,
            jnp.stack([gain_one, shift_one, gain_two, shift_two]),
            qkv_bias[None],
            up_bias[None],
            rope_tables(length, head_cols // HD),
        )
        d_qkv_bias, d_up_bias = d_qkv_bias[0], d_up_bias[0]
    else:

        def over_shards(own):
            return lax.all_gather(own, "fsdp", axis=0, tiled=True)

        x_all = lax.all_gather(tokens_in, "dp", axis=0, tiled=True)
        cotangent_all = lax.all_gather(cotangent, "dp", axis=0, tiled=True)
        lengths_all = lax.all_gather(lengths, "dp", axis=0, tiled=True)
        qkv_weight, up_weight, down_weight = (over_shards(w) for w in (qkv_own, up_own, down_own))
        out_weight = lax.dynamic_slice_in_dim(over_shards(out_own), part * head_cols, head_cols)
        gain_one, shift_one, gain_two, shift_two, qkv_bias, out_bias, up_bias, down_bias = (
            small_vectors(over_shards(small_own).astype(jnp.float32))
        )
        out_part, scaled_part, terms, sums = layer(
            x_all,
            cotangent_all,
            lengths_all,
            (qkv_weight, out_weight, up_weight, down_weight),
            (gain_one, shift_one, gain_two, shift_two, qkv_bias, up_bias),
            part,
        )
        norm_sums, d_qkv_bias, d_up_bias = sums
        out_sum = lax.psum_scatter(out_part, "dp", scatter_dimension=0, tiled=True)
        scaled = lax.psum_scatter(scaled_part, "dp", scatter_dimension=0, tiled=True)
        out_sum, scaled = out_sum.astype(jnp.float32), scaled.astype(jnp.float32)

    inputs = tokens_in[0].astype(jnp.float32)
    live = (jnp.arange(length) < lengths[0]).astype(jnp.float32)[:, None]
    back = cotangent[0].astype(jnp.float32) * live
    back_total = jnp.sum(back, axis=0)

    def spread(values, pieces):
        wide = jnp.zeros((pieces, parts, values.shape[0] // pieces), jnp.float32)
        return lax.dynamic_update_index_in_dim(
            wide, values.reshape(pieces, -1), part, axis=1
        ).reshape(-1)

    small_grad = jnp.concatenate(
        [
            norm_sums.reshape(4 * D),
            spread(d_qkv_bias, 3),
            back_total,
            spread(d_up_bias, shards),
            back_total,
        ]
    )
    if own:
        padded = jnp.pad(small_grad.reshape(shards, small_rows), ((0, 0), (0, 2048 - small_rows)))
        out_sum, scaled, down_grad, up_grad, qkv_grad, out_grad, small_sum = reduce(
            out_part, scaled_part, terms, out_term, padded.reshape(shards, 16, 128)
        )
        reduced = (qkv_grad, out_grad, up_grad, down_grad, small_sum[: small_rows // 128])
    else:
        small_sum = lax.psum(small_grad, ("dp", "fsdp"))
        small_rows = small_master.shape[0]
        small_sum = lax.dynamic_slice_in_dim(small_sum, shard * small_rows, small_rows)
        qkv_term, out_term, up_term, down_term = terms
        out_wide = lax.dynamic_update_slice_in_dim(
            jnp.zeros((D, D), jnp.bfloat16), out_term, part * head_cols, axis=0
        )

        def to_owner(term):
            own = lax.psum_scatter(term, "fsdp", scatter_dimension=0, tiled=True)
            return lax.all_gather(own, "dp", axis=0, tiled=False).astype(jnp.float32)

        reduced = (
            joined(to_owner(qkv_term), 3),
            lax.psum(
                lax.psum_scatter(out_wide, "fsdp", scatter_dimension=0, tiled=True), "dp"
            ).astype(jnp.float32),
            joined(to_owner(up_term), shards),
            to_owner(down_term).reshape(down_master.shape),
            small_sum,
        )

    unit_rows, inverse_rows = normalize(inputs)
    output = ((inputs + out_sum + out_bias + down_bias) * live).astype(jnp.bfloat16)
    input_grad = back + inverse_rows * (
        scaled
        - jnp.mean(scaled, axis=-1, keepdims=True)
        - unit_rows * jnp.mean(scaled * unit_rows, axis=-1, keepdims=True)
    )
    update = lamb_split if own else lamb
    return (output[None], input_grad.astype(jnp.bfloat16)[None]) + update(
        masters, firsts, seconds, reduced
    )


def lamb_rows(first_old, second_old, master, grad):
    first_new = BETA_ONE * first_old + (1.0 - BETA_ONE) * grad
    second_new = BETA_TWO * second_old + (1.0 - BETA_TWO) * grad * grad
    update = first_new / (jnp.sqrt(second_new) + ADAM_EPSILON) + DECAY * master
    return first_new, second_new, update


def lane_sums(values):
    squares = jnp.sum(values * values, axis=0, keepdims=True)
    total = squares[:, 0:128]
    for n in range(1, squares.shape[1] // 128):
        total = total + squares[:, n * 128 : (n + 1) * 128]
    return total


def moments_kernel(*refs):
    qkv_grad, out_grad, up_grad, down_grad, small_grad = refs[0:5]
    masters, firsts, seconds = refs[5:10], refs[10:15], refs[15:20]
    first_news, second_news, updates = refs[20:25], refs[25:30], refs[30:35]
    squares = refs[35]
    step = pl.program_id(0)

    @pl.when(step == 0)
    def _():
        squares[...] = jnp.zeros_like(squares)

    def one(number, span, grad):
        index = (slice(None), span)
        first_new, second_new, update = lamb_rows(
            firsts[number][index], seconds[number][index], masters[number][index], grad
        )
        first_news[number][index] = first_new
        second_news[number][index] = second_new
        updates[number][index] = update
        return lane_sums(masters[number][index]), lane_sums(update)

    def add(number, pairs):
        weight, update = pairs[0]
        for more_weight, more_update in pairs[1:]:
            weight, update = weight + more_weight, update + more_update
        squares[number : number + 1] += weight
        squares[8 + number : 9 + number] += update

    f32 = jnp.float32
    parts = qkv_grad.shape[0]
    width = qkv_grad.shape[2] // 3
    add(
        0,
        [
            one(
                0,
                slice((c * parts + d) * width, (c * parts + d + 1) * width),
                qkv_grad[d, :, c * width : (c + 1) * width].astype(f32),
            )
            for c in range(3)
            for d in range(parts)
        ],
    )
    add(1, [one(1, slice(None), out_grad[...].astype(f32))])
    pieces = up_grad.shape[2] // 128
    add(
        2,
        [
            one(
                2,
                slice((g * parts + d) * 128, (g * parts + d + 1) * 128),
                up_grad[d, :, g * 128 : (g + 1) * 128].astype(f32),
            )
            for g in range(pieces)
            for d in range(parts)
        ],
    )
    add(3, [one(3, slice(None), down_grad[0].astype(f32))])

    @pl.when(step == 0)
    def _():
        first_new, second_new, update = lamb_rows(
            firsts[4][...], seconds[4][...], masters[4][...], small_grad[...]
        )
        first_news[4][...] = first_new
        second_news[4][...] = second_new
        updates[4][...] = update
        squares[4:5] += lane_sums(masters[4][...])
        squares[12:13] += lane_sums(update)


def lamb_specs(masters, steps):
    specs = [pl.BlockSpec((m.shape[0] // steps, m.shape[1]), lambda i: (i, 0)) for m in masters[:4]]
    return specs + [pl.BlockSpec(masters[4].shape, lambda i: (0, 0))]


def moments(grads, masters, firsts, seconds, steps=8):
    qkv_grad, out_grad, up_grad, down_grad, small_grad = grads
    shape = jax.ShapeDtypeStruct
    each = lamb_specs(masters, steps)
    rows = qkv_grad.shape[1]
    halves = steps // qkv_grad.shape[0]
    grad_specs = [
        pl.BlockSpec((qkv_grad.shape[0], rows // steps, qkv_grad.shape[2]), lambda i: (0, i, 0)),
        each[1],
        pl.BlockSpec((up_grad.shape[0], rows // steps, up_grad.shape[2]), lambda i: (0, i, 0)),
        pl.BlockSpec(
            (1, rows // halves, down_grad.shape[2]), lambda i: (i // halves, i % halves, 0)
        ),
        each[4],
    ]
    out = [shape(m.shape, jnp.float32) for m in masters]
    results = pl.pallas_call(
        moments_kernel,
        grid=(steps,),
        in_specs=grad_specs + each * 3,
        out_specs=each * 3 + [pl.BlockSpec((16, 128), lambda i: (0, 0))],
        out_shape=out * 3 + [shape((16, 128), jnp.float32)],
        compiler_params=pltpu.CompilerParams(vmem_limit_bytes=40 << 20),
        name="moments",
    )(*grads, *masters, *firsts, *seconds)
    return results[0:5], results[5:10], results[10:15], results[15]


def norms_kernel(squares, total, steps, everyone, send_sem, recv_sem):
    shard, part = lax.axis_index("fsdp"), lax.axis_index("dp")
    peers = [(part, (shard + k) % 8) for k in range(1, 8)]
    barrier = pltpu.get_barrier_semaphore()
    for peer in peers:
        pl.semaphore_signal(barrier, inc=1, device_id=peer, device_id_type=MESH_ID)
    pl.semaphore_wait(barrier, 7)
    for k in range(1, 8):
        send(
            squares, everyone.at[shard], send_sem.at[k - 1], recv_sem.at[k - 1], peers[k - 1]
        ).start()
    everyone[shard] = squares[...]
    for k in range(1, 8):
        arrived(everyone.at[(shard + 8 - k) % 8], recv_sem.at[k - 1], peers[7 - k])
    for k in range(1, 8):
        sent(squares, send_sem.at[k - 1], peers[k - 1])
    summed = everyone[0]
    for k in range(1, 8):
        summed = summed + everyone[k]
    norms = jnp.sqrt(jnp.sum(summed, axis=1, keepdims=True))
    total[...] = jnp.broadcast_to(norms, (16, 128))
    steps[...] = jnp.broadcast_to(RATE * (norms[0:8] / norms[8:16]), (8, 128))


def norms(squares):
    shape = jax.ShapeDtypeStruct
    dma = pltpu.SemaphoreType.DMA
    return pl.pallas_call(
        norms_kernel,
        out_shape=(shape((16, 128), jnp.float32), shape((8, 128), jnp.float32)),
        in_specs=[VMEM_SPEC],
        out_specs=(VMEM_SPEC,) * 2,
        scratch_shapes=[pltpu.VMEM((8, 16, 128), jnp.float32), dma((7,)), dma((7,))],
        compiler_params=pltpu.CompilerParams(collective_id=2, has_side_effects=True),
        name="norms",
    )(squares)


def step_kernel(*refs):
    scales, masters, updates, news = refs[0], refs[1:6], refs[6:11], refs[11:16]
    for number in range(5):
        scale = scales[number : number + 1, 0:1]
        news[number][...] = masters[number][...] - scale * updates[number][...]


def step_masters(scales, masters, updates, steps=8):
    each = lamb_specs(masters, steps)
    return pl.pallas_call(
        step_kernel,
        grid=(steps,),
        in_specs=[pl.BlockSpec((8, 128), lambda i: (0, 0))] + each * 2,
        out_specs=each,
        out_shape=[jax.ShapeDtypeStruct(m.shape, jnp.float32) for m in masters],
        compiler_params=pltpu.CompilerParams(vmem_limit_bytes=40 << 20),
        name="step_masters",
    )(scales, *masters, *updates)


def lamb_split(masters, firsts, seconds, grads):
    def tall(arrays):
        return tuple(arrays[:4]) + (arrays[4].reshape(-1, 128),)

    def flat_small(arrays):
        return tuple(arrays[:4]) + (arrays[4].reshape(-1),)

    masters, firsts, seconds = tall(masters), tall(firsts), tall(seconds)
    first_news, second_news, updates, squares = moments(grads, masters, firsts, seconds)
    total, scales = norms(squares)
    news = step_masters(scales, masters, updates)
    lamb_norms = jnp.stack([total[0:5, 0], total[8:13, 0]])
    return flat_small(news) + flat_small(first_news) + flat_small(second_news) + (lamb_norms,)


def lamb(masters, firsts, seconds, reduced):
    updates = []
    first_news = []
    second_news = []
    for first_old, second_old, master, grad_sum in zip(firsts, seconds, masters, reduced):
        first_new = BETA_ONE * first_old + (1.0 - BETA_ONE) * grad_sum
        second_new = BETA_TWO * second_old + (1.0 - BETA_TWO) * grad_sum * grad_sum
        updates.append(first_new / (jnp.sqrt(second_new) + ADAM_EPSILON) + DECAY * master)
        first_news.append(first_new)
        second_news.append(second_new)
    weight_squares, update_squares = lax.psum(
        (local_squares(masters), local_squares(updates)), "fsdp"
    )
    weight_norms = jnp.sqrt(weight_squares)
    update_norms = jnp.sqrt(update_squares)
    new_masters = [
        masters[number] - RATE * (weight_norms[number] / update_norms[number]) * updates[number]
        for number in range(5)
    ]
    lamb_norms = jnp.stack([weight_norms, update_norms])
    return tuple(new_masters) + tuple(first_news) + tuple(second_news) + (lamb_norms,)


def solution(mesh):
    in_specs = (
        P(("dp", "fsdp"), None, None),
        P(("dp", "fsdp"), None, None),
        P(("dp", "fsdp")),
        P("fsdp", None),
        P("fsdp", None),
        P("fsdp", None),
        P("fsdp", None),
        P("fsdp"),
        P("fsdp", None),
        P("fsdp", None),
        P("fsdp", None),
        P("fsdp", None),
        P("fsdp"),
        P("fsdp", None),
        P("fsdp", None),
        P("fsdp", None),
        P("fsdp", None),
        P("fsdp"),
    )
    out_specs = (
        P(("dp", "fsdp"), None, None),
        P(("dp", "fsdp"), None, None),
        P("fsdp", None),
        P("fsdp", None),
        P("fsdp", None),
        P("fsdp", None),
        P("fsdp"),
        P("fsdp", None),
        P("fsdp", None),
        P("fsdp", None),
        P("fsdp", None),
        P("fsdp"),
        P("fsdp", None),
        P("fsdp", None),
        P("fsdp", None),
        P("fsdp", None),
        P("fsdp"),
        P(),
    )
    return jax.shard_map(local_split, mesh=mesh, in_specs=in_specs, out_specs=out_specs, check_vma=False)
```

```python
import math

import jax
import jax.numpy as jnp
import numpy as np
from jax import lax
from jax.experimental import pallas as pl
from jax.experimental.pallas import tpu as pltpu
from jax.sharding import PartitionSpec as P

D = 1024
HEADS = 16
HD = 64
FF = 4096
ROT = 16
SMALL = 13312


NORM_EPSILON = 1e-05
ADAM_EPSILON = 1e-06
ROPE_BASE = 10000.0
RATE = 0.5
DECAY = 0.01
BETA_ONE = 0.5
BETA_TWO = 0.5


def split_small(small_vector):
    bounds = [0, D, 2 * D, 3 * D, 4 * D, 7 * D, 8 * D, 8 * D + FF, 9 * D + FF]
    return [small_vector[bounds[number] : bounds[number + 1]] for number in range(8)]


def normalize(values):
    average = jnp.mean(values, axis=-1, keepdims=True)
    centred = values - average
    variance = jnp.mean(centred * centred, axis=-1, keepdims=True)
    inverse = lax.rsqrt(variance + NORM_EPSILON)
    return (centred * inverse, inverse)


def rotary_tables(length):
    half_dims = ROT // 2
    position = jnp.arange(length, dtype=jnp.float32)[:, None]
    number = jnp.arange(half_dims, dtype=jnp.float32)[None, :]
    angle = position * jnp.exp(number * (-2.0 * math.log(ROPE_BASE) / ROT))
    return (jnp.cos(angle)[:, None, :], jnp.sin(angle)[:, None, :])


def rotate(heads_in, cosine_table, sine_table):
    half_dims = ROT // 2
    first_half = heads_in[..., :half_dims]
    second_half = heads_in[..., half_dims:ROT]
    return jnp.concatenate(
        [
            first_half * cosine_table - second_half * sine_table,
            second_half * cosine_table + first_half * sine_table,
            heads_in[..., ROT:],
        ],
        axis=-1,
    )


def rotate_back(grads_in, cosine_table, sine_table):
    half_dims = ROT // 2
    first_half = grads_in[..., :half_dims]
    second_half = grads_in[..., half_dims:ROT]
    return jnp.concatenate(
        [
            first_half * cosine_table + second_half * sine_table,
            second_half * cosine_table - first_half * sine_table,
            grads_in[..., ROT:],
        ],
        axis=-1,
    )


def gelu_slope(values):
    return 0.5 * (1.0 + lax.erf(values * 2.0 ** (-0.5))) + values * jnp.exp(
        -0.5 * values * values
    ) * (2.0 * math.pi) ** (-0.5)


def against(left, right):
    return lax.dot_general(
        left, right, (((1,), (1,)), ((), ())), preferred_element_type=jnp.float32
    )


def outer_sum(columns, right):
    return lax.dot_general(
        columns, right, (((0,), (0,)), ((), ())), preferred_element_type=jnp.float32
    )


def local_squares(arrays):
    return jnp.stack([jnp.sum(array_in * array_in) for array_in in arrays])


def sliced(master, part, parts, pieces):
    rows, columns = master.shape
    width = columns // (pieces * parts)
    return lax.dynamic_index_in_dim(
        master.reshape(rows, pieces, parts, width), part, axis=2, keepdims=False
    ).reshape(rows, pieces * width)


def joined(slices, pieces):
    parts, rows, columns = slices.shape
    width = columns // pieces
    return (
        slices.reshape(parts, rows, pieces, width)
        .transpose(1, 2, 0, 3)
        .reshape(rows, pieces * parts * width)
    )


def layer(x_all, cotangent_all, lengths_all, weights, small_all, part):
    qkv_weight, out_weight, up_weight, down_weight = weights
    group, length, _ = x_all.shape
    tokens = group * length
    head_cols = out_weight.shape[0]
    heads = head_cols // HD
    gain_one, shift_one, gain_two, shift_two, qkv_bias, up_bias = small_all
    inputs = x_all.reshape(tokens, D).astype(jnp.float32)
    position = jnp.arange(length)
    live = (position[None, :] < lengths_all[:, None]).astype(jnp.float32).reshape(tokens, 1)
    allowed = (position[None, None, :] <= position[None, :, None]) & (
        position[None, None, :] < lengths_all[:, None, None]
    )
    unit_rows, _ = normalize(inputs)
    normed_one = (unit_rows * gain_one + shift_one).astype(jnp.bfloat16)
    normed_two = (unit_rows * gain_two + shift_two).astype(jnp.bfloat16)
    projected = jnp.dot(normed_one, qkv_weight, preferred_element_type=jnp.float32) + qkv_bias
    projected = projected.reshape(group, length, 3, heads, HD)
    cosine_table, sine_table = rotary_tables(length)
    query_heads = rotate(projected[:, :, 0], cosine_table, sine_table).astype(jnp.bfloat16)
    key_heads = rotate(projected[:, :, 1], cosine_table, sine_table).astype(jnp.bfloat16)
    value_heads = projected[:, :, 2].astype(jnp.bfloat16)
    scores = jnp.einsum(
        "gqhd,gkhd->ghqk", query_heads, key_heads, preferred_element_type=jnp.float32
    ) * HD ** (-0.5)
    scores = jnp.where(allowed[:, None], scores, -1e30)
    row_top = jnp.max(scores, axis=-1, keepdims=True)
    raised = jnp.exp(scores - row_top)
    attend = raised / jnp.sum(raised, axis=-1, keepdims=True)
    attend_low = attend.astype(jnp.bfloat16)
    mixed = jnp.einsum(
        "ghqk,gkhd->gqhd", attend_low, value_heads, preferred_element_type=jnp.float32
    )
    mixed = mixed.reshape(tokens, head_cols).astype(jnp.bfloat16)
    hidden = jnp.dot(normed_two, up_weight, preferred_element_type=jnp.float32) + up_bias
    activated = jax.nn.gelu(hidden, approximate=False).astype(jnp.bfloat16)
    out_part = jnp.dot(mixed, out_weight, preferred_element_type=jnp.float32) + jnp.dot(
        activated, down_weight, preferred_element_type=jnp.float32
    )

    back = (cotangent_all.reshape(tokens, D).astype(jnp.float32) * live).astype(jnp.bfloat16)
    d_hidden = (against(back, down_weight) * gelu_slope(hidden)).astype(jnp.bfloat16)
    d_mixed = against(back, out_weight).astype(jnp.bfloat16).reshape(group, length, heads, HD)
    d_attend = jnp.einsum(
        "gqhd,gkhd->ghqk", d_mixed, value_heads, preferred_element_type=jnp.float32
    )
    row_inner = jnp.sum(attend * d_attend, axis=-1, keepdims=True)
    d_scores = (attend * (d_attend - row_inner)).astype(jnp.bfloat16)
    d_queries = jnp.einsum(
        "ghqk,gkhd->gqhd", d_scores, key_heads, preferred_element_type=jnp.float32
    ) * HD ** (-0.5)
    d_keys = jnp.einsum(
        "ghqk,gqhd->gkhd", d_scores, query_heads, preferred_element_type=jnp.float32
    ) * HD ** (-0.5)
    d_values = jnp.einsum(
        "ghqk,gqhd->gkhd", attend_low, d_mixed, preferred_element_type=jnp.float32
    )
    d_projected = jnp.stack(
        [
            rotate_back(d_queries, cosine_table, sine_table),
            rotate_back(d_keys, cosine_table, sine_table),
            d_values,
        ],
        axis=2,
    )
    d_projected = d_projected.reshape(tokens, 3 * head_cols).astype(jnp.bfloat16)
    d_normed_one = against(d_projected, qkv_weight)
    d_normed_two = against(d_hidden, up_weight)
    scaled_part = d_normed_one * gain_one + d_normed_two * gain_two
    norm_sums = jnp.stack(
        [
            jnp.sum(d_normed_one * unit_rows, axis=0),
            jnp.sum(d_normed_one, axis=0),
            jnp.sum(d_normed_two * unit_rows, axis=0),
            jnp.sum(d_normed_two, axis=0),
        ]
    )
    d_qkv_bias = jnp.sum(d_projected, axis=0, dtype=jnp.float32)
    d_up_bias = jnp.sum(d_hidden, axis=0, dtype=jnp.float32)
    terms = (
        outer_sum(normed_one, d_projected),
        outer_sum(mixed, back),
        outer_sum(normed_two, d_hidden),
        outer_sum(activated, back),
    )
    return (
        out_part.astype(jnp.bfloat16),
        scaled_part.astype(jnp.bfloat16),
        tuple(term.astype(jnp.bfloat16) for term in terms),
        (norm_sums, d_qkv_bias, d_up_bias),
    )


MESH_ID = pl.DeviceIdType.MESH
HALF = 128


class Place:
    def __init__(self):
        self.part = lax.axis_index("dp")
        self.shard = lax.axis_index("fsdp")
        self.z = self.shard // 2
        self.core = self.shard % 2
        self.x_part = 2 * (self.part // 2) + 1 - self.part % 2
        self.y_part = (self.part + 2) % 4
        self.far_part = 3 - self.part
        self.across_x = (self.x_part, self.shard)
        self.across_y = (self.y_part, self.shard)
        self.across_far = (self.far_part, self.shard)
        self.other_core = (self.part, 2 * self.z + 1 - self.core)
        self.up = (self.part, jnp.minimum(self.shard + 2, 7))
        self.down = (self.part, jnp.maximum(self.shard - 2, 0))

    def shard_after(self, k):
        return (self.part, (self.shard + k) % 8)


def send(source, target, send_sem, recv_sem, device):
    return pltpu.make_async_remote_copy(
        src_ref=source,
        dst_ref=target,
        send_sem=send_sem,
        recv_sem=recv_sem,
        device_id=device,
        device_id_type=MESH_ID,
    )


def arrived(target, recv_sem, device):
    send(target, target, recv_sem, recv_sem, device).wait_recv()


def sent(source, send_sem, device):
    send(source, source, send_sem, send_sem, device).wait_send()


def greet(at):
    barrier = pltpu.get_barrier_semaphore()
    peers = [at.across_x, at.across_y, at.across_far] + [at.shard_after(k) for k in range(1, 8)]
    for peer in peers:
        pl.semaphore_signal(barrier, inc=1, device_id=peer, device_id_type=MESH_ID)
    pl.semaphore_wait(barrier, len(peers))


SPANS = ((0, 768), (768, 1792), (1792, 2816))
Q, U, N = 0, 1, 2


def nt(left, right):
    return lax.dot_general(
        left, right, (((1,), (1,)), ((), ())), preferred_element_type=jnp.float32
    )


def tn(left, right):
    return lax.dot_general(
        left, right, (((0,), (0,)), ((), ())), preferred_element_type=jnp.float32
    )


def nn(left, right):
    return jnp.dot(left, right, preferred_element_type=jnp.float32)


def flat(value):
    return value.reshape(value.shape[0] * value.shape[1], value.shape[2])


def layer_kernel(
    length_own,
    x_own,
    cot_own,
    qkv_master,
    out_master,
    up_master,
    down_master,
    small_master,
    tables,
    output,
    input_grad,
    qkv_all,
    up_all,
    down_all,
    out_grad,
    small_sum,
    x_all,
    cot_all,
    len_all,
    w_all,
    out_all,
    small_own,
    small_all,
    vectors,
    qkv_bias,
    up_bias,
    stats,
    normed_one,
    normed_two,
    back,
    heads_qkv,
    mixed,
    d_projected,
    hidden,
    d_hidden,
    out_part,
    dx_part,
    terms,
    out_term,
    sums,
    d_qkv_bias,
    d_up_bias,
    small_part,
    plane_one,
    plane_two,
    plane_turn,
    core_in,
    line_in,
    out_core_in,
    out_line,
    out_line_in,
    small_in,
    small_total,
    small_plane,
    load_sem,
    plane_send,
    plane_recv,
    len_send,
    len_recv,
    w_send,
    w_recv,
    out_send,
    out_recv,
    small_send,
    small_recv,
    part_send,
    part_recv,
    core_send,
    core_recv,
    line_send,
    line_recv,
    rows_send,
    rows_recv,
    all_send,
    all_recv,
    keep_sem,
    total_send,
    total_recv,
):
    f32, bf16 = jnp.float32, jnp.bfloat16
    at = Place()
    z, core, part, shard = at.z, at.core, at.part, at.shard
    length = x_own.shape[0]
    head_cols = mixed.shape[2]
    activated = normed_one
    place_x, place_y = part % 2, part // 2

    def near_first(i):
        return 2 * ((place_y + i // 2) % 2) + (place_x + i % 2) % 2

    def far_first(i):
        return 2 * ((place_y + 1 - i % 2) % 2) + (place_x + 1 - i // 2) % 2

    def piece(ref, slot, n):
        return ref.at[slot, :, SPANS[n][0] : SPANS[n][1]]

    plane_peers = (
        (at.across_x, at.x_part),
        (at.across_y, at.y_part),
        (at.across_far, at.far_part),
    )

    stage = [hidden.at[n, 0:128] for n in range(4)]
    loads = []
    for c in range(3):
        columns = pl.ds(pl.multiple_of(c * D + part * head_cols, 128), head_cols)
        target = stage[0].at[:, c * head_cols : (c + 1) * head_cols]
        loads.append((qkv_master.at[:, columns], target))
    loads.append((out_master, stage[1]))
    for g in range(8):
        columns = pl.ds(pl.multiple_of(g * (FF // 8) + part * 128, 128), 128)
        loads.append((up_master.at[:, columns], stage[2].at[:, g * 128 : (g + 1) * 128]))
    rows = pl.ds(pl.multiple_of(part * 128, 128), 128)
    loads.append((down_master.at[rows], stage[3]))
    loads.append((x_own, x_all.at[part]))
    loads.append((cot_own, cot_all.at[part]))

    def load(n):
        return pltpu.make_async_copy(loads[n][0], loads[n][1], load_sem.at[n])

    for n in range(len(loads)):
        load(n).start()
    len_all[part] = jnp.full((8, 128), length_own[0], jnp.int32).astype(f32)
    small_own[...] = jnp.zeros_like(small_own)
    small_own[0:13] = small_master[...].astype(bf16).astype(f32)
    small_all[shard] = small_own[...]
    greet(at)

    activations = ((x_own, x_all), (cot_own, cot_all))
    for n, (own, whole) in enumerate(activations):
        send(own, whole.at[part], plane_send.at[n, 0], plane_recv.at[n, 0], at.across_x).start()
        send(own, whole.at[part], plane_send.at[n, 1], plane_recv.at[n, 1], at.across_y).start()

    def cast(n, first, last):
        for m in range(first, last):
            load(m).wait()
        low, high = SPANS[n]
        w_all[shard, :, low:high] = stage[(0, 2, 3)[n]][:, 0 : high - low].astype(bf16)

    def send_own(n):
        block = piece(w_all, shard, n)

        @pl.when(z < 3)
        def _():
            send(block, block, w_send.at[0, n, z], w_recv.at[n, shard], at.up).start()

        @pl.when(z > 0)
        def _():
            send(block, block, w_send.at[1, n, z], w_recv.at[n, shard], at.down).start()

        send(block, block, w_send.at[2, n, z], w_recv.at[n, shard], at.other_core).start()

    def forward(k, n):
        @pl.when(z >= k)
        def _():
            source = 2 * (z - k) + core
            block = piece(w_all, source, n)
            arrived(block, w_recv.at[n, source], at.down)

            @pl.when(z < 3)
            def _():
                send(block, block, w_send.at[0, n, z - k], w_recv.at[n, source], at.up).start()

            send(
                block, block, w_send.at[2, n, z - k], w_recv.at[n, source], at.other_core
            ).start()

        @pl.when(z + k <= 3)
        def _():
            source = 2 * (z + k) + core
            block = piece(w_all, source, n)
            arrived(block, w_recv.at[n, source], at.up)

            @pl.when(z > 0)
            def _():
                send(block, block, w_send.at[1, n, z + k], w_recv.at[n, source], at.down).start()

            send(
                block, block, w_send.at[2, n, z + k], w_recv.at[n, source], at.other_core
            ).start()

    def from_core(n):
        for other in range(4):
            source = 2 * other + 1 - core
            arrived(piece(w_all, source, n), w_recv.at[n, source], at.other_core)

    def send_out_rows():
        block = out_all.at[core]

        @pl.when(z < 3)
        def _():
            send(block, block, out_send.at[0], out_recv.at[core], at.up).start()

        @pl.when(z > 0)
        def _():
            send(block, block, out_send.at[1], out_recv.at[core], at.down).start()

        send(block, block, out_send.at[2], out_recv.at[core], at.other_core).start()

    def forward_out(k):
        @pl.when((z - k == part) | (z + k == part))
        def _():
            block = out_all.at[core]
            arrived(block, out_recv.at[core], at.up)

            @pl.when((z > part) & (z < 3))
            def _():
                send(block, block, out_send.at[0], out_recv.at[core], at.up).start()

            @pl.when((z < part) & (z > 0))
            def _():
                send(block, block, out_send.at[1], out_recv.at[core], at.down).start()

            send(block, block, out_send.at[2], out_recv.at[core], at.other_core).start()

    def forward_x(n):
        whole = activations[n][1]
        arrived(whole.at[at.x_part], plane_recv.at[n, 0], at.across_x)
        block = whole.at[at.x_part, 0:HALF]
        send(block, block, plane_send.at[n, 2], plane_recv.at[n, 2], at.across_y).start()

    def forward_y(n):
        whole = activations[n][1]
        arrived(whole.at[at.y_part], plane_recv.at[n, 1], at.across_y)
        block = whole.at[at.y_part, HALF : 2 * HALF]
        send(block, block, plane_send.at[n, 3], plane_recv.at[n, 3], at.across_x).start()

    def far_halves(n):
        whole = activations[n][1]
        arrived(whole.at[at.far_part, 0:HALF], plane_recv.at[n, 2], at.across_y)
        arrived(whole.at[at.far_part, HALF : 2 * HALF], plane_recv.at[n, 3], at.across_x)

    cast(Q, 0, 3)
    send_own(Q)
    load(3).wait()

    @pl.when(z == part)
    def _():
        out_all[core] = stage[1][...].astype(bf16)
        send_out_rows()

    for n, (peer, _) in enumerate(plane_peers):
        send(len_all.at[part], len_all.at[part], len_send.at[n], len_recv.at[n], peer).start()
    for k in range(1, 8):
        send(
            small_own,
            small_all.at[shard],
            small_send.at[k - 1],
            small_recv.at[k - 1],
            at.shard_after(k),
        ).start()
    cast(U, 4, 12)
    cast(N, 12, 13)
    load(13).wait()
    load(14).wait()
    forward(1, Q)
    forward_out(1)
    forward(2, Q)
    send_own(U)
    send_own(N)
    for n, (peer, other) in enumerate(plane_peers):
        arrived(len_all.at[other], len_recv.at[n], peer)
    for k in range(1, 8):
        arrived(small_all.at[(shard + 8 - k) % 8], small_recv.at[k - 1], at.shard_after(8 - k))
    for number, row in enumerate((0, 8, 16, 24, 56, 96)):
        for n in range(8):
            source = row + n
            vectors[number : number + 1, n * 128 : (n + 1) * 128] = small_all[
                source // 13, source % 13 : source % 13 + 1
            ]
    for c in range(3):
        for n in range(2):
            source = 32 + 8 * c + 2 * part + n
            columns = slice((2 * c + n) * 128, (2 * c + n + 1) * 128)
            qkv_bias[:, columns] = small_all[source // 13, pl.ds(source % 13, 1)]
    for g in range(8):
        source = 64 + 4 * g + part
        up_bias[:, g * 128 : (g + 1) * 128] = small_all[source // 13, pl.ds(source % 13, 1)]

    sums[...] = jnp.zeros_like(sums)
    d_qkv_bias[...] = jnp.zeros_like(d_qkv_bias)
    d_up_bias[...] = jnp.zeros_like(d_up_bias)
    block_rows = 64

    def norm_rows(s):
        @pl.loop(0, length // block_rows)
        def _(i):
            r = pl.ds(pl.multiple_of(i * block_rows, block_rows), block_rows)
            values = x_all[s, r, :].astype(f32)
            mean = jnp.mean(values, axis=-1, keepdims=True)
            centred = values - mean
            inverse = lax.rsqrt(
                jnp.mean(centred * centred, axis=-1, keepdims=True) + NORM_EPSILON
            )
            stats[s, r, 0:1] = mean
            stats[s, r, 1:2] = inverse
            unit = centred * inverse
            normed_one[s, r, :] = (unit * vectors[0:1] + vectors[1:2]).astype(bf16)
            normed_two[s, r, :] = (unit * vectors[2:3] + vectors[3:4]).astype(bf16)

    def live_rows(s):
        index = lax.broadcasted_iota(jnp.int32, (length, 1), 0)
        return index.astype(f32) < len_all[s][0:1, 0:1]

    def rotate(value, sign):
        return (
            value * tables[0]
            + sign * pltpu.roll(value, head_cols - ROT // 2, 1) * tables[1]
            + sign * pltpu.roll(value, ROT // 2, 1) * tables[2]
        )

    def project(s):
        norm_rows(s)
        low, high = SPANS[Q]
        value = nn(normed_one[s], flat(w_all[:, :, low:high])) + qkv_bias[...]
        heads_qkv[s, :, 0:head_cols] = rotate(value[:, 0:head_cols], 1.0).astype(bf16)
        heads_qkv[s, :, head_cols : 2 * head_cols] = rotate(
            value[:, head_cols : 2 * head_cols], 1.0
        ).astype(bf16)
        heads_qkv[s, :, 2 * head_cols :] = value[:, 2 * head_cols :].astype(bf16)

    def attend(s):
        cot = cot_all[s]
        back[s] = jnp.where(live_rows(s), cot, jnp.zeros_like(cot))
        queries = heads_qkv[s, :, 0:head_cols]
        keys = heads_qkv[s, :, head_cols : 2 * head_cols]
        values = heads_qkv[s, :, 2 * head_cols :]
        d_mixed = nt(back[s], flat(out_all[...])).astype(bf16)
        row = lax.broadcasted_iota(jnp.int32, (length, length), 0)
        column = lax.broadcasted_iota(jnp.int32, (length, length), 1)
        allowed = (column <= row) & (column.astype(f32) < len_all[s][0:1, 0:1])
        lane = lax.broadcasted_iota(jnp.int32, (length, head_cols), 1)
        zero = jnp.zeros((), bf16)
        mixed_sum = jnp.zeros((length, head_cols), f32)
        d_queries = d_keys = d_values = mixed_sum
        for h in range(head_cols // HD):
            of_head = (lane >= h * HD) & (lane < (h + 1) * HD)
            q_h, k_h, v_h, d_h = (
                jnp.where(of_head, t, zero) for t in (queries, keys, values, d_mixed)
            )
            scores = jnp.where(allowed, nt(q_h, keys) * HD**-0.5, -1e30)
            raised = jnp.exp(scores - jnp.max(scores, axis=-1, keepdims=True))
            weights = raised * (1.0 / jnp.sum(raised, axis=-1, keepdims=True))
            low = weights.astype(bf16)
            mixed_sum = mixed_sum + nn(low, v_h)
            d_weights = nt(d_h, values)
            inner = jnp.sum(weights * d_weights, axis=-1, keepdims=True)
            d_scores = (weights * (d_weights - inner)).astype(bf16)
            d_queries = d_queries + nn(d_scores, k_h)
            d_keys = d_keys + tn(d_scores, q_h)
            d_values = d_values + tn(low, d_h)
        mixed[s] = mixed_sum.astype(bf16)
        for n, value in enumerate(
            (rotate(d_queries * HD**-0.5, -1.0), rotate(d_keys * HD**-0.5, -1.0), d_values)
        ):
            rounded = value.astype(bf16)
            columns = slice(n * head_cols, (n + 1) * head_cols)
            d_projected[s, :, columns] = rounded
            d_qkv_bias[:, columns] += jnp.sum(rounded.astype(f32), axis=0, keepdims=True)

    forward(3, Q)
    from_core(Q)

    @pl.loop(0, 4)
    def _(i):
        @pl.when(i == 1)
        def _():
            forward_x(0)

        @pl.when(i == 2)
        def _():
            forward_y(0)

        @pl.when(i == 3)
        def _():
            far_halves(0)

        project(near_first(i))

        @pl.when(i == 0)
        def _():
            forward_out(2)
            forward(1, U)

        @pl.when(i == 2)
        def _():
            forward(1, N)

    forward_out(3)
    arrived(out_all.at[1 - core], out_recv.at[1 - core], at.other_core)

    @pl.loop(0, 4)
    def _(i):
        @pl.when(i == 3)
        def _():
            far_halves(1)

        attend(near_first(i))

        @pl.when(i == 0)
        def _():
            forward_x(1)
            forward_y(1)
            forward(2, U)

        @pl.when(i == 1)
        def _():
            forward(2, N)

    def gradient(left, right, n):
        low, high = SPANS[n]

        @pl.loop(0, 8)
        def _(f):
            columns = pl.ds(pl.multiple_of(f * 128, 128), 128)
            terms[f, :, low:high] = tn(flat(left[:, :, columns]), flat(right[...])).astype(bf16)

    def to_core(n):
        for other in range(4):
            send(
                piece(terms, 2 * other + 1 - core, n),
                piece(core_in, other, n),
                core_send.at[n, other],
                core_recv.at[n, other],
                at.other_core,
            ).start()

    def add_core(n):
        low, high = SPANS[n]
        for other in (3, 0, 2, 1):
            arrived(piece(core_in, other, n), core_recv.at[n, other], at.other_core)
            terms[2 * other + core, :, low:high] = (
                terms[2 * other + core, :, low:high].astype(f32)
                + core_in[other, :, low:high].astype(f32)
            ).astype(bf16)

    def pass_on(n, me, target):
        low, high = SPANS[n]

        @pl.when(z == me)
        def _():
            own = piece(terms, 2 * target + core, n)
            if me not in (0, 3):
                source = at.down if me < target else at.up
                arrived(piece(line_in, target, n), line_recv.at[n, target], source)
                terms[2 * target + core, :, low:high] = (
                    terms[2 * target + core, :, low:high].astype(f32)
                    + line_in[target, :, low:high].astype(f32)
                ).astype(bf16)
            slot = 4 if me == target + 1 else target
            send(
                own,
                piece(line_in, slot, n),
                line_send.at[n, target],
                line_recv.at[n, slot],
                at.up if me < target else at.down,
            ).start()

    def line_starts(n):
        for target in (3, 2, 1):
            pass_on(n, 0, target)
        for target in (0, 1, 2):
            pass_on(n, 3, target)

    def line_step(n, step):
        for me, target in (((1, 3), (2, 0)), ((1, 2), (2, 1)), ((2, 3), (1, 0)))[step]:
            pass_on(n, me, target)

    wholes = (qkv_all, up_all, down_all)

    def line_ends(n):
        low, high = SPANS[n]
        total = 2 * z + core

        def add(slot, source):
            arrived(piece(line_in, slot, n), line_recv.at[n, slot], source)
            terms[total, :, low:high] = (
                terms[total, :, low:high].astype(f32) + line_in[slot, :, low:high].astype(f32)
            ).astype(bf16)

        @pl.when(z > 0)
        def _():
            add(z, at.down)

        @pl.when(z < 3)
        def _():
            add(4, at.up)

        own = piece(terms, total, n)
        target = wholes[n].at[part]
        send(own, target, all_send.at[n, 0], all_recv.at[n, 0], at.across_x).start()
        send(own, target, all_send.at[n, 1], all_recv.at[n, 1], at.across_y).start()
        pltpu.make_async_copy(own, target, keep_sem.at[n]).start()

    def share(n):
        whole = wholes[n]
        arrived(whole.at[at.x_part], all_recv.at[n, 0], at.across_x)
        block = whole.at[at.x_part, 0:64]
        send(block, block, all_send.at[n, 2], all_recv.at[n, 2], at.across_y).start()
        arrived(whole.at[at.y_part], all_recv.at[n, 1], at.across_y)
        block = whole.at[at.y_part, 64:128]
        send(block, block, all_send.at[n, 3], all_recv.at[n, 3], at.across_x).start()

    def out_to_core():
        send(
            out_term.at[1 - core], out_core_in, rows_send.at[0], rows_recv.at[0], at.other_core
        ).start()

    def out_add(block):
        out_line[...] = (out_line[...].astype(f32) + block.astype(f32)).astype(bf16)

    def out_add_core():
        arrived(out_core_in, rows_recv.at[0], at.other_core)
        out_line[...] = out_term[core]
        out_add(out_core_in[...])

    def out_step(step):
        @pl.when((z == step) & (z < part))
        def _():
            if step > 0:
                arrived(out_line_in.at[0], rows_recv.at[1], at.down)
                out_add(out_line_in[0])
            send(out_line, out_line_in.at[0], rows_send.at[1], rows_recv.at[1], at.up).start()

        @pl.when((z == 3 - step) & (z > part))
        def _():
            if step > 0:
                arrived(out_line_in.at[1], rows_recv.at[2], at.up)
                out_add(out_line_in[1])
            send(out_line, out_line_in.at[1], rows_send.at[1], rows_recv.at[2], at.down).start()

    def out_ends():
        @pl.when(z == part)
        def _():
            @pl.when(z > 0)
            def _():
                arrived(out_line_in.at[0], rows_recv.at[1], at.down)
                out_add(out_line_in[0])

            @pl.when(z < 3)
            def _():
                arrived(out_line_in.at[1], rows_recv.at[2], at.up)
                out_add(out_line_in[1])

            for n, (peer, _) in enumerate(plane_peers):
                send(out_line, out_grad, rows_send.at[2 + n], rows_recv.at[3], peer).start()
            pltpu.make_async_copy(out_line, out_grad, keep_sem.at[3]).start()

    gradient(normed_one, d_projected, Q)
    to_core(Q)
    for n in range(2):
        out_term[n] = tn(flat(mixed[:, :, n * 128 : (n + 1) * 128]), flat(back[...])).astype(bf16)
    out_to_core()
    add_core(Q)
    line_starts(Q)
    out_add_core()
    out_step(0)
    forward(3, U)
    forward(3, N)
    from_core(U)
    from_core(N)

    halves = (slice(0, HALF), slice(HALF, 2 * HALF))
    part_refs = (out_part, dx_part)
    routes = (
        (halves[0], at.across_x, at.x_part, at.across_y, at.y_part),
        (halves[1], at.across_y, at.y_part, at.across_x, at.x_part),
    )

    def send_part(n, r, m):
        half, peer, peer_part, _, _ = routes[r]
        target = (at.far_part, peer_part)[m]
        send(
            part_refs[n].at[target, half],
            plane_one.at[n, r, m],
            part_send.at[n, r, m],
            part_recv.at[n, r, m],
            peer,
        ).start()

    def send_parts(n, i):
        @pl.when(i == 0)
        def _():
            send_part(n, 0, 0)
            send_part(n, 1, 0)

        @pl.when(i == 1)
        def _():
            send_part(n, 0, 1)

        @pl.when(i == 2)
        def _():
            send_part(n, 1, 1)

    def turn_part(n, r):
        half, peer, _, turn, turned = routes[r]
        arrived(plane_one.at[n, r, 0], part_recv.at[n, r, 0], peer)
        plane_turn[n, r] = (
            part_refs[n][turned, half].astype(f32) + plane_one[n, r, 0].astype(f32)
        ).astype(bf16)
        send(
            plane_turn.at[n, r],
            plane_two.at[n, r],
            part_send.at[n, r, 2],
            part_recv.at[n, r, 2],
            turn,
        ).start()

    def whole_part(n, r):
        half, peer, _, turn, _ = routes[r]
        arrived(plane_one.at[n, r, 1], part_recv.at[n, r, 1], peer)
        arrived(plane_two.at[n, r], part_recv.at[n, r, 2], turn)
        return (
            part_refs[n][part, half].astype(f32)
            + plane_one[n, r, 1].astype(f32)
            + plane_two[n, r].astype(f32)
        )

    up_low, up_high = SPANS[U]
    down_low, down_high = SPANS[N]

    def feed(s):
        value = nn(normed_two[s], flat(w_all[:, :, up_low:up_high])) + up_bias[...]
        hidden[s] = value
        low = (value * (0.5 * (1.0 + lax.erf(value * 2.0**-0.5)))).astype(bf16)
        activated[s] = low
        out_part[s] = (
            nn(low, flat(w_all[:, :, down_low:down_high])) + nn(mixed[s], flat(out_all[...]))
        ).astype(bf16)

    def feed_back(s):
        value = hidden[s]
        slope = gelu_slope(value)
        low = (nt(back[s], flat(w_all[:, :, down_low:down_high])) * slope).astype(bf16)
        d_hidden[s] = low
        d_up_bias[...] += jnp.sum(low.astype(f32), axis=0, keepdims=True)
        d_two = nt(low, flat(w_all[:, :, up_low:up_high]))
        d_one = nt(d_projected[s], flat(w_all[:, :, SPANS[Q][0] : SPANS[Q][1]]))
        unit = (x_all[s].astype(f32) - stats[s][:, 0:1]) * stats[s][:, 1:2]
        sums[0:1] += jnp.sum(d_one * unit, axis=0, keepdims=True)
        sums[1:2] += jnp.sum(d_one, axis=0, keepdims=True)
        sums[2:3] += jnp.sum(d_two * unit, axis=0, keepdims=True)
        sums[3:4] += jnp.sum(d_two, axis=0, keepdims=True)
        dx_part[s] = (d_one * vectors[0:1] + d_two * vectors[2:3]).astype(bf16)

    @pl.loop(0, 4)
    def _(i):
        feed(far_first(i))
        send_parts(0, i)

        @pl.when(i == 1)
        def _():
            line_step(Q, 0)
            out_step(1)

        @pl.when(i == 3)
        def _():
            line_step(Q, 1)

    gradient(activated, back, N)
    to_core(N)
    turn_part(0, 1)
    turn_part(0, 0)
    line_step(Q, 2)
    out_step(2)
    add_core(N)
    line_starts(N)

    @pl.loop(0, 4)
    def _(i):
        feed_back(far_first(i))
        send_parts(1, i)

        @pl.when(i == 1)
        def _():
            line_step(N, 0)
            line_ends(Q)
            out_ends()

        @pl.when(i == 2)
        def _():
            line_step(N, 1)

    gradient(normed_two, d_hidden, U)
    to_core(U)
    share(Q)
    line_step(N, 2)
    turn_part(1, 1)
    turn_part(1, 0)
    add_core(U)
    line_starts(U)

    small_part[...] = jnp.zeros_like(small_part)

    def place(row, value):
        small_part[row // 13, pl.ds(row % 13, 1)] = value

    back_total = jnp.sum(back[part].astype(f32), axis=0, keepdims=True)
    for n in range(8):
        columns = slice(n * 128, (n + 1) * 128)
        for number in range(4):
            place(8 * number + n, sums[number : number + 1, columns])
        place(56 + n, back_total[:, columns])
        place(96 + n, back_total[:, columns])
        place(64 + 4 * n + part, d_up_bias[:, columns])
    for c in range(3):
        for n in range(2):
            columns = slice((2 * c + n) * 128, (2 * c + n + 1) * 128)
            place(32 + 8 * c + 2 * part + n, d_qkv_bias[:, columns])
    for k in range(1, 8):
        send(
            small_part.at[(shard + k) % 8],
            small_in.at[k - 1],
            total_send.at[k - 1],
            total_recv.at[k - 1],
            at.shard_after(k),
        ).start()

    line_step(U, 0)

    for r in range(2):
        half = halves[r]
        live = live_rows(part)[half]
        values = x_all[part, half].astype(f32)
        summed = values + whole_part(0, r) + vectors[4:5] + vectors[5:6]
        output[half] = jnp.where(live, summed, 0.0).astype(bf16)
    line_ends(N)
    line_step(U, 1)
    total = small_part[shard]
    for k in range(1, 8):
        arrived(small_in.at[k - 1], total_recv.at[k - 1], at.shard_after(8 - k))
        total = total + small_in[k - 1]
    small_total[...] = total
    for n, (peer, _) in enumerate(plane_peers):
        send(
            small_total, small_plane.at[part], total_send.at[7 + n], total_recv.at[7 + n], peer
        ).start()
    small_plane[part] = total
    for r in range(2):
        half = halves[r]
        scaled = whole_part(1, r)
        inverse = stats[part, half, 1:2]
        unit = (x_all[part, half].astype(f32) - stats[part, half, 0:1]) * inverse
        result = back[part, half].astype(f32) + inverse * (
            scaled
            - jnp.mean(scaled, axis=-1, keepdims=True)
            - unit * jnp.mean(scaled * unit, axis=-1, keepdims=True)
        )
        input_grad[half] = result.astype(bf16)
    line_step(U, 2)
    share(N)
    for n, (peer, other) in enumerate(plane_peers):
        arrived(small_plane.at[other], total_recv.at[7 + n], peer)
    small_sum[...] = (small_plane[0] + small_plane[1]) + (small_plane[2] + small_plane[3])
    line_ends(U)
    share(U)

    @pl.when(z != part)
    def _():
        arrived(out_grad, rows_recv.at[3], at.across_x)
        sent(out_line, rows_send.at[1], at.up)

    @pl.when(z == part)
    def _():
        for n, (peer, _) in enumerate(plane_peers):
            sent(out_line, rows_send.at[2 + n], peer)
        pltpu.make_async_copy(out_line, out_grad, keep_sem.at[3]).wait()

    sent(out_line, rows_send.at[0], at.other_core)
    for n, (own, whole) in enumerate(activations):
        sent(own, plane_send.at[n, 0], at.across_x)
        sent(own, plane_send.at[n, 1], at.across_y)
        sent(whole.at[part, 0:HALF], plane_send.at[n, 2], at.across_y)
        sent(whole.at[part, 0:HALF], plane_send.at[n, 3], at.across_x)
    for n, (peer, _) in enumerate(plane_peers):
        sent(len_all.at[part], len_send.at[n], peer)
        sent(small_total, total_send.at[7 + n], peer)
    for k in range(1, 8):
        sent(small_own, small_send.at[k - 1], at.shard_after(k))
        sent(small_total, total_send.at[k - 1], at.shard_after(k))
    for n in range(3):
        for other in range(4):
            block = piece(w_all, 2 * other + core, n)
            sent(block, w_send.at[2, n, other], at.other_core)
            sent(block, core_send.at[n, other], at.other_core)

            @pl.when((other <= z) & (z < 3))
            def _():
                sent(block, w_send.at[0, n, other], at.up)

            @pl.when((other >= z) & (z > 0))
            def _():
                sent(block, w_send.at[1, n, other], at.down)

            @pl.when(z != other)
            def _():
                sent(block, line_send.at[n, other], at.up)

    block = out_all.at[core]
    sent(block, out_send.at[2], at.other_core)

    @pl.when((z >= part) & (z < 3))
    def _():
        sent(block, out_send.at[0], at.up)

    @pl.when((z <= part) & (z > 0))
    def _():
        sent(block, out_send.at[1], at.down)

    for n in range(2):
        for r in range(2):
            for m in range(3):
                sent(plane_turn.at[n, r], part_send.at[n, r, m], at.across_x)
    for n, whole in enumerate(wholes):
        arrived(whole.at[at.far_part, 0:64], all_recv.at[n, 2], at.across_y)
        arrived(whole.at[at.far_part, 64:128], all_recv.at[n, 3], at.across_x)
        own = piece(terms, shard, n)
        sent(own, all_send.at[n, 0], at.across_x)
        sent(own, all_send.at[n, 1], at.across_y)
        sent(whole.at[part, 0:64], all_send.at[n, 2], at.across_y)
        sent(whole.at[part, 64:128], all_send.at[n, 3], at.across_x)
        pltpu.make_async_copy(own, whole.at[part], keep_sem.at[n]).wait()


VMEM_SPEC = pl.BlockSpec(memory_space=pltpu.VMEM)
HBM_SPEC = pl.BlockSpec(memory_space=pl.ANY)


def whole_layer(lengths, x_own, cot_own, masters, tables):
    shape = jax.ShapeDtypeStruct
    vmem, dma = pltpu.VMEM, pltpu.SemaphoreType.DMA
    bf16, f32 = jnp.bfloat16, jnp.float32
    length = x_own.shape[0]
    group = 4
    head_cols, wide, rows = D // group, 2816, 128

    def by_sequence(width, kind=bf16):
        return vmem((group, length, width), kind)

    return pl.pallas_call(
        layer_kernel,
        out_shape=(
            shape(x_own.shape, bf16),
            shape(x_own.shape, bf16),
            shape((group, rows, 3 * head_cols), bf16),
            shape((group, rows, FF // group), bf16),
            shape((group, rows, D), bf16),
            shape((rows, D), bf16),
            shape((16, 128), f32),
        ),
        in_specs=[pl.BlockSpec(memory_space=pltpu.SMEM)]
        + [HBM_SPEC] * 6
        + [VMEM_SPEC, VMEM_SPEC],
        out_specs=(VMEM_SPEC, VMEM_SPEC) + (HBM_SPEC,) * 4 + (VMEM_SPEC,),
        scratch_shapes=[
            by_sequence(D),
            by_sequence(D),
            vmem((group, 8, 128), f32),
            vmem((8, rows, wide), bf16),
            vmem((2, rows, D), bf16),
            vmem((16, 128), f32),
            vmem((8, 16, 128), f32),
            vmem((8, D), f32),
            vmem((1, 3 * head_cols), f32),
            vmem((1, FF // group), f32),
            by_sequence(128, f32),
            by_sequence(D),
            by_sequence(D),
            by_sequence(D),
            by_sequence(3 * head_cols),
            by_sequence(head_cols),
            by_sequence(3 * head_cols),
            by_sequence(FF // group, f32),
            by_sequence(FF // group),
            by_sequence(D),
            by_sequence(D),
            vmem((8, rows, wide), bf16),
            vmem((2, rows, D), bf16),
            vmem((8, D), f32),
            vmem((1, 3 * head_cols), f32),
            vmem((1, FF // group), f32),
            vmem((8, 16, 128), f32),
            vmem((2, 2, 2, HALF, D), bf16),
            vmem((2, 2, HALF, D), bf16),
            vmem((2, 2, HALF, D), bf16),
            vmem((4, rows, wide), bf16),
            vmem((5, rows, wide), bf16),
            vmem((rows, D), bf16),
            vmem((rows, D), bf16),
            vmem((2, rows, D), bf16),
            vmem((7, 16, 128), f32),
            vmem((16, 128), f32),
            vmem((4, 16, 128), f32),
            dma((15,)),
            dma((2, 4)),
            dma((2, 4)),
            dma((3,)),
            dma((3,)),
            dma((3, 3, 4)),
            dma((3, 8)),
            dma((3,)),
            dma((2,)),
            dma((7,)),
            dma((7,)),
            dma((2, 2, 3)),
            dma((2, 2, 3)),
            dma((3, 4)),
            dma((3, 4)),
            dma((3, 4)),
            dma((3, 5)),
            dma((5,)),
            dma((4,)),
            dma((3, 4)),
            dma((3, 4)),
            dma((4,)),
            dma((10,)),
            dma((10,)),
        ],
        compiler_params=pltpu.CompilerParams(
            collective_id=0, has_side_effects=True, vmem_limit_bytes=62 << 20
        ),
        name="layer",
    )(lengths, x_own, cot_own, *masters, tables)


def rope_tables(length, heads):
    half = ROT // 2
    angle = np.arange(length)[:, None] * ROPE_BASE ** (-2.0 * np.arange(half) / ROT)[None]
    table = np.zeros((3, length, HD), np.float32)
    table[0] = 1.0
    table[0, :, :half] = table[0, :, half:ROT] = np.cos(angle)
    table[1, :, :half] = -np.sin(angle)
    table[2, :, half:ROT] = np.sin(angle)
    return jnp.asarray(np.tile(table, (1, 1, heads)))


def local_split(
    tokens_in,
    cotangent,
    lengths,
    qkv_master,
    out_master,
    up_master,
    down_master,
    small_master,
    qkv_first,
    out_first,
    up_first,
    down_first,
    small_first,
    qkv_second,
    out_second,
    up_second,
    down_second,
    small_second,
):
    masters = (qkv_master, out_master, up_master, down_master, small_master)
    firsts = (qkv_first, out_first, up_first, down_first, small_first)
    seconds = (qkv_second, out_second, up_second, down_second, small_second)
    parts, shards = lax.axis_size("dp"), lax.axis_size("fsdp")
    part, shard = lax.axis_index("dp"), lax.axis_index("fsdp")
    length = tokens_in.shape[1]
    update = (masters, firsts, seconds)
    if (parts, shards) == (4, 8):
        tall = tuple(masters[:4]) + (small_master.reshape(-1, 128),)
        output, input_grad, qkv_grad, up_grad, down_grad, out_grad, small_sum = whole_layer(
            lengths, tokens_in[0], cotangent[0], tall, rope_tables(length, HEADS // parts)
        )
        grads = (qkv_grad, out_grad, up_grad, down_grad, small_sum[: tall[4].shape[0]])
        return (output[None], input_grad[None]) + lamb_split(*update, grads)

    head_cols = D // parts
    ff_rows = down_master.shape[0] // parts
    qkv_own = sliced(qkv_master, part, parts, 3).astype(jnp.bfloat16)
    up_own = sliced(up_master, part, parts, shards).astype(jnp.bfloat16)
    down_own = lax.dynamic_slice_in_dim(down_master, part * ff_rows, ff_rows).astype(jnp.bfloat16)
    out_own = out_master.astype(jnp.bfloat16)
    small_own = small_master.astype(jnp.bfloat16)

    def small_vectors(small_all):
        vectors = split_small(small_all)
        vectors[4] = sliced(vectors[4][None], part, parts, 3)[0]
        vectors[6] = sliced(vectors[6][None], part, parts, shards)[0]
        return vectors

    def over_shards(own):
        return lax.all_gather(own, "fsdp", axis=0, tiled=True)

    x_all = lax.all_gather(tokens_in, "dp", axis=0, tiled=True)
    cotangent_all = lax.all_gather(cotangent, "dp", axis=0, tiled=True)
    lengths_all = lax.all_gather(lengths, "dp", axis=0, tiled=True)
    qkv_weight, up_weight, down_weight = (over_shards(w) for w in (qkv_own, up_own, down_own))
    out_weight = lax.dynamic_slice_in_dim(over_shards(out_own), part * head_cols, head_cols)
    gain_one, shift_one, gain_two, shift_two, qkv_bias, out_bias, up_bias, down_bias = (
        small_vectors(over_shards(small_own).astype(jnp.float32))
    )
    out_part, scaled_part, terms, sums = layer(
        x_all,
        cotangent_all,
        lengths_all,
        (qkv_weight, out_weight, up_weight, down_weight),
        (gain_one, shift_one, gain_two, shift_two, qkv_bias, up_bias),
        part,
    )
    norm_sums, d_qkv_bias, d_up_bias = sums
    out_sum = lax.psum_scatter(out_part, "dp", scatter_dimension=0, tiled=True)
    scaled = lax.psum_scatter(scaled_part, "dp", scatter_dimension=0, tiled=True)
    out_sum, scaled = out_sum.astype(jnp.float32), scaled.astype(jnp.float32)

    inputs = tokens_in[0].astype(jnp.float32)
    live = (jnp.arange(length) < lengths[0]).astype(jnp.float32)[:, None]
    back = cotangent[0].astype(jnp.float32) * live
    back_total = jnp.sum(back, axis=0)

    def spread(values, pieces):
        wide = jnp.zeros((pieces, parts, values.shape[0] // pieces), jnp.float32)
        return lax.dynamic_update_index_in_dim(
            wide, values.reshape(pieces, -1), part, axis=1
        ).reshape(-1)

    small_grad = jnp.concatenate(
        [
            norm_sums.reshape(4 * D),
            spread(d_qkv_bias, 3),
            back_total,
            spread(d_up_bias, shards),
            back_total,
        ]
    )
    small_sum = lax.psum(small_grad, ("dp", "fsdp"))
    small_rows = small_master.shape[0]
    small_sum = lax.dynamic_slice_in_dim(small_sum, shard * small_rows, small_rows)
    qkv_term, out_term, up_term, down_term = terms
    out_wide = lax.dynamic_update_slice_in_dim(
        jnp.zeros((D, D), jnp.bfloat16), out_term, part * head_cols, axis=0
    )

    def to_owner(term):
        own = lax.psum_scatter(term, "fsdp", scatter_dimension=0, tiled=True)
        return lax.all_gather(own, "dp", axis=0, tiled=False).astype(jnp.float32)

    reduced = (
        joined(to_owner(qkv_term), 3),
        lax.psum(
            lax.psum_scatter(out_wide, "fsdp", scatter_dimension=0, tiled=True), "dp"
        ).astype(jnp.float32),
        joined(to_owner(up_term), shards),
        to_owner(down_term).reshape(down_master.shape),
        small_sum,
    )

    unit_rows, inverse_rows = normalize(inputs)
    output = ((inputs + out_sum + out_bias + down_bias) * live).astype(jnp.bfloat16)
    input_grad = back + inverse_rows * (
        scaled
        - jnp.mean(scaled, axis=-1, keepdims=True)
        - unit_rows * jnp.mean(scaled * unit_rows, axis=-1, keepdims=True)
    )
    return (output[None], input_grad.astype(jnp.bfloat16)[None]) + lamb(*update, reduced)


def lamb_rows(first_old, second_old, master, grad):
    first_new = BETA_ONE * first_old + (1.0 - BETA_ONE) * grad
    second_new = BETA_TWO * second_old + (1.0 - BETA_TWO) * grad * grad
    update = first_new / (jnp.sqrt(second_new) + ADAM_EPSILON) + DECAY * master
    return first_new, second_new, update


def lane_sums(values):
    squares = jnp.sum(values * values, axis=0, keepdims=True)
    total = squares[:, 0:128]
    for n in range(1, squares.shape[1] // 128):
        total = total + squares[:, n * 128 : (n + 1) * 128]
    return total


def moments_kernel(*refs):
    qkv_grad, out_grad, up_grad, down_grad, small_grad = refs[0:5]
    masters, firsts, seconds = refs[5:10], refs[10:15], refs[15:20]
    first_news, second_news, updates = refs[20:25], refs[25:30], refs[30:35]
    squares = refs[35]
    step = pl.program_id(0)

    @pl.when(step == 0)
    def _():
        squares[...] = jnp.zeros_like(squares)

    def one(number, span, grad):
        index = (slice(None), span)
        first_new, second_new, update = lamb_rows(
            firsts[number][index], seconds[number][index], masters[number][index], grad
        )
        first_news[number][index] = first_new
        second_news[number][index] = second_new
        updates[number][index] = update
        return lane_sums(masters[number][index]), lane_sums(update)

    def add(number, pairs):
        weight, update = pairs[0]
        for more_weight, more_update in pairs[1:]:
            weight, update = weight + more_weight, update + more_update
        squares[number : number + 1] += weight
        squares[8 + number : 9 + number] += update

    f32 = jnp.float32
    parts = qkv_grad.shape[0]
    width = qkv_grad.shape[2] // 3
    add(
        0,
        [
            one(
                0,
                slice((c * parts + d) * width, (c * parts + d + 1) * width),
                qkv_grad[d, :, c * width : (c + 1) * width].astype(f32),
            )
            for c in range(3)
            for d in range(parts)
        ],
    )
    add(1, [one(1, slice(None), out_grad[...].astype(f32))])
    pieces = up_grad.shape[2] // 128
    add(
        2,
        [
            one(
                2,
                slice((g * parts + d) * 128, (g * parts + d + 1) * 128),
                up_grad[d, :, g * 128 : (g + 1) * 128].astype(f32),
            )
            for g in range(pieces)
            for d in range(parts)
        ],
    )
    add(3, [one(3, slice(None), down_grad[0].astype(f32))])

    @pl.when(step == 0)
    def _():
        first_new, second_new, update = lamb_rows(
            firsts[4][...], seconds[4][...], masters[4][...], small_grad[...]
        )
        first_news[4][...] = first_new
        second_news[4][...] = second_new
        updates[4][...] = update
        squares[4:5] += lane_sums(masters[4][...])
        squares[12:13] += lane_sums(update)


def lamb_specs(masters, steps):
    specs = [pl.BlockSpec((m.shape[0] // steps, m.shape[1]), lambda i: (i, 0)) for m in masters[:4]]
    return specs + [pl.BlockSpec(masters[4].shape, lambda i: (0, 0))]


def moments(grads, masters, firsts, seconds, steps=8):
    qkv_grad, out_grad, up_grad, down_grad, small_grad = grads
    shape = jax.ShapeDtypeStruct
    each = lamb_specs(masters, steps)
    rows = qkv_grad.shape[1]
    halves = steps // qkv_grad.shape[0]
    grad_specs = [
        pl.BlockSpec((qkv_grad.shape[0], rows // steps, qkv_grad.shape[2]), lambda i: (0, i, 0)),
        each[1],
        pl.BlockSpec((up_grad.shape[0], rows // steps, up_grad.shape[2]), lambda i: (0, i, 0)),
        pl.BlockSpec(
            (1, rows // halves, down_grad.shape[2]), lambda i: (i // halves, i % halves, 0)
        ),
        each[4],
    ]
    out = [shape(m.shape, jnp.float32) for m in masters]
    results = pl.pallas_call(
        moments_kernel,
        grid=(steps,),
        in_specs=grad_specs + each * 3,
        out_specs=each * 3 + [pl.BlockSpec((16, 128), lambda i: (0, 0))],
        out_shape=out * 3 + [shape((16, 128), jnp.float32)],
        compiler_params=pltpu.CompilerParams(vmem_limit_bytes=40 << 20),
        name="moments",
    )(*grads, *masters, *firsts, *seconds)
    return results[0:5], results[5:10], results[10:15], results[15]


def norms_kernel(squares, total, steps, everyone, send_sem, recv_sem):
    shard, part = lax.axis_index("fsdp"), lax.axis_index("dp")
    peers = [(part, (shard + k) % 8) for k in range(1, 8)]
    barrier = pltpu.get_barrier_semaphore()
    for peer in peers:
        pl.semaphore_signal(barrier, inc=1, device_id=peer, device_id_type=MESH_ID)
    pl.semaphore_wait(barrier, 7)
    for k in range(1, 8):
        send(
            squares, everyone.at[shard], send_sem.at[k - 1], recv_sem.at[k - 1], peers[k - 1]
        ).start()
    everyone[shard] = squares[...]
    for k in range(1, 8):
        arrived(everyone.at[(shard + 8 - k) % 8], recv_sem.at[k - 1], peers[7 - k])
    for k in range(1, 8):
        sent(squares, send_sem.at[k - 1], peers[k - 1])
    summed = everyone[0]
    for k in range(1, 8):
        summed = summed + everyone[k]
    norms = jnp.sqrt(jnp.sum(summed, axis=1, keepdims=True))
    total[...] = jnp.broadcast_to(norms, (16, 128))
    steps[...] = jnp.broadcast_to(RATE * (norms[0:8] / norms[8:16]), (8, 128))


def norms(squares):
    shape = jax.ShapeDtypeStruct
    dma = pltpu.SemaphoreType.DMA
    return pl.pallas_call(
        norms_kernel,
        out_shape=(shape((16, 128), jnp.float32), shape((8, 128), jnp.float32)),
        in_specs=[VMEM_SPEC],
        out_specs=(VMEM_SPEC,) * 2,
        scratch_shapes=[pltpu.VMEM((8, 16, 128), jnp.float32), dma((7,)), dma((7,))],
        compiler_params=pltpu.CompilerParams(collective_id=2, has_side_effects=True),
        name="norms",
    )(squares)


def step_kernel(*refs):
    scales, masters, updates, news = refs[0], refs[1:6], refs[6:11], refs[11:16]
    for number in range(5):
        scale = scales[number : number + 1, 0:1]
        news[number][...] = masters[number][...] - scale * updates[number][...]


def step_masters(scales, masters, updates, steps=8):
    each = lamb_specs(masters, steps)
    return pl.pallas_call(
        step_kernel,
        grid=(steps,),
        in_specs=[pl.BlockSpec((8, 128), lambda i: (0, 0))] + each * 2,
        out_specs=each,
        out_shape=[jax.ShapeDtypeStruct(m.shape, jnp.float32) for m in masters],
        compiler_params=pltpu.CompilerParams(vmem_limit_bytes=40 << 20),
        name="step_masters",
    )(scales, *masters, *updates)


def lamb_split(masters, firsts, seconds, grads):
    def tall(arrays):
        return tuple(arrays[:4]) + (arrays[4].reshape(-1, 128),)

    def flat_small(arrays):
        return tuple(arrays[:4]) + (arrays[4].reshape(-1),)

    masters, firsts, seconds = tall(masters), tall(firsts), tall(seconds)
    first_news, second_news, updates, squares = moments(grads, masters, firsts, seconds)
    total, scales = norms(squares)
    news = step_masters(scales, masters, updates)
    lamb_norms = jnp.stack([total[0:5, 0], total[8:13, 0]])
    return flat_small(news) + flat_small(first_news) + flat_small(second_news) + (lamb_norms,)


def lamb(masters, firsts, seconds, reduced):
    updates = []
    first_news = []
    second_news = []
    for first_old, second_old, master, grad_sum in zip(firsts, seconds, masters, reduced):
        first_new = BETA_ONE * first_old + (1.0 - BETA_ONE) * grad_sum
        second_new = BETA_TWO * second_old + (1.0 - BETA_TWO) * grad_sum * grad_sum
        updates.append(first_new / (jnp.sqrt(second_new) + ADAM_EPSILON) + DECAY * master)
        first_news.append(first_new)
        second_news.append(second_new)
    weight_squares, update_squares = lax.psum(
        (local_squares(masters), local_squares(updates)), "fsdp"
    )
    weight_norms = jnp.sqrt(weight_squares)
    update_norms = jnp.sqrt(update_squares)
    new_masters = [
        masters[number] - RATE * (weight_norms[number] / update_norms[number]) * updates[number]
        for number in range(5)
    ]
    lamb_norms = jnp.stack([weight_norms, update_norms])
    return tuple(new_masters) + tuple(first_news) + tuple(second_news) + (lamb_norms,)


def solution(mesh):
    in_specs = (
        P(("dp", "fsdp"), None, None),
        P(("dp", "fsdp"), None, None),
        P(("dp", "fsdp")),
        P("fsdp", None),
        P("fsdp", None),
        P("fsdp", None),
        P("fsdp", None),
        P("fsdp"),
        P("fsdp", None),
        P("fsdp", None),
        P("fsdp", None),
        P("fsdp", None),
        P("fsdp"),
        P("fsdp", None),
        P("fsdp", None),
        P("fsdp", None),
        P("fsdp", None),
        P("fsdp"),
    )
    out_specs = (
        P(("dp", "fsdp"), None, None),
        P(("dp", "fsdp"), None, None),
        P("fsdp", None),
        P("fsdp", None),
        P("fsdp", None),
        P("fsdp", None),
        P("fsdp"),
        P("fsdp", None),
        P("fsdp", None),
        P("fsdp", None),
        P("fsdp", None),
        P("fsdp"),
        P("fsdp", None),
        P("fsdp", None),
        P("fsdp", None),
        P("fsdp", None),
        P("fsdp"),
        P(),
    )
    return jax.shard_map(local_split, mesh=mesh, in_specs=in_specs, out_specs=out_specs, check_vma=False)
```

```python
import math

import jax
import jax.numpy as jnp
import numpy as np
from jax import lax
from jax.experimental import pallas as pl
from jax.experimental.pallas import tpu as pltpu
from jax.sharding import PartitionSpec as P

D = 1024
HEADS = 16
HD = 64
FF = 4096
ROT = 16
SMALL = 13312


NORM_EPSILON = 1e-05
ADAM_EPSILON = 1e-06
ROPE_BASE = 10000.0
RATE = 0.5
DECAY = 0.01
BETA_ONE = 0.5
BETA_TWO = 0.5


def split_small(small_vector):
    bounds = [0, D, 2 * D, 3 * D, 4 * D, 7 * D, 8 * D, 8 * D + FF, 9 * D + FF]
    return [small_vector[bounds[number] : bounds[number + 1]] for number in range(8)]


def normalize(values):
    average = jnp.mean(values, axis=-1, keepdims=True)
    centred = values - average
    variance = jnp.mean(centred * centred, axis=-1, keepdims=True)
    inverse = lax.rsqrt(variance + NORM_EPSILON)
    return (centred * inverse, inverse)


def rotary_tables(length):
    half_dims = ROT // 2
    position = jnp.arange(length, dtype=jnp.float32)[:, None]
    number = jnp.arange(half_dims, dtype=jnp.float32)[None, :]
    angle = position * jnp.exp(number * (-2.0 * math.log(ROPE_BASE) / ROT))
    return (jnp.cos(angle)[:, None, :], jnp.sin(angle)[:, None, :])


def rotate(heads_in, cosine_table, sine_table):
    half_dims = ROT // 2
    first_half = heads_in[..., :half_dims]
    second_half = heads_in[..., half_dims:ROT]
    return jnp.concatenate(
        [
            first_half * cosine_table - second_half * sine_table,
            second_half * cosine_table + first_half * sine_table,
            heads_in[..., ROT:],
        ],
        axis=-1,
    )


def rotate_back(grads_in, cosine_table, sine_table):
    half_dims = ROT // 2
    first_half = grads_in[..., :half_dims]
    second_half = grads_in[..., half_dims:ROT]
    return jnp.concatenate(
        [
            first_half * cosine_table + second_half * sine_table,
            second_half * cosine_table - first_half * sine_table,
            grads_in[..., ROT:],
        ],
        axis=-1,
    )


def gelu_slope(values):
    return 0.5 * (1.0 + lax.erf(values * 2.0 ** (-0.5))) + values * jnp.exp(
        -0.5 * values * values
    ) * (2.0 * math.pi) ** (-0.5)


def against(left, right):
    return lax.dot_general(
        left, right, (((1,), (1,)), ((), ())), preferred_element_type=jnp.float32
    )


def outer_sum(columns, right):
    return lax.dot_general(
        columns, right, (((0,), (0,)), ((), ())), preferred_element_type=jnp.float32
    )


def local_squares(arrays):
    return jnp.stack([jnp.sum(array_in * array_in) for array_in in arrays])


def sliced(master, part, parts, pieces):
    rows, columns = master.shape
    width = columns // (pieces * parts)
    return lax.dynamic_index_in_dim(
        master.reshape(rows, pieces, parts, width), part, axis=2, keepdims=False
    ).reshape(rows, pieces * width)


def joined(slices, pieces):
    parts, rows, columns = slices.shape
    width = columns // pieces
    return (
        slices.reshape(parts, rows, pieces, width)
        .transpose(1, 2, 0, 3)
        .reshape(rows, pieces * parts * width)
    )


def layer(x_all, cotangent_all, lengths_all, weights, small_all, part):
    qkv_weight, out_weight, up_weight, down_weight = weights
    group, length, _ = x_all.shape
    tokens = group * length
    head_cols = out_weight.shape[0]
    heads = head_cols // HD
    gain_one, shift_one, gain_two, shift_two, qkv_bias, up_bias = small_all
    inputs = x_all.reshape(tokens, D).astype(jnp.float32)
    position = jnp.arange(length)
    live = (position[None, :] < lengths_all[:, None]).astype(jnp.float32).reshape(tokens, 1)
    allowed = (position[None, None, :] <= position[None, :, None]) & (
        position[None, None, :] < lengths_all[:, None, None]
    )
    unit_rows, _ = normalize(inputs)
    normed_one = (unit_rows * gain_one + shift_one).astype(jnp.bfloat16)
    normed_two = (unit_rows * gain_two + shift_two).astype(jnp.bfloat16)
    projected = jnp.dot(normed_one, qkv_weight, preferred_element_type=jnp.float32) + qkv_bias
    projected = projected.reshape(group, length, 3, heads, HD)
    cosine_table, sine_table = rotary_tables(length)
    query_heads = rotate(projected[:, :, 0], cosine_table, sine_table).astype(jnp.bfloat16)
    key_heads = rotate(projected[:, :, 1], cosine_table, sine_table).astype(jnp.bfloat16)
    value_heads = projected[:, :, 2].astype(jnp.bfloat16)
    scores = jnp.einsum(
        "gqhd,gkhd->ghqk", query_heads, key_heads, preferred_element_type=jnp.float32
    ) * HD ** (-0.5)
    scores = jnp.where(allowed[:, None], scores, -1e30)
    row_top = jnp.max(scores, axis=-1, keepdims=True)
    raised = jnp.exp(scores - row_top)
    attend = raised / jnp.sum(raised, axis=-1, keepdims=True)
    attend_low = attend.astype(jnp.bfloat16)
    mixed = jnp.einsum(
        "ghqk,gkhd->gqhd", attend_low, value_heads, preferred_element_type=jnp.float32
    )
    mixed = mixed.reshape(tokens, head_cols).astype(jnp.bfloat16)
    hidden = jnp.dot(normed_two, up_weight, preferred_element_type=jnp.float32) + up_bias
    activated = jax.nn.gelu(hidden, approximate=False).astype(jnp.bfloat16)
    out_part = jnp.dot(mixed, out_weight, preferred_element_type=jnp.float32) + jnp.dot(
        activated, down_weight, preferred_element_type=jnp.float32
    )

    back = (cotangent_all.reshape(tokens, D).astype(jnp.float32) * live).astype(jnp.bfloat16)
    d_hidden = (against(back, down_weight) * gelu_slope(hidden)).astype(jnp.bfloat16)
    d_mixed = against(back, out_weight).astype(jnp.bfloat16).reshape(group, length, heads, HD)
    d_attend = jnp.einsum(
        "gqhd,gkhd->ghqk", d_mixed, value_heads, preferred_element_type=jnp.float32
    )
    row_inner = jnp.sum(attend * d_attend, axis=-1, keepdims=True)
    d_scores = (attend * (d_attend - row_inner)).astype(jnp.bfloat16)
    d_queries = jnp.einsum(
        "ghqk,gkhd->gqhd", d_scores, key_heads, preferred_element_type=jnp.float32
    ) * HD ** (-0.5)
    d_keys = jnp.einsum(
        "ghqk,gqhd->gkhd", d_scores, query_heads, preferred_element_type=jnp.float32
    ) * HD ** (-0.5)
    d_values = jnp.einsum(
        "ghqk,gqhd->gkhd", attend_low, d_mixed, preferred_element_type=jnp.float32
    )
    d_projected = jnp.stack(
        [
            rotate_back(d_queries, cosine_table, sine_table),
            rotate_back(d_keys, cosine_table, sine_table),
            d_values,
        ],
        axis=2,
    )
    d_projected = d_projected.reshape(tokens, 3 * head_cols).astype(jnp.bfloat16)
    d_normed_one = against(d_projected, qkv_weight)
    d_normed_two = against(d_hidden, up_weight)
    scaled_part = d_normed_one * gain_one + d_normed_two * gain_two
    norm_sums = jnp.stack(
        [
            jnp.sum(d_normed_one * unit_rows, axis=0),
            jnp.sum(d_normed_one, axis=0),
            jnp.sum(d_normed_two * unit_rows, axis=0),
            jnp.sum(d_normed_two, axis=0),
        ]
    )
    d_qkv_bias = jnp.sum(d_projected, axis=0, dtype=jnp.float32)
    d_up_bias = jnp.sum(d_hidden, axis=0, dtype=jnp.float32)
    terms = (
        outer_sum(normed_one, d_projected),
        outer_sum(mixed, back),
        outer_sum(normed_two, d_hidden),
        outer_sum(activated, back),
    )
    return (
        out_part.astype(jnp.bfloat16),
        scaled_part.astype(jnp.bfloat16),
        tuple(term.astype(jnp.bfloat16) for term in terms),
        (norm_sums, d_qkv_bias, d_up_bias),
    )


MESH_ID = pl.DeviceIdType.MESH
HALF = 128


class Place:
    def __init__(self):
        self.part = lax.axis_index("dp")
        self.shard = lax.axis_index("fsdp")
        self.z = self.shard // 2
        self.core = self.shard % 2
        self.x_part = 2 * (self.part // 2) + 1 - self.part % 2
        self.y_part = (self.part + 2) % 4
        self.far_part = 3 - self.part
        self.across_x = (self.x_part, self.shard)
        self.across_y = (self.y_part, self.shard)
        self.across_far = (self.far_part, self.shard)
        self.other_core = (self.part, 2 * self.z + 1 - self.core)
        self.up = (self.part, jnp.minimum(self.shard + 2, 7))
        self.down = (self.part, jnp.maximum(self.shard - 2, 0))

    def shard_after(self, k):
        return (self.part, (self.shard + k) % 8)


def send(source, target, send_sem, recv_sem, device):
    return pltpu.make_async_remote_copy(
        src_ref=source,
        dst_ref=target,
        send_sem=send_sem,
        recv_sem=recv_sem,
        device_id=device,
        device_id_type=MESH_ID,
    )


def arrived(target, recv_sem, device):
    send(target, target, recv_sem, recv_sem, device).wait_recv()


def sent(source, send_sem, device):
    send(source, source, send_sem, send_sem, device).wait_send()


def greet(at):
    barrier = pltpu.get_barrier_semaphore()
    peers = [at.across_x, at.across_y, at.across_far] + [at.shard_after(k) for k in range(1, 8)]
    for peer in peers:
        pl.semaphore_signal(barrier, inc=1, device_id=peer, device_id_type=MESH_ID)
    pl.semaphore_wait(barrier, len(peers))


SPANS = ((0, 768), (768, 1792), (1792, 2816))
Q, U, N = 0, 1, 2


def nt(left, right):
    return lax.dot_general(
        left, right, (((1,), (1,)), ((), ())), preferred_element_type=jnp.float32
    )


def tn(left, right):
    return lax.dot_general(
        left, right, (((0,), (0,)), ((), ())), preferred_element_type=jnp.float32
    )


def nn(left, right):
    return jnp.dot(left, right, preferred_element_type=jnp.float32)


def flat(value):
    return value.reshape(value.shape[0] * value.shape[1], value.shape[2])


def layer_kernel(
    length_own,
    x_own,
    cot_own,
    qkv_master,
    out_master,
    up_master,
    down_master,
    small_master,
    tables,
    output,
    input_grad,
    qkv_all,
    up_all,
    down_all,
    out_grad,
    small_sum,
    x_all,
    cot_all,
    len_all,
    w_all,
    out_all,
    small_own,
    small_all,
    vectors,
    qkv_bias,
    up_bias,
    stats,
    normed_one,
    normed_two,
    back,
    heads_qkv,
    mixed,
    d_projected,
    hidden,
    d_hidden,
    out_part,
    dx_part,
    terms,
    out_term,
    sums,
    d_qkv_bias,
    d_up_bias,
    small_part,
    plane_one,
    plane_two,
    plane_turn,
    core_in,
    line_in,
    out_core_in,
    out_line,
    out_line_in,
    small_in,
    small_total,
    small_plane,
    load_sem,
    plane_send,
    plane_recv,
    len_send,
    len_recv,
    w_send,
    w_recv,
    out_send,
    out_recv,
    small_send,
    small_recv,
    part_send,
    part_recv,
    core_send,
    core_recv,
    line_send,
    line_recv,
    rows_send,
    rows_recv,
    all_send,
    all_recv,
    keep_sem,
    total_send,
    total_recv,
):
    f32, bf16 = jnp.float32, jnp.bfloat16
    at = Place()
    z, core, part, shard = at.z, at.core, at.part, at.shard
    length = x_own.shape[0]
    head_cols = mixed.shape[2]
    activated = normed_one
    place_x, place_y = part % 2, part // 2

    def near_first(i):
        return 2 * ((place_y + i // 2) % 2) + (place_x + i % 2) % 2

    def far_first(i):
        return 2 * ((place_y + 1 - i % 2) % 2) + (place_x + 1 - i // 2) % 2

    def piece(ref, slot, n):
        return ref.at[slot, :, SPANS[n][0] : SPANS[n][1]]

    plane_peers = (
        (at.across_x, at.x_part),
        (at.across_y, at.y_part),
        (at.across_far, at.far_part),
    )

    stage = [hidden.at[n, 0:128] for n in range(4)]
    loads = []
    for c in range(3):
        columns = pl.ds(pl.multiple_of(c * D + part * head_cols, 128), head_cols)
        target = stage[0].at[:, c * head_cols : (c + 1) * head_cols]
        loads.append((qkv_master.at[:, columns], target))
    loads.append((out_master, stage[1]))
    for g in range(8):
        columns = pl.ds(pl.multiple_of(g * (FF // 8) + part * 128, 128), 128)
        loads.append((up_master.at[:, columns], stage[2].at[:, g * 128 : (g + 1) * 128]))
    rows = pl.ds(pl.multiple_of(part * 128, 128), 128)
    loads.append((down_master.at[rows], stage[3]))
    loads.append((x_own, x_all.at[part]))
    loads.append((cot_own, cot_all.at[part]))

    def load(n):
        return pltpu.make_async_copy(loads[n][0], loads[n][1], load_sem.at[n])

    for n in range(len(loads)):
        load(n).start()
    len_all[part] = jnp.full((8, 128), length_own[0], jnp.int32).astype(f32)
    small_own[...] = jnp.zeros_like(small_own)
    small_own[0:13] = small_master[...].astype(bf16).astype(f32)
    small_all[shard] = small_own[...]
    greet(at)

    activations = ((x_own, x_all), (cot_own, cot_all))
    for n, (own, whole) in enumerate(activations):
        send(own, whole.at[part], plane_send.at[n, 0], plane_recv.at[n, 0], at.across_x).start()
        send(own, whole.at[part], plane_send.at[n, 1], plane_recv.at[n, 1], at.across_y).start()

    def cast(n, first, last):
        for m in range(first, last):
            load(m).wait()
        low, high = SPANS[n]
        w_all[shard, :, low:high] = stage[(0, 2, 3)[n]][:, 0 : high - low].astype(bf16)

    def send_own(n):
        block = piece(w_all, shard, n)

        @pl.when(z < 3)
        def _():
            send(block, block, w_send.at[0, n, z], w_recv.at[n, shard], at.up).start()

        @pl.when(z > 0)
        def _():
            send(block, block, w_send.at[1, n, z], w_recv.at[n, shard], at.down).start()

        send(block, block, w_send.at[2, n, z], w_recv.at[n, shard], at.other_core).start()

    def forward(k, n):
        @pl.when(z >= k)
        def _():
            source = 2 * (z - k) + core
            block = piece(w_all, source, n)
            arrived(block, w_recv.at[n, source], at.down)

            @pl.when(z < 3)
            def _():
                send(block, block, w_send.at[0, n, z - k], w_recv.at[n, source], at.up).start()

            send(
                block, block, w_send.at[2, n, z - k], w_recv.at[n, source], at.other_core
            ).start()

        @pl.when(z + k <= 3)
        def _():
            source = 2 * (z + k) + core
            block = piece(w_all, source, n)
            arrived(block, w_recv.at[n, source], at.up)

            @pl.when(z > 0)
            def _():
                send(block, block, w_send.at[1, n, z + k], w_recv.at[n, source], at.down).start()

            send(
                block, block, w_send.at[2, n, z + k], w_recv.at[n, source], at.other_core
            ).start()

    def from_core(n):
        for other in range(4):
            source = 2 * other + 1 - core
            arrived(piece(w_all, source, n), w_recv.at[n, source], at.other_core)

    def send_out_rows():
        block = out_all.at[core]

        @pl.when(z < 3)
        def _():
            send(block, block, out_send.at[0], out_recv.at[core], at.up).start()

        @pl.when(z > 0)
        def _():
            send(block, block, out_send.at[1], out_recv.at[core], at.down).start()

        send(block, block, out_send.at[2], out_recv.at[core], at.other_core).start()

    def forward_out(k):
        @pl.when((z - k == part) | (z + k == part))
        def _():
            block = out_all.at[core]
            arrived(block, out_recv.at[core], at.up)

            @pl.when((z > part) & (z < 3))
            def _():
                send(block, block, out_send.at[0], out_recv.at[core], at.up).start()

            @pl.when((z < part) & (z > 0))
            def _():
                send(block, block, out_send.at[1], out_recv.at[core], at.down).start()

            send(block, block, out_send.at[2], out_recv.at[core], at.other_core).start()

    def forward_x(n):
        whole = activations[n][1]
        arrived(whole.at[at.x_part], plane_recv.at[n, 0], at.across_x)
        block = whole.at[at.x_part, 0:HALF]
        send(block, block, plane_send.at[n, 2], plane_recv.at[n, 2], at.across_y).start()

    def forward_y(n):
        whole = activations[n][1]
        arrived(whole.at[at.y_part], plane_recv.at[n, 1], at.across_y)
        block = whole.at[at.y_part, HALF : 2 * HALF]
        send(block, block, plane_send.at[n, 3], plane_recv.at[n, 3], at.across_x).start()

    def far_halves(n):
        whole = activations[n][1]
        arrived(whole.at[at.far_part, 0:HALF], plane_recv.at[n, 2], at.across_y)
        arrived(whole.at[at.far_part, HALF : 2 * HALF], plane_recv.at[n, 3], at.across_x)

    cast(Q, 0, 3)
    send_own(Q)
    load(3).wait()

    @pl.when(z == part)
    def _():
        out_all[core] = stage[1][...].astype(bf16)
        send_out_rows()

    for n, (peer, _) in enumerate(plane_peers):
        send(len_all.at[part], len_all.at[part], len_send.at[n], len_recv.at[n], peer).start()
    for k in range(1, 8):
        send(
            small_own,
            small_all.at[shard],
            small_send.at[k - 1],
            small_recv.at[k - 1],
            at.shard_after(k),
        ).start()
    cast(U, 4, 12)
    cast(N, 12, 13)
    load(13).wait()
    load(14).wait()
    forward(1, Q)
    forward_out(1)
    forward(2, Q)
    send_own(U)
    send_own(N)
    for n, (peer, other) in enumerate(plane_peers):
        arrived(len_all.at[other], len_recv.at[n], peer)
    for k in range(1, 8):
        arrived(small_all.at[(shard + 8 - k) % 8], small_recv.at[k - 1], at.shard_after(8 - k))
    for number, row in enumerate((0, 8, 16, 24, 56, 96)):
        for n in range(8):
            source = row + n
            vectors[number : number + 1, n * 128 : (n + 1) * 128] = small_all[
                source // 13, source % 13 : source % 13 + 1
            ]
    for c in range(3):
        for n in range(2):
            source = 32 + 8 * c + 2 * part + n
            columns = slice((2 * c + n) * 128, (2 * c + n + 1) * 128)
            qkv_bias[:, columns] = small_all[source // 13, pl.ds(source % 13, 1)]
    for g in range(8):
        source = 64 + 4 * g + part
        up_bias[:, g * 128 : (g + 1) * 128] = small_all[source // 13, pl.ds(source % 13, 1)]

    sums[...] = jnp.zeros_like(sums)
    d_qkv_bias[...] = jnp.zeros_like(d_qkv_bias)
    d_up_bias[...] = jnp.zeros_like(d_up_bias)
    block_rows = 64

    def norm_rows(s):
        @pl.loop(0, length // block_rows)
        def _(i):
            r = pl.ds(pl.multiple_of(i * block_rows, block_rows), block_rows)
            values = x_all[s, r, :].astype(f32)
            mean = jnp.mean(values, axis=-1, keepdims=True)
            centred = values - mean
            inverse = lax.rsqrt(
                jnp.mean(centred * centred, axis=-1, keepdims=True) + NORM_EPSILON
            )
            stats[s, r, 0:1] = mean
            stats[s, r, 1:2] = inverse
            unit = centred * inverse
            normed_one[s, r, :] = (unit * vectors[0:1] + vectors[1:2]).astype(bf16)
            normed_two[s, r, :] = (unit * vectors[2:3] + vectors[3:4]).astype(bf16)

    def live_rows(s):
        index = lax.broadcasted_iota(jnp.int32, (length, 1), 0)
        return index.astype(f32) < len_all[s][0:1, 0:1]

    def rotate(value, sign):
        return (
            value * tables[0]
            + sign * pltpu.roll(value, head_cols - ROT // 2, 1) * tables[1]
            + sign * pltpu.roll(value, ROT // 2, 1) * tables[2]
        )

    def project(s):
        norm_rows(s)
        low, high = SPANS[Q]
        value = nn(normed_one[s], flat(w_all[:, :, low:high])) + qkv_bias[...]
        heads_qkv[s, :, 0:head_cols] = rotate(value[:, 0:head_cols], 1.0).astype(bf16)
        heads_qkv[s, :, head_cols : 2 * head_cols] = rotate(
            value[:, head_cols : 2 * head_cols], 1.0
        ).astype(bf16)
        heads_qkv[s, :, 2 * head_cols :] = value[:, 2 * head_cols :].astype(bf16)

    def attend(s):
        cot = cot_all[s]
        back[s] = jnp.where(live_rows(s), cot, jnp.zeros_like(cot))
        queries = heads_qkv[s, :, 0:head_cols]
        keys = heads_qkv[s, :, head_cols : 2 * head_cols]
        values = heads_qkv[s, :, 2 * head_cols :]
        d_mixed = nt(back[s], flat(out_all[...])).astype(bf16)
        row = lax.broadcasted_iota(jnp.int32, (length, length), 0)
        column = lax.broadcasted_iota(jnp.int32, (length, length), 1)
        allowed = (column <= row) & (column.astype(f32) < len_all[s][0:1, 0:1])
        lane = lax.broadcasted_iota(jnp.int32, (length, head_cols), 1)
        zero = jnp.zeros((), bf16)
        mixed_sum = jnp.zeros((length, head_cols), f32)
        d_queries = d_keys = d_values = mixed_sum
        for h in range(head_cols // HD):
            of_head = (lane >= h * HD) & (lane < (h + 1) * HD)
            q_h, k_h, v_h, d_h = (
                jnp.where(of_head, t, zero) for t in (queries, keys, values, d_mixed)
            )
            scores = jnp.where(allowed, nt(q_h, keys) * HD**-0.5, -1e30)
            raised = jnp.exp(scores - jnp.max(scores, axis=-1, keepdims=True))
            weights = raised * (1.0 / jnp.sum(raised, axis=-1, keepdims=True))
            low = weights.astype(bf16)
            mixed_sum = mixed_sum + nn(low, v_h)
            d_weights = nt(d_h, values)
            inner = jnp.sum(weights * d_weights, axis=-1, keepdims=True)
            d_scores = (weights * (d_weights - inner)).astype(bf16)
            d_queries = d_queries + nn(d_scores, k_h)
            d_keys = d_keys + tn(d_scores, q_h)
            d_values = d_values + tn(low, d_h)
        mixed[s] = mixed_sum.astype(bf16)
        for n, value in enumerate(
            (rotate(d_queries * HD**-0.5, -1.0), rotate(d_keys * HD**-0.5, -1.0), d_values)
        ):
            rounded = value.astype(bf16)
            columns = slice(n * head_cols, (n + 1) * head_cols)
            d_projected[s, :, columns] = rounded
            d_qkv_bias[:, columns] += jnp.sum(rounded.astype(f32), axis=0, keepdims=True)

    forward(3, Q)
    from_core(Q)

    @pl.loop(0, 4)
    def _(i):
        @pl.when(i == 1)
        def _():
            forward_x(0)

        @pl.when(i == 2)
        def _():
            forward_y(0)

        @pl.when(i == 3)
        def _():
            far_halves(0)

        project(near_first(i))

        @pl.when(i == 0)
        def _():
            forward_out(2)
            forward(1, U)

        @pl.when(i == 2)
        def _():
            forward(1, N)

    forward_out(3)
    arrived(out_all.at[1 - core], out_recv.at[1 - core], at.other_core)

    @pl.loop(0, 4)
    def _(i):
        @pl.when(i == 3)
        def _():
            far_halves(1)

        attend(near_first(i))

        @pl.when(i == 0)
        def _():
            forward_x(1)
            forward_y(1)
            forward(2, U)

        @pl.when(i == 1)
        def _():
            forward(2, N)

    def gradient(left, right, n):
        low, high = SPANS[n]

        @pl.loop(0, 8)
        def _(f):
            columns = pl.ds(pl.multiple_of(f * 128, 128), 128)
            terms[f, :, low:high] = tn(flat(left[:, :, columns]), flat(right[...])).astype(bf16)

    def to_core(n):
        for other in range(4):
            send(
                piece(terms, 2 * other + 1 - core, n),
                piece(core_in, other, n),
                core_send.at[n, other],
                core_recv.at[n, other],
                at.other_core,
            ).start()

    def add_core(n):
        low, high = SPANS[n]
        for other in (3, 0, 2, 1):
            arrived(piece(core_in, other, n), core_recv.at[n, other], at.other_core)
            terms[2 * other + core, :, low:high] = (
                terms[2 * other + core, :, low:high].astype(f32)
                + core_in[other, :, low:high].astype(f32)
            ).astype(bf16)

    def pass_on(n, me, target):
        low, high = SPANS[n]

        @pl.when(z == me)
        def _():
            own = piece(terms, 2 * target + core, n)
            if me not in (0, 3):
                source = at.down if me < target else at.up
                arrived(piece(line_in, target, n), line_recv.at[n, target], source)
                terms[2 * target + core, :, low:high] = (
                    terms[2 * target + core, :, low:high].astype(f32)
                    + line_in[target, :, low:high].astype(f32)
                ).astype(bf16)
            slot = 4 if me == target + 1 else target
            send(
                own,
                piece(line_in, slot, n),
                line_send.at[n, target],
                line_recv.at[n, slot],
                at.up if me < target else at.down,
            ).start()

    def line_starts(n):
        for target in (3, 2, 1):
            pass_on(n, 0, target)
        for target in (0, 1, 2):
            pass_on(n, 3, target)

    def line_step(n, step):
        for me, target in (((1, 3), (2, 0)), ((1, 2), (2, 1)), ((2, 3), (1, 0)))[step]:
            pass_on(n, me, target)

    wholes = (qkv_all, up_all, down_all)

    def line_ends(n):
        low, high = SPANS[n]
        total = 2 * z + core

        def add(slot, source):
            arrived(piece(line_in, slot, n), line_recv.at[n, slot], source)
            terms[total, :, low:high] = (
                terms[total, :, low:high].astype(f32) + line_in[slot, :, low:high].astype(f32)
            ).astype(bf16)

        @pl.when(z > 0)
        def _():
            add(z, at.down)

        @pl.when(z < 3)
        def _():
            add(4, at.up)

        own = piece(terms, total, n)
        target = wholes[n].at[part]
        send(own, target, all_send.at[n, 0], all_recv.at[n, 0], at.across_x).start()
        send(own, target, all_send.at[n, 1], all_recv.at[n, 1], at.across_y).start()
        pltpu.make_async_copy(own, target, keep_sem.at[n]).start()

    def share(n):
        whole = wholes[n]
        arrived(whole.at[at.x_part], all_recv.at[n, 0], at.across_x)
        block = whole.at[at.x_part, 0:64]
        send(block, block, all_send.at[n, 2], all_recv.at[n, 2], at.across_y).start()
        arrived(whole.at[at.y_part], all_recv.at[n, 1], at.across_y)
        block = whole.at[at.y_part, 64:128]
        send(block, block, all_send.at[n, 3], all_recv.at[n, 3], at.across_x).start()

    def out_to_core():
        send(
            out_term.at[1 - core], out_core_in, rows_send.at[0], rows_recv.at[0], at.other_core
        ).start()

    def out_add(block):
        out_line[...] = (out_line[...].astype(f32) + block.astype(f32)).astype(bf16)

    def out_add_core():
        arrived(out_core_in, rows_recv.at[0], at.other_core)
        out_line[...] = out_term[core]
        out_add(out_core_in[...])

    def out_step(step):
        @pl.when((z == step) & (z < part))
        def _():
            if step > 0:
                arrived(out_line_in.at[0], rows_recv.at[1], at.down)
                out_add(out_line_in[0])
            send(out_line, out_line_in.at[0], rows_send.at[1], rows_recv.at[1], at.up).start()

        @pl.when((z == 3 - step) & (z > part))
        def _():
            if step > 0:
                arrived(out_line_in.at[1], rows_recv.at[2], at.up)
                out_add(out_line_in[1])
            send(out_line, out_line_in.at[1], rows_send.at[1], rows_recv.at[2], at.down).start()

    def out_ends():
        @pl.when(z == part)
        def _():
            @pl.when(z > 0)
            def _():
                arrived(out_line_in.at[0], rows_recv.at[1], at.down)
                out_add(out_line_in[0])

            @pl.when(z < 3)
            def _():
                arrived(out_line_in.at[1], rows_recv.at[2], at.up)
                out_add(out_line_in[1])

            for n, (peer, _) in enumerate(plane_peers):
                send(out_line, out_grad, rows_send.at[2 + n], rows_recv.at[3], peer).start()
            pltpu.make_async_copy(out_line, out_grad, keep_sem.at[3]).start()

    gradient(normed_one, d_projected, Q)
    to_core(Q)
    for n in range(2):
        out_term[n] = tn(flat(mixed[:, :, n * 128 : (n + 1) * 128]), flat(back[...])).astype(bf16)
    out_to_core()
    add_core(Q)
    line_starts(Q)
    out_add_core()
    out_step(0)
    forward(3, U)
    forward(3, N)
    from_core(U)
    from_core(N)

    halves = (slice(0, HALF), slice(HALF, 2 * HALF))
    part_refs = (out_part, dx_part)
    routes = (
        (halves[0], at.across_x, at.x_part, at.across_y, at.y_part),
        (halves[1], at.across_y, at.y_part, at.across_x, at.x_part),
    )

    def send_part(n, r, m):
        half, peer, peer_part, _, _ = routes[r]
        target = (at.far_part, peer_part)[m]
        send(
            part_refs[n].at[target, half],
            plane_one.at[n, r, m],
            part_send.at[n, r, m],
            part_recv.at[n, r, m],
            peer,
        ).start()

    def send_parts(n, i):
        @pl.when(i == 0)
        def _():
            send_part(n, 0, 0)
            send_part(n, 1, 0)

        @pl.when(i == 1)
        def _():
            send_part(n, 0, 1)

        @pl.when(i == 2)
        def _():
            send_part(n, 1, 1)

    def turn_part(n, r):
        half, peer, _, turn, turned = routes[r]
        arrived(plane_one.at[n, r, 0], part_recv.at[n, r, 0], peer)
        plane_turn[n, r] = (
            part_refs[n][turned, half].astype(f32) + plane_one[n, r, 0].astype(f32)
        ).astype(bf16)
        send(
            plane_turn.at[n, r],
            plane_two.at[n, r],
            part_send.at[n, r, 2],
            part_recv.at[n, r, 2],
            turn,
        ).start()

    def whole_part(n, r):
        half, peer, _, turn, _ = routes[r]
        arrived(plane_one.at[n, r, 1], part_recv.at[n, r, 1], peer)
        arrived(plane_two.at[n, r], part_recv.at[n, r, 2], turn)
        return (
            part_refs[n][part, half].astype(f32)
            + plane_one[n, r, 1].astype(f32)
            + plane_two[n, r].astype(f32)
        )

    up_low, up_high = SPANS[U]
    down_low, down_high = SPANS[N]

    def feed(s):
        value = nn(normed_two[s], flat(w_all[:, :, up_low:up_high])) + up_bias[...]
        hidden[s] = value
        low = (value * (0.5 * (1.0 + lax.erf(value * 2.0**-0.5)))).astype(bf16)
        activated[s] = low
        out_part[s] = (
            nn(low, flat(w_all[:, :, down_low:down_high])) + nn(mixed[s], flat(out_all[...]))
        ).astype(bf16)

    def feed_back(s):
        value = hidden[s]
        slope = gelu_slope(value)
        low = (nt(back[s], flat(w_all[:, :, down_low:down_high])) * slope).astype(bf16)
        d_hidden[s] = low
        d_up_bias[...] += jnp.sum(low.astype(f32), axis=0, keepdims=True)
        d_two = nt(low, flat(w_all[:, :, up_low:up_high]))
        d_one = nt(d_projected[s], flat(w_all[:, :, SPANS[Q][0] : SPANS[Q][1]]))
        unit = (x_all[s].astype(f32) - stats[s][:, 0:1]) * stats[s][:, 1:2]
        sums[0:1] += jnp.sum(d_one * unit, axis=0, keepdims=True)
        sums[1:2] += jnp.sum(d_one, axis=0, keepdims=True)
        sums[2:3] += jnp.sum(d_two * unit, axis=0, keepdims=True)
        sums[3:4] += jnp.sum(d_two, axis=0, keepdims=True)
        dx_part[s] = (d_one * vectors[0:1] + d_two * vectors[2:3]).astype(bf16)

    @pl.loop(0, 4)
    def _(i):
        feed(far_first(i))
        send_parts(0, i)

        @pl.when(i == 1)
        def _():
            line_step(Q, 0)
            out_step(1)

        @pl.when(i == 3)
        def _():
            line_step(Q, 1)

    gradient(activated, back, N)
    to_core(N)
    turn_part(0, 1)
    turn_part(0, 0)
    line_step(Q, 2)
    out_step(2)
    add_core(N)
    line_starts(N)

    @pl.loop(0, 4)
    def _(i):
        feed_back(far_first(i))
        send_parts(1, i)

        @pl.when(i == 1)
        def _():
            line_step(N, 0)
            line_ends(Q)
            out_ends()

        @pl.when(i == 2)
        def _():
            line_step(N, 1)

    gradient(normed_two, d_hidden, U)
    to_core(U)
    share(Q)
    line_step(N, 2)
    turn_part(1, 1)
    turn_part(1, 0)
    add_core(U)
    line_starts(U)

    small_part[...] = jnp.zeros_like(small_part)

    def place(row, value):
        small_part[row // 13, pl.ds(row % 13, 1)] = value

    back_total = jnp.sum(back[part].astype(f32), axis=0, keepdims=True)
    for n in range(8):
        columns = slice(n * 128, (n + 1) * 128)
        for number in range(4):
            place(8 * number + n, sums[number : number + 1, columns])
        place(56 + n, back_total[:, columns])
        place(96 + n, back_total[:, columns])
        place(64 + 4 * n + part, d_up_bias[:, columns])
    for c in range(3):
        for n in range(2):
            columns = slice((2 * c + n) * 128, (2 * c + n + 1) * 128)
            place(32 + 8 * c + 2 * part + n, d_qkv_bias[:, columns])
    for k in range(1, 8):
        send(
            small_part.at[(shard + k) % 8],
            small_in.at[k - 1],
            total_send.at[k - 1],
            total_recv.at[k - 1],
            at.shard_after(k),
        ).start()

    line_step(U, 0)

    for r in range(2):
        half = halves[r]
        live = live_rows(part)[half]
        values = x_all[part, half].astype(f32)
        summed = values + whole_part(0, r) + vectors[4:5] + vectors[5:6]
        output[half] = jnp.where(live, summed, 0.0).astype(bf16)
    line_ends(N)
    line_step(U, 1)
    total = small_part[shard]
    for k in range(1, 8):
        arrived(small_in.at[k - 1], total_recv.at[k - 1], at.shard_after(8 - k))
        total = total + small_in[k - 1]
    small_total[...] = total
    for n, (peer, _) in enumerate(plane_peers):
        send(
            small_total, small_plane.at[part], total_send.at[7 + n], total_recv.at[7 + n], peer
        ).start()
    small_plane[part] = total
    for r in range(2):
        half = halves[r]
        scaled = whole_part(1, r)
        inverse = stats[part, half, 1:2]
        unit = (x_all[part, half].astype(f32) - stats[part, half, 0:1]) * inverse
        result = back[part, half].astype(f32) + inverse * (
            scaled
            - jnp.mean(scaled, axis=-1, keepdims=True)
            - unit * jnp.mean(scaled * unit, axis=-1, keepdims=True)
        )
        input_grad[half] = result.astype(bf16)
    line_step(U, 2)
    share(N)
    for n, (peer, other) in enumerate(plane_peers):
        arrived(small_plane.at[other], total_recv.at[7 + n], peer)
    small_sum[...] = (small_plane[0] + small_plane[1]) + (small_plane[2] + small_plane[3])
    line_ends(U)
    share(U)

    @pl.when(z != part)
    def _():
        arrived(out_grad, rows_recv.at[3], at.across_x)
        sent(out_line, rows_send.at[1], at.up)

    @pl.when(z == part)
    def _():
        for n, (peer, _) in enumerate(plane_peers):
            sent(out_line, rows_send.at[2 + n], peer)
        pltpu.make_async_copy(out_line, out_grad, keep_sem.at[3]).wait()

    sent(out_line, rows_send.at[0], at.other_core)
    for n, (own, whole) in enumerate(activations):
        sent(own, plane_send.at[n, 0], at.across_x)
        sent(own, plane_send.at[n, 1], at.across_y)
        sent(whole.at[part, 0:HALF], plane_send.at[n, 2], at.across_y)
        sent(whole.at[part, 0:HALF], plane_send.at[n, 3], at.across_x)
    for n, (peer, _) in enumerate(plane_peers):
        sent(len_all.at[part], len_send.at[n], peer)
        sent(small_total, total_send.at[7 + n], peer)
    for k in range(1, 8):
        sent(small_own, small_send.at[k - 1], at.shard_after(k))
        sent(small_total, total_send.at[k - 1], at.shard_after(k))
    for n in range(3):
        for other in range(4):
            block = piece(w_all, 2 * other + core, n)
            sent(block, w_send.at[2, n, other], at.other_core)
            sent(block, core_send.at[n, other], at.other_core)

            @pl.when((other <= z) & (z < 3))
            def _():
                sent(block, w_send.at[0, n, other], at.up)

            @pl.when((other >= z) & (z > 0))
            def _():
                sent(block, w_send.at[1, n, other], at.down)

            @pl.when(z != other)
            def _():
                sent(block, line_send.at[n, other], at.up)

    block = out_all.at[core]
    sent(block, out_send.at[2], at.other_core)

    @pl.when((z >= part) & (z < 3))
    def _():
        sent(block, out_send.at[0], at.up)

    @pl.when((z <= part) & (z > 0))
    def _():
        sent(block, out_send.at[1], at.down)

    for n in range(2):
        for r in range(2):
            for m in range(3):
                sent(plane_turn.at[n, r], part_send.at[n, r, m], at.across_x)
    for n, whole in enumerate(wholes):
        arrived(whole.at[at.far_part, 0:64], all_recv.at[n, 2], at.across_y)
        arrived(whole.at[at.far_part, 64:128], all_recv.at[n, 3], at.across_x)
        own = piece(terms, shard, n)
        sent(own, all_send.at[n, 0], at.across_x)
        sent(own, all_send.at[n, 1], at.across_y)
        sent(whole.at[part, 0:64], all_send.at[n, 2], at.across_y)
        sent(whole.at[part, 64:128], all_send.at[n, 3], at.across_x)
        pltpu.make_async_copy(own, whole.at[part], keep_sem.at[n]).wait()


VMEM_SPEC = pl.BlockSpec(memory_space=pltpu.VMEM)
HBM_SPEC = pl.BlockSpec(memory_space=pl.ANY)


def whole_layer(lengths, x_own, cot_own, masters, tables):
    shape = jax.ShapeDtypeStruct
    vmem, dma = pltpu.VMEM, pltpu.SemaphoreType.DMA
    bf16, f32 = jnp.bfloat16, jnp.float32
    length = x_own.shape[0]
    group = 4
    head_cols, wide, rows = D // group, 2816, 128

    def by_sequence(width, kind=bf16):
        return vmem((group, length, width), kind)

    return pl.pallas_call(
        layer_kernel,
        out_shape=(
            shape(x_own.shape, bf16),
            shape(x_own.shape, bf16),
            shape((group, rows, 3 * head_cols), bf16),
            shape((group, rows, FF // group), bf16),
            shape((group, rows, D), bf16),
            shape((rows, D), bf16),
            shape((16, 128), f32),
        ),
        in_specs=[pl.BlockSpec(memory_space=pltpu.SMEM)]
        + [HBM_SPEC] * 6
        + [VMEM_SPEC, VMEM_SPEC],
        out_specs=(VMEM_SPEC, VMEM_SPEC) + (HBM_SPEC,) * 4 + (VMEM_SPEC,),
        scratch_shapes=[
            by_sequence(D),
            by_sequence(D),
            vmem((group, 8, 128), f32),
            vmem((8, rows, wide), bf16),
            vmem((2, rows, D), bf16),
            vmem((16, 128), f32),
            vmem((8, 16, 128), f32),
            vmem((8, D), f32),
            vmem((1, 3 * head_cols), f32),
            vmem((1, FF // group), f32),
            by_sequence(128, f32),
            by_sequence(D),
            by_sequence(D),
            by_sequence(D),
            by_sequence(3 * head_cols),
            by_sequence(head_cols),
            by_sequence(3 * head_cols),
            by_sequence(FF // group, f32),
            by_sequence(FF // group),
            by_sequence(D),
            by_sequence(D),
            vmem((8, rows, wide), bf16),
            vmem((2, rows, D), bf16),
            vmem((8, D), f32),
            vmem((1, 3 * head_cols), f32),
            vmem((1, FF // group), f32),
            vmem((8, 16, 128), f32),
            vmem((2, 2, 2, HALF, D), bf16),
            vmem((2, 2, HALF, D), bf16),
            vmem((2, 2, HALF, D), bf16),
            vmem((4, rows, wide), bf16),
            vmem((5, rows, wide), bf16),
            vmem((rows, D), bf16),
            vmem((rows, D), bf16),
            vmem((2, rows, D), bf16),
            vmem((7, 16, 128), f32),
            vmem((16, 128), f32),
            vmem((4, 16, 128), f32),
            dma((15,)),
            dma((2, 4)),
            dma((2, 4)),
            dma((3,)),
            dma((3,)),
            dma((3, 3, 4)),
            dma((3, 8)),
            dma((3,)),
            dma((2,)),
            dma((7,)),
            dma((7,)),
            dma((2, 2, 3)),
            dma((2, 2, 3)),
            dma((3, 4)),
            dma((3, 4)),
            dma((3, 4)),
            dma((3, 5)),
            dma((5,)),
            dma((4,)),
            dma((3, 4)),
            dma((3, 4)),
            dma((4,)),
            dma((10,)),
            dma((10,)),
        ],
        compiler_params=pltpu.CompilerParams(
            collective_id=0, has_side_effects=True, vmem_limit_bytes=62 << 20
        ),
        name="layer",
    )(lengths, x_own, cot_own, *masters, tables)


def rope_tables(length, heads):
    half = ROT // 2
    angle = np.arange(length)[:, None] * ROPE_BASE ** (-2.0 * np.arange(half) / ROT)[None]
    table = np.zeros((3, length, HD), np.float32)
    table[0] = 1.0
    table[0, :, :half] = table[0, :, half:ROT] = np.cos(angle)
    table[1, :, :half] = -np.sin(angle)
    table[2, :, half:ROT] = np.sin(angle)
    return jnp.asarray(np.tile(table, (1, 1, heads)))


def local_split(
    tokens_in,
    cotangent,
    lengths,
    qkv_master,
    out_master,
    up_master,
    down_master,
    small_master,
    qkv_first,
    out_first,
    up_first,
    down_first,
    small_first,
    qkv_second,
    out_second,
    up_second,
    down_second,
    small_second,
):
    masters = (qkv_master, out_master, up_master, down_master, small_master)
    firsts = (qkv_first, out_first, up_first, down_first, small_first)
    seconds = (qkv_second, out_second, up_second, down_second, small_second)
    parts, shards = lax.axis_size("dp"), lax.axis_size("fsdp")
    part, shard = lax.axis_index("dp"), lax.axis_index("fsdp")
    length = tokens_in.shape[1]
    update = (masters, firsts, seconds)
    if (parts, shards) == (4, 8):
        tall = tuple(masters[:4]) + (small_master.reshape(-1, 128),)
        output, input_grad, qkv_grad, up_grad, down_grad, out_grad, small_sum = whole_layer(
            lengths, tokens_in[0], cotangent[0], tall, rope_tables(length, HEADS // parts)
        )
        grads = (qkv_grad, out_grad, up_grad, down_grad, small_sum[: tall[4].shape[0]])
        return lamb_split(*update, grads, (output, input_grad))

    head_cols = D // parts
    ff_rows = down_master.shape[0] // parts
    qkv_own = sliced(qkv_master, part, parts, 3).astype(jnp.bfloat16)
    up_own = sliced(up_master, part, parts, shards).astype(jnp.bfloat16)
    down_own = lax.dynamic_slice_in_dim(down_master, part * ff_rows, ff_rows).astype(jnp.bfloat16)
    out_own = out_master.astype(jnp.bfloat16)
    small_own = small_master.astype(jnp.bfloat16)

    def small_vectors(small_all):
        vectors = split_small(small_all)
        vectors[4] = sliced(vectors[4][None], part, parts, 3)[0]
        vectors[6] = sliced(vectors[6][None], part, parts, shards)[0]
        return vectors

    def over_shards(own):
        return lax.all_gather(own, "fsdp", axis=0, tiled=True)

    x_all = lax.all_gather(tokens_in, "dp", axis=0, tiled=True)
    cotangent_all = lax.all_gather(cotangent, "dp", axis=0, tiled=True)
    lengths_all = lax.all_gather(lengths, "dp", axis=0, tiled=True)
    qkv_weight, up_weight, down_weight = (over_shards(w) for w in (qkv_own, up_own, down_own))
    out_weight = lax.dynamic_slice_in_dim(over_shards(out_own), part * head_cols, head_cols)
    gain_one, shift_one, gain_two, shift_two, qkv_bias, out_bias, up_bias, down_bias = (
        small_vectors(over_shards(small_own).astype(jnp.float32))
    )
    out_part, scaled_part, terms, sums = layer(
        x_all,
        cotangent_all,
        lengths_all,
        (qkv_weight, out_weight, up_weight, down_weight),
        (gain_one, shift_one, gain_two, shift_two, qkv_bias, up_bias),
        part,
    )
    norm_sums, d_qkv_bias, d_up_bias = sums
    out_sum = lax.psum_scatter(out_part, "dp", scatter_dimension=0, tiled=True)
    scaled = lax.psum_scatter(scaled_part, "dp", scatter_dimension=0, tiled=True)
    out_sum, scaled = out_sum.astype(jnp.float32), scaled.astype(jnp.float32)

    inputs = tokens_in[0].astype(jnp.float32)
    live = (jnp.arange(length) < lengths[0]).astype(jnp.float32)[:, None]
    back = cotangent[0].astype(jnp.float32) * live
    back_total = jnp.sum(back, axis=0)

    def spread(values, pieces):
        wide = jnp.zeros((pieces, parts, values.shape[0] // pieces), jnp.float32)
        return lax.dynamic_update_index_in_dim(
            wide, values.reshape(pieces, -1), part, axis=1
        ).reshape(-1)

    small_grad = jnp.concatenate(
        [
            norm_sums.reshape(4 * D),
            spread(d_qkv_bias, 3),
            back_total,
            spread(d_up_bias, shards),
            back_total,
        ]
    )
    small_sum = lax.psum(small_grad, ("dp", "fsdp"))
    small_rows = small_master.shape[0]
    small_sum = lax.dynamic_slice_in_dim(small_sum, shard * small_rows, small_rows)
    qkv_term, out_term, up_term, down_term = terms
    out_wide = lax.dynamic_update_slice_in_dim(
        jnp.zeros((D, D), jnp.bfloat16), out_term, part * head_cols, axis=0
    )

    def to_owner(term):
        own = lax.psum_scatter(term, "fsdp", scatter_dimension=0, tiled=True)
        return lax.all_gather(own, "dp", axis=0, tiled=False).astype(jnp.float32)

    reduced = (
        joined(to_owner(qkv_term), 3),
        lax.psum(
            lax.psum_scatter(out_wide, "fsdp", scatter_dimension=0, tiled=True), "dp"
        ).astype(jnp.float32),
        joined(to_owner(up_term), shards),
        to_owner(down_term).reshape(down_master.shape),
        small_sum,
    )

    unit_rows, inverse_rows = normalize(inputs)
    output = ((inputs + out_sum + out_bias + down_bias) * live).astype(jnp.bfloat16)
    input_grad = back + inverse_rows * (
        scaled
        - jnp.mean(scaled, axis=-1, keepdims=True)
        - unit_rows * jnp.mean(scaled * unit_rows, axis=-1, keepdims=True)
    )
    return (output[None], input_grad.astype(jnp.bfloat16)[None]) + lamb(*update, reduced)


def lamb_rows(first_old, second_old, master, grad):
    first_new = BETA_ONE * first_old + (1.0 - BETA_ONE) * grad
    second_new = BETA_TWO * second_old + (1.0 - BETA_TWO) * grad * grad
    update = first_new / (jnp.sqrt(second_new) + ADAM_EPSILON) + DECAY * master
    return first_new, second_new, update


def lane_sums(values):
    squares = jnp.sum(values * values, axis=0, keepdims=True)
    total = squares[:, 0:128]
    for n in range(1, squares.shape[1] // 128):
        total = total + squares[:, n * 128 : (n + 1) * 128]
    return total


def moments_kernel(*refs):
    qkv_grad, out_grad, up_grad, down_grad, small_grad = refs[0:5]
    masters, firsts, seconds = refs[5:10], refs[10:15], refs[15:20]
    first_news, second_news, updates, kept = refs[20:25], refs[25:30], refs[30:35], refs[35:40]
    squares = refs[40]
    step = pl.program_id(0)

    @pl.when(step == 0)
    def _():
        squares[...] = jnp.zeros_like(squares)

    def one(number, span, grad):
        index = (slice(None), span)
        master = masters[number][index]
        first_new, second_new, update = lamb_rows(
            firsts[number][index], seconds[number][index], master, grad
        )
        first_news[number][index] = first_new
        second_news[number][index] = second_new
        rows = masters[number].shape[0]
        place = (pl.ds(pl.multiple_of(step * rows, rows), rows), span)
        updates[number][place] = update
        kept[number][place] = master
        return lane_sums(master), lane_sums(update)

    def add(number, pairs):
        weight, update = pairs[0]
        for more_weight, more_update in pairs[1:]:
            weight, update = weight + more_weight, update + more_update
        squares[number : number + 1] += weight
        squares[8 + number : 9 + number] += update

    f32 = jnp.float32
    parts = qkv_grad.shape[0]
    width = qkv_grad.shape[2] // 3
    add(
        0,
        [
            one(
                0,
                slice((c * parts + d) * width, (c * parts + d + 1) * width),
                qkv_grad[d, :, c * width : (c + 1) * width].astype(f32),
            )
            for c in range(3)
            for d in range(parts)
        ],
    )
    add(1, [one(1, slice(None), out_grad[...].astype(f32))])
    pieces = up_grad.shape[2] // 128
    add(
        2,
        [
            one(
                2,
                slice((g * parts + d) * 128, (g * parts + d + 1) * 128),
                up_grad[d, :, g * 128 : (g + 1) * 128].astype(f32),
            )
            for g in range(pieces)
            for d in range(parts)
        ],
    )
    add(3, [one(3, slice(None), down_grad[0].astype(f32))])

    @pl.when(step == 0)
    def _():
        first_new, second_new, update = lamb_rows(
            firsts[4][...], seconds[4][...], masters[4][...], small_grad[...]
        )
        first_news[4][...] = first_new
        second_news[4][...] = second_new
        updates[4][...] = update
        kept[4][...] = masters[4][...]
        squares[4:5] += lane_sums(masters[4][...])
        squares[12:13] += lane_sums(update)


def lamb_specs(masters, steps):
    specs = [pl.BlockSpec((m.shape[0] // steps, m.shape[1]), lambda i: (i, 0)) for m in masters[:4]]
    return specs + [pl.BlockSpec(masters[4].shape, lambda i: (0, 0))]


def moments(grads, masters, firsts, seconds, steps=8):
    qkv_grad, out_grad, up_grad, down_grad, small_grad = grads
    shape = jax.ShapeDtypeStruct
    each = lamb_specs(masters, steps)
    rows = qkv_grad.shape[1]
    halves = steps // qkv_grad.shape[0]
    grad_specs = [
        pl.BlockSpec((qkv_grad.shape[0], rows // steps, qkv_grad.shape[2]), lambda i: (0, i, 0)),
        each[1],
        pl.BlockSpec((up_grad.shape[0], rows // steps, up_grad.shape[2]), lambda i: (0, i, 0)),
        pl.BlockSpec(
            (1, rows // halves, down_grad.shape[2]), lambda i: (i // halves, i % halves, 0)
        ),
        each[4],
    ]
    out = [shape(m.shape, jnp.float32) for m in masters]
    near = [pltpu.VMEM(m.shape, jnp.float32) for m in masters]
    results = pl.pallas_call(
        moments_kernel,
        grid=(steps,),
        in_specs=grad_specs + each * 3,
        out_specs=each * 2 + [VMEM_SPEC] * 10 + [pl.BlockSpec((16, 128), lambda i: (0, 0))],
        out_shape=out * 2 + near * 2 + [shape((16, 128), jnp.float32)],
        compiler_params=pltpu.CompilerParams(vmem_limit_bytes=44 << 20),
        name="moments",
    )(*grads, *masters, *firsts, *seconds)
    return results[0:5], results[5:10], results[10:15], results[15:20], results[20]


def norms_kernel(squares, total, everyone, send_sem, recv_sem):
    shard, part = lax.axis_index("fsdp"), lax.axis_index("dp")
    peers = [(part, (shard + k) % 8) for k in range(1, 8)]
    barrier = pltpu.get_barrier_semaphore()
    for peer in peers:
        pl.semaphore_signal(barrier, inc=1, device_id=peer, device_id_type=MESH_ID)
    pl.semaphore_wait(barrier, 7)
    for k in range(1, 8):
        send(
            squares, everyone.at[shard], send_sem.at[k - 1], recv_sem.at[k - 1], peers[k - 1]
        ).start()
    everyone[shard] = squares[...]
    for k in range(1, 8):
        arrived(everyone.at[(shard + 8 - k) % 8], recv_sem.at[k - 1], peers[7 - k])
    summed = everyone[0]
    for k in range(1, 8):
        summed = summed + everyone[k]
    norms = jnp.sqrt(jnp.sum(summed, axis=1, keepdims=True))
    total[...] = jnp.broadcast_to(norms, (16, 128))
    for k in range(1, 8):
        sent(squares, send_sem.at[k - 1], peers[k - 1])


def norms(squares):
    dma = pltpu.SemaphoreType.DMA
    return pl.pallas_call(
        norms_kernel,
        out_shape=jax.ShapeDtypeStruct((16, 128), jnp.float32),
        in_specs=[VMEM_SPEC],
        out_specs=VMEM_SPEC,
        scratch_shapes=[pltpu.VMEM((8, 16, 128), jnp.float32), dma((7,)), dma((7,))],
        compiler_params=pltpu.CompilerParams(
            collective_id=1, has_side_effects=True, vmem_limit_bytes=2 << 20
        ),
        name="norms",
    )(squares)


def step_kernel(*refs):
    total, masters, updates, layer_outs = refs[0], refs[1:6], refs[6:11], refs[11:13]
    news, outs, lamb_norms = refs[13:18], refs[18:20], refs[20]
    step = pl.program_id(0)
    for number in range(5):
        weight_norm = total[number : number + 1, 0:1]
        update_norm = total[8 + number : 9 + number, 0:1]
        scale = RATE * (weight_norm / update_norm)
        rows = news[number].shape[0]
        place = slice(None)
        if rows < masters[number].shape[0]:
            place = pl.ds(pl.multiple_of(step * rows, rows), rows)
        news[number][...] = masters[number][place] - scale * updates[number][place]
    for source, target in zip(layer_outs, outs):
        target[...] = source[...]

    @pl.when(step == 0)
    def _():
        row = lax.broadcasted_iota(jnp.int32, (8, 128), 0)
        lane = lax.broadcasted_iota(jnp.int32, (8, 128), 1)
        for n in range(2):
            half = jnp.where(row == lane, total[8 * n : 8 * n + 8], 0.0)
            lamb_norms[n : n + 1] = jnp.sum(half, axis=0, keepdims=True)[:, 0:5]


def step_masters(total, masters, updates, layer_outs, steps=4):
    shape = jax.ShapeDtypeStruct
    out_specs = [
        pl.BlockSpec((o.shape[0] // steps, o.shape[1]), lambda i: (i, 0)) for o in layer_outs
    ]
    results = pl.pallas_call(
        step_kernel,
        grid=(steps,),
        in_specs=[pl.BlockSpec((16, 128), lambda i: (0, 0))] + [VMEM_SPEC] * 10 + out_specs,
        out_specs=lamb_specs(masters, steps)
        + out_specs
        + [pl.BlockSpec((2, 5), lambda i: (0, 0))],
        out_shape=[shape(m.shape, jnp.float32) for m in masters]
        + [shape(o.shape, o.dtype) for o in layer_outs]
        + [shape((2, 5), jnp.float32)],
        compiler_params=pltpu.CompilerParams(vmem_limit_bytes=40 << 20),
        name="step_masters",
    )(total, *masters, *updates, *layer_outs)
    return results[0:5], results[5:7], results[7]


def lamb_split(masters, firsts, seconds, grads, layer_outs):
    def tall(arrays):
        return tuple(arrays[:4]) + (arrays[4].reshape(-1, 128),)

    def flat_small(arrays):
        return tuple(arrays[:4]) + (arrays[4].reshape(-1),)

    masters, firsts, seconds = tall(masters), tall(firsts), tall(seconds)
    first_news, second_news, updates, kept, squares = moments(grads, masters, firsts, seconds)
    news, outs, lamb_norms = step_masters(norms(squares), kept, updates, layer_outs)
    return (
        tuple(out[None] for out in outs)
        + flat_small(news)
        + flat_small(first_news)
        + flat_small(second_news)
        + (lamb_norms,)
    )


def lamb(masters, firsts, seconds, reduced):
    updates = []
    first_news = []
    second_news = []
    for first_old, second_old, master, grad_sum in zip(firsts, seconds, masters, reduced):
        first_new = BETA_ONE * first_old + (1.0 - BETA_ONE) * grad_sum
        second_new = BETA_TWO * second_old + (1.0 - BETA_TWO) * grad_sum * grad_sum
        updates.append(first_new / (jnp.sqrt(second_new) + ADAM_EPSILON) + DECAY * master)
        first_news.append(first_new)
        second_news.append(second_new)
    weight_squares, update_squares = lax.psum(
        (local_squares(masters), local_squares(updates)), "fsdp"
    )
    weight_norms = jnp.sqrt(weight_squares)
    update_norms = jnp.sqrt(update_squares)
    new_masters = [
        masters[number] - RATE * (weight_norms[number] / update_norms[number]) * updates[number]
        for number in range(5)
    ]
    lamb_norms = jnp.stack([weight_norms, update_norms])
    return tuple(new_masters) + tuple(first_news) + tuple(second_news) + (lamb_norms,)


def solution(mesh):
    in_specs = (
        P(("dp", "fsdp"), None, None),
        P(("dp", "fsdp"), None, None),
        P(("dp", "fsdp")),
        P("fsdp", None),
        P("fsdp", None),
        P("fsdp", None),
        P("fsdp", None),
        P("fsdp"),
        P("fsdp", None),
        P("fsdp", None),
        P("fsdp", None),
        P("fsdp", None),
        P("fsdp"),
        P("fsdp", None),
        P("fsdp", None),
        P("fsdp", None),
        P("fsdp", None),
        P("fsdp"),
    )
    out_specs = (
        P(("dp", "fsdp"), None, None),
        P(("dp", "fsdp"), None, None),
        P("fsdp", None),
        P("fsdp", None),
        P("fsdp", None),
        P("fsdp", None),
        P("fsdp"),
        P("fsdp", None),
        P("fsdp", None),
        P("fsdp", None),
        P("fsdp", None),
        P("fsdp"),
        P("fsdp", None),
        P("fsdp", None),
        P("fsdp", None),
        P("fsdp", None),
        P("fsdp"),
        P(),
    )
    return jax.shard_map(local_split, mesh=mesh, in_specs=in_specs, out_specs=out_specs, check_vma=False)
```

```python
import math

import jax
import jax.numpy as jnp
import numpy as np
from jax import lax
from jax.experimental import pallas as pl
from jax.experimental.pallas import tpu as pltpu
from jax.sharding import PartitionSpec as P

D = 1024
HEADS = 16
HD = 64
FF = 4096
ROT = 16
SMALL = 13312


NORM_EPSILON = 1e-05
ADAM_EPSILON = 1e-06
ROPE_BASE = 10000.0
RATE = 0.5
DECAY = 0.01
BETA_ONE = 0.5
BETA_TWO = 0.5


def split_small(small_vector):
    bounds = [0, D, 2 * D, 3 * D, 4 * D, 7 * D, 8 * D, 8 * D + FF, 9 * D + FF]
    return [small_vector[bounds[number] : bounds[number + 1]] for number in range(8)]


def normalize(values):
    average = jnp.mean(values, axis=-1, keepdims=True)
    centred = values - average
    variance = jnp.mean(centred * centred, axis=-1, keepdims=True)
    inverse = lax.rsqrt(variance + NORM_EPSILON)
    return (centred * inverse, inverse)


def rotary_tables(length):
    half_dims = ROT // 2
    position = jnp.arange(length, dtype=jnp.float32)[:, None]
    number = jnp.arange(half_dims, dtype=jnp.float32)[None, :]
    angle = position * jnp.exp(number * (-2.0 * math.log(ROPE_BASE) / ROT))
    return (jnp.cos(angle)[:, None, :], jnp.sin(angle)[:, None, :])


def rotate(heads_in, cosine_table, sine_table):
    half_dims = ROT // 2
    first_half = heads_in[..., :half_dims]
    second_half = heads_in[..., half_dims:ROT]
    return jnp.concatenate(
        [
            first_half * cosine_table - second_half * sine_table,
            second_half * cosine_table + first_half * sine_table,
            heads_in[..., ROT:],
        ],
        axis=-1,
    )


def rotate_back(grads_in, cosine_table, sine_table):
    half_dims = ROT // 2
    first_half = grads_in[..., :half_dims]
    second_half = grads_in[..., half_dims:ROT]
    return jnp.concatenate(
        [
            first_half * cosine_table + second_half * sine_table,
            second_half * cosine_table - first_half * sine_table,
            grads_in[..., ROT:],
        ],
        axis=-1,
    )


def gelu_slope(values):
    return 0.5 * (1.0 + lax.erf(values * 2.0 ** (-0.5))) + values * jnp.exp(
        -0.5 * values * values
    ) * (2.0 * math.pi) ** (-0.5)


def against(left, right):
    return lax.dot_general(
        left, right, (((1,), (1,)), ((), ())), preferred_element_type=jnp.float32
    )


def outer_sum(columns, right):
    return lax.dot_general(
        columns, right, (((0,), (0,)), ((), ())), preferred_element_type=jnp.float32
    )


def local_squares(arrays):
    return jnp.stack([jnp.sum(array_in * array_in) for array_in in arrays])


def sliced(master, part, parts, pieces):
    rows, columns = master.shape
    width = columns // (pieces * parts)
    return lax.dynamic_index_in_dim(
        master.reshape(rows, pieces, parts, width), part, axis=2, keepdims=False
    ).reshape(rows, pieces * width)


def joined(slices, pieces):
    parts, rows, columns = slices.shape
    width = columns // pieces
    return (
        slices.reshape(parts, rows, pieces, width)
        .transpose(1, 2, 0, 3)
        .reshape(rows, pieces * parts * width)
    )


def layer(x_all, cotangent_all, lengths_all, weights, small_all, part):
    qkv_weight, out_weight, up_weight, down_weight = weights
    group, length, _ = x_all.shape
    tokens = group * length
    head_cols = out_weight.shape[0]
    heads = head_cols // HD
    gain_one, shift_one, gain_two, shift_two, qkv_bias, up_bias = small_all
    inputs = x_all.reshape(tokens, D).astype(jnp.float32)
    position = jnp.arange(length)
    live = (position[None, :] < lengths_all[:, None]).astype(jnp.float32).reshape(tokens, 1)
    allowed = (position[None, None, :] <= position[None, :, None]) & (
        position[None, None, :] < lengths_all[:, None, None]
    )
    unit_rows, _ = normalize(inputs)
    normed_one = (unit_rows * gain_one + shift_one).astype(jnp.bfloat16)
    normed_two = (unit_rows * gain_two + shift_two).astype(jnp.bfloat16)
    projected = jnp.dot(normed_one, qkv_weight, preferred_element_type=jnp.float32) + qkv_bias
    projected = projected.reshape(group, length, 3, heads, HD)
    cosine_table, sine_table = rotary_tables(length)
    query_heads = rotate(projected[:, :, 0], cosine_table, sine_table).astype(jnp.bfloat16)
    key_heads = rotate(projected[:, :, 1], cosine_table, sine_table).astype(jnp.bfloat16)
    value_heads = projected[:, :, 2].astype(jnp.bfloat16)
    scores = jnp.einsum(
        "gqhd,gkhd->ghqk", query_heads, key_heads, preferred_element_type=jnp.float32
    ) * HD ** (-0.5)
    scores = jnp.where(allowed[:, None], scores, -1e30)
    row_top = jnp.max(scores, axis=-1, keepdims=True)
    raised = jnp.exp(scores - row_top)
    attend = raised / jnp.sum(raised, axis=-1, keepdims=True)
    attend_low = attend.astype(jnp.bfloat16)
    mixed = jnp.einsum(
        "ghqk,gkhd->gqhd", attend_low, value_heads, preferred_element_type=jnp.float32
    )
    mixed = mixed.reshape(tokens, head_cols).astype(jnp.bfloat16)
    hidden = jnp.dot(normed_two, up_weight, preferred_element_type=jnp.float32) + up_bias
    activated = jax.nn.gelu(hidden, approximate=False).astype(jnp.bfloat16)
    out_part = jnp.dot(mixed, out_weight, preferred_element_type=jnp.float32) + jnp.dot(
        activated, down_weight, preferred_element_type=jnp.float32
    )

    back = (cotangent_all.reshape(tokens, D).astype(jnp.float32) * live).astype(jnp.bfloat16)
    d_hidden = (against(back, down_weight) * gelu_slope(hidden)).astype(jnp.bfloat16)
    d_mixed = against(back, out_weight).astype(jnp.bfloat16).reshape(group, length, heads, HD)
    d_attend = jnp.einsum(
        "gqhd,gkhd->ghqk", d_mixed, value_heads, preferred_element_type=jnp.float32
    )
    row_inner = jnp.sum(attend * d_attend, axis=-1, keepdims=True)
    d_scores = (attend * (d_attend - row_inner)).astype(jnp.bfloat16)
    d_queries = jnp.einsum(
        "ghqk,gkhd->gqhd", d_scores, key_heads, preferred_element_type=jnp.float32
    ) * HD ** (-0.5)
    d_keys = jnp.einsum(
        "ghqk,gqhd->gkhd", d_scores, query_heads, preferred_element_type=jnp.float32
    ) * HD ** (-0.5)
    d_values = jnp.einsum(
        "ghqk,gqhd->gkhd", attend_low, d_mixed, preferred_element_type=jnp.float32
    )
    d_projected = jnp.stack(
        [
            rotate_back(d_queries, cosine_table, sine_table),
            rotate_back(d_keys, cosine_table, sine_table),
            d_values,
        ],
        axis=2,
    )
    d_projected = d_projected.reshape(tokens, 3 * head_cols).astype(jnp.bfloat16)
    d_normed_one = against(d_projected, qkv_weight)
    d_normed_two = against(d_hidden, up_weight)
    scaled_part = d_normed_one * gain_one + d_normed_two * gain_two
    norm_sums = jnp.stack(
        [
            jnp.sum(d_normed_one * unit_rows, axis=0),
            jnp.sum(d_normed_one, axis=0),
            jnp.sum(d_normed_two * unit_rows, axis=0),
            jnp.sum(d_normed_two, axis=0),
        ]
    )
    d_qkv_bias = jnp.sum(d_projected, axis=0, dtype=jnp.float32)
    d_up_bias = jnp.sum(d_hidden, axis=0, dtype=jnp.float32)
    terms = (
        outer_sum(normed_one, d_projected),
        outer_sum(mixed, back),
        outer_sum(normed_two, d_hidden),
        outer_sum(activated, back),
    )
    return (
        out_part.astype(jnp.bfloat16),
        scaled_part.astype(jnp.bfloat16),
        tuple(term.astype(jnp.bfloat16) for term in terms),
        (norm_sums, d_qkv_bias, d_up_bias),
    )


MESH_ID = pl.DeviceIdType.MESH
HALF = 128


class Place:
    def __init__(self):
        self.part = lax.axis_index("dp")
        self.shard = lax.axis_index("fsdp")
        self.z = self.shard // 2
        self.core = self.shard % 2
        self.x_part = 2 * (self.part // 2) + 1 - self.part % 2
        self.y_part = (self.part + 2) % 4
        self.far_part = 3 - self.part
        self.across_x = (self.x_part, self.shard)
        self.across_y = (self.y_part, self.shard)
        self.across_far = (self.far_part, self.shard)
        self.other_core = (self.part, 2 * self.z + 1 - self.core)
        self.up = (self.part, jnp.minimum(self.shard + 2, 7))
        self.down = (self.part, jnp.maximum(self.shard - 2, 0))

    def shard_after(self, k):
        return (self.part, (self.shard + k) % 8)


def send(source, target, send_sem, recv_sem, device):
    return pltpu.make_async_remote_copy(
        src_ref=source,
        dst_ref=target,
        send_sem=send_sem,
        recv_sem=recv_sem,
        device_id=device,
        device_id_type=MESH_ID,
    )


def arrived(target, recv_sem, device):
    send(target, target, recv_sem, recv_sem, device).wait_recv()


def sent(source, send_sem, device):
    send(source, source, send_sem, send_sem, device).wait_send()


def greet(at):
    barrier = pltpu.get_barrier_semaphore()
    peers = [at.across_x, at.across_y, at.across_far] + [at.shard_after(k) for k in range(1, 8)]
    for peer in peers:
        pl.semaphore_signal(barrier, inc=1, device_id=peer, device_id_type=MESH_ID)
    pl.semaphore_wait(barrier, len(peers))


SPANS = ((0, 768), (768, 1792), (1792, 2816))
Q, U, N = 0, 1, 2


def nt(left, right):
    return lax.dot_general(
        left, right, (((1,), (1,)), ((), ())), preferred_element_type=jnp.float32
    )


def tn(left, right):
    return lax.dot_general(
        left, right, (((0,), (0,)), ((), ())), preferred_element_type=jnp.float32
    )


def nn(left, right):
    return jnp.dot(left, right, preferred_element_type=jnp.float32)


def flat(value):
    return value.reshape(value.shape[0] * value.shape[1], value.shape[2])


def layer_kernel(
    length_own,
    x_own,
    cot_own,
    qkv_master,
    out_master,
    up_master,
    down_master,
    small_master,
    tables_in,
    output_out,
    input_grad_out,
    qkv_all,
    up_all,
    down_all,
    out_grad,
    small_sum,
    tables,
    output,
    input_grad,
    x_all,
    cot_all,
    len_all,
    w_all,
    out_all,
    small_own,
    small_all,
    vectors,
    qkv_bias,
    up_bias,
    stats,
    normed_one,
    normed_two,
    back,
    heads_qkv,
    mixed,
    d_projected,
    hidden,
    d_hidden,
    out_part,
    dx_part,
    terms,
    out_term,
    sums,
    d_qkv_bias,
    d_up_bias,
    small_part,
    plane_one,
    plane_two,
    plane_turn,
    core_in,
    line_in,
    out_core_in,
    out_line,
    out_line_in,
    small_in,
    small_total,
    small_plane,
    load_sem,
    plane_send,
    plane_recv,
    early_send,
    early_recv,
    len_send,
    len_recv,
    w_send,
    w_recv,
    out_send,
    out_recv,
    small_send,
    small_recv,
    part_send,
    part_recv,
    core_send,
    core_recv,
    line_send,
    line_recv,
    rows_send,
    rows_recv,
    all_send,
    all_recv,
    keep_sem,
    total_send,
    total_recv,
    store_sem,
):
    f32, bf16 = jnp.float32, jnp.bfloat16
    at = Place()
    z, core, part, shard = at.z, at.core, at.part, at.shard
    length = x_own.shape[0]
    head_cols = mixed.shape[2]
    activated = normed_one
    place_x, place_y = part % 2, part // 2

    def near_first(i):
        return 2 * ((place_y + i // 2) % 2) + (place_x + i % 2) % 2

    def far_first(i):
        return 2 * ((place_y + 1 - i % 2) % 2) + (place_x + 1 - i // 2) % 2

    def piece(ref, slot, n):
        return ref.at[slot, :, SPANS[n][0] : SPANS[n][1]]

    plane_peers = (
        (at.across_x, at.x_part),
        (at.across_y, at.y_part),
        (at.across_far, at.far_part),
    )

    stage = [hidden.at[n, 0:128] for n in range(4)]
    loads = []
    for c in range(3):
        columns = pl.ds(pl.multiple_of(c * D + part * head_cols, 128), head_cols)
        target = stage[0].at[:, c * head_cols : (c + 1) * head_cols]
        loads.append((qkv_master.at[:, columns], target))
    loads.append((out_master, stage[1]))
    for g in range(8):
        columns = pl.ds(pl.multiple_of(g * (FF // 8) + part * 128, 128), 128)
        loads.append((up_master.at[:, columns], stage[2].at[:, g * 128 : (g + 1) * 128]))
    rows = pl.ds(pl.multiple_of(part * 128, 128), 128)
    loads.append((down_master.at[rows], stage[3]))
    loads.append((x_own, x_all.at[part]))
    loads.append((cot_own, cot_all.at[part]))
    loads.append((tables_in, tables))

    def load(n):
        return pltpu.make_async_copy(loads[n][0], loads[n][1], load_sem.at[n])

    for n in range(len(loads)):
        load(n).start()
    len_all[part] = jnp.full((8, 128), length_own[0], jnp.int32).astype(f32)
    small_own[...] = jnp.zeros_like(small_own)
    small_own[0:13] = small_master[...].astype(bf16).astype(f32)
    small_all[shard] = small_own[...]
    greet(at)

    halves = (slice(0, HALF), slice(HALF, 2 * HALF))
    activations = ((x_own, x_all), (cot_own, cot_all))
    neighbours = ((at.across_x, at.x_part), (at.across_y, at.y_part))

    def send_activations():
        for r, (peer, _) in enumerate(neighbours):
            send(
                x_own, x_all.at[part], plane_send.at[0, r], plane_recv.at[0, r], peer
            ).start()
        for r, (peer, _) in enumerate(neighbours):
            send(
                cot_own.at[halves[0]],
                cot_all.at[part, halves[0]],
                early_send.at[r],
                early_recv.at[r],
                peer,
            ).start()

    def send_rest():
        for r, (peer, _) in enumerate(neighbours):
            send(
                cot_own.at[halves[1]],
                cot_all.at[part, halves[1]],
                plane_send.at[1, r],
                plane_recv.at[1, r],
                peer,
            ).start()

    def cast(n, first, last):
        for m in range(first, last):
            load(m).wait()
        low, high = SPANS[n]
        w_all[shard, :, low:high] = stage[(0, 2, 3)[n]][:, 0 : high - low].astype(bf16)

    def send_own(n):
        cast(n, *((0, 3), (4, 12), (12, 13))[n])
        block = piece(w_all, shard, n)

        @pl.when(z < 3)
        def _():
            send(block, block, w_send.at[0, n, z], w_recv.at[n, shard], at.up).start()

        @pl.when(z > 0)
        def _():
            send(block, block, w_send.at[1, n, z], w_recv.at[n, shard], at.down).start()

        send(block, block, w_send.at[2, n, z], w_recv.at[n, shard], at.other_core).start()

    def forward(k, n):
        @pl.when(z >= k)
        def _():
            source = 2 * (z - k) + core
            block = piece(w_all, source, n)
            arrived(block, w_recv.at[n, source], at.down)

            @pl.when(z < 3)
            def _():
                send(block, block, w_send.at[0, n, z - k], w_recv.at[n, source], at.up).start()

            send(
                block, block, w_send.at[2, n, z - k], w_recv.at[n, source], at.other_core
            ).start()

        @pl.when(z + k <= 3)
        def _():
            source = 2 * (z + k) + core
            block = piece(w_all, source, n)
            arrived(block, w_recv.at[n, source], at.up)

            @pl.when(z > 0)
            def _():
                send(block, block, w_send.at[1, n, z + k], w_recv.at[n, source], at.down).start()

            send(
                block, block, w_send.at[2, n, z + k], w_recv.at[n, source], at.other_core
            ).start()

    def from_core(n):
        for other in range(4):
            source = 2 * other + 1 - core
            arrived(piece(w_all, source, n), w_recv.at[n, source], at.other_core)

    def send_out_rows():
        load(3).wait()

        @pl.when(z == part)
        def _():
            out_all[core] = stage[1][...].astype(bf16)
            block = out_all.at[core]

            @pl.when(z < 3)
            def _():
                send(block, block, out_send.at[0], out_recv.at[core], at.up).start()

            @pl.when(z > 0)
            def _():
                send(block, block, out_send.at[1], out_recv.at[core], at.down).start()

            send(block, block, out_send.at[2], out_recv.at[core], at.other_core).start()

    def out_from_core():
        arrived(out_all.at[1 - core], out_recv.at[1 - core], at.other_core)

    def forward_out(k):
        @pl.when((z - k == part) | (z + k == part))
        def _():
            block = out_all.at[core]
            arrived(block, out_recv.at[core], at.up)

            @pl.when((z > part) & (z < 3))
            def _():
                send(block, block, out_send.at[0], out_recv.at[core], at.up).start()

            @pl.when((z < part) & (z > 0))
            def _():
                send(block, block, out_send.at[1], out_recv.at[core], at.down).start()

            send(block, block, out_send.at[2], out_recv.at[core], at.other_core).start()

    def forward_neighbour(n, r):
        peer, source = neighbours[r]
        whole = activations[n][1]
        if n == 0:
            arrived(whole.at[source], plane_recv.at[0, r], peer)
        else:
            arrived(whole.at[source, halves[0]], early_recv.at[r], peer)
            arrived(whole.at[source, halves[1]], plane_recv.at[1, r], peer)
        block = whole.at[source, halves[r]]
        onward = neighbours[1 - r][0]
        send(block, block, plane_send.at[n, 2 + r], plane_recv.at[n, 2 + r], onward).start()

    def forward_x(n):
        forward_neighbour(n, 0)

    def forward_y(n):
        forward_neighbour(n, 1)

    def far_halves(n):
        whole = activations[n][1]
        arrived(whole.at[at.far_part, 0:HALF], plane_recv.at[n, 2], at.across_y)
        arrived(whole.at[at.far_part, HALF : 2 * HALF], plane_recv.at[n, 3], at.across_x)

    def send_small():
        for n, (peer, _) in enumerate(plane_peers):
            send(len_all.at[part], len_all.at[part], len_send.at[n], len_recv.at[n], peer).start()
        for k in range(1, 8):
            send(
                small_own,
                small_all.at[shard],
                small_send.at[k - 1],
                small_recv.at[k - 1],
                at.shard_after(k),
            ).start()

    def unpack_small():
        for n in (13, 14, 15):
            load(n).wait()
        for n, (peer, other) in enumerate(plane_peers):
            arrived(len_all.at[other], len_recv.at[n], peer)
        for k in range(1, 8):
            arrived(
                small_all.at[(shard + 8 - k) % 8], small_recv.at[k - 1], at.shard_after(8 - k)
            )
        for number, row in enumerate((0, 8, 16, 24, 56, 96)):
            for n in range(8):
                source = row + n
                vectors[number : number + 1, n * 128 : (n + 1) * 128] = small_all[
                    source // 13, source % 13 : source % 13 + 1
                ]
        for c in range(3):
            for n in range(2):
                source = 32 + 8 * c + 2 * part + n
                columns = slice((2 * c + n) * 128, (2 * c + n + 1) * 128)
                qkv_bias[:, columns] = small_all[source // 13, pl.ds(source % 13, 1)]
        for g in range(8):
            source = 64 + 4 * g + part
            up_bias[:, g * 128 : (g + 1) * 128] = small_all[source // 13, pl.ds(source % 13, 1)]

    sums[...] = jnp.zeros_like(sums)
    d_qkv_bias[...] = jnp.zeros_like(d_qkv_bias)
    d_up_bias[...] = jnp.zeros_like(d_up_bias)
    block_rows = 64

    def norm_rows(s):
        @pl.loop(0, length // block_rows)
        def _(i):
            r = pl.ds(pl.multiple_of(i * block_rows, block_rows), block_rows)
            values = x_all[s, r, :].astype(f32)
            mean = jnp.mean(values, axis=-1, keepdims=True)
            centred = values - mean
            inverse = lax.rsqrt(
                jnp.mean(centred * centred, axis=-1, keepdims=True) + NORM_EPSILON
            )
            stats[s, r, 0:1] = mean
            stats[s, r, 1:2] = inverse
            unit = centred * inverse
            normed_one[s, r, :] = (unit * vectors[0:1] + vectors[1:2]).astype(bf16)
            normed_two[s, r, :] = (unit * vectors[2:3] + vectors[3:4]).astype(bf16)

    def live_rows(s):
        index = lax.broadcasted_iota(jnp.int32, (length, 1), 0)
        return index.astype(f32) < len_all[s][0:1, 0:1]

    def rotate(value, sign):
        return (
            value * tables[0]
            + sign * pltpu.roll(value, head_cols - ROT // 2, 1) * tables[1]
            + sign * pltpu.roll(value, ROT // 2, 1) * tables[2]
        )

    def project(s):
        norm_rows(s)
        low, high = SPANS[Q]
        value = nn(normed_one[s], flat(w_all[:, :, low:high])) + qkv_bias[...]
        heads_qkv[s, :, 0:head_cols] = rotate(value[:, 0:head_cols], 1.0).astype(bf16)
        heads_qkv[s, :, head_cols : 2 * head_cols] = rotate(
            value[:, head_cols : 2 * head_cols], 1.0
        ).astype(bf16)
        heads_qkv[s, :, 2 * head_cols :] = value[:, 2 * head_cols :].astype(bf16)

    def attend(s):
        cot = cot_all[s]
        back[s] = jnp.where(live_rows(s), cot, jnp.zeros_like(cot))
        queries = heads_qkv[s, :, 0:head_cols]
        keys = heads_qkv[s, :, head_cols : 2 * head_cols]
        values = heads_qkv[s, :, 2 * head_cols :]
        d_mixed = nt(back[s], flat(out_all[...])).astype(bf16)
        row = lax.broadcasted_iota(jnp.int32, (length, length), 0)
        column = lax.broadcasted_iota(jnp.int32, (length, length), 1)
        allowed = (column <= row) & (column.astype(f32) < len_all[s][0:1, 0:1])
        lane = lax.broadcasted_iota(jnp.int32, (length, head_cols), 1)
        zero = jnp.zeros((), bf16)
        mixed_sum = jnp.zeros((length, head_cols), f32)
        d_queries = d_keys = d_values = mixed_sum
        for h in range(head_cols // HD):
            of_head = (lane >= h * HD) & (lane < (h + 1) * HD)
            q_h, k_h, v_h, d_h = (
                jnp.where(of_head, t, zero) for t in (queries, keys, values, d_mixed)
            )
            scores = jnp.where(allowed, nt(q_h, keys) * HD**-0.5, -1e30)
            raised = jnp.exp(scores - jnp.max(scores, axis=-1, keepdims=True))
            weights = raised * (1.0 / jnp.sum(raised, axis=-1, keepdims=True))
            low = weights.astype(bf16)
            mixed_sum = mixed_sum + nn(low, v_h)
            d_weights = nt(d_h, values)
            inner = jnp.sum(weights * d_weights, axis=-1, keepdims=True)
            d_scores = (weights * (d_weights - inner)).astype(bf16)
            d_queries = d_queries + nn(d_scores, k_h)
            d_keys = d_keys + tn(d_scores, q_h)
            d_values = d_values + tn(low, d_h)
        mixed[s] = mixed_sum.astype(bf16)
        for n, value in enumerate(
            (rotate(d_queries * HD**-0.5, -1.0), rotate(d_keys * HD**-0.5, -1.0), d_values)
        ):
            rounded = value.astype(bf16)
            columns = slice(n * head_cols, (n + 1) * head_cols)
            d_projected[s, :, columns] = rounded
            d_qkv_bias[:, columns] += jnp.sum(rounded.astype(f32), axis=0, keepdims=True)

    def gradient(left, right, n):
        low, high = SPANS[n]

        @pl.loop(0, 8)
        def _(f):
            columns = pl.ds(pl.multiple_of(f * 128, 128), 128)
            terms[f, :, low:high] = tn(flat(left[:, :, columns]), flat(right[...])).astype(bf16)

    def to_core(n):
        for other in range(4):
            send(
                piece(terms, 2 * other + 1 - core, n),
                piece(core_in, other, n),
                core_send.at[n, other],
                core_recv.at[n, other],
                at.other_core,
            ).start()

    def add_core(n):
        low, high = SPANS[n]
        for other in (3, 0, 2, 1):
            arrived(piece(core_in, other, n), core_recv.at[n, other], at.other_core)
            terms[2 * other + core, :, low:high] = (
                terms[2 * other + core, :, low:high].astype(f32)
                + core_in[other, :, low:high].astype(f32)
            ).astype(bf16)

    def pass_on(n, me, target):
        low, high = SPANS[n]

        @pl.when(z == me)
        def _():
            own = piece(terms, 2 * target + core, n)
            if me not in (0, 3):
                source = at.down if me < target else at.up
                arrived(piece(line_in, target, n), line_recv.at[n, target], source)
                terms[2 * target + core, :, low:high] = (
                    terms[2 * target + core, :, low:high].astype(f32)
                    + line_in[target, :, low:high].astype(f32)
                ).astype(bf16)
            slot = 4 if me == target + 1 else target
            send(
                own,
                piece(line_in, slot, n),
                line_send.at[n, target],
                line_recv.at[n, slot],
                at.up if me < target else at.down,
            ).start()

    def line_starts(n):
        for target in (3, 2, 1):
            pass_on(n, 0, target)
        for target in (0, 1, 2):
            pass_on(n, 3, target)

    def line_step(n, step):
        for me, target in (((1, 3), (2, 0)), ((1, 2), (2, 1)), ((2, 3), (1, 0)))[step]:
            pass_on(n, me, target)

    wholes = (qkv_all, up_all, down_all)

    def line_ends(n):
        low, high = SPANS[n]
        total = 2 * z + core

        def add(slot, source):
            arrived(piece(line_in, slot, n), line_recv.at[n, slot], source)
            terms[total, :, low:high] = (
                terms[total, :, low:high].astype(f32) + line_in[slot, :, low:high].astype(f32)
            ).astype(bf16)

        @pl.when(z > 0)
        def _():
            add(z, at.down)

        @pl.when(z < 3)
        def _():
            add(4, at.up)

        own = piece(terms, total, n)
        target = wholes[n].at[part]
        send(own, target, all_send.at[n, 0], all_recv.at[n, 0], at.across_x).start()
        send(own, target, all_send.at[n, 1], all_recv.at[n, 1], at.across_y).start()
        pltpu.make_async_copy(own, target, keep_sem.at[n]).start()

    def share(n):
        whole = wholes[n]
        arrived(whole.at[at.x_part], all_recv.at[n, 0], at.across_x)
        block = whole.at[at.x_part, 0:64]
        send(block, block, all_send.at[n, 2], all_recv.at[n, 2], at.across_y).start()
        arrived(whole.at[at.y_part], all_recv.at[n, 1], at.across_y)
        block = whole.at[at.y_part, 64:128]
        send(block, block, all_send.at[n, 3], all_recv.at[n, 3], at.across_x).start()

    def out_to_core():
        send(
            out_term.at[1 - core], out_core_in, rows_send.at[0], rows_recv.at[0], at.other_core
        ).start()

    def out_add(block):
        out_line[...] = (out_line[...].astype(f32) + block.astype(f32)).astype(bf16)

    def out_add_core():
        arrived(out_core_in, rows_recv.at[0], at.other_core)
        out_line[...] = out_term[core]
        out_add(out_core_in[...])

    def out_step(step):
        @pl.when((z == step) & (z < part))
        def _():
            if step > 0:
                arrived(out_line_in.at[0], rows_recv.at[1], at.down)
                out_add(out_line_in[0])
            send(out_line, out_line_in.at[0], rows_send.at[1], rows_recv.at[1], at.up).start()

        @pl.when((z == 3 - step) & (z > part))
        def _():
            if step > 0:
                arrived(out_line_in.at[1], rows_recv.at[2], at.up)
                out_add(out_line_in[1])
            send(out_line, out_line_in.at[1], rows_send.at[1], rows_recv.at[2], at.down).start()

    def out_ends():
        @pl.when(z == part)
        def _():
            @pl.when(z > 0)
            def _():
                arrived(out_line_in.at[0], rows_recv.at[1], at.down)
                out_add(out_line_in[0])

            @pl.when(z < 3)
            def _():
                arrived(out_line_in.at[1], rows_recv.at[2], at.up)
                out_add(out_line_in[1])

            for r, (peer, _) in enumerate(neighbours):
                send(out_line, out_grad, rows_send.at[2 + r], rows_recv.at[3], peer).start()
            pltpu.make_async_copy(out_line, out_grad, keep_sem.at[3]).start()

    def out_share():
        for r, (peer, source) in enumerate(neighbours):

            @pl.when(z == source)
            def _():
                arrived(out_grad, rows_recv.at[3], peer)
                block = out_grad.at[64 * r : 64 * r + 64]
                onward = neighbours[1 - r][0]
                send(block, block, rows_send.at[4], rows_recv.at[4 + r], onward).start()

    def out_gradient():
        for n in range(2):
            columns = slice(n * 128, (n + 1) * 128)
            out_term[n] = tn(flat(mixed[:, :, columns]), flat(back[...])).astype(bf16)

    part_refs = (out_part, dx_part)
    routes = (
        (halves[0], at.across_x, at.x_part, at.across_y, at.y_part),
        (halves[1], at.across_y, at.y_part, at.across_x, at.x_part),
    )

    def send_part(n, r, m):
        half, peer, peer_part, _, _ = routes[r]
        target = (at.far_part, peer_part)[m]
        send(
            part_refs[n].at[target, half],
            plane_one.at[n, r, m],
            part_send.at[n, r, m],
            part_recv.at[n, r, m],
            peer,
        ).start()

    def turn_part(n, r):
        half, peer, _, turn, turned = routes[r]
        arrived(plane_one.at[n, r, 0], part_recv.at[n, r, 0], peer)
        plane_turn[n, r] = (
            part_refs[n][turned, half].astype(f32) + plane_one[n, r, 0].astype(f32)
        ).astype(bf16)
        send(
            plane_turn.at[n, r],
            plane_two.at[n, r],
            part_send.at[n, r, 2],
            part_recv.at[n, r, 2],
            turn,
        ).start()

    def whole_part(n, r):
        half, peer, _, turn, _ = routes[r]
        arrived(plane_one.at[n, r, 1], part_recv.at[n, r, 1], peer)
        arrived(plane_two.at[n, r], part_recv.at[n, r, 2], turn)
        return (
            part_refs[n][part, half].astype(f32)
            + plane_one[n, r, 1].astype(f32)
            + plane_two[n, r].astype(f32)
        )

    up_low, up_high = SPANS[U]
    down_low, down_high = SPANS[N]

    def feed_in(s):
        value = nn(normed_two[s], flat(w_all[:, :, up_low:up_high])) + up_bias[...]
        hidden[s] = value
        activated[s] = (value * (0.5 * (1.0 + lax.erf(value * 2.0**-0.5)))).astype(bf16)

    def feed_out(s):
        out_part[s] = (
            nn(activated[s], flat(w_all[:, :, down_low:down_high]))
            + nn(mixed[s], flat(out_all[...]))
        ).astype(bf16)

    def feed_back(s):
        slope = gelu_slope(hidden[s])
        low = (nt(back[s], flat(w_all[:, :, down_low:down_high])) * slope).astype(bf16)
        d_hidden[s] = low
        d_up_bias[...] += jnp.sum(low.astype(f32), axis=0, keepdims=True)

    def norm_back(s):
        d_two = nt(d_hidden[s], flat(w_all[:, :, up_low:up_high]))
        d_one = nt(d_projected[s], flat(w_all[:, :, SPANS[Q][0] : SPANS[Q][1]]))
        unit = (x_all[s].astype(f32) - stats[s][:, 0:1]) * stats[s][:, 1:2]
        sums[0:1] += jnp.sum(d_one * unit, axis=0, keepdims=True)
        sums[1:2] += jnp.sum(d_one, axis=0, keepdims=True)
        sums[2:3] += jnp.sum(d_two * unit, axis=0, keepdims=True)
        sums[3:4] += jnp.sum(d_two, axis=0, keepdims=True)
        dx_part[s] = (d_one * vectors[0:1] + d_two * vectors[2:3]).astype(bf16)

    def place(row, value):
        small_part[row // 13, pl.ds(row % 13, 1)] = value

    def small_start():
        small_part[...] = jnp.zeros_like(small_part)
        back_total = jnp.sum(back[part].astype(f32), axis=0, keepdims=True)
        for n in range(8):
            columns = slice(n * 128, (n + 1) * 128)
            for number in range(4):
                place(8 * number + n, sums[number : number + 1, columns])
            place(56 + n, back_total[:, columns])
            place(96 + n, back_total[:, columns])
            place(64 + 4 * n + part, d_up_bias[:, columns])
        for c in range(3):
            for n in range(2):
                columns = slice((2 * c + n) * 128, (2 * c + n + 1) * 128)
                place(32 + 8 * c + 2 * part + n, d_qkv_bias[:, columns])
        for k in range(1, 8):
            send(
                small_part.at[(shard + k) % 8],
                small_in.at[k - 1],
                total_send.at[k - 1],
                total_recv.at[k - 1],
                at.shard_after(k),
            ).start()

    def small_turn():
        total = small_part[shard]
        for k in range(1, 8):
            arrived(small_in.at[k - 1], total_recv.at[k - 1], at.shard_after(8 - k))
            total = total + small_in[k - 1]
        small_total[...] = total
        for n, (peer, _) in enumerate(plane_peers):
            send(
                small_total, small_plane.at[part], total_send.at[7 + n], total_recv.at[7 + n], peer
            ).start()
        small_plane[part] = total

    def small_end():
        for n, (peer, other) in enumerate(plane_peers):
            arrived(small_plane.at[other], total_recv.at[7 + n], peer)
        small_sum[...] = (small_plane[0] + small_plane[1]) + (small_plane[2] + small_plane[3])

    def write_output(r):
        half = halves[r]
        values = x_all[part, half].astype(f32)
        summed = values + whole_part(0, r) + vectors[4:5] + vectors[5:6]
        output[half] = jnp.where(live_rows(part)[half], summed, 0.0).astype(bf16)
        pltpu.make_async_copy(output.at[half], output_out.at[half], store_sem.at[0, r]).start()

    def write_input_grad(r):
        half = halves[r]
        scaled = whole_part(1, r)
        inverse = stats[part, half, 1:2]
        unit = (x_all[part, half].astype(f32) - stats[part, half, 0:1]) * inverse
        result = back[part, half].astype(f32) + inverse * (
            scaled
            - jnp.mean(scaled, axis=-1, keepdims=True)
            - unit * jnp.mean(scaled * unit, axis=-1, keepdims=True)
        )
        input_grad[half] = result.astype(bf16)
        pltpu.make_async_copy(
            input_grad.at[half], input_grad_out.at[half], store_sem.at[1, r]
        ).start()

    at_end = (z == 0) | (z == 3)
    middle = (z == 1) | (z == 2)
    send_activations()
    send_own(Q)
    send_out_rows()
    send_small()

    @pl.when(at_end)
    def _():
        send_rest()

    @pl.when(middle)
    def _():
        forward(1, Q)
        forward_out(1)
        forward(2, Q)

    send_own(U)
    forward_x(0)

    @pl.when(at_end)
    def _():
        forward_out(1)

    @pl.when(middle)
    def _():
        forward_out(2)
        from_core(Q)
        send_own(N)
        send_rest()

    forward_y(0)

    @pl.when(at_end)
    def _():
        forward(1, Q)
        forward(2, Q)
        forward(3, Q)
        send_own(N)
        from_core(Q)

    unpack_small()

    @pl.loop(0, 4)
    def _(i):
        project(near_first(i))

        @pl.when((i == 0) & at_end)
        def _():
            forward_y(1)
            forward_out(2)

        @pl.when(i == 2)
        def _():
            forward_x(1)

        @pl.when((i == 2) & at_end)
        def _():
            forward_out(3)

        @pl.when((i == 2) & middle)
        def _():
            forward(1, U)
            forward_y(1)

        @pl.when(i == 2)
        def _():
            far_halves(0)

        @pl.when((i == 2) & middle)
        def _():
            forward(1, N)

    out_from_core()

    @pl.loop(0, 4)
    def _(i):
        attend(near_first(i))

        @pl.when((i == 0) & middle)
        def _():
            forward(2, U)

        @pl.when((i == 1) & middle)
        def _():
            far_halves(1)

        @pl.when((i == 2) & at_end)
        def _():
            forward(1, U)
            far_halves(1)

        @pl.when((i == 2) & middle)
        def _():
            forward(2, N)

    gradient(normed_one, d_projected, Q)

    @pl.when(at_end)
    def _():
        to_core(Q)

    @pl.when(middle)
    def _():
        from_core(U)
        from_core(N)

    out_gradient()

    @pl.when(at_end)
    def _():
        forward(2, U)
        forward(3, U)
        forward(1, N)
        add_core(Q)
        line_starts(Q)
        from_core(U)

    @pl.loop(0, 4)
    def _(i):
        feed_in(i)

        @pl.when((i == 0) & at_end)
        def _():
            forward(2, N)

        @pl.when((i == 0) & middle)
        def _():
            to_core(Q)

    @pl.when(at_end)
    def _():
        forward(3, N)

    gradient(activated, back, N)

    @pl.when(at_end)
    def _():
        out_to_core()
        from_core(N)

    @pl.loop(0, 4)
    def _(i):
        feed_out(far_first(i))

        @pl.when((i == 0) & middle)
        def _():
            add_core(Q)

        @pl.when(i == 0)
        def _():
            send_part(0, 0, 0)
            send_part(0, 1, 0)

        @pl.when((i == 1) & at_end)
        def _():
            out_add_core()
            out_step(0)
            to_core(N)

        @pl.when((i == 2) & middle)
        def _():
            send_part(0, 1, 1)

    @pl.loop(0, 4)
    def _(i):
        feed_back(far_first(i))

        @pl.when((i == 0) & middle)
        def _():
            out_to_core()
            out_add_core()
            line_step(Q, 0)
            line_step(Q, 1)
            send_part(0, 0, 1)
            to_core(N)

        @pl.when((i == 1) & at_end)
        def _():
            send_part(0, 1, 1)
            add_core(N)
            line_starts(N)
            turn_part(0, 0)

        @pl.when((i == 2) & at_end)
        def _():
            send_part(1, 0, 1)

        @pl.when((i == 2) & middle)
        def _():
            out_step(1)

        @pl.when((i == 3) & at_end)
        def _():
            send_part(0, 0, 1)

        @pl.when((i == 3) & middle)
        def _():
            line_step(Q, 2)
            send_part(1, 1, 1)

        norm_back(far_first(i))

        @pl.when((i == 0) & at_end)
        def _():
            send_part(1, 0, 0)
            send_part(1, 1, 0)

        @pl.when((i == 0) & middle)
        def _():
            add_core(N)

        @pl.when((i == 1) & middle)
        def _():
            send_part(1, 0, 0)
            send_part(1, 1, 0)
            turn_part(0, 1)

    @pl.when(middle)
    def _():
        turn_part(0, 0)
        line_ends(Q)

    gradient(normed_two, d_hidden, U)

    @pl.when(middle)
    def _():
        to_core(U)
        send_part(1, 0, 1)
        line_step(N, 0)

    turn_part(1, 1)

    @pl.when(at_end)
    def _():
        to_core(U)
        send_part(1, 1, 1)

    @pl.when(middle)
    def _():
        turn_part(1, 0)

    add_core(U)

    @pl.when(at_end)
    def _():
        line_starts(U)
        line_ends(Q)
        turn_part(1, 0)

    @pl.when(middle)
    def _():
        line_step(N, 1)
        out_step(2)

    small_start()

    @pl.when(middle)
    def _():
        write_output(1)
        line_step(N, 2)
        line_step(U, 0)
        write_output(0)
        line_ends(N)
        share(Q)

    out_ends()

    @pl.when(at_end)
    def _():
        turn_part(0, 1)
        write_output(0)
        share(Q)
        line_ends(N)

    @pl.when(middle)
    def _():
        line_step(U, 1)
        line_step(U, 2)
        share(N)
        write_input_grad(0)
        line_ends(U)
        out_share()

    small_turn()

    @pl.when(at_end)
    def _():
        out_share()
        line_ends(U)

    @pl.when(middle)
    def _():
        share(U)

    write_input_grad(1)
    small_end()

    @pl.when(at_end)
    def _():
        write_output(1)
        share(N)
        share(U)
        write_input_grad(0)

    for r, half in enumerate(halves):
        pltpu.make_async_copy(output.at[half], output_out.at[half], store_sem.at[0, r]).wait()
        pltpu.make_async_copy(
            input_grad.at[half], input_grad_out.at[half], store_sem.at[1, r]
        ).wait()
    @pl.when(z == at.far_part)
    def _():
        for r, (peer, _) in enumerate(neighbours):
            arrived(out_grad.at[64 * r : 64 * r + 64], rows_recv.at[4 + r], neighbours[1 - r][0])

    @pl.when(z != part)
    def _():
        sent(out_line, rows_send.at[1], at.up)

    @pl.when((z == at.x_part) | (z == at.y_part))
    def _():
        sent(out_line.at[0:64], rows_send.at[4], at.across_x)

    @pl.when(z == part)
    def _():
        for r, (peer, _) in enumerate(neighbours):
            sent(out_line, rows_send.at[2 + r], peer)
        pltpu.make_async_copy(out_line, out_grad, keep_sem.at[3]).wait()

    sent(out_line, rows_send.at[0], at.other_core)
    for r, (peer, _) in enumerate(neighbours):
        sent(x_own, plane_send.at[0, r], peer)
        sent(cot_own.at[halves[0]], early_send.at[r], peer)
        sent(cot_own.at[halves[1]], plane_send.at[1, r], peer)
        for n in range(2):
            sent(x_all.at[part, halves[0]], plane_send.at[n, 2 + r], peer)
    for n, (peer, _) in enumerate(plane_peers):
        sent(len_all.at[part], len_send.at[n], peer)
        sent(small_total, total_send.at[7 + n], peer)
    for k in range(1, 8):
        sent(small_own, small_send.at[k - 1], at.shard_after(k))
        sent(small_total, total_send.at[k - 1], at.shard_after(k))
    for n in range(3):
        for other in range(4):
            block = piece(w_all, 2 * other + core, n)
            sent(block, w_send.at[2, n, other], at.other_core)
            sent(block, core_send.at[n, other], at.other_core)

            @pl.when((other <= z) & (z < 3))
            def _():
                sent(block, w_send.at[0, n, other], at.up)

            @pl.when((other >= z) & (z > 0))
            def _():
                sent(block, w_send.at[1, n, other], at.down)

            @pl.when(z != other)
            def _():
                sent(block, line_send.at[n, other], at.up)

    block = out_all.at[core]
    sent(block, out_send.at[2], at.other_core)

    @pl.when((z >= part) & (z < 3))
    def _():
        sent(block, out_send.at[0], at.up)

    @pl.when((z <= part) & (z > 0))
    def _():
        sent(block, out_send.at[1], at.down)

    for n in range(2):
        for r in range(2):
            for m in range(3):
                sent(plane_turn.at[n, r], part_send.at[n, r, m], at.across_x)
    for n, whole in enumerate(wholes):
        arrived(whole.at[at.far_part, 0:64], all_recv.at[n, 2], at.across_y)
        arrived(whole.at[at.far_part, 64:128], all_recv.at[n, 3], at.across_x)
        own = piece(terms, shard, n)
        sent(own, all_send.at[n, 0], at.across_x)
        sent(own, all_send.at[n, 1], at.across_y)
        sent(whole.at[part, 0:64], all_send.at[n, 2], at.across_y)
        sent(whole.at[part, 64:128], all_send.at[n, 3], at.across_x)
        pltpu.make_async_copy(own, whole.at[part], keep_sem.at[n]).wait()


VMEM_SPEC = pl.BlockSpec(memory_space=pltpu.VMEM)
HBM_SPEC = pl.BlockSpec(memory_space=pl.ANY)


def whole_layer(lengths, x_own, cot_own, masters, tables):
    shape = jax.ShapeDtypeStruct
    vmem, dma = pltpu.VMEM, pltpu.SemaphoreType.DMA
    bf16, f32 = jnp.bfloat16, jnp.float32
    length = x_own.shape[0]
    group = 4
    head_cols, wide, rows = D // group, 2816, 128

    def by_sequence(width, kind=bf16):
        return vmem((group, length, width), kind)

    return pl.pallas_call(
        layer_kernel,
        out_shape=(
            shape(x_own.shape, bf16),
            shape(x_own.shape, bf16),
            shape((group, rows, 3 * head_cols), bf16),
            shape((group, rows, FF // group), bf16),
            shape((group, rows, D), bf16),
            shape((rows, D), bf16),
            shape((16, 128), f32),
        ),
        in_specs=[pl.BlockSpec(memory_space=pltpu.SMEM)]
        + [HBM_SPEC] * 6
        + [VMEM_SPEC, HBM_SPEC],
        out_specs=(HBM_SPEC,) * 6 + (VMEM_SPEC,),
        scratch_shapes=[
            vmem(tables.shape, f32),
            vmem(x_own.shape, bf16),
            vmem(x_own.shape, bf16),
            by_sequence(D),
            by_sequence(D),
            vmem((group, 8, 128), f32),
            vmem((8, rows, wide), bf16),
            vmem((2, rows, D), bf16),
            vmem((16, 128), f32),
            vmem((8, 16, 128), f32),
            vmem((8, D), f32),
            vmem((1, 3 * head_cols), f32),
            vmem((1, FF // group), f32),
            by_sequence(128, f32),
            by_sequence(D),
            by_sequence(D),
            by_sequence(D),
            by_sequence(3 * head_cols),
            by_sequence(head_cols),
            by_sequence(3 * head_cols),
            by_sequence(FF // group, f32),
            by_sequence(FF // group),
            by_sequence(D),
            by_sequence(D),
            vmem((8, rows, wide), bf16),
            vmem((2, rows, D), bf16),
            vmem((8, D), f32),
            vmem((1, 3 * head_cols), f32),
            vmem((1, FF // group), f32),
            vmem((8, 16, 128), f32),
            vmem((2, 2, 2, HALF, D), bf16),
            vmem((2, 2, HALF, D), bf16),
            vmem((2, 2, HALF, D), bf16),
            vmem((4, rows, wide), bf16),
            vmem((5, rows, wide), bf16),
            vmem((rows, D), bf16),
            vmem((rows, D), bf16),
            vmem((2, rows, D), bf16),
            vmem((7, 16, 128), f32),
            vmem((16, 128), f32),
            vmem((4, 16, 128), f32),
            dma((16,)),
            dma((2, 4)),
            dma((2, 4)),
            dma((2,)),
            dma((2,)),
            dma((3,)),
            dma((3,)),
            dma((3, 3, 4)),
            dma((3, 8)),
            dma((3,)),
            dma((2,)),
            dma((7,)),
            dma((7,)),
            dma((2, 2, 3)),
            dma((2, 2, 3)),
            dma((3, 4)),
            dma((3, 4)),
            dma((3, 4)),
            dma((3, 5)),
            dma((5,)),
            dma((6,)),
            dma((3, 4)),
            dma((3, 4)),
            dma((4,)),
            dma((10,)),
            dma((10,)),
            dma((2, 2)),
        ],
        compiler_params=pltpu.CompilerParams(
            collective_id=0, has_side_effects=True, vmem_limit_bytes=62 << 20
        ),
        name="layer",
    )(lengths, x_own, cot_own, *masters, tables)


def rope_tables(length, heads):
    half = ROT // 2
    angle = np.arange(length)[:, None] * ROPE_BASE ** (-2.0 * np.arange(half) / ROT)[None]
    table = np.zeros((3, length, HD), np.float32)
    table[0] = 1.0
    table[0, :, :half] = table[0, :, half:ROT] = np.cos(angle)
    table[1, :, :half] = -np.sin(angle)
    table[2, :, half:ROT] = np.sin(angle)
    return jnp.asarray(np.tile(table, (1, 1, heads)))


def local_split(
    tokens_in,
    cotangent,
    lengths,
    qkv_master,
    out_master,
    up_master,
    down_master,
    small_master,
    qkv_first,
    out_first,
    up_first,
    down_first,
    small_first,
    qkv_second,
    out_second,
    up_second,
    down_second,
    small_second,
):
    masters = (qkv_master, out_master, up_master, down_master, small_master)
    firsts = (qkv_first, out_first, up_first, down_first, small_first)
    seconds = (qkv_second, out_second, up_second, down_second, small_second)
    parts, shards = lax.axis_size("dp"), lax.axis_size("fsdp")
    part, shard = lax.axis_index("dp"), lax.axis_index("fsdp")
    length = tokens_in.shape[1]
    update = (masters, firsts, seconds)
    if (parts, shards) == (4, 8):
        tall = tuple(masters[:4]) + (small_master.reshape(-1, 128),)
        output, input_grad, qkv_grad, up_grad, down_grad, out_grad, small_sum = whole_layer(
            lengths, tokens_in[0], cotangent[0], tall, rope_tables(length, HEADS // parts)
        )
        grads = (qkv_grad, out_grad, up_grad, down_grad, small_sum[: tall[4].shape[0]])
        return lamb_split(*update, grads, (output, input_grad))

    head_cols = D // parts
    ff_rows = down_master.shape[0] // parts
    qkv_own = sliced(qkv_master, part, parts, 3).astype(jnp.bfloat16)
    up_own = sliced(up_master, part, parts, shards).astype(jnp.bfloat16)
    down_own = lax.dynamic_slice_in_dim(down_master, part * ff_rows, ff_rows).astype(jnp.bfloat16)
    out_own = out_master.astype(jnp.bfloat16)
    small_own = small_master.astype(jnp.bfloat16)

    def small_vectors(small_all):
        vectors = split_small(small_all)
        vectors[4] = sliced(vectors[4][None], part, parts, 3)[0]
        vectors[6] = sliced(vectors[6][None], part, parts, shards)[0]
        return vectors

    def over_shards(own):
        return lax.all_gather(own, "fsdp", axis=0, tiled=True)

    x_all = lax.all_gather(tokens_in, "dp", axis=0, tiled=True)
    cotangent_all = lax.all_gather(cotangent, "dp", axis=0, tiled=True)
    lengths_all = lax.all_gather(lengths, "dp", axis=0, tiled=True)
    qkv_weight, up_weight, down_weight = (over_shards(w) for w in (qkv_own, up_own, down_own))
    out_weight = lax.dynamic_slice_in_dim(over_shards(out_own), part * head_cols, head_cols)
    gain_one, shift_one, gain_two, shift_two, qkv_bias, out_bias, up_bias, down_bias = (
        small_vectors(over_shards(small_own).astype(jnp.float32))
    )
    out_part, scaled_part, terms, sums = layer(
        x_all,
        cotangent_all,
        lengths_all,
        (qkv_weight, out_weight, up_weight, down_weight),
        (gain_one, shift_one, gain_two, shift_two, qkv_bias, up_bias),
        part,
    )
    norm_sums, d_qkv_bias, d_up_bias = sums
    out_sum = lax.psum_scatter(out_part, "dp", scatter_dimension=0, tiled=True)
    scaled = lax.psum_scatter(scaled_part, "dp", scatter_dimension=0, tiled=True)
    out_sum, scaled = out_sum.astype(jnp.float32), scaled.astype(jnp.float32)

    inputs = tokens_in[0].astype(jnp.float32)
    live = (jnp.arange(length) < lengths[0]).astype(jnp.float32)[:, None]
    back = cotangent[0].astype(jnp.float32) * live
    back_total = jnp.sum(back, axis=0)

    def spread(values, pieces):
        wide = jnp.zeros((pieces, parts, values.shape[0] // pieces), jnp.float32)
        return lax.dynamic_update_index_in_dim(
            wide, values.reshape(pieces, -1), part, axis=1
        ).reshape(-1)

    small_grad = jnp.concatenate(
        [
            norm_sums.reshape(4 * D),
            spread(d_qkv_bias, 3),
            back_total,
            spread(d_up_bias, shards),
            back_total,
        ]
    )
    small_sum = lax.psum(small_grad, ("dp", "fsdp"))
    small_rows = small_master.shape[0]
    small_sum = lax.dynamic_slice_in_dim(small_sum, shard * small_rows, small_rows)
    qkv_term, out_term, up_term, down_term = terms
    out_wide = lax.dynamic_update_slice_in_dim(
        jnp.zeros((D, D), jnp.bfloat16), out_term, part * head_cols, axis=0
    )

    def to_owner(term):
        own = lax.psum_scatter(term, "fsdp", scatter_dimension=0, tiled=True)
        return lax.all_gather(own, "dp", axis=0, tiled=False).astype(jnp.float32)

    reduced = (
        joined(to_owner(qkv_term), 3),
        lax.psum(
            lax.psum_scatter(out_wide, "fsdp", scatter_dimension=0, tiled=True), "dp"
        ).astype(jnp.float32),
        joined(to_owner(up_term), shards),
        to_owner(down_term).reshape(down_master.shape),
        small_sum,
    )

    unit_rows, inverse_rows = normalize(inputs)
    output = ((inputs + out_sum + out_bias + down_bias) * live).astype(jnp.bfloat16)
    input_grad = back + inverse_rows * (
        scaled
        - jnp.mean(scaled, axis=-1, keepdims=True)
        - unit_rows * jnp.mean(scaled * unit_rows, axis=-1, keepdims=True)
    )
    return (output[None], input_grad.astype(jnp.bfloat16)[None]) + lamb(*update, reduced)


def lamb_rows(first_old, second_old, master, grad):
    first_new = BETA_ONE * first_old + (1.0 - BETA_ONE) * grad
    second_new = BETA_TWO * second_old + (1.0 - BETA_TWO) * grad * grad
    update = first_new / (jnp.sqrt(second_new) + ADAM_EPSILON) + DECAY * master
    return first_new, second_new, update


def lane_sums(values):
    squares = jnp.sum(values * values, axis=0, keepdims=True)
    total = squares[:, 0:128]
    for n in range(1, squares.shape[1] // 128):
        total = total + squares[:, n * 128 : (n + 1) * 128]
    return total


def moments_kernel(*refs):
    qkv_grad, out_grad, up_grad, down_grad, small_grad = refs[0:5]
    masters, firsts, seconds = refs[5:10], refs[10:15], refs[15:20]
    first_news, second_news, updates, kept = refs[20:25], refs[25:30], refs[30:35], refs[35:40]
    squares = refs[40]
    step = pl.program_id(0)

    @pl.when(step == 0)
    def _():
        squares[...] = jnp.zeros_like(squares)

    def one(number, span, grad):
        index = (slice(None), span)
        master = masters[number][index]
        first_new, second_new, update = lamb_rows(
            firsts[number][index], seconds[number][index], master, grad
        )
        first_news[number][index] = first_new
        second_news[number][index] = second_new
        rows = masters[number].shape[0]
        place = (pl.ds(pl.multiple_of(step * rows, rows), rows), span)
        updates[number][place] = update
        kept[number][place] = master
        return lane_sums(master), lane_sums(update)

    def add(number, pairs):
        weight, update = pairs[0]
        for more_weight, more_update in pairs[1:]:
            weight, update = weight + more_weight, update + more_update
        squares[number : number + 1] += weight
        squares[8 + number : 9 + number] += update

    f32 = jnp.float32
    parts = qkv_grad.shape[0]
    width = qkv_grad.shape[2] // 3
    add(
        0,
        [
            one(
                0,
                slice((c * parts + d) * width, (c * parts + d + 1) * width),
                qkv_grad[d, :, c * width : (c + 1) * width].astype(f32),
            )
            for c in range(3)
            for d in range(parts)
        ],
    )
    add(1, [one(1, slice(None), out_grad[...].astype(f32))])
    pieces = up_grad.shape[2] // 128
    add(
        2,
        [
            one(
                2,
                slice((g * parts + d) * 128, (g * parts + d + 1) * 128),
                up_grad[d, :, g * 128 : (g + 1) * 128].astype(f32),
            )
            for g in range(pieces)
            for d in range(parts)
        ],
    )
    add(3, [one(3, slice(None), down_grad[0].astype(f32))])

    @pl.when(step == 0)
    def _():
        first_new, second_new, update = lamb_rows(
            firsts[4][...], seconds[4][...], masters[4][...], small_grad[...]
        )
        first_news[4][...] = first_new
        second_news[4][...] = second_new
        updates[4][...] = update
        kept[4][...] = masters[4][...]
        squares[4:5] += lane_sums(masters[4][...])
        squares[12:13] += lane_sums(update)


def lamb_specs(masters, steps):
    specs = [pl.BlockSpec((m.shape[0] // steps, m.shape[1]), lambda i: (i, 0)) for m in masters[:4]]
    return specs + [pl.BlockSpec(masters[4].shape, lambda i: (0, 0))]


def moments(grads, masters, firsts, seconds, steps=8):
    qkv_grad, out_grad, up_grad, down_grad, small_grad = grads
    shape = jax.ShapeDtypeStruct
    each = lamb_specs(masters, steps)
    rows = qkv_grad.shape[1]
    halves = steps // qkv_grad.shape[0]
    grad_specs = [
        pl.BlockSpec((qkv_grad.shape[0], rows // steps, qkv_grad.shape[2]), lambda i: (0, i, 0)),
        each[1],
        pl.BlockSpec((up_grad.shape[0], rows // steps, up_grad.shape[2]), lambda i: (0, i, 0)),
        pl.BlockSpec(
            (1, rows // halves, down_grad.shape[2]), lambda i: (i // halves, i % halves, 0)
        ),
        each[4],
    ]
    out = [shape(m.shape, jnp.float32) for m in masters]
    near = [pltpu.VMEM(m.shape, jnp.float32) for m in masters]
    results = pl.pallas_call(
        moments_kernel,
        grid=(steps,),
        in_specs=grad_specs + each * 3,
        out_specs=each * 2 + [VMEM_SPEC] * 10 + [pl.BlockSpec((16, 128), lambda i: (0, 0))],
        out_shape=out * 2 + near * 2 + [shape((16, 128), jnp.float32)],
        compiler_params=pltpu.CompilerParams(vmem_limit_bytes=44 << 20),
        name="moments",
    )(*grads, *masters, *firsts, *seconds)
    return results[0:5], results[5:10], results[10:15], results[15:20], results[20]


def norms_kernel(squares, total, everyone, send_sem, recv_sem):
    shard, part = lax.axis_index("fsdp"), lax.axis_index("dp")
    peers = [(part, (shard + k) % 8) for k in range(1, 8)]
    barrier = pltpu.get_barrier_semaphore()
    for peer in peers:
        pl.semaphore_signal(barrier, inc=1, device_id=peer, device_id_type=MESH_ID)
    pl.semaphore_wait(barrier, 7)
    for k in range(1, 8):
        send(
            squares, everyone.at[shard], send_sem.at[k - 1], recv_sem.at[k - 1], peers[k - 1]
        ).start()
    everyone[shard] = squares[...]
    for k in range(1, 8):
        arrived(everyone.at[(shard + 8 - k) % 8], recv_sem.at[k - 1], peers[7 - k])
    summed = everyone[0]
    for k in range(1, 8):
        summed = summed + everyone[k]
    norms = jnp.sqrt(jnp.sum(summed, axis=1, keepdims=True))
    total[...] = jnp.broadcast_to(norms, (16, 128))
    for k in range(1, 8):
        sent(squares, send_sem.at[k - 1], peers[k - 1])


def norms(squares):
    dma = pltpu.SemaphoreType.DMA
    return pl.pallas_call(
        norms_kernel,
        out_shape=jax.ShapeDtypeStruct((16, 128), jnp.float32),
        in_specs=[VMEM_SPEC],
        out_specs=VMEM_SPEC,
        scratch_shapes=[pltpu.VMEM((8, 16, 128), jnp.float32), dma((7,)), dma((7,))],
        compiler_params=pltpu.CompilerParams(
            collective_id=1, has_side_effects=True, vmem_limit_bytes=2 << 20
        ),
        name="norms",
    )(squares)


def step_kernel(*refs):
    total, masters, updates, layer_outs = refs[0], refs[1:6], refs[6:11], refs[11:13]
    news, outs, lamb_norms = refs[13:18], refs[18:20], refs[20]
    step = pl.program_id(0)
    for number in range(5):
        weight_norm = total[number : number + 1, 0:1]
        update_norm = total[8 + number : 9 + number, 0:1]
        scale = RATE * (weight_norm / update_norm)
        rows = news[number].shape[0]
        place = slice(None)
        if rows < masters[number].shape[0]:
            place = pl.ds(pl.multiple_of(step * rows, rows), rows)
        news[number][...] = masters[number][place] - scale * updates[number][place]
    for source, target in zip(layer_outs, outs):
        target[...] = source[...]

    @pl.when(step == 0)
    def _():
        row = lax.broadcasted_iota(jnp.int32, (8, 128), 0)
        lane = lax.broadcasted_iota(jnp.int32, (8, 128), 1)
        for n in range(2):
            half = jnp.where(row == lane, total[8 * n : 8 * n + 8], 0.0)
            lamb_norms[n : n + 1] = jnp.sum(half, axis=0, keepdims=True)[:, 0:5]


def step_masters(total, masters, updates, layer_outs, steps=4):
    shape = jax.ShapeDtypeStruct
    out_specs = [
        pl.BlockSpec((o.shape[0] // steps, o.shape[1]), lambda i: (i, 0)) for o in layer_outs
    ]
    results = pl.pallas_call(
        step_kernel,
        grid=(steps,),
        in_specs=[pl.BlockSpec((16, 128), lambda i: (0, 0))] + [VMEM_SPEC] * 10 + out_specs,
        out_specs=lamb_specs(masters, steps)
        + out_specs
        + [pl.BlockSpec((2, 5), lambda i: (0, 0))],
        out_shape=[shape(m.shape, jnp.float32) for m in masters]
        + [shape(o.shape, o.dtype) for o in layer_outs]
        + [shape((2, 5), jnp.float32)],
        compiler_params=pltpu.CompilerParams(vmem_limit_bytes=40 << 20),
        name="step_masters",
    )(total, *masters, *updates, *layer_outs)
    return results[0:5], results[5:7], results[7]


def lamb_split(masters, firsts, seconds, grads, layer_outs):
    def tall(arrays):
        return tuple(arrays[:4]) + (arrays[4].reshape(-1, 128),)

    def flat_small(arrays):
        return tuple(arrays[:4]) + (arrays[4].reshape(-1),)

    masters, firsts, seconds = tall(masters), tall(firsts), tall(seconds)
    first_news, second_news, updates, kept, squares = moments(grads, masters, firsts, seconds)
    news, outs, lamb_norms = step_masters(norms(squares), kept, updates, layer_outs)
    return (
        tuple(out[None] for out in outs)
        + flat_small(news)
        + flat_small(first_news)
        + flat_small(second_news)
        + (lamb_norms,)
    )


def lamb(masters, firsts, seconds, reduced):
    updates = []
    first_news = []
    second_news = []
    for first_old, second_old, master, grad_sum in zip(firsts, seconds, masters, reduced):
        first_new = BETA_ONE * first_old + (1.0 - BETA_ONE) * grad_sum
        second_new = BETA_TWO * second_old + (1.0 - BETA_TWO) * grad_sum * grad_sum
        updates.append(first_new / (jnp.sqrt(second_new) + ADAM_EPSILON) + DECAY * master)
        first_news.append(first_new)
        second_news.append(second_new)
    weight_squares, update_squares = lax.psum(
        (local_squares(masters), local_squares(updates)), "fsdp"
    )
    weight_norms = jnp.sqrt(weight_squares)
    update_norms = jnp.sqrt(update_squares)
    new_masters = [
        masters[number] - RATE * (weight_norms[number] / update_norms[number]) * updates[number]
        for number in range(5)
    ]
    lamb_norms = jnp.stack([weight_norms, update_norms])
    return tuple(new_masters) + tuple(first_news) + tuple(second_news) + (lamb_norms,)


def solution(mesh):
    in_specs = (
        P(("dp", "fsdp"), None, None),
        P(("dp", "fsdp"), None, None),
        P(("dp", "fsdp")),
        P("fsdp", None),
        P("fsdp", None),
        P("fsdp", None),
        P("fsdp", None),
        P("fsdp"),
        P("fsdp", None),
        P("fsdp", None),
        P("fsdp", None),
        P("fsdp", None),
        P("fsdp"),
        P("fsdp", None),
        P("fsdp", None),
        P("fsdp", None),
        P("fsdp", None),
        P("fsdp"),
    )
    out_specs = (
        P(("dp", "fsdp"), None, None),
        P(("dp", "fsdp"), None, None),
        P("fsdp", None),
        P("fsdp", None),
        P("fsdp", None),
        P("fsdp", None),
        P("fsdp"),
        P("fsdp", None),
        P("fsdp", None),
        P("fsdp", None),
        P("fsdp", None),
        P("fsdp"),
        P("fsdp", None),
        P("fsdp", None),
        P("fsdp", None),
        P("fsdp", None),
        P("fsdp"),
        P(),
    )
    return jax.shard_map(local_split, mesh=mesh, in_specs=in_specs, out_specs=out_specs, check_vma=False)
```

```python
import math

import jax
import jax.numpy as jnp
import numpy as np
from jax import lax
from jax.experimental import pallas as pl
from jax.experimental.pallas import tpu as pltpu
from jax.sharding import PartitionSpec as P

D = 1024
HEADS = 16
HD = 64
FF = 4096
ROT = 16
SMALL = 13312


NORM_EPSILON = 1e-05
ADAM_EPSILON = 1e-06
ROPE_BASE = 10000.0
RATE = 0.5
DECAY = 0.01
BETA_ONE = 0.5
BETA_TWO = 0.5


def split_small(small_vector):
    bounds = [0, D, 2 * D, 3 * D, 4 * D, 7 * D, 8 * D, 8 * D + FF, 9 * D + FF]
    return [small_vector[bounds[number] : bounds[number + 1]] for number in range(8)]


def normalize(values):
    average = jnp.mean(values, axis=-1, keepdims=True)
    centred = values - average
    variance = jnp.mean(centred * centred, axis=-1, keepdims=True)
    inverse = lax.rsqrt(variance + NORM_EPSILON)
    return (centred * inverse, inverse)


def rotary_tables(length):
    half_dims = ROT // 2
    position = jnp.arange(length, dtype=jnp.float32)[:, None]
    number = jnp.arange(half_dims, dtype=jnp.float32)[None, :]
    angle = position * jnp.exp(number * (-2.0 * math.log(ROPE_BASE) / ROT))
    return (jnp.cos(angle)[:, None, :], jnp.sin(angle)[:, None, :])


def rotate(heads_in, cosine_table, sine_table):
    half_dims = ROT // 2
    first_half = heads_in[..., :half_dims]
    second_half = heads_in[..., half_dims:ROT]
    return jnp.concatenate(
        [
            first_half * cosine_table - second_half * sine_table,
            second_half * cosine_table + first_half * sine_table,
            heads_in[..., ROT:],
        ],
        axis=-1,
    )


def rotate_back(grads_in, cosine_table, sine_table):
    half_dims = ROT // 2
    first_half = grads_in[..., :half_dims]
    second_half = grads_in[..., half_dims:ROT]
    return jnp.concatenate(
        [
            first_half * cosine_table + second_half * sine_table,
            second_half * cosine_table - first_half * sine_table,
            grads_in[..., ROT:],
        ],
        axis=-1,
    )


def gelu_slope(values):
    return 0.5 * (1.0 + lax.erf(values * 2.0 ** (-0.5))) + values * jnp.exp(
        -0.5 * values * values
    ) * (2.0 * math.pi) ** (-0.5)


def against(left, right):
    return lax.dot_general(
        left, right, (((1,), (1,)), ((), ())), preferred_element_type=jnp.float32
    )


def outer_sum(columns, right):
    return lax.dot_general(
        columns, right, (((0,), (0,)), ((), ())), preferred_element_type=jnp.float32
    )


def local_squares(arrays):
    return jnp.stack([jnp.sum(array_in * array_in) for array_in in arrays])


def sliced(master, part, parts, pieces):
    rows, columns = master.shape
    width = columns // (pieces * parts)
    return lax.dynamic_index_in_dim(
        master.reshape(rows, pieces, parts, width), part, axis=2, keepdims=False
    ).reshape(rows, pieces * width)


def joined(slices, pieces):
    parts, rows, columns = slices.shape
    width = columns // pieces
    return (
        slices.reshape(parts, rows, pieces, width)
        .transpose(1, 2, 0, 3)
        .reshape(rows, pieces * parts * width)
    )


def layer(x_all, cotangent_all, lengths_all, weights, small_all, part):
    qkv_weight, out_weight, up_weight, down_weight = weights
    group, length, _ = x_all.shape
    tokens = group * length
    head_cols = out_weight.shape[0]
    heads = head_cols // HD
    gain_one, shift_one, gain_two, shift_two, qkv_bias, up_bias = small_all
    inputs = x_all.reshape(tokens, D).astype(jnp.float32)
    position = jnp.arange(length)
    live = (position[None, :] < lengths_all[:, None]).astype(jnp.float32).reshape(tokens, 1)
    allowed = (position[None, None, :] <= position[None, :, None]) & (
        position[None, None, :] < lengths_all[:, None, None]
    )
    unit_rows, _ = normalize(inputs)
    normed_one = (unit_rows * gain_one + shift_one).astype(jnp.bfloat16)
    normed_two = (unit_rows * gain_two + shift_two).astype(jnp.bfloat16)
    projected = jnp.dot(normed_one, qkv_weight, preferred_element_type=jnp.float32) + qkv_bias
    projected = projected.reshape(group, length, 3, heads, HD)
    cosine_table, sine_table = rotary_tables(length)
    query_heads = rotate(projected[:, :, 0], cosine_table, sine_table).astype(jnp.bfloat16)
    key_heads = rotate(projected[:, :, 1], cosine_table, sine_table).astype(jnp.bfloat16)
    value_heads = projected[:, :, 2].astype(jnp.bfloat16)
    scores = jnp.einsum(
        "gqhd,gkhd->ghqk", query_heads, key_heads, preferred_element_type=jnp.float32
    ) * HD ** (-0.5)
    scores = jnp.where(allowed[:, None], scores, -1e30)
    row_top = jnp.max(scores, axis=-1, keepdims=True)
    raised = jnp.exp(scores - row_top)
    attend = raised / jnp.sum(raised, axis=-1, keepdims=True)
    attend_low = attend.astype(jnp.bfloat16)
    mixed = jnp.einsum(
        "ghqk,gkhd->gqhd", attend_low, value_heads, preferred_element_type=jnp.float32
    )
    mixed = mixed.reshape(tokens, head_cols).astype(jnp.bfloat16)
    hidden = jnp.dot(normed_two, up_weight, preferred_element_type=jnp.float32) + up_bias
    activated = jax.nn.gelu(hidden, approximate=False).astype(jnp.bfloat16)
    out_part = jnp.dot(mixed, out_weight, preferred_element_type=jnp.float32) + jnp.dot(
        activated, down_weight, preferred_element_type=jnp.float32
    )

    back = (cotangent_all.reshape(tokens, D).astype(jnp.float32) * live).astype(jnp.bfloat16)
    d_hidden = (against(back, down_weight) * gelu_slope(hidden)).astype(jnp.bfloat16)
    d_mixed = against(back, out_weight).astype(jnp.bfloat16).reshape(group, length, heads, HD)
    d_attend = jnp.einsum(
        "gqhd,gkhd->ghqk", d_mixed, value_heads, preferred_element_type=jnp.float32
    )
    row_inner = jnp.sum(attend * d_attend, axis=-1, keepdims=True)
    d_scores = (attend * (d_attend - row_inner)).astype(jnp.bfloat16)
    d_queries = jnp.einsum(
        "ghqk,gkhd->gqhd", d_scores, key_heads, preferred_element_type=jnp.float32
    ) * HD ** (-0.5)
    d_keys = jnp.einsum(
        "ghqk,gqhd->gkhd", d_scores, query_heads, preferred_element_type=jnp.float32
    ) * HD ** (-0.5)
    d_values = jnp.einsum(
        "ghqk,gqhd->gkhd", attend_low, d_mixed, preferred_element_type=jnp.float32
    )
    d_projected = jnp.stack(
        [
            rotate_back(d_queries, cosine_table, sine_table),
            rotate_back(d_keys, cosine_table, sine_table),
            d_values,
        ],
        axis=2,
    )
    d_projected = d_projected.reshape(tokens, 3 * head_cols).astype(jnp.bfloat16)
    d_normed_one = against(d_projected, qkv_weight)
    d_normed_two = against(d_hidden, up_weight)
    scaled_part = d_normed_one * gain_one + d_normed_two * gain_two
    norm_sums = jnp.stack(
        [
            jnp.sum(d_normed_one * unit_rows, axis=0),
            jnp.sum(d_normed_one, axis=0),
            jnp.sum(d_normed_two * unit_rows, axis=0),
            jnp.sum(d_normed_two, axis=0),
        ]
    )
    d_qkv_bias = jnp.sum(d_projected, axis=0, dtype=jnp.float32)
    d_up_bias = jnp.sum(d_hidden, axis=0, dtype=jnp.float32)
    terms = (
        outer_sum(normed_one, d_projected),
        outer_sum(mixed, back),
        outer_sum(normed_two, d_hidden),
        outer_sum(activated, back),
    )
    return (
        out_part.astype(jnp.bfloat16),
        scaled_part.astype(jnp.bfloat16),
        tuple(term.astype(jnp.bfloat16) for term in terms),
        (norm_sums, d_qkv_bias, d_up_bias),
    )


MESH_ID = pl.DeviceIdType.MESH
HALF = 128


class Place:
    def __init__(self):
        self.part = lax.axis_index("dp")
        self.shard = lax.axis_index("fsdp")
        self.z = self.shard // 2
        self.core = self.shard % 2
        self.x_part = 2 * (self.part // 2) + 1 - self.part % 2
        self.y_part = (self.part + 2) % 4
        self.far_part = 3 - self.part
        self.across_x = (self.x_part, self.shard)
        self.across_y = (self.y_part, self.shard)
        self.across_far = (self.far_part, self.shard)
        self.other_core = (self.part, 2 * self.z + 1 - self.core)
        self.up = (self.part, jnp.minimum(self.shard + 2, 7))
        self.down = (self.part, jnp.maximum(self.shard - 2, 0))

    def shard_after(self, k):
        return (self.part, (self.shard + k) % 8)


def send(source, target, send_sem, recv_sem, device):
    return pltpu.make_async_remote_copy(
        src_ref=source,
        dst_ref=target,
        send_sem=send_sem,
        recv_sem=recv_sem,
        device_id=device,
        device_id_type=MESH_ID,
    )


def arrived(target, recv_sem, device):
    send(target, target, recv_sem, recv_sem, device).wait_recv()


def sent(source, send_sem, device):
    send(source, source, send_sem, send_sem, device).wait_send()


def greet(at):
    barrier = pltpu.get_barrier_semaphore()
    peers = [at.across_x, at.across_y, at.across_far] + [at.shard_after(k) for k in range(1, 8)]
    for peer in peers:
        pl.semaphore_signal(barrier, inc=1, device_id=peer, device_id_type=MESH_ID)
    pl.semaphore_wait(barrier, len(peers))


SPANS = ((0, 768), (768, 1792), (1792, 2816))
Q, U, N = 0, 1, 2


def nt(left, right):
    return lax.dot_general(
        left, right, (((1,), (1,)), ((), ())), preferred_element_type=jnp.float32
    )


def tn(left, right):
    return lax.dot_general(
        left, right, (((0,), (0,)), ((), ())), preferred_element_type=jnp.float32
    )


def nn(left, right):
    return jnp.dot(left, right, preferred_element_type=jnp.float32)


def flat(value):
    return value.reshape(value.shape[0] * value.shape[1], value.shape[2])


def layer_kernel(
    length_own,
    x_own,
    cot_own,
    qkv_master,
    out_master,
    up_master,
    down_master,
    small_master,
    tables_in,
    output_out,
    input_grad_out,
    qkv_all,
    up_all,
    down_all,
    out_grad,
    small_sum,
    tables,
    output,
    input_grad,
    x_all,
    cot_all,
    len_all,
    w_all,
    out_all,
    small_own,
    small_all,
    vectors,
    qkv_bias,
    up_bias,
    stats,
    normed_one,
    normed_two,
    back,
    heads_qkv,
    mixed,
    d_projected,
    hidden,
    d_hidden,
    out_part,
    dx_part,
    terms,
    out_term,
    sums,
    d_qkv_bias,
    d_up_bias,
    small_part,
    plane_one,
    plane_two,
    plane_turn,
    core_in,
    line_in,
    out_core_in,
    out_line,
    out_line_in,
    small_in,
    small_total,
    small_plane,
    load_sem,
    plane_send,
    plane_recv,
    early_send,
    early_recv,
    len_send,
    len_recv,
    w_send,
    w_recv,
    out_send,
    out_recv,
    small_send,
    small_recv,
    part_send,
    part_recv,
    core_send,
    core_recv,
    line_send,
    line_recv,
    rows_send,
    rows_recv,
    all_send,
    all_recv,
    keep_sem,
    total_send,
    total_recv,
    store_sem,
):
    f32, bf16 = jnp.float32, jnp.bfloat16
    at = Place()
    z, core, part, shard = at.z, at.core, at.part, at.shard
    length = x_own.shape[0]
    head_cols = mixed.shape[2]
    activated = normed_one
    place_x, place_y = part % 2, part // 2

    def near_first(i):
        return 2 * ((place_y + i // 2) % 2) + (place_x + i % 2) % 2

    def far_first(i):
        return 2 * ((place_y + 1 - i % 2) % 2) + (place_x + 1 - i // 2) % 2

    def piece(ref, slot, n):
        return ref.at[slot, :, SPANS[n][0] : SPANS[n][1]]

    plane_peers = (
        (at.across_x, at.x_part),
        (at.across_y, at.y_part),
        (at.across_far, at.far_part),
    )

    stage = [hidden.at[n, 0:128] for n in range(4)]
    loads = []
    for c in range(3):
        columns = pl.ds(pl.multiple_of(c * D + part * head_cols, 128), head_cols)
        target = stage[0].at[:, c * head_cols : (c + 1) * head_cols]
        loads.append((qkv_master.at[:, columns], target))
    loads.append((out_master, stage[1]))
    for g in range(8):
        columns = pl.ds(pl.multiple_of(g * (FF // 8) + part * 128, 128), 128)
        loads.append((up_master.at[:, columns], stage[2].at[:, g * 128 : (g + 1) * 128]))
    rows = pl.ds(pl.multiple_of(part * 128, 128), 128)
    loads.append((down_master.at[rows], stage[3]))
    loads.append((x_own, x_all.at[part]))
    loads.append((cot_own, cot_all.at[part]))
    loads.append((tables_in, tables))

    def load(n):
        return pltpu.make_async_copy(loads[n][0], loads[n][1], load_sem.at[n])

    for n in range(len(loads)):
        load(n).start()
    len_all[part] = jnp.full((8, 128), length_own[0], jnp.int32).astype(f32)
    small_own[...] = jnp.zeros_like(small_own)
    small_own[0:13] = small_master[...].astype(bf16).astype(f32)
    small_all[shard] = small_own[...]
    greet(at)

    halves = (slice(0, HALF), slice(HALF, 2 * HALF))
    activations = ((x_own, x_all), (cot_own, cot_all))
    neighbours = ((at.across_x, at.x_part), (at.across_y, at.y_part))

    def send_activations():
        for r, (peer, _) in enumerate(neighbours):
            send(
                x_own, x_all.at[part], plane_send.at[0, r], plane_recv.at[0, r], peer
            ).start()
        for r, (peer, _) in enumerate(neighbours):
            send(
                cot_own.at[halves[0]],
                cot_all.at[part, halves[0]],
                early_send.at[r],
                early_recv.at[r],
                peer,
            ).start()

    def send_rest():
        for r, (peer, _) in enumerate(neighbours):
            send(
                cot_own.at[halves[1]],
                cot_all.at[part, halves[1]],
                plane_send.at[1, r],
                plane_recv.at[1, r],
                peer,
            ).start()

    def cast(n, first, last):
        for m in range(first, last):
            load(m).wait()
        low, high = SPANS[n]
        w_all[shard, :, low:high] = stage[(0, 2, 3)[n]][:, 0 : high - low].astype(bf16)

    def send_own(n):
        cast(n, *((0, 3), (4, 12), (12, 13))[n])
        block = piece(w_all, shard, n)

        @pl.when(z < 3)
        def _():
            send(block, block, w_send.at[0, n, z], w_recv.at[n, shard], at.up).start()

        @pl.when(z > 0)
        def _():
            send(block, block, w_send.at[1, n, z], w_recv.at[n, shard], at.down).start()

        send(block, block, w_send.at[2, n, z], w_recv.at[n, shard], at.other_core).start()

    def forward(k, n):
        @pl.when(z >= k)
        def _():
            source = 2 * (z - k) + core
            block = piece(w_all, source, n)
            arrived(block, w_recv.at[n, source], at.down)

            @pl.when(z < 3)
            def _():
                send(block, block, w_send.at[0, n, z - k], w_recv.at[n, source], at.up).start()

            send(
                block, block, w_send.at[2, n, z - k], w_recv.at[n, source], at.other_core
            ).start()

        @pl.when(z + k <= 3)
        def _():
            source = 2 * (z + k) + core
            block = piece(w_all, source, n)
            arrived(block, w_recv.at[n, source], at.up)

            @pl.when(z > 0)
            def _():
                send(block, block, w_send.at[1, n, z + k], w_recv.at[n, source], at.down).start()

            send(
                block, block, w_send.at[2, n, z + k], w_recv.at[n, source], at.other_core
            ).start()

    def from_core(n):
        for other in range(4):
            source = 2 * other + 1 - core
            arrived(piece(w_all, source, n), w_recv.at[n, source], at.other_core)

    def send_out_rows():
        load(3).wait()

        @pl.when(z == part)
        def _():
            out_all[core] = stage[1][...].astype(bf16)
            block = out_all.at[core]

            @pl.when(z < 3)
            def _():
                send(block, block, out_send.at[0], out_recv.at[core], at.up).start()

            @pl.when(z > 0)
            def _():
                send(block, block, out_send.at[1], out_recv.at[core], at.down).start()

            send(block, block, out_send.at[2], out_recv.at[core], at.other_core).start()

    def out_from_core():
        arrived(out_all.at[1 - core], out_recv.at[1 - core], at.other_core)

    def forward_out(k):
        @pl.when((z - k == part) | (z + k == part))
        def _():
            block = out_all.at[core]
            arrived(block, out_recv.at[core], at.up)

            @pl.when((z > part) & (z < 3))
            def _():
                send(block, block, out_send.at[0], out_recv.at[core], at.up).start()

            @pl.when((z < part) & (z > 0))
            def _():
                send(block, block, out_send.at[1], out_recv.at[core], at.down).start()

            send(block, block, out_send.at[2], out_recv.at[core], at.other_core).start()

    def forward_neighbour(n, r):
        peer, source = neighbours[r]
        whole = activations[n][1]
        if n == 0:
            arrived(whole.at[source], plane_recv.at[0, r], peer)
        else:
            arrived(whole.at[source, halves[0]], early_recv.at[r], peer)
            arrived(whole.at[source, halves[1]], plane_recv.at[1, r], peer)
        block = whole.at[source, halves[r]]
        onward = neighbours[1 - r][0]
        send(block, block, plane_send.at[n, 2 + r], plane_recv.at[n, 2 + r], onward).start()

    def forward_x(n):
        forward_neighbour(n, 0)

    def forward_y(n):
        forward_neighbour(n, 1)

    def far_halves(n):
        whole = activations[n][1]
        arrived(whole.at[at.far_part, 0:HALF], plane_recv.at[n, 2], at.across_y)
        arrived(whole.at[at.far_part, HALF : 2 * HALF], plane_recv.at[n, 3], at.across_x)

    def send_small():
        for n, (peer, _) in enumerate(plane_peers):
            send(len_all.at[part], len_all.at[part], len_send.at[n], len_recv.at[n], peer).start()
        for k in range(1, 8):
            send(
                small_own,
                small_all.at[shard],
                small_send.at[k - 1],
                small_recv.at[k - 1],
                at.shard_after(k),
            ).start()

    def unpack_small():
        for n in (13, 14, 15):
            load(n).wait()
        for n, (peer, other) in enumerate(plane_peers):
            arrived(len_all.at[other], len_recv.at[n], peer)
        for k in range(1, 8):
            arrived(
                small_all.at[(shard + 8 - k) % 8], small_recv.at[k - 1], at.shard_after(8 - k)
            )
        for number, row in enumerate((0, 8, 16, 24, 56, 96)):
            for n in range(8):
                source = row + n
                vectors[number : number + 1, n * 128 : (n + 1) * 128] = small_all[
                    source // 13, source % 13 : source % 13 + 1
                ]
        for c in range(3):
            for n in range(2):
                source = 32 + 8 * c + 2 * part + n
                columns = slice((2 * c + n) * 128, (2 * c + n + 1) * 128)
                qkv_bias[:, columns] = small_all[source // 13, pl.ds(source % 13, 1)]
        for g in range(8):
            source = 64 + 4 * g + part
            up_bias[:, g * 128 : (g + 1) * 128] = small_all[source // 13, pl.ds(source % 13, 1)]

    sums[...] = jnp.zeros_like(sums)
    d_qkv_bias[...] = jnp.zeros_like(d_qkv_bias)
    d_up_bias[...] = jnp.zeros_like(d_up_bias)
    block_rows = 64

    def norm_rows(s):
        @pl.loop(0, length // block_rows)
        def _(i):
            r = pl.ds(pl.multiple_of(i * block_rows, block_rows), block_rows)
            values = x_all[s, r, :].astype(f32)
            mean = jnp.mean(values, axis=-1, keepdims=True)
            centred = values - mean
            inverse = lax.rsqrt(
                jnp.mean(centred * centred, axis=-1, keepdims=True) + NORM_EPSILON
            )
            stats[s, r, 0:1] = mean
            stats[s, r, 1:2] = inverse
            unit = centred * inverse
            normed_one[s, r, :] = (unit * vectors[0:1] + vectors[1:2]).astype(bf16)
            normed_two[s, r, :] = (unit * vectors[2:3] + vectors[3:4]).astype(bf16)

    def live_rows(s):
        index = lax.broadcasted_iota(jnp.int32, (length, 1), 0)
        return index.astype(f32) < len_all[s][0:1, 0:1]

    def rotate(value, sign):
        return (
            value * tables[0]
            + sign * pltpu.roll(value, head_cols - ROT // 2, 1) * tables[1]
            + sign * pltpu.roll(value, ROT // 2, 1) * tables[2]
        )

    def project(s):
        norm_rows(s)
        low, high = SPANS[Q]
        value = nn(normed_one[s], flat(w_all[:, :, low:high])) + qkv_bias[...]
        heads_qkv[s, :, 0:head_cols] = rotate(value[:, 0:head_cols], 1.0).astype(bf16)
        heads_qkv[s, :, head_cols : 2 * head_cols] = rotate(
            value[:, head_cols : 2 * head_cols], 1.0
        ).astype(bf16)
        heads_qkv[s, :, 2 * head_cols :] = value[:, 2 * head_cols :].astype(bf16)

    def attend(s):
        cot = cot_all[s]
        back[s] = jnp.where(live_rows(s), cot, jnp.zeros_like(cot))
        queries = heads_qkv[s, :, 0:head_cols]
        keys = heads_qkv[s, :, head_cols : 2 * head_cols]
        values = heads_qkv[s, :, 2 * head_cols :]
        d_mixed = nt(back[s], flat(out_all[...])).astype(bf16)
        row = lax.broadcasted_iota(jnp.int32, (length, length), 0)
        column = lax.broadcasted_iota(jnp.int32, (length, length), 1)
        allowed = (column <= row) & (column.astype(f32) < len_all[s][0:1, 0:1])
        lane = lax.broadcasted_iota(jnp.int32, (length, head_cols), 1)
        zero = jnp.zeros((), bf16)
        mixed_sum = jnp.zeros((length, head_cols), f32)
        d_queries = d_keys = d_values = mixed_sum
        for h in range(head_cols // HD):
            of_head = (lane >= h * HD) & (lane < (h + 1) * HD)
            q_h, k_h, v_h, d_h = (
                jnp.where(of_head, t, zero) for t in (queries, keys, values, d_mixed)
            )
            scores = jnp.where(allowed, nt(q_h, keys) * HD**-0.5, -1e30)
            raised = jnp.exp(scores - jnp.max(scores, axis=-1, keepdims=True))
            weights = raised * (1.0 / jnp.sum(raised, axis=-1, keepdims=True))
            low = weights.astype(bf16)
            mixed_sum = mixed_sum + nn(low, v_h)
            d_weights = nt(d_h, values)
            inner = jnp.sum(weights * d_weights, axis=-1, keepdims=True)
            d_scores = (weights * (d_weights - inner)).astype(bf16)
            d_queries = d_queries + nn(d_scores, k_h)
            d_keys = d_keys + tn(d_scores, q_h)
            d_values = d_values + tn(low, d_h)
        mixed[s] = mixed_sum.astype(bf16)
        for n, value in enumerate(
            (rotate(d_queries * HD**-0.5, -1.0), rotate(d_keys * HD**-0.5, -1.0), d_values)
        ):
            rounded = value.astype(bf16)
            columns = slice(n * head_cols, (n + 1) * head_cols)
            d_projected[s, :, columns] = rounded
            d_qkv_bias[:, columns] += jnp.sum(rounded.astype(f32), axis=0, keepdims=True)

    def gradient(left, right, n):
        low, high = SPANS[n]

        @pl.loop(0, 8)
        def _(f):
            columns = pl.ds(pl.multiple_of(f * 128, 128), 128)
            terms[f, :, low:high] = tn(flat(left[:, :, columns]), flat(right[...])).astype(bf16)

    def to_core(n):
        for other in range(4):
            send(
                piece(terms, 2 * other + 1 - core, n),
                piece(core_in, other, n),
                core_send.at[n, other],
                core_recv.at[n, other],
                at.other_core,
            ).start()

    def add_core(n):
        low, high = SPANS[n]
        for other in (3, 0, 2, 1):
            arrived(piece(core_in, other, n), core_recv.at[n, other], at.other_core)
            terms[2 * other + core, :, low:high] = (
                terms[2 * other + core, :, low:high].astype(f32)
                + core_in[other, :, low:high].astype(f32)
            ).astype(bf16)

    def pass_on(n, me, target):
        low, high = SPANS[n]

        @pl.when(z == me)
        def _():
            own = piece(terms, 2 * target + core, n)
            if me not in (0, 3):
                source = at.down if me < target else at.up
                arrived(piece(line_in, target, n), line_recv.at[n, target], source)
                terms[2 * target + core, :, low:high] = (
                    terms[2 * target + core, :, low:high].astype(f32)
                    + line_in[target, :, low:high].astype(f32)
                ).astype(bf16)
            slot = 4 if me == target + 1 else target
            send(
                own,
                piece(line_in, slot, n),
                line_send.at[n, target],
                line_recv.at[n, slot],
                at.up if me < target else at.down,
            ).start()

    def line_starts(n):
        for target in (3, 2, 1):
            pass_on(n, 0, target)
        for target in (0, 1, 2):
            pass_on(n, 3, target)

    def line_step(n, step):
        for me, target in (((1, 3), (2, 0)), ((1, 2), (2, 1)), ((2, 3), (1, 0)))[step]:
            pass_on(n, me, target)

    wholes = (qkv_all, up_all, down_all)

    def line_ends(n):
        low, high = SPANS[n]
        total = 2 * z + core

        def add(slot, source):
            arrived(piece(line_in, slot, n), line_recv.at[n, slot], source)
            terms[total, :, low:high] = (
                terms[total, :, low:high].astype(f32) + line_in[slot, :, low:high].astype(f32)
            ).astype(bf16)

        @pl.when(z > 0)
        def _():
            add(z, at.down)

        @pl.when(z < 3)
        def _():
            add(4, at.up)

        own = piece(terms, total, n)
        target = wholes[n].at[part]
        send(own, target, all_send.at[n, 0], all_recv.at[n, 0], at.across_x).start()
        send(own, target, all_send.at[n, 1], all_recv.at[n, 1], at.across_y).start()
        pltpu.make_async_copy(own, target, keep_sem.at[n]).start()

    def share(n):
        whole = wholes[n]
        arrived(whole.at[at.x_part], all_recv.at[n, 0], at.across_x)
        block = whole.at[at.x_part, 0:64]
        send(block, block, all_send.at[n, 2], all_recv.at[n, 2], at.across_y).start()
        arrived(whole.at[at.y_part], all_recv.at[n, 1], at.across_y)
        block = whole.at[at.y_part, 64:128]
        send(block, block, all_send.at[n, 3], all_recv.at[n, 3], at.across_x).start()

    def out_to_core():
        send(
            out_term.at[1 - core], out_core_in, rows_send.at[0], rows_recv.at[0], at.other_core
        ).start()

    def out_add(block):
        out_line[...] = (out_line[...].astype(f32) + block.astype(f32)).astype(bf16)

    def out_add_core():
        arrived(out_core_in, rows_recv.at[0], at.other_core)
        out_line[...] = out_term[core]
        out_add(out_core_in[...])

    def out_step(step):
        @pl.when((z == step) & (z < part))
        def _():
            if step > 0:
                arrived(out_line_in.at[0], rows_recv.at[1], at.down)
                out_add(out_line_in[0])
            send(out_line, out_line_in.at[0], rows_send.at[1], rows_recv.at[1], at.up).start()

        @pl.when((z == 3 - step) & (z > part))
        def _():
            if step > 0:
                arrived(out_line_in.at[1], rows_recv.at[2], at.up)
                out_add(out_line_in[1])
            send(out_line, out_line_in.at[1], rows_send.at[1], rows_recv.at[2], at.down).start()

    def out_ends():
        @pl.when(z == part)
        def _():
            @pl.when(z > 0)
            def _():
                arrived(out_line_in.at[0], rows_recv.at[1], at.down)
                out_add(out_line_in[0])

            @pl.when(z < 3)
            def _():
                arrived(out_line_in.at[1], rows_recv.at[2], at.up)
                out_add(out_line_in[1])

            for r, (peer, _) in enumerate(neighbours):
                send(out_line, out_grad, rows_send.at[2 + r], rows_recv.at[3], peer).start()
            pltpu.make_async_copy(out_line, out_grad, keep_sem.at[3]).start()

    def out_share():
        for r, (peer, source) in enumerate(neighbours):

            @pl.when(z == source)
            def _():
                arrived(out_grad, rows_recv.at[3], peer)
                block = out_grad.at[64 * r : 64 * r + 64]
                onward = neighbours[1 - r][0]
                send(block, block, rows_send.at[4], rows_recv.at[4 + r], onward).start()

    def out_gradient():
        for n in range(2):
            columns = slice(n * 128, (n + 1) * 128)
            out_term[n] = tn(flat(mixed[:, :, columns]), flat(back[...])).astype(bf16)

    part_refs = (out_part, dx_part)
    routes = (
        (halves[0], at.across_x, at.x_part, at.across_y, at.y_part),
        (halves[1], at.across_y, at.y_part, at.across_x, at.x_part),
    )

    def send_part(n, r, m):
        half, peer, peer_part, _, _ = routes[r]
        target = (at.far_part, peer_part)[m]
        send(
            part_refs[n].at[target, half],
            plane_one.at[n, r, m],
            part_send.at[n, r, m],
            part_recv.at[n, r, m],
            peer,
        ).start()

    def turn_part(n, r):
        half, peer, _, turn, turned = routes[r]
        arrived(plane_one.at[n, r, 0], part_recv.at[n, r, 0], peer)
        plane_turn[n, r] = (
            part_refs[n][turned, half].astype(f32) + plane_one[n, r, 0].astype(f32)
        ).astype(bf16)
        send(
            plane_turn.at[n, r],
            plane_two.at[n, r],
            part_send.at[n, r, 2],
            part_recv.at[n, r, 2],
            turn,
        ).start()

    def whole_part(n, r):
        half, peer, _, turn, _ = routes[r]
        arrived(plane_one.at[n, r, 1], part_recv.at[n, r, 1], peer)
        arrived(plane_two.at[n, r], part_recv.at[n, r, 2], turn)
        return (
            part_refs[n][part, half].astype(f32)
            + plane_one[n, r, 1].astype(f32)
            + plane_two[n, r].astype(f32)
        )

    up_low, up_high = SPANS[U]
    down_low, down_high = SPANS[N]

    def feed_in(s):
        value = nn(normed_two[s], flat(w_all[:, :, up_low:up_high])) + up_bias[...]
        hidden[s] = value
        activated[s] = (value * (0.5 * (1.0 + lax.erf(value * 2.0**-0.5)))).astype(bf16)

    def feed_out(s):
        out_part[s] = (
            nn(activated[s], flat(w_all[:, :, down_low:down_high]))
            + nn(mixed[s], flat(out_all[...]))
        ).astype(bf16)

    def feed_back(s):
        slope = gelu_slope(hidden[s])
        low = (nt(back[s], flat(w_all[:, :, down_low:down_high])) * slope).astype(bf16)
        d_hidden[s] = low
        d_up_bias[...] += jnp.sum(low.astype(f32), axis=0, keepdims=True)

    def norm_back(s):
        d_two = nt(d_hidden[s], flat(w_all[:, :, up_low:up_high]))
        d_one = nt(d_projected[s], flat(w_all[:, :, SPANS[Q][0] : SPANS[Q][1]]))
        unit = (x_all[s].astype(f32) - stats[s][:, 0:1]) * stats[s][:, 1:2]
        sums[0:1] += jnp.sum(d_one * unit, axis=0, keepdims=True)
        sums[1:2] += jnp.sum(d_one, axis=0, keepdims=True)
        sums[2:3] += jnp.sum(d_two * unit, axis=0, keepdims=True)
        sums[3:4] += jnp.sum(d_two, axis=0, keepdims=True)
        dx_part[s] = (d_one * vectors[0:1] + d_two * vectors[2:3]).astype(bf16)

    def place(row, value):
        small_part[row // 13, pl.ds(row % 13, 1)] = value

    def small_start():
        small_part[...] = jnp.zeros_like(small_part)
        back_total = jnp.sum(back[part].astype(f32), axis=0, keepdims=True)
        for n in range(8):
            columns = slice(n * 128, (n + 1) * 128)
            for number in range(4):
                place(8 * number + n, sums[number : number + 1, columns])
            place(56 + n, back_total[:, columns])
            place(96 + n, back_total[:, columns])
            place(64 + 4 * n + part, d_up_bias[:, columns])
        for c in range(3):
            for n in range(2):
                columns = slice((2 * c + n) * 128, (2 * c + n + 1) * 128)
                place(32 + 8 * c + 2 * part + n, d_qkv_bias[:, columns])
        for k in range(1, 8):
            send(
                small_part.at[(shard + k) % 8],
                small_in.at[k - 1],
                total_send.at[k - 1],
                total_recv.at[k - 1],
                at.shard_after(k),
            ).start()

    def small_turn():
        total = small_part[shard]
        for k in range(1, 8):
            arrived(small_in.at[k - 1], total_recv.at[k - 1], at.shard_after(8 - k))
            total = total + small_in[k - 1]
        small_total[...] = total
        for n, (peer, _) in enumerate(plane_peers):
            send(
                small_total, small_plane.at[part], total_send.at[7 + n], total_recv.at[7 + n], peer
            ).start()
        small_plane[part] = total

    def small_end():
        for n, (peer, other) in enumerate(plane_peers):
            arrived(small_plane.at[other], total_recv.at[7 + n], peer)
        small_sum[...] = (small_plane[0] + small_plane[1]) + (small_plane[2] + small_plane[3])

    def write_output(r):
        half = halves[r]
        values = x_all[part, half].astype(f32)
        summed = values + whole_part(0, r) + vectors[4:5] + vectors[5:6]
        output[half] = jnp.where(live_rows(part)[half], summed, 0.0).astype(bf16)
        pltpu.make_async_copy(output.at[half], output_out.at[half], store_sem.at[0, r]).start()

    def write_input_grad(r):
        half = halves[r]
        scaled = whole_part(1, r)
        inverse = stats[part, half, 1:2]
        unit = (x_all[part, half].astype(f32) - stats[part, half, 0:1]) * inverse
        result = back[part, half].astype(f32) + inverse * (
            scaled
            - jnp.mean(scaled, axis=-1, keepdims=True)
            - unit * jnp.mean(scaled * unit, axis=-1, keepdims=True)
        )
        input_grad[half] = result.astype(bf16)
        pltpu.make_async_copy(
            input_grad.at[half], input_grad_out.at[half], store_sem.at[1, r]
        ).start()

    at_end = (z == 0) | (z == 3)
    middle = (z == 1) | (z == 2)
    send_activations()
    send_own(Q)
    send_out_rows()
    send_small()

    @pl.when(at_end)
    def _():
        send_rest()

    @pl.when(middle)
    def _():
        forward(1, Q)
        forward_out(1)
        forward(2, Q)

    send_own(U)
    forward_x(0)

    @pl.when(at_end)
    def _():
        forward_out(1)

    @pl.when(middle)
    def _():
        forward_out(2)
        from_core(Q)
        send_own(N)
        send_rest()

    forward_y(0)

    @pl.when(at_end)
    def _():
        forward(1, Q)
        forward(2, Q)
        forward(3, Q)
        send_own(N)
        from_core(Q)

    unpack_small()

    @pl.loop(0, 4)
    def _(i):
        project(near_first(i))

        @pl.when((i == 0) & at_end)
        def _():
            forward_y(1)
            forward_out(2)

        @pl.when(i == 2)
        def _():
            forward_x(1)

        @pl.when((i == 2) & at_end)
        def _():
            forward_out(3)

        @pl.when((i == 2) & middle)
        def _():
            forward(1, U)
            forward_y(1)

        @pl.when(i == 2)
        def _():
            far_halves(0)

        @pl.when((i == 2) & middle)
        def _():
            forward(1, N)

    out_from_core()

    @pl.loop(0, 4)
    def _(i):
        attend(near_first(i))

        @pl.when((i == 0) & middle)
        def _():
            forward(2, U)

        @pl.when((i == 1) & middle)
        def _():
            far_halves(1)

        @pl.when((i == 2) & at_end)
        def _():
            forward(1, U)
            far_halves(1)

        @pl.when((i == 2) & middle)
        def _():
            forward(2, N)

    gradient(normed_one, d_projected, Q)

    @pl.when(at_end)
    def _():
        to_core(Q)

    @pl.when(middle)
    def _():
        from_core(U)
        from_core(N)

    out_gradient()

    @pl.when(at_end)
    def _():
        forward(2, U)
        forward(3, U)
        forward(1, N)
        add_core(Q)
        line_starts(Q)
        from_core(U)

    @pl.loop(0, 4)
    def _(i):
        feed_in(i)

        @pl.when((i == 0) & at_end)
        def _():
            forward(2, N)

        @pl.when((i == 0) & middle)
        def _():
            to_core(Q)

    @pl.when(at_end)
    def _():
        forward(3, N)

    gradient(activated, back, N)

    @pl.when(at_end)
    def _():
        out_to_core()
        from_core(N)

    @pl.loop(0, 4)
    def _(i):
        feed_out(far_first(i))

        @pl.when((i == 0) & middle)
        def _():
            add_core(Q)

        @pl.when(i == 0)
        def _():
            send_part(0, 0, 0)
            send_part(0, 1, 0)

        @pl.when((i == 1) & at_end)
        def _():
            out_add_core()
            out_step(0)
            to_core(N)

        @pl.when((i == 2) & middle)
        def _():
            send_part(0, 1, 1)

    @pl.loop(0, 4)
    def _(i):
        feed_back(far_first(i))

        @pl.when((i == 0) & middle)
        def _():
            out_to_core()
            out_add_core()
            line_step(Q, 0)
            line_step(Q, 1)
            send_part(0, 0, 1)
            to_core(N)

        @pl.when((i == 1) & at_end)
        def _():
            send_part(0, 1, 1)
            add_core(N)
            line_starts(N)
            turn_part(0, 0)

        @pl.when((i == 2) & at_end)
        def _():
            send_part(1, 0, 1)

        @pl.when((i == 2) & middle)
        def _():
            out_step(1)

        @pl.when((i == 3) & at_end)
        def _():
            send_part(0, 0, 1)

        @pl.when((i == 3) & middle)
        def _():
            line_step(Q, 2)
            send_part(1, 1, 1)

        norm_back(far_first(i))

        @pl.when((i == 0) & at_end)
        def _():
            send_part(1, 0, 0)
            send_part(1, 1, 0)

        @pl.when((i == 0) & middle)
        def _():
            add_core(N)

        @pl.when((i == 1) & middle)
        def _():
            send_part(1, 0, 0)
            send_part(1, 1, 0)
            turn_part(0, 1)

    @pl.when(middle)
    def _():
        turn_part(0, 0)
        line_ends(Q)

    gradient(normed_two, d_hidden, U)

    @pl.when(middle)
    def _():
        to_core(U)
        send_part(1, 0, 1)
        line_step(N, 0)

    turn_part(1, 1)

    @pl.when(at_end)
    def _():
        to_core(U)
        send_part(1, 1, 1)

    @pl.when(middle)
    def _():
        turn_part(1, 0)

    add_core(U)

    @pl.when(at_end)
    def _():
        line_starts(U)
        line_ends(Q)
        turn_part(1, 0)

    @pl.when(middle)
    def _():
        line_step(N, 1)
        out_step(2)

    small_start()

    @pl.when(middle)
    def _():
        write_output(1)
        line_step(N, 2)
        line_step(U, 0)
        write_output(0)
        line_ends(N)
        share(Q)

    out_ends()

    @pl.when(at_end)
    def _():
        turn_part(0, 1)
        write_output(0)
        share(Q)
        line_ends(N)

    @pl.when(middle)
    def _():
        line_step(U, 1)
        line_step(U, 2)
        share(N)
        write_input_grad(0)
        line_ends(U)
        out_share()

    small_turn()

    @pl.when(at_end)
    def _():
        out_share()
        line_ends(U)

    @pl.when(middle)
    def _():
        share(U)

    write_input_grad(1)
    small_end()

    @pl.when(at_end)
    def _():
        write_output(1)
        share(N)
        share(U)
        write_input_grad(0)

    for r, half in enumerate(halves):
        pltpu.make_async_copy(output.at[half], output_out.at[half], store_sem.at[0, r]).wait()
        pltpu.make_async_copy(
            input_grad.at[half], input_grad_out.at[half], store_sem.at[1, r]
        ).wait()
    @pl.when(z == at.far_part)
    def _():
        for r, (peer, _) in enumerate(neighbours):
            arrived(out_grad.at[64 * r : 64 * r + 64], rows_recv.at[4 + r], neighbours[1 - r][0])

    @pl.when(z != part)
    def _():
        sent(out_line, rows_send.at[1], at.up)

    @pl.when((z == at.x_part) | (z == at.y_part))
    def _():
        sent(out_line.at[0:64], rows_send.at[4], at.across_x)

    @pl.when(z == part)
    def _():
        for r, (peer, _) in enumerate(neighbours):
            sent(out_line, rows_send.at[2 + r], peer)
        pltpu.make_async_copy(out_line, out_grad, keep_sem.at[3]).wait()

    sent(out_line, rows_send.at[0], at.other_core)
    for r, (peer, _) in enumerate(neighbours):
        sent(x_own, plane_send.at[0, r], peer)
        sent(cot_own.at[halves[0]], early_send.at[r], peer)
        sent(cot_own.at[halves[1]], plane_send.at[1, r], peer)
        for n in range(2):
            sent(x_all.at[part, halves[0]], plane_send.at[n, 2 + r], peer)
    for n, (peer, _) in enumerate(plane_peers):
        sent(len_all.at[part], len_send.at[n], peer)
        sent(small_total, total_send.at[7 + n], peer)
    for k in range(1, 8):
        sent(small_own, small_send.at[k - 1], at.shard_after(k))
        sent(small_total, total_send.at[k - 1], at.shard_after(k))
    for n in range(3):
        for other in range(4):
            block = piece(w_all, 2 * other + core, n)
            sent(block, w_send.at[2, n, other], at.other_core)
            sent(block, core_send.at[n, other], at.other_core)

            @pl.when((other <= z) & (z < 3))
            def _():
                sent(block, w_send.at[0, n, other], at.up)

            @pl.when((other >= z) & (z > 0))
            def _():
                sent(block, w_send.at[1, n, other], at.down)

            @pl.when(z != other)
            def _():
                sent(block, line_send.at[n, other], at.up)

    block = out_all.at[core]
    sent(block, out_send.at[2], at.other_core)

    @pl.when((z >= part) & (z < 3))
    def _():
        sent(block, out_send.at[0], at.up)

    @pl.when((z <= part) & (z > 0))
    def _():
        sent(block, out_send.at[1], at.down)

    for n in range(2):
        for r in range(2):
            for m in range(3):
                sent(plane_turn.at[n, r], part_send.at[n, r, m], at.across_x)
    for n, whole in enumerate(wholes):
        arrived(whole.at[at.far_part, 0:64], all_recv.at[n, 2], at.across_y)
        arrived(whole.at[at.far_part, 64:128], all_recv.at[n, 3], at.across_x)
        own = piece(terms, shard, n)
        sent(own, all_send.at[n, 0], at.across_x)
        sent(own, all_send.at[n, 1], at.across_y)
        sent(whole.at[part, 0:64], all_send.at[n, 2], at.across_y)
        sent(whole.at[part, 64:128], all_send.at[n, 3], at.across_x)
        pltpu.make_async_copy(own, whole.at[part], keep_sem.at[n]).wait()


VMEM_SPEC = pl.BlockSpec(memory_space=pltpu.VMEM)
HBM_SPEC = pl.BlockSpec(memory_space=pl.ANY)


def whole_layer(lengths, x_own, cot_own, masters, tables):
    shape = jax.ShapeDtypeStruct
    vmem, dma = pltpu.VMEM, pltpu.SemaphoreType.DMA
    bf16, f32 = jnp.bfloat16, jnp.float32
    length = x_own.shape[0]
    group = 4
    head_cols, wide, rows = D // group, 2816, 128

    def by_sequence(width, kind=bf16):
        return vmem((group, length, width), kind)

    return pl.pallas_call(
        layer_kernel,
        out_shape=(
            shape(x_own.shape, bf16),
            shape(x_own.shape, bf16),
            shape((group, rows, 3 * head_cols), bf16),
            shape((group, rows, FF // group), bf16),
            shape((group, rows, D), bf16),
            shape((rows, D), bf16),
            shape((16, 128), f32),
        ),
        in_specs=[pl.BlockSpec(memory_space=pltpu.SMEM)]
        + [HBM_SPEC] * 6
        + [VMEM_SPEC, HBM_SPEC],
        out_specs=(HBM_SPEC,) * 6 + (VMEM_SPEC,),
        scratch_shapes=[
            vmem(tables.shape, f32),
            vmem(x_own.shape, bf16),
            vmem(x_own.shape, bf16),
            by_sequence(D),
            by_sequence(D),
            vmem((group, 8, 128), f32),
            vmem((8, rows, wide), bf16),
            vmem((2, rows, D), bf16),
            vmem((16, 128), f32),
            vmem((8, 16, 128), f32),
            vmem((8, D), f32),
            vmem((1, 3 * head_cols), f32),
            vmem((1, FF // group), f32),
            by_sequence(128, f32),
            by_sequence(D),
            by_sequence(D),
            by_sequence(D),
            by_sequence(3 * head_cols),
            by_sequence(head_cols),
            by_sequence(3 * head_cols),
            by_sequence(FF // group, f32),
            by_sequence(FF // group),
            by_sequence(D),
            by_sequence(D),
            vmem((8, rows, wide), bf16),
            vmem((2, rows, D), bf16),
            vmem((8, D), f32),
            vmem((1, 3 * head_cols), f32),
            vmem((1, FF // group), f32),
            vmem((8, 16, 128), f32),
            vmem((2, 2, 2, HALF, D), bf16),
            vmem((2, 2, HALF, D), bf16),
            vmem((2, 2, HALF, D), bf16),
            vmem((4, rows, wide), bf16),
            vmem((5, rows, wide), bf16),
            vmem((rows, D), bf16),
            vmem((rows, D), bf16),
            vmem((2, rows, D), bf16),
            vmem((7, 16, 128), f32),
            vmem((16, 128), f32),
            vmem((4, 16, 128), f32),
            dma((16,)),
            dma((2, 4)),
            dma((2, 4)),
            dma((2,)),
            dma((2,)),
            dma((3,)),
            dma((3,)),
            dma((3, 3, 4)),
            dma((3, 8)),
            dma((3,)),
            dma((2,)),
            dma((7,)),
            dma((7,)),
            dma((2, 2, 3)),
            dma((2, 2, 3)),
            dma((3, 4)),
            dma((3, 4)),
            dma((3, 4)),
            dma((3, 5)),
            dma((5,)),
            dma((6,)),
            dma((3, 4)),
            dma((3, 4)),
            dma((4,)),
            dma((10,)),
            dma((10,)),
            dma((2, 2)),
        ],
        compiler_params=pltpu.CompilerParams(
            collective_id=0, has_side_effects=True, vmem_limit_bytes=56 << 20
        ),
        name="layer",
    )(lengths, x_own, cot_own, *masters, tables)


def rope_tables(length, heads):
    half = ROT // 2
    angle = np.arange(length)[:, None] * ROPE_BASE ** (-2.0 * np.arange(half) / ROT)[None]
    table = np.zeros((3, length, HD), np.float32)
    table[0] = 1.0
    table[0, :, :half] = table[0, :, half:ROT] = np.cos(angle)
    table[1, :, :half] = -np.sin(angle)
    table[2, :, half:ROT] = np.sin(angle)
    return jnp.asarray(np.tile(table, (1, 1, heads)))


def local_split(
    tokens_in,
    cotangent,
    lengths,
    qkv_master,
    out_master,
    up_master,
    down_master,
    small_master,
    qkv_first,
    out_first,
    up_first,
    down_first,
    small_first,
    qkv_second,
    out_second,
    up_second,
    down_second,
    small_second,
):
    masters = (qkv_master, out_master, up_master, down_master, small_master)
    firsts = (qkv_first, out_first, up_first, down_first, small_first)
    seconds = (qkv_second, out_second, up_second, down_second, small_second)
    parts, shards = lax.axis_size("dp"), lax.axis_size("fsdp")
    part, shard = lax.axis_index("dp"), lax.axis_index("fsdp")
    length = tokens_in.shape[1]
    update = (masters, firsts, seconds)
    if (parts, shards) == (4, 8):
        tall = tuple(masters[:4]) + (small_master.reshape(-1, 128),)
        output, input_grad, qkv_grad, up_grad, down_grad, out_grad, small_sum = whole_layer(
            lengths, tokens_in[0], cotangent[0], tall, rope_tables(length, HEADS // parts)
        )
        grads = (qkv_grad, out_grad, up_grad, down_grad, small_sum[: tall[4].shape[0]])
        return lamb_split(*update, grads, (output, input_grad))

    head_cols = D // parts
    ff_rows = down_master.shape[0] // parts
    qkv_own = sliced(qkv_master, part, parts, 3).astype(jnp.bfloat16)
    up_own = sliced(up_master, part, parts, shards).astype(jnp.bfloat16)
    down_own = lax.dynamic_slice_in_dim(down_master, part * ff_rows, ff_rows).astype(jnp.bfloat16)
    out_own = out_master.astype(jnp.bfloat16)
    small_own = small_master.astype(jnp.bfloat16)

    def small_vectors(small_all):
        vectors = split_small(small_all)
        vectors[4] = sliced(vectors[4][None], part, parts, 3)[0]
        vectors[6] = sliced(vectors[6][None], part, parts, shards)[0]
        return vectors

    def over_shards(own):
        return lax.all_gather(own, "fsdp", axis=0, tiled=True)

    x_all = lax.all_gather(tokens_in, "dp", axis=0, tiled=True)
    cotangent_all = lax.all_gather(cotangent, "dp", axis=0, tiled=True)
    lengths_all = lax.all_gather(lengths, "dp", axis=0, tiled=True)
    qkv_weight, up_weight, down_weight = (over_shards(w) for w in (qkv_own, up_own, down_own))
    out_weight = lax.dynamic_slice_in_dim(over_shards(out_own), part * head_cols, head_cols)
    gain_one, shift_one, gain_two, shift_two, qkv_bias, out_bias, up_bias, down_bias = (
        small_vectors(over_shards(small_own).astype(jnp.float32))
    )
    out_part, scaled_part, terms, sums = layer(
        x_all,
        cotangent_all,
        lengths_all,
        (qkv_weight, out_weight, up_weight, down_weight),
        (gain_one, shift_one, gain_two, shift_two, qkv_bias, up_bias),
        part,
    )
    norm_sums, d_qkv_bias, d_up_bias = sums
    out_sum = lax.psum_scatter(out_part, "dp", scatter_dimension=0, tiled=True)
    scaled = lax.psum_scatter(scaled_part, "dp", scatter_dimension=0, tiled=True)
    out_sum, scaled = out_sum.astype(jnp.float32), scaled.astype(jnp.float32)

    inputs = tokens_in[0].astype(jnp.float32)
    live = (jnp.arange(length) < lengths[0]).astype(jnp.float32)[:, None]
    back = cotangent[0].astype(jnp.float32) * live
    back_total = jnp.sum(back, axis=0)

    def spread(values, pieces):
        wide = jnp.zeros((pieces, parts, values.shape[0] // pieces), jnp.float32)
        return lax.dynamic_update_index_in_dim(
            wide, values.reshape(pieces, -1), part, axis=1
        ).reshape(-1)

    small_grad = jnp.concatenate(
        [
            norm_sums.reshape(4 * D),
            spread(d_qkv_bias, 3),
            back_total,
            spread(d_up_bias, shards),
            back_total,
        ]
    )
    small_sum = lax.psum(small_grad, ("dp", "fsdp"))
    small_rows = small_master.shape[0]
    small_sum = lax.dynamic_slice_in_dim(small_sum, shard * small_rows, small_rows)
    qkv_term, out_term, up_term, down_term = terms
    out_wide = lax.dynamic_update_slice_in_dim(
        jnp.zeros((D, D), jnp.bfloat16), out_term, part * head_cols, axis=0
    )

    def to_owner(term):
        own = lax.psum_scatter(term, "fsdp", scatter_dimension=0, tiled=True)
        return lax.all_gather(own, "dp", axis=0, tiled=False).astype(jnp.float32)

    reduced = (
        joined(to_owner(qkv_term), 3),
        lax.psum(
            lax.psum_scatter(out_wide, "fsdp", scatter_dimension=0, tiled=True), "dp"
        ).astype(jnp.float32),
        joined(to_owner(up_term), shards),
        to_owner(down_term).reshape(down_master.shape),
        small_sum,
    )

    unit_rows, inverse_rows = normalize(inputs)
    output = ((inputs + out_sum + out_bias + down_bias) * live).astype(jnp.bfloat16)
    input_grad = back + inverse_rows * (
        scaled
        - jnp.mean(scaled, axis=-1, keepdims=True)
        - unit_rows * jnp.mean(scaled * unit_rows, axis=-1, keepdims=True)
    )
    return (output[None], input_grad.astype(jnp.bfloat16)[None]) + lamb(*update, reduced)


def lamb_rows(first_old, second_old, master, grad):
    first_new = BETA_ONE * first_old + (1.0 - BETA_ONE) * grad
    second_new = BETA_TWO * second_old + (1.0 - BETA_TWO) * grad * grad
    update = first_new / (jnp.sqrt(second_new) + ADAM_EPSILON) + DECAY * master
    return first_new, second_new, update


def lane_sums(values):
    squares = jnp.sum(values * values, axis=0, keepdims=True)
    total = squares[:, 0:128]
    for n in range(1, squares.shape[1] // 128):
        total = total + squares[:, n * 128 : (n + 1) * 128]
    return total


def moments_kernel(*refs):
    qkv_grad, out_grad, up_grad, down_grad, small_grad = refs[0:5]
    masters, firsts, seconds = refs[5:10], refs[10:15], refs[15:20]
    first_news, second_news, updates, squares = refs[20:25], refs[25:30], refs[30:35], refs[35]
    step = pl.program_id(0)

    @pl.when(step == 0)
    def _():
        squares[...] = jnp.zeros_like(squares)

    def one(number, span, grad):
        index = (slice(None), span)
        rows = firsts[number].shape[0]
        place = (pl.ds(pl.multiple_of(step * rows, rows), rows), span)
        master = masters[number][place]
        first_new, second_new, update = lamb_rows(
            firsts[number][index], seconds[number][index], master, grad
        )
        first_news[number][index] = first_new
        second_news[number][index] = second_new
        updates[number][place] = update
        return lane_sums(master), lane_sums(update)

    def add(number, pairs):
        weight, update = pairs[0]
        for more_weight, more_update in pairs[1:]:
            weight, update = weight + more_weight, update + more_update
        squares[number : number + 1] += weight
        squares[8 + number : 9 + number] += update

    f32 = jnp.float32
    parts = qkv_grad.shape[0]
    width = qkv_grad.shape[2] // 3
    add(
        0,
        [
            one(
                0,
                slice((c * parts + d) * width, (c * parts + d + 1) * width),
                qkv_grad[d, :, c * width : (c + 1) * width].astype(f32),
            )
            for c in range(3)
            for d in range(parts)
        ],
    )
    add(1, [one(1, slice(None), out_grad[...].astype(f32))])
    pieces = up_grad.shape[2] // 128
    add(
        2,
        [
            one(
                2,
                slice((g * parts + d) * 128, (g * parts + d + 1) * 128),
                up_grad[d, :, g * 128 : (g + 1) * 128].astype(f32),
            )
            for g in range(pieces)
            for d in range(parts)
        ],
    )
    add(3, [one(3, slice(None), down_grad[0].astype(f32))])

    @pl.when(step == 0)
    def _():
        first_new, second_new, update = lamb_rows(
            firsts[4][...], seconds[4][...], masters[4][...], small_grad[...]
        )
        first_news[4][...] = first_new
        second_news[4][...] = second_new
        updates[4][...] = update
        squares[4:5] += lane_sums(masters[4][...])
        squares[12:13] += lane_sums(update)


def lamb_specs(masters, steps):
    specs = [pl.BlockSpec((m.shape[0] // steps, m.shape[1]), lambda i: (i, 0)) for m in masters[:4]]
    return specs + [pl.BlockSpec(masters[4].shape, lambda i: (0, 0))]


def moments(grads, masters, firsts, seconds, steps=8):
    qkv_grad, out_grad, up_grad, down_grad, small_grad = grads
    shape = jax.ShapeDtypeStruct
    each = lamb_specs(masters, steps)
    rows = qkv_grad.shape[1]
    halves = steps // qkv_grad.shape[0]
    grad_specs = [
        pl.BlockSpec((qkv_grad.shape[0], rows // steps, qkv_grad.shape[2]), lambda i: (0, i, 0)),
        each[1],
        pl.BlockSpec((up_grad.shape[0], rows // steps, up_grad.shape[2]), lambda i: (0, i, 0)),
        pl.BlockSpec(
            (1, rows // halves, down_grad.shape[2]), lambda i: (i // halves, i % halves, 0)
        ),
        each[4],
    ]
    out = [shape(m.shape, jnp.float32) for m in masters]
    near = [pltpu.VMEM(m.shape, jnp.float32) for m in masters]
    results = pl.pallas_call(
        moments_kernel,
        grid=(steps,),
        in_specs=grad_specs + [VMEM_SPEC] * 5 + each * 2,
        out_specs=each * 2 + [VMEM_SPEC] * 5 + [pl.BlockSpec((16, 128), lambda i: (0, 0))],
        out_shape=out * 2 + near + [shape((16, 128), jnp.float32)],
        compiler_params=pltpu.CompilerParams(vmem_limit_bytes=12 << 20),
        name="moments",
    )(*grads, *masters, *firsts, *seconds)
    return results[0:5], results[5:10], results[10:15], results[15]


def norms_kernel(squares, total, everyone, send_sem, recv_sem):
    shard, part = lax.axis_index("fsdp"), lax.axis_index("dp")
    peers = [(part, (shard + k) % 8) for k in range(1, 8)]
    barrier = pltpu.get_barrier_semaphore()
    for peer in peers:
        pl.semaphore_signal(barrier, inc=1, device_id=peer, device_id_type=MESH_ID)
    pl.semaphore_wait(barrier, 7)
    for k in range(1, 8):
        send(
            squares, everyone.at[shard], send_sem.at[k - 1], recv_sem.at[k - 1], peers[k - 1]
        ).start()
    everyone[shard] = squares[...]
    for k in range(1, 8):
        arrived(everyone.at[(shard + 8 - k) % 8], recv_sem.at[k - 1], peers[7 - k])
    summed = everyone[0]
    for k in range(1, 8):
        summed = summed + everyone[k]
    norms = jnp.sqrt(jnp.sum(summed, axis=1, keepdims=True))
    total[...] = jnp.broadcast_to(norms, (16, 128))
    for k in range(1, 8):
        sent(squares, send_sem.at[k - 1], peers[k - 1])


def norms(squares):
    dma = pltpu.SemaphoreType.DMA
    return pl.pallas_call(
        norms_kernel,
        out_shape=jax.ShapeDtypeStruct((16, 128), jnp.float32),
        in_specs=[VMEM_SPEC],
        out_specs=VMEM_SPEC,
        scratch_shapes=[pltpu.VMEM((8, 16, 128), jnp.float32), dma((7,)), dma((7,))],
        compiler_params=pltpu.CompilerParams(
            collective_id=1, has_side_effects=True, vmem_limit_bytes=2 << 20
        ),
        name="norms",
    )(squares)


def step_kernel(*refs):
    total, masters, updates, layer_outs = refs[0], refs[1:6], refs[6:11], refs[11:13]
    news, outs, lamb_norms = refs[13:18], refs[18:20], refs[20]
    step = pl.program_id(0)
    for number in range(5):
        weight_norm = total[number : number + 1, 0:1]
        update_norm = total[8 + number : 9 + number, 0:1]
        scale = RATE * (weight_norm / update_norm)
        rows = news[number].shape[0]
        place = slice(None)
        if rows < masters[number].shape[0]:
            place = pl.ds(pl.multiple_of(step * rows, rows), rows)
        news[number][...] = masters[number][place] - scale * updates[number][place]
    for source, target in zip(layer_outs, outs):
        target[...] = source[...]

    @pl.when(step == 0)
    def _():
        row = lax.broadcasted_iota(jnp.int32, (8, 128), 0)
        lane = lax.broadcasted_iota(jnp.int32, (8, 128), 1)
        for n in range(2):
            half = jnp.where(row == lane, total[8 * n : 8 * n + 8], 0.0)
            lamb_norms[n : n + 1] = jnp.sum(half, axis=0, keepdims=True)[:, 0:5]


def step_masters(total, masters, updates, layer_outs, steps=4):
    shape = jax.ShapeDtypeStruct
    out_specs = [
        pl.BlockSpec((o.shape[0] // steps, o.shape[1]), lambda i: (i, 0)) for o in layer_outs
    ]
    results = pl.pallas_call(
        step_kernel,
        grid=(steps,),
        in_specs=[pl.BlockSpec((16, 128), lambda i: (0, 0))] + [VMEM_SPEC] * 10 + out_specs,
        out_specs=lamb_specs(masters, steps)
        + out_specs
        + [pl.BlockSpec((2, 5), lambda i: (0, 0))],
        out_shape=[shape(m.shape, jnp.float32) for m in masters]
        + [shape(o.shape, o.dtype) for o in layer_outs]
        + [shape((2, 5), jnp.float32)],
        compiler_params=pltpu.CompilerParams(vmem_limit_bytes=12 << 20),
        name="step_masters",
    )(total, *masters, *updates, *layer_outs)
    return results[0:5], results[5:7], results[7]


def lamb_split(masters, firsts, seconds, grads, layer_outs):
    def tall(arrays):
        return tuple(arrays[:4]) + (arrays[4].reshape(-1, 128),)

    def flat_small(arrays):
        return tuple(arrays[:4]) + (arrays[4].reshape(-1),)

    def placed(arrays, space):
        return tuple(pltpu.with_memory_space_constraint(a, space) for a in arrays)

    masters = placed(tall(masters), pltpu.VMEM)
    firsts, seconds = placed(tall(firsts), pltpu.HBM), placed(tall(seconds), pltpu.HBM)
    grads = placed(grads[:4], pltpu.HBM) + (grads[4],)
    layer_outs = placed(layer_outs, pltpu.HBM)
    first_news, second_news, updates, squares = moments(grads, masters, firsts, seconds)
    news, outs, lamb_norms = step_masters(norms(squares), masters, updates, layer_outs)
    return (
        tuple(out[None] for out in outs)
        + flat_small(news)
        + flat_small(first_news)
        + flat_small(second_news)
        + (lamb_norms,)
    )


def lamb(masters, firsts, seconds, reduced):
    updates = []
    first_news = []
    second_news = []
    for first_old, second_old, master, grad_sum in zip(firsts, seconds, masters, reduced):
        first_new = BETA_ONE * first_old + (1.0 - BETA_ONE) * grad_sum
        second_new = BETA_TWO * second_old + (1.0 - BETA_TWO) * grad_sum * grad_sum
        updates.append(first_new / (jnp.sqrt(second_new) + ADAM_EPSILON) + DECAY * master)
        first_news.append(first_new)
        second_news.append(second_new)
    weight_squares, update_squares = lax.psum(
        (local_squares(masters), local_squares(updates)), "fsdp"
    )
    weight_norms = jnp.sqrt(weight_squares)
    update_norms = jnp.sqrt(update_squares)
    new_masters = [
        masters[number] - RATE * (weight_norms[number] / update_norms[number]) * updates[number]
        for number in range(5)
    ]
    lamb_norms = jnp.stack([weight_norms, update_norms])
    return tuple(new_masters) + tuple(first_news) + tuple(second_news) + (lamb_norms,)


def solution(mesh):
    in_specs = (
        P(("dp", "fsdp"), None, None),
        P(("dp", "fsdp"), None, None),
        P(("dp", "fsdp")),
        P("fsdp", None),
        P("fsdp", None),
        P("fsdp", None),
        P("fsdp", None),
        P("fsdp"),
        P("fsdp", None),
        P("fsdp", None),
        P("fsdp", None),
        P("fsdp", None),
        P("fsdp"),
        P("fsdp", None),
        P("fsdp", None),
        P("fsdp", None),
        P("fsdp", None),
        P("fsdp"),
    )
    out_specs = (
        P(("dp", "fsdp"), None, None),
        P(("dp", "fsdp"), None, None),
        P("fsdp", None),
        P("fsdp", None),
        P("fsdp", None),
        P("fsdp", None),
        P("fsdp"),
        P("fsdp", None),
        P("fsdp", None),
        P("fsdp", None),
        P("fsdp", None),
        P("fsdp"),
        P("fsdp", None),
        P("fsdp", None),
        P("fsdp", None),
        P("fsdp", None),
        P("fsdp"),
        P(),
    )
    return jax.shard_map(local_split, mesh=mesh, in_specs=in_specs, out_specs=out_specs, check_vma=False)
```

```python
import math

import jax
import jax.numpy as jnp
import numpy as np
from jax import lax
from jax.experimental import pallas as pl
from jax.experimental.pallas import tpu as pltpu
from jax.sharding import PartitionSpec as P

D = 1024
HEADS = 16
HD = 64
FF = 4096
ROT = 16
SMALL = 13312


NORM_EPSILON = 1e-05
ADAM_EPSILON = 1e-06
ROPE_BASE = 10000.0
RATE = 0.5
DECAY = 0.01
BETA_ONE = 0.5
BETA_TWO = 0.5


def split_small(small_vector):
    bounds = [0, D, 2 * D, 3 * D, 4 * D, 7 * D, 8 * D, 8 * D + FF, 9 * D + FF]
    return [small_vector[bounds[number] : bounds[number + 1]] for number in range(8)]


def normalize(values):
    average = jnp.mean(values, axis=-1, keepdims=True)
    centred = values - average
    variance = jnp.mean(centred * centred, axis=-1, keepdims=True)
    inverse = lax.rsqrt(variance + NORM_EPSILON)
    return (centred * inverse, inverse)


def rotary_tables(length):
    half_dims = ROT // 2
    position = jnp.arange(length, dtype=jnp.float32)[:, None]
    number = jnp.arange(half_dims, dtype=jnp.float32)[None, :]
    angle = position * jnp.exp(number * (-2.0 * math.log(ROPE_BASE) / ROT))
    return (jnp.cos(angle)[:, None, :], jnp.sin(angle)[:, None, :])


def rotate(heads_in, cosine_table, sine_table):
    half_dims = ROT // 2
    first_half = heads_in[..., :half_dims]
    second_half = heads_in[..., half_dims:ROT]
    return jnp.concatenate(
        [
            first_half * cosine_table - second_half * sine_table,
            second_half * cosine_table + first_half * sine_table,
            heads_in[..., ROT:],
        ],
        axis=-1,
    )


def rotate_back(grads_in, cosine_table, sine_table):
    half_dims = ROT // 2
    first_half = grads_in[..., :half_dims]
    second_half = grads_in[..., half_dims:ROT]
    return jnp.concatenate(
        [
            first_half * cosine_table + second_half * sine_table,
            second_half * cosine_table - first_half * sine_table,
            grads_in[..., ROT:],
        ],
        axis=-1,
    )


def gelu_slope(values):
    return 0.5 * (1.0 + lax.erf(values * 2.0 ** (-0.5))) + values * jnp.exp(
        -0.5 * values * values
    ) * (2.0 * math.pi) ** (-0.5)


def against(left, right):
    return lax.dot_general(
        left, right, (((1,), (1,)), ((), ())), preferred_element_type=jnp.float32
    )


def outer_sum(columns, right):
    return lax.dot_general(
        columns, right, (((0,), (0,)), ((), ())), preferred_element_type=jnp.float32
    )


def local_squares(arrays):
    return jnp.stack([jnp.sum(array_in * array_in) for array_in in arrays])


def sliced(master, part, parts, pieces):
    rows, columns = master.shape
    width = columns // (pieces * parts)
    return lax.dynamic_index_in_dim(
        master.reshape(rows, pieces, parts, width), part, axis=2, keepdims=False
    ).reshape(rows, pieces * width)


def joined(slices, pieces):
    parts, rows, columns = slices.shape
    width = columns // pieces
    return (
        slices.reshape(parts, rows, pieces, width)
        .transpose(1, 2, 0, 3)
        .reshape(rows, pieces * parts * width)
    )


def layer(x_all, cotangent_all, lengths_all, weights, small_all, part):
    qkv_weight, out_weight, up_weight, down_weight = weights
    group, length, _ = x_all.shape
    tokens = group * length
    head_cols = out_weight.shape[0]
    heads = head_cols // HD
    gain_one, shift_one, gain_two, shift_two, qkv_bias, up_bias = small_all
    inputs = x_all.reshape(tokens, D).astype(jnp.float32)
    position = jnp.arange(length)
    live = (position[None, :] < lengths_all[:, None]).astype(jnp.float32).reshape(tokens, 1)
    allowed = (position[None, None, :] <= position[None, :, None]) & (
        position[None, None, :] < lengths_all[:, None, None]
    )
    unit_rows, _ = normalize(inputs)
    normed_one = (unit_rows * gain_one + shift_one).astype(jnp.bfloat16)
    normed_two = (unit_rows * gain_two + shift_two).astype(jnp.bfloat16)
    projected = jnp.dot(normed_one, qkv_weight, preferred_element_type=jnp.float32) + qkv_bias
    projected = projected.reshape(group, length, 3, heads, HD)
    cosine_table, sine_table = rotary_tables(length)
    query_heads = rotate(projected[:, :, 0], cosine_table, sine_table).astype(jnp.bfloat16)
    key_heads = rotate(projected[:, :, 1], cosine_table, sine_table).astype(jnp.bfloat16)
    value_heads = projected[:, :, 2].astype(jnp.bfloat16)
    scores = jnp.einsum(
        "gqhd,gkhd->ghqk", query_heads, key_heads, preferred_element_type=jnp.float32
    ) * HD ** (-0.5)
    scores = jnp.where(allowed[:, None], scores, -1e30)
    row_top = jnp.max(scores, axis=-1, keepdims=True)
    raised = jnp.exp(scores - row_top)
    attend = raised / jnp.sum(raised, axis=-1, keepdims=True)
    attend_low = attend.astype(jnp.bfloat16)
    mixed = jnp.einsum(
        "ghqk,gkhd->gqhd", attend_low, value_heads, preferred_element_type=jnp.float32
    )
    mixed = mixed.reshape(tokens, head_cols).astype(jnp.bfloat16)
    hidden = jnp.dot(normed_two, up_weight, preferred_element_type=jnp.float32) + up_bias
    activated = jax.nn.gelu(hidden, approximate=False).astype(jnp.bfloat16)
    out_part = jnp.dot(mixed, out_weight, preferred_element_type=jnp.float32) + jnp.dot(
        activated, down_weight, preferred_element_type=jnp.float32
    )

    back = (cotangent_all.reshape(tokens, D).astype(jnp.float32) * live).astype(jnp.bfloat16)
    d_hidden = (against(back, down_weight) * gelu_slope(hidden)).astype(jnp.bfloat16)
    d_mixed = against(back, out_weight).astype(jnp.bfloat16).reshape(group, length, heads, HD)
    d_attend = jnp.einsum(
        "gqhd,gkhd->ghqk", d_mixed, value_heads, preferred_element_type=jnp.float32
    )
    row_inner = jnp.sum(attend * d_attend, axis=-1, keepdims=True)
    d_scores = (attend * (d_attend - row_inner)).astype(jnp.bfloat16)
    d_queries = jnp.einsum(
        "ghqk,gkhd->gqhd", d_scores, key_heads, preferred_element_type=jnp.float32
    ) * HD ** (-0.5)
    d_keys = jnp.einsum(
        "ghqk,gqhd->gkhd", d_scores, query_heads, preferred_element_type=jnp.float32
    ) * HD ** (-0.5)
    d_values = jnp.einsum(
        "ghqk,gqhd->gkhd", attend_low, d_mixed, preferred_element_type=jnp.float32
    )
    d_projected = jnp.stack(
        [
            rotate_back(d_queries, cosine_table, sine_table),
            rotate_back(d_keys, cosine_table, sine_table),
            d_values,
        ],
        axis=2,
    )
    d_projected = d_projected.reshape(tokens, 3 * head_cols).astype(jnp.bfloat16)
    d_normed_one = against(d_projected, qkv_weight)
    d_normed_two = against(d_hidden, up_weight)
    scaled_part = d_normed_one * gain_one + d_normed_two * gain_two
    norm_sums = jnp.stack(
        [
            jnp.sum(d_normed_one * unit_rows, axis=0),
            jnp.sum(d_normed_one, axis=0),
            jnp.sum(d_normed_two * unit_rows, axis=0),
            jnp.sum(d_normed_two, axis=0),
        ]
    )
    d_qkv_bias = jnp.sum(d_projected, axis=0, dtype=jnp.float32)
    d_up_bias = jnp.sum(d_hidden, axis=0, dtype=jnp.float32)
    terms = (
        outer_sum(normed_one, d_projected),
        outer_sum(mixed, back),
        outer_sum(normed_two, d_hidden),
        outer_sum(activated, back),
    )
    return (
        out_part.astype(jnp.bfloat16),
        scaled_part.astype(jnp.bfloat16),
        tuple(term.astype(jnp.bfloat16) for term in terms),
        (norm_sums, d_qkv_bias, d_up_bias),
    )


MESH_ID = pl.DeviceIdType.MESH
HALF = 128


class Place:
    def __init__(self):
        self.part = lax.axis_index("dp")
        self.shard = lax.axis_index("fsdp")
        self.z = self.shard // 2
        self.core = self.shard % 2
        self.x_part = 2 * (self.part // 2) + 1 - self.part % 2
        self.y_part = (self.part + 2) % 4
        self.far_part = 3 - self.part
        self.across_x = (self.x_part, self.shard)
        self.across_y = (self.y_part, self.shard)
        self.across_far = (self.far_part, self.shard)
        self.other_core = (self.part, 2 * self.z + 1 - self.core)
        self.up = (self.part, jnp.minimum(self.shard + 2, 7))
        self.down = (self.part, jnp.maximum(self.shard - 2, 0))

    def shard_after(self, k):
        return (self.part, (self.shard + k) % 8)


def send(source, target, send_sem, recv_sem, device):
    return pltpu.make_async_remote_copy(
        src_ref=source,
        dst_ref=target,
        send_sem=send_sem,
        recv_sem=recv_sem,
        device_id=device,
        device_id_type=MESH_ID,
    )


def arrived(target, recv_sem, device):
    send(target, target, recv_sem, recv_sem, device).wait_recv()


def sent(source, send_sem, device):
    send(source, source, send_sem, send_sem, device).wait_send()


def greet(at):
    barrier = pltpu.get_barrier_semaphore()
    peers = [at.across_x, at.across_y, at.across_far] + [at.shard_after(k) for k in range(1, 8)]
    for peer in peers:
        pl.semaphore_signal(barrier, inc=1, device_id=peer, device_id_type=MESH_ID)
    pl.semaphore_wait(barrier, len(peers))


SPANS = ((0, 768), (768, 1792), (1792, 2816))
Q, U, N = 0, 1, 2


def nt(left, right):
    return lax.dot_general(
        left, right, (((1,), (1,)), ((), ())), preferred_element_type=jnp.float32
    )


def tn(left, right):
    return lax.dot_general(
        left, right, (((0,), (0,)), ((), ())), preferred_element_type=jnp.float32
    )


def nn(left, right):
    return jnp.dot(left, right, preferred_element_type=jnp.float32)


def flat(value):
    return value.reshape(value.shape[0] * value.shape[1], value.shape[2])


def layer_kernel(
    length_own,
    x_own,
    cot_own,
    qkv_master,
    out_master,
    up_master,
    down_master,
    small_master,
    tables_in,
    output_out,
    input_grad_out,
    qkv_all,
    up_all,
    down_all,
    out_grad,
    small_sum,
    tables,
    output,
    input_grad,
    x_all,
    cot_all,
    len_all,
    w_all,
    out_all,
    small_own,
    small_all,
    vectors,
    qkv_bias,
    up_bias,
    stats,
    normed_one,
    normed_two,
    back,
    heads_qkv,
    mixed,
    d_projected,
    hidden,
    d_hidden,
    out_part,
    dx_part,
    terms,
    out_term,
    sums,
    d_qkv_bias,
    d_up_bias,
    small_part,
    plane_one,
    plane_two,
    plane_turn,
    core_in,
    line_in,
    out_core_in,
    out_line,
    out_line_in,
    small_in,
    small_total,
    small_plane,
    load_sem,
    plane_send,
    plane_recv,
    early_send,
    early_recv,
    len_send,
    len_recv,
    w_send,
    w_recv,
    out_send,
    out_recv,
    small_send,
    small_recv,
    part_send,
    part_recv,
    core_send,
    core_recv,
    line_send,
    line_recv,
    rows_send,
    rows_recv,
    all_send,
    all_recv,
    keep_sem,
    total_send,
    total_recv,
    store_sem,
):
    f32, bf16 = jnp.float32, jnp.bfloat16
    at = Place()
    z, core, part, shard = at.z, at.core, at.part, at.shard
    length = x_own.shape[0]
    head_cols = mixed.shape[2]
    activated = normed_one
    place_x, place_y = part % 2, part // 2

    def near_first(i):
        return 2 * ((place_y + i // 2) % 2) + (place_x + i % 2) % 2

    def far_first(i):
        return 2 * ((place_y + 1 - i % 2) % 2) + (place_x + 1 - i // 2) % 2

    def piece(ref, slot, n):
        return ref.at[slot, :, SPANS[n][0] : SPANS[n][1]]

    plane_peers = (
        (at.across_x, at.x_part),
        (at.across_y, at.y_part),
        (at.across_far, at.far_part),
    )

    stage = [hidden.at[n, 0:128] for n in range(4)]
    loads = []
    for c in range(3):
        columns = pl.ds(pl.multiple_of(c * D + part * head_cols, 128), head_cols)
        target = stage[0].at[:, c * head_cols : (c + 1) * head_cols]
        loads.append((qkv_master.at[:, columns], target))
    loads.append((out_master, stage[1]))
    for g in range(8):
        columns = pl.ds(pl.multiple_of(g * (FF // 8) + part * 128, 128), 128)
        loads.append((up_master.at[:, columns], stage[2].at[:, g * 128 : (g + 1) * 128]))
    rows = pl.ds(pl.multiple_of(part * 128, 128), 128)
    loads.append((down_master.at[rows], stage[3]))
    loads.append((x_own, x_all.at[part]))
    loads.append((cot_own, cot_all.at[part]))
    loads.append((tables_in, tables))

    def load(n):
        return pltpu.make_async_copy(loads[n][0], loads[n][1], load_sem.at[n])

    for n in range(len(loads)):
        load(n).start()
    len_all[part] = jnp.full((8, 128), length_own[0], jnp.int32).astype(f32)
    small_own[...] = jnp.zeros_like(small_own)
    small_own[0:13] = small_master[...].astype(bf16).astype(f32)
    small_all[shard] = small_own[...]
    greet(at)

    halves = (slice(0, HALF), slice(HALF, 2 * HALF))
    activations = ((x_own, x_all), (cot_own, cot_all))
    neighbours = ((at.across_x, at.x_part), (at.across_y, at.y_part))

    def send_activations():
        for r, (peer, _) in enumerate(neighbours):
            send(
                x_own, x_all.at[part], plane_send.at[0, r], plane_recv.at[0, r], peer
            ).start()
        for r, (peer, _) in enumerate(neighbours):
            send(
                cot_own.at[halves[0]],
                cot_all.at[part, halves[0]],
                early_send.at[r],
                early_recv.at[r],
                peer,
            ).start()

    def send_rest():
        for r, (peer, _) in enumerate(neighbours):
            send(
                cot_own.at[halves[1]],
                cot_all.at[part, halves[1]],
                plane_send.at[1, r],
                plane_recv.at[1, r],
                peer,
            ).start()

    def cast(n, first, last):
        for m in range(first, last):
            load(m).wait()
        low, high = SPANS[n]
        w_all[shard, :, low:high] = stage[(0, 2, 3)[n]][:, 0 : high - low].astype(bf16)

    def send_own(n):
        cast(n, *((0, 3), (4, 12), (12, 13))[n])
        block = piece(w_all, shard, n)

        @pl.when(z < 3)
        def _():
            send(block, block, w_send.at[0, n, z], w_recv.at[n, shard], at.up).start()

        @pl.when(z > 0)
        def _():
            send(block, block, w_send.at[1, n, z], w_recv.at[n, shard], at.down).start()

        send(block, block, w_send.at[2, n, z], w_recv.at[n, shard], at.other_core).start()

    def forward(k, n):
        @pl.when(z >= k)
        def _():
            source = 2 * (z - k) + core
            block = piece(w_all, source, n)
            arrived(block, w_recv.at[n, source], at.down)

            @pl.when(z < 3)
            def _():
                send(block, block, w_send.at[0, n, z - k], w_recv.at[n, source], at.up).start()

            send(
                block, block, w_send.at[2, n, z - k], w_recv.at[n, source], at.other_core
            ).start()

        @pl.when(z + k <= 3)
        def _():
            source = 2 * (z + k) + core
            block = piece(w_all, source, n)
            arrived(block, w_recv.at[n, source], at.up)

            @pl.when(z > 0)
            def _():
                send(block, block, w_send.at[1, n, z + k], w_recv.at[n, source], at.down).start()

            send(
                block, block, w_send.at[2, n, z + k], w_recv.at[n, source], at.other_core
            ).start()

    def from_core(n):
        for other in range(4):
            source = 2 * other + 1 - core
            arrived(piece(w_all, source, n), w_recv.at[n, source], at.other_core)

    def send_out_rows():
        load(3).wait()

        @pl.when(z == part)
        def _():
            out_all[core] = stage[1][...].astype(bf16)
            block = out_all.at[core]

            @pl.when(z < 3)
            def _():
                send(block, block, out_send.at[0], out_recv.at[core], at.up).start()

            @pl.when(z > 0)
            def _():
                send(block, block, out_send.at[1], out_recv.at[core], at.down).start()

            send(block, block, out_send.at[2], out_recv.at[core], at.other_core).start()

    def out_from_core():
        arrived(out_all.at[1 - core], out_recv.at[1 - core], at.other_core)

    def forward_out(k):
        @pl.when((z - k == part) | (z + k == part))
        def _():
            block = out_all.at[core]
            arrived(block, out_recv.at[core], at.up)

            @pl.when((z > part) & (z < 3))
            def _():
                send(block, block, out_send.at[0], out_recv.at[core], at.up).start()

            @pl.when((z < part) & (z > 0))
            def _():
                send(block, block, out_send.at[1], out_recv.at[core], at.down).start()

            send(block, block, out_send.at[2], out_recv.at[core], at.other_core).start()

    def forward_neighbour(n, r):
        peer, source = neighbours[r]
        whole = activations[n][1]
        if n == 0:
            arrived(whole.at[source], plane_recv.at[0, r], peer)
        else:
            arrived(whole.at[source, halves[0]], early_recv.at[r], peer)
            arrived(whole.at[source, halves[1]], plane_recv.at[1, r], peer)
        block = whole.at[source, halves[r]]
        onward = neighbours[1 - r][0]
        send(block, block, plane_send.at[n, 2 + r], plane_recv.at[n, 2 + r], onward).start()

    def forward_x(n):
        forward_neighbour(n, 0)

    def forward_y(n):
        forward_neighbour(n, 1)

    def far_halves(n):
        whole = activations[n][1]
        arrived(whole.at[at.far_part, 0:HALF], plane_recv.at[n, 2], at.across_y)
        arrived(whole.at[at.far_part, HALF : 2 * HALF], plane_recv.at[n, 3], at.across_x)

    def send_small():
        for n, (peer, _) in enumerate(plane_peers):
            send(len_all.at[part], len_all.at[part], len_send.at[n], len_recv.at[n], peer).start()
        for k in range(1, 8):
            send(
                small_own,
                small_all.at[shard],
                small_send.at[k - 1],
                small_recv.at[k - 1],
                at.shard_after(k),
            ).start()

    def unpack_small():
        for n in (13, 14, 15):
            load(n).wait()
        for n, (peer, other) in enumerate(plane_peers):
            arrived(len_all.at[other], len_recv.at[n], peer)
        for k in range(1, 8):
            arrived(
                small_all.at[(shard + 8 - k) % 8], small_recv.at[k - 1], at.shard_after(8 - k)
            )
        for number, row in enumerate((0, 8, 16, 24, 56, 96)):
            for n in range(8):
                source = row + n
                vectors[number : number + 1, n * 128 : (n + 1) * 128] = small_all[
                    source // 13, source % 13 : source % 13 + 1
                ]
        for c in range(3):
            for n in range(2):
                source = 32 + 8 * c + 2 * part + n
                columns = slice((2 * c + n) * 128, (2 * c + n + 1) * 128)
                qkv_bias[:, columns] = small_all[source // 13, pl.ds(source % 13, 1)]
        for g in range(8):
            source = 64 + 4 * g + part
            up_bias[:, g * 128 : (g + 1) * 128] = small_all[source // 13, pl.ds(source % 13, 1)]

    sums[...] = jnp.zeros_like(sums)
    d_qkv_bias[...] = jnp.zeros_like(d_qkv_bias)
    d_up_bias[...] = jnp.zeros_like(d_up_bias)
    block_rows = 64

    def norm_rows(s):
        @pl.loop(0, length // block_rows)
        def _(i):
            r = pl.ds(pl.multiple_of(i * block_rows, block_rows), block_rows)
            values = x_all[s, r, :].astype(f32)
            mean = jnp.mean(values, axis=-1, keepdims=True)
            centred = values - mean
            inverse = lax.rsqrt(
                jnp.mean(centred * centred, axis=-1, keepdims=True) + NORM_EPSILON
            )
            stats[s, r, 0:1] = mean
            stats[s, r, 1:2] = inverse
            unit = centred * inverse
            normed_one[s, r, :] = (unit * vectors[0:1] + vectors[1:2]).astype(bf16)
            normed_two[s, r, :] = (unit * vectors[2:3] + vectors[3:4]).astype(bf16)

    def live_rows(s):
        index = lax.broadcasted_iota(jnp.int32, (length, 1), 0)
        return index.astype(f32) < len_all[s][0:1, 0:1]

    def rotate(value, sign):
        return (
            value * tables[0]
            + sign * pltpu.roll(value, head_cols - ROT // 2, 1) * tables[1]
            + sign * pltpu.roll(value, ROT // 2, 1) * tables[2]
        )

    def project(s):
        norm_rows(s)
        low, high = SPANS[Q]
        value = nn(normed_one[s], flat(w_all[:, :, low:high])) + qkv_bias[...]
        heads_qkv[s, :, 0:head_cols] = rotate(value[:, 0:head_cols], 1.0).astype(bf16)
        heads_qkv[s, :, head_cols : 2 * head_cols] = rotate(
            value[:, head_cols : 2 * head_cols], 1.0
        ).astype(bf16)
        heads_qkv[s, :, 2 * head_cols :] = value[:, 2 * head_cols :].astype(bf16)

    def attend(s):
        cot = cot_all[s]
        back[s] = jnp.where(live_rows(s), cot, jnp.zeros_like(cot))
        queries = heads_qkv[s, :, 0:head_cols]
        keys = heads_qkv[s, :, head_cols : 2 * head_cols]
        values = heads_qkv[s, :, 2 * head_cols :]
        d_mixed = nt(back[s], flat(out_all[...])).astype(bf16)
        row = lax.broadcasted_iota(jnp.int32, (length, length), 0)
        column = lax.broadcasted_iota(jnp.int32, (length, length), 1)
        allowed = (column <= row) & (column.astype(f32) < len_all[s][0:1, 0:1])
        lane = lax.broadcasted_iota(jnp.int32, (length, head_cols), 1)
        zero = jnp.zeros((), bf16)
        mixed_sum = jnp.zeros((length, head_cols), f32)
        d_queries = d_keys = d_values = mixed_sum
        for h in range(head_cols // HD):
            of_head = (lane >= h * HD) & (lane < (h + 1) * HD)
            q_h, k_h, v_h, d_h = (
                jnp.where(of_head, t, zero) for t in (queries, keys, values, d_mixed)
            )
            scores = jnp.where(allowed, nt(q_h, keys) * HD**-0.5, -1e30)
            raised = jnp.exp(scores - jnp.max(scores, axis=-1, keepdims=True))
            weights = raised * (1.0 / jnp.sum(raised, axis=-1, keepdims=True))
            low = weights.astype(bf16)
            mixed_sum = mixed_sum + nn(low, v_h)
            d_weights = nt(d_h, values)
            inner = jnp.sum(weights * d_weights, axis=-1, keepdims=True)
            d_scores = (weights * (d_weights - inner)).astype(bf16)
            d_queries = d_queries + nn(d_scores, k_h)
            d_keys = d_keys + tn(d_scores, q_h)
            d_values = d_values + tn(low, d_h)
        mixed[s] = mixed_sum.astype(bf16)
        for n, value in enumerate(
            (rotate(d_queries * HD**-0.5, -1.0), rotate(d_keys * HD**-0.5, -1.0), d_values)
        ):
            rounded = value.astype(bf16)
            columns = slice(n * head_cols, (n + 1) * head_cols)
            d_projected[s, :, columns] = rounded
            d_qkv_bias[:, columns] += jnp.sum(rounded.astype(f32), axis=0, keepdims=True)

    def gradient(left, right, n):
        low, high = SPANS[n]

        @pl.loop(0, 8)
        def _(f):
            columns = pl.ds(pl.multiple_of(f * 128, 128), 128)
            terms[f, :, low:high] = tn(flat(left[:, :, columns]), flat(right[...])).astype(bf16)

    def to_core(n):
        for other in range(4):
            send(
                piece(terms, 2 * other + 1 - core, n),
                piece(core_in, other, n),
                core_send.at[n, other],
                core_recv.at[n, other],
                at.other_core,
            ).start()

    def add_core(n):
        low, high = SPANS[n]
        for other in (3, 0, 2, 1):
            arrived(piece(core_in, other, n), core_recv.at[n, other], at.other_core)
            terms[2 * other + core, :, low:high] = (
                terms[2 * other + core, :, low:high].astype(f32)
                + core_in[other, :, low:high].astype(f32)
            ).astype(bf16)

    def pass_on(n, me, target):
        low, high = SPANS[n]

        @pl.when(z == me)
        def _():
            own = piece(terms, 2 * target + core, n)
            if me not in (0, 3):
                source = at.down if me < target else at.up
                arrived(piece(line_in, target, n), line_recv.at[n, target], source)
                terms[2 * target + core, :, low:high] = (
                    terms[2 * target + core, :, low:high].astype(f32)
                    + line_in[target, :, low:high].astype(f32)
                ).astype(bf16)
            slot = 4 if me == target + 1 else target
            send(
                own,
                piece(line_in, slot, n),
                line_send.at[n, target],
                line_recv.at[n, slot],
                at.up if me < target else at.down,
            ).start()

    def line_starts(n):
        for target in (3, 2, 1):
            pass_on(n, 0, target)
        for target in (0, 1, 2):
            pass_on(n, 3, target)

    def line_step(n, step):
        for me, target in (((1, 3), (2, 0)), ((1, 2), (2, 1)), ((2, 3), (1, 0)))[step]:
            pass_on(n, me, target)

    wholes = (qkv_all, up_all, down_all)

    def line_ends(n):
        low, high = SPANS[n]
        total = 2 * z + core

        def add(slot, source):
            arrived(piece(line_in, slot, n), line_recv.at[n, slot], source)
            terms[total, :, low:high] = (
                terms[total, :, low:high].astype(f32) + line_in[slot, :, low:high].astype(f32)
            ).astype(bf16)

        @pl.when(z > 0)
        def _():
            add(z, at.down)

        @pl.when(z < 3)
        def _():
            add(4, at.up)

        own = piece(terms, total, n)
        target = wholes[n].at[part]
        send(own, target, all_send.at[n, 0], all_recv.at[n, 0], at.across_x).start()
        send(own, target, all_send.at[n, 1], all_recv.at[n, 1], at.across_y).start()
        pltpu.make_async_copy(own, target, keep_sem.at[n]).start()

    def share(n):
        whole = wholes[n]
        arrived(whole.at[at.x_part], all_recv.at[n, 0], at.across_x)
        block = whole.at[at.x_part, 0:64]
        send(block, block, all_send.at[n, 2], all_recv.at[n, 2], at.across_y).start()
        arrived(whole.at[at.y_part], all_recv.at[n, 1], at.across_y)
        block = whole.at[at.y_part, 64:128]
        send(block, block, all_send.at[n, 3], all_recv.at[n, 3], at.across_x).start()

    def out_to_core():
        send(
            out_term.at[1 - core], out_core_in, rows_send.at[0], rows_recv.at[0], at.other_core
        ).start()

    def out_add(block):
        out_line[...] = (out_line[...].astype(f32) + block.astype(f32)).astype(bf16)

    def out_add_core():
        arrived(out_core_in, rows_recv.at[0], at.other_core)
        out_line[...] = out_term[core]
        out_add(out_core_in[...])

    def out_step(step):
        @pl.when((z == step) & (z < part))
        def _():
            if step > 0:
                arrived(out_line_in.at[0], rows_recv.at[1], at.down)
                out_add(out_line_in[0])
            send(out_line, out_line_in.at[0], rows_send.at[1], rows_recv.at[1], at.up).start()

        @pl.when((z == 3 - step) & (z > part))
        def _():
            if step > 0:
                arrived(out_line_in.at[1], rows_recv.at[2], at.up)
                out_add(out_line_in[1])
            send(out_line, out_line_in.at[1], rows_send.at[1], rows_recv.at[2], at.down).start()

    def out_ends():
        @pl.when(z == part)
        def _():
            @pl.when(z > 0)
            def _():
                arrived(out_line_in.at[0], rows_recv.at[1], at.down)
                out_add(out_line_in[0])

            @pl.when(z < 3)
            def _():
                arrived(out_line_in.at[1], rows_recv.at[2], at.up)
                out_add(out_line_in[1])

            for r, (peer, _) in enumerate(neighbours):
                send(out_line, out_grad, rows_send.at[2 + r], rows_recv.at[3], peer).start()
            pltpu.make_async_copy(out_line, out_grad, keep_sem.at[3]).start()

    def out_share():
        for r, (peer, source) in enumerate(neighbours):

            @pl.when(z == source)
            def _():
                arrived(out_grad, rows_recv.at[3], peer)
                block = out_grad.at[64 * r : 64 * r + 64]
                onward = neighbours[1 - r][0]
                send(block, block, rows_send.at[4], rows_recv.at[4 + r], onward).start()

    def out_gradient():
        for n in range(2):
            columns = slice(n * 128, (n + 1) * 128)
            out_term[n] = tn(flat(mixed[:, :, columns]), flat(back[...])).astype(bf16)

    part_refs = (out_part, dx_part)
    routes = (
        (halves[0], at.across_x, at.x_part, at.across_y, at.y_part),
        (halves[1], at.across_y, at.y_part, at.across_x, at.x_part),
    )

    def send_part(n, r, m):
        half, peer, peer_part, _, _ = routes[r]
        target = (at.far_part, peer_part)[m]
        send(
            part_refs[n].at[target, half],
            plane_one.at[n, r, m],
            part_send.at[n, r, m],
            part_recv.at[n, r, m],
            peer,
        ).start()

    def turn_part(n, r):
        half, peer, _, turn, turned = routes[r]
        arrived(plane_one.at[n, r, 0], part_recv.at[n, r, 0], peer)
        plane_turn[n, r] = (
            part_refs[n][turned, half].astype(f32) + plane_one[n, r, 0].astype(f32)
        ).astype(bf16)
        send(
            plane_turn.at[n, r],
            plane_two.at[n, r],
            part_send.at[n, r, 2],
            part_recv.at[n, r, 2],
            turn,
        ).start()

    def whole_part(n, r):
        half, peer, _, turn, _ = routes[r]
        arrived(plane_one.at[n, r, 1], part_recv.at[n, r, 1], peer)
        arrived(plane_two.at[n, r], part_recv.at[n, r, 2], turn)
        return (
            part_refs[n][part, half].astype(f32)
            + plane_one[n, r, 1].astype(f32)
            + plane_two[n, r].astype(f32)
        )

    up_low, up_high = SPANS[U]
    down_low, down_high = SPANS[N]

    def feed_in(s):
        value = nn(normed_two[s], flat(w_all[:, :, up_low:up_high])) + up_bias[...]
        hidden[s] = value
        activated[s] = (value * (0.5 * (1.0 + lax.erf(value * 2.0**-0.5)))).astype(bf16)

    def feed_out(s):
        out_part[s] = (
            nn(activated[s], flat(w_all[:, :, down_low:down_high]))
            + nn(mixed[s], flat(out_all[...]))
        ).astype(bf16)

    def feed_back(s):
        slope = gelu_slope(hidden[s])
        low = (nt(back[s], flat(w_all[:, :, down_low:down_high])) * slope).astype(bf16)
        d_hidden[s] = low
        d_up_bias[...] += jnp.sum(low.astype(f32), axis=0, keepdims=True)

    def norm_back(s):
        d_two = nt(d_hidden[s], flat(w_all[:, :, up_low:up_high]))
        d_one = nt(d_projected[s], flat(w_all[:, :, SPANS[Q][0] : SPANS[Q][1]]))
        unit = (x_all[s].astype(f32) - stats[s][:, 0:1]) * stats[s][:, 1:2]
        sums[0:1] += jnp.sum(d_one * unit, axis=0, keepdims=True)
        sums[1:2] += jnp.sum(d_one, axis=0, keepdims=True)
        sums[2:3] += jnp.sum(d_two * unit, axis=0, keepdims=True)
        sums[3:4] += jnp.sum(d_two, axis=0, keepdims=True)
        dx_part[s] = (d_one * vectors[0:1] + d_two * vectors[2:3]).astype(bf16)

    def place(row, value):
        small_part[row // 13, pl.ds(row % 13, 1)] = value

    def small_start():
        small_part[...] = jnp.zeros_like(small_part)
        back_total = jnp.sum(back[part].astype(f32), axis=0, keepdims=True)
        for n in range(8):
            columns = slice(n * 128, (n + 1) * 128)
            for number in range(4):
                place(8 * number + n, sums[number : number + 1, columns])
            place(56 + n, back_total[:, columns])
            place(96 + n, back_total[:, columns])
            place(64 + 4 * n + part, d_up_bias[:, columns])
        for c in range(3):
            for n in range(2):
                columns = slice((2 * c + n) * 128, (2 * c + n + 1) * 128)
                place(32 + 8 * c + 2 * part + n, d_qkv_bias[:, columns])
        for k in range(1, 8):
            send(
                small_part.at[(shard + k) % 8],
                small_in.at[k - 1],
                total_send.at[k - 1],
                total_recv.at[k - 1],
                at.shard_after(k),
            ).start()

    def small_turn():
        total = small_part[shard]
        for k in range(1, 8):
            arrived(small_in.at[k - 1], total_recv.at[k - 1], at.shard_after(8 - k))
            total = total + small_in[k - 1]
        small_total[...] = total
        for n, (peer, _) in enumerate(plane_peers):
            send(
                small_total, small_plane.at[part], total_send.at[7 + n], total_recv.at[7 + n], peer
            ).start()
        small_plane[part] = total

    def small_end():
        for n, (peer, other) in enumerate(plane_peers):
            arrived(small_plane.at[other], total_recv.at[7 + n], peer)
        small_sum[...] = (small_plane[0] + small_plane[1]) + (small_plane[2] + small_plane[3])

    def write_output(r):
        half = halves[r]
        values = x_all[part, half].astype(f32)
        summed = values + whole_part(0, r) + vectors[4:5] + vectors[5:6]
        output[half] = jnp.where(live_rows(part)[half], summed, 0.0).astype(bf16)
        pltpu.make_async_copy(output.at[half], output_out.at[half], store_sem.at[0, r]).start()

    def write_input_grad(r):
        half = halves[r]
        scaled = whole_part(1, r)
        inverse = stats[part, half, 1:2]
        unit = (x_all[part, half].astype(f32) - stats[part, half, 0:1]) * inverse
        result = back[part, half].astype(f32) + inverse * (
            scaled
            - jnp.mean(scaled, axis=-1, keepdims=True)
            - unit * jnp.mean(scaled * unit, axis=-1, keepdims=True)
        )
        input_grad[half] = result.astype(bf16)
        pltpu.make_async_copy(
            input_grad.at[half], input_grad_out.at[half], store_sem.at[1, r]
        ).start()

    at_end = (z == 0) | (z == 3)
    middle = (z == 1) | (z == 2)
    send_activations()
    send_own(Q)
    send_out_rows()
    send_small()

    @pl.when(at_end)
    def _():
        send_rest()

    @pl.when(middle)
    def _():
        forward(1, Q)
        forward_out(1)
        forward(2, Q)

    send_own(U)
    forward_x(0)

    @pl.when(at_end)
    def _():
        forward_out(1)

    @pl.when(middle)
    def _():
        forward_out(2)
        from_core(Q)
        send_own(N)
        send_rest()

    forward_y(0)

    @pl.when(at_end)
    def _():
        forward(1, Q)
        forward(2, Q)
        forward(3, Q)
        send_own(N)
        from_core(Q)

    unpack_small()

    @pl.loop(0, 4)
    def _(i):
        project(near_first(i))

        @pl.when((i == 0) & at_end)
        def _():
            forward_y(1)
            forward_out(2)

        @pl.when(i == 2)
        def _():
            forward_x(1)

        @pl.when((i == 2) & at_end)
        def _():
            forward_out(3)

        @pl.when((i == 2) & middle)
        def _():
            forward(1, U)
            forward_y(1)

        @pl.when(i == 2)
        def _():
            far_halves(0)

        @pl.when((i == 2) & middle)
        def _():
            forward(1, N)

    out_from_core()

    @pl.loop(0, 4)
    def _(i):
        attend(near_first(i))

        @pl.when((i == 0) & middle)
        def _():
            forward(2, U)

        @pl.when((i == 1) & middle)
        def _():
            far_halves(1)

        @pl.when((i == 2) & at_end)
        def _():
            forward(1, U)
            far_halves(1)

        @pl.when((i == 2) & middle)
        def _():
            forward(2, N)

    gradient(normed_one, d_projected, Q)

    @pl.when(at_end)
    def _():
        to_core(Q)

    @pl.when(middle)
    def _():
        from_core(U)
        from_core(N)

    out_gradient()

    @pl.when(at_end)
    def _():
        forward(2, U)
        forward(3, U)
        forward(1, N)
        add_core(Q)
        line_starts(Q)
        from_core(U)

    @pl.loop(0, 4)
    def _(i):
        feed_in(i)

        @pl.when((i == 0) & at_end)
        def _():
            forward(2, N)

        @pl.when((i == 0) & middle)
        def _():
            to_core(Q)

    @pl.when(at_end)
    def _():
        forward(3, N)

    gradient(activated, back, N)

    @pl.when(at_end)
    def _():
        out_to_core()
        from_core(N)

    @pl.loop(0, 4)
    def _(i):
        feed_out(far_first(i))

        @pl.when((i == 0) & middle)
        def _():
            add_core(Q)

        @pl.when(i == 0)
        def _():
            send_part(0, 0, 0)
            send_part(0, 1, 0)

        @pl.when((i == 1) & at_end)
        def _():
            out_add_core()
            out_step(0)
            to_core(N)

        @pl.when((i == 2) & middle)
        def _():
            send_part(0, 1, 1)

    @pl.loop(0, 4)
    def _(i):
        feed_back(far_first(i))

        @pl.when((i == 0) & middle)
        def _():
            out_to_core()
            out_add_core()
            line_step(Q, 0)
            line_step(Q, 1)
            send_part(0, 0, 1)
            to_core(N)

        @pl.when((i == 1) & at_end)
        def _():
            send_part(0, 1, 1)
            add_core(N)
            line_starts(N)
            turn_part(0, 0)

        @pl.when((i == 2) & at_end)
        def _():
            send_part(1, 0, 1)

        @pl.when((i == 2) & middle)
        def _():
            out_step(1)

        @pl.when((i == 3) & at_end)
        def _():
            send_part(0, 0, 1)

        @pl.when((i == 3) & middle)
        def _():
            line_step(Q, 2)
            send_part(1, 1, 1)

        norm_back(far_first(i))

        @pl.when((i == 0) & at_end)
        def _():
            send_part(1, 0, 0)
            send_part(1, 1, 0)

        @pl.when((i == 0) & middle)
        def _():
            add_core(N)

        @pl.when((i == 1) & middle)
        def _():
            send_part(1, 0, 0)
            send_part(1, 1, 0)
            turn_part(0, 1)

    @pl.when(middle)
    def _():
        turn_part(0, 0)
        line_ends(Q)

    gradient(normed_two, d_hidden, U)

    @pl.when(middle)
    def _():
        to_core(U)
        send_part(1, 0, 1)
        line_step(N, 0)

    turn_part(1, 1)

    @pl.when(at_end)
    def _():
        to_core(U)
        send_part(1, 1, 1)

    @pl.when(middle)
    def _():
        turn_part(1, 0)

    add_core(U)

    @pl.when(at_end)
    def _():
        line_starts(U)
        line_ends(Q)
        turn_part(1, 0)

    @pl.when(middle)
    def _():
        line_step(N, 1)
        out_step(2)

    small_start()

    @pl.when(middle)
    def _():
        write_output(1)
        line_step(N, 2)
        line_step(U, 0)
        write_output(0)
        line_ends(N)
        share(Q)

    out_ends()

    @pl.when(at_end)
    def _():
        turn_part(0, 1)
        write_output(0)
        share(Q)
        line_ends(N)

    @pl.when(middle)
    def _():
        line_step(U, 1)
        line_step(U, 2)
        share(N)
        write_input_grad(0)
        line_ends(U)
        out_share()

    small_turn()

    @pl.when(at_end)
    def _():
        out_share()
        line_ends(U)

    @pl.when(middle)
    def _():
        share(U)

    write_input_grad(1)
    small_end()

    @pl.when(at_end)
    def _():
        write_output(1)
        share(N)
        share(U)
        write_input_grad(0)

    for r, half in enumerate(halves):
        pltpu.make_async_copy(output.at[half], output_out.at[half], store_sem.at[0, r]).wait()
        pltpu.make_async_copy(
            input_grad.at[half], input_grad_out.at[half], store_sem.at[1, r]
        ).wait()
    @pl.when(z == at.far_part)
    def _():
        for r, (peer, _) in enumerate(neighbours):
            arrived(out_grad.at[64 * r : 64 * r + 64], rows_recv.at[4 + r], neighbours[1 - r][0])

    @pl.when(z != part)
    def _():
        sent(out_line, rows_send.at[1], at.up)

    @pl.when((z == at.x_part) | (z == at.y_part))
    def _():
        sent(out_line.at[0:64], rows_send.at[4], at.across_x)

    @pl.when(z == part)
    def _():
        for r, (peer, _) in enumerate(neighbours):
            sent(out_line, rows_send.at[2 + r], peer)
        pltpu.make_async_copy(out_line, out_grad, keep_sem.at[3]).wait()

    sent(out_line, rows_send.at[0], at.other_core)
    for r, (peer, _) in enumerate(neighbours):
        sent(x_own, plane_send.at[0, r], peer)
        sent(cot_own.at[halves[0]], early_send.at[r], peer)
        sent(cot_own.at[halves[1]], plane_send.at[1, r], peer)
        for n in range(2):
            sent(x_all.at[part, halves[0]], plane_send.at[n, 2 + r], peer)
    for n, (peer, _) in enumerate(plane_peers):
        sent(len_all.at[part], len_send.at[n], peer)
        sent(small_total, total_send.at[7 + n], peer)
    for k in range(1, 8):
        sent(small_own, small_send.at[k - 1], at.shard_after(k))
        sent(small_total, total_send.at[k - 1], at.shard_after(k))
    for n in range(3):
        for other in range(4):
            block = piece(w_all, 2 * other + core, n)
            sent(block, w_send.at[2, n, other], at.other_core)
            sent(block, core_send.at[n, other], at.other_core)

            @pl.when((other <= z) & (z < 3))
            def _():
                sent(block, w_send.at[0, n, other], at.up)

            @pl.when((other >= z) & (z > 0))
            def _():
                sent(block, w_send.at[1, n, other], at.down)

            @pl.when(z != other)
            def _():
                sent(block, line_send.at[n, other], at.up)

    block = out_all.at[core]
    sent(block, out_send.at[2], at.other_core)

    @pl.when((z >= part) & (z < 3))
    def _():
        sent(block, out_send.at[0], at.up)

    @pl.when((z <= part) & (z > 0))
    def _():
        sent(block, out_send.at[1], at.down)

    for n in range(2):
        for r in range(2):
            for m in range(3):
                sent(plane_turn.at[n, r], part_send.at[n, r, m], at.across_x)
    for n, whole in enumerate(wholes):
        arrived(whole.at[at.far_part, 0:64], all_recv.at[n, 2], at.across_y)
        arrived(whole.at[at.far_part, 64:128], all_recv.at[n, 3], at.across_x)
        own = piece(terms, shard, n)
        sent(own, all_send.at[n, 0], at.across_x)
        sent(own, all_send.at[n, 1], at.across_y)
        sent(whole.at[part, 0:64], all_send.at[n, 2], at.across_y)
        sent(whole.at[part, 64:128], all_send.at[n, 3], at.across_x)
        pltpu.make_async_copy(own, whole.at[part], keep_sem.at[n]).wait()


VMEM_SPEC = pl.BlockSpec(memory_space=pltpu.VMEM)
HBM_SPEC = pl.BlockSpec(memory_space=pl.ANY)


def whole_layer(lengths, x_own, cot_own, masters, tables):
    shape = jax.ShapeDtypeStruct
    vmem, dma = pltpu.VMEM, pltpu.SemaphoreType.DMA
    bf16, f32 = jnp.bfloat16, jnp.float32
    length = x_own.shape[0]
    group = 4
    head_cols, wide, rows = D // group, 2816, 128

    def by_sequence(width, kind=bf16):
        return vmem((group, length, width), kind)

    return pl.pallas_call(
        layer_kernel,
        out_shape=(
            shape(x_own.shape, bf16),
            shape(x_own.shape, bf16),
            shape((group, rows, 3 * head_cols), bf16),
            shape((group, rows, FF // group), bf16),
            shape((group, rows, D), bf16),
            shape((rows, D), bf16),
            shape((16, 128), f32),
        ),
        in_specs=[pl.BlockSpec(memory_space=pltpu.SMEM)]
        + [HBM_SPEC] * 6
        + [VMEM_SPEC, HBM_SPEC],
        out_specs=(HBM_SPEC,) * 6 + (VMEM_SPEC,),
        scratch_shapes=[
            vmem(tables.shape, f32),
            vmem(x_own.shape, bf16),
            vmem(x_own.shape, bf16),
            by_sequence(D),
            by_sequence(D),
            vmem((group, 8, 128), f32),
            vmem((8, rows, wide), bf16),
            vmem((2, rows, D), bf16),
            vmem((16, 128), f32),
            vmem((8, 16, 128), f32),
            vmem((8, D), f32),
            vmem((1, 3 * head_cols), f32),
            vmem((1, FF // group), f32),
            by_sequence(128, f32),
            by_sequence(D),
            by_sequence(D),
            by_sequence(D),
            by_sequence(3 * head_cols),
            by_sequence(head_cols),
            by_sequence(3 * head_cols),
            by_sequence(FF // group, f32),
            by_sequence(FF // group),
            by_sequence(D),
            by_sequence(D),
            vmem((8, rows, wide), bf16),
            vmem((2, rows, D), bf16),
            vmem((8, D), f32),
            vmem((1, 3 * head_cols), f32),
            vmem((1, FF // group), f32),
            vmem((8, 16, 128), f32),
            vmem((2, 2, 2, HALF, D), bf16),
            vmem((2, 2, HALF, D), bf16),
            vmem((2, 2, HALF, D), bf16),
            vmem((4, rows, wide), bf16),
            vmem((5, rows, wide), bf16),
            vmem((rows, D), bf16),
            vmem((rows, D), bf16),
            vmem((2, rows, D), bf16),
            vmem((7, 16, 128), f32),
            vmem((16, 128), f32),
            vmem((4, 16, 128), f32),
            dma((16,)),
            dma((2, 4)),
            dma((2, 4)),
            dma((2,)),
            dma((2,)),
            dma((3,)),
            dma((3,)),
            dma((3, 3, 4)),
            dma((3, 8)),
            dma((3,)),
            dma((2,)),
            dma((7,)),
            dma((7,)),
            dma((2, 2, 3)),
            dma((2, 2, 3)),
            dma((3, 4)),
            dma((3, 4)),
            dma((3, 4)),
            dma((3, 5)),
            dma((5,)),
            dma((6,)),
            dma((3, 4)),
            dma((3, 4)),
            dma((4,)),
            dma((10,)),
            dma((10,)),
            dma((2, 2)),
        ],
        compiler_params=pltpu.CompilerParams(
            collective_id=0, has_side_effects=True, vmem_limit_bytes=56 << 20
        ),
        name="layer",
    )(lengths, x_own, cot_own, *masters, tables)


def rope_tables(length, heads):
    half = ROT // 2
    angle = np.arange(length)[:, None] * ROPE_BASE ** (-2.0 * np.arange(half) / ROT)[None]
    table = np.zeros((3, length, HD), np.float32)
    table[0] = 1.0
    table[0, :, :half] = table[0, :, half:ROT] = np.cos(angle)
    table[1, :, :half] = -np.sin(angle)
    table[2, :, half:ROT] = np.sin(angle)
    return jnp.asarray(np.tile(table, (1, 1, heads)))


def local_split(
    tokens_in,
    cotangent,
    lengths,
    qkv_master,
    out_master,
    up_master,
    down_master,
    small_master,
    qkv_first,
    out_first,
    up_first,
    down_first,
    small_first,
    qkv_second,
    out_second,
    up_second,
    down_second,
    small_second,
):
    masters = (qkv_master, out_master, up_master, down_master, small_master)
    firsts = (qkv_first, out_first, up_first, down_first, small_first)
    seconds = (qkv_second, out_second, up_second, down_second, small_second)
    parts, shards = lax.axis_size("dp"), lax.axis_size("fsdp")
    part, shard = lax.axis_index("dp"), lax.axis_index("fsdp")
    length = tokens_in.shape[1]
    update = (masters, firsts, seconds)
    if (parts, shards) == (4, 8):
        tall = tuple(masters[:4]) + (small_master.reshape(-1, 128),)
        output, input_grad, qkv_grad, up_grad, down_grad, out_grad, small_sum = whole_layer(
            lengths, tokens_in[0], cotangent[0], tall, rope_tables(length, HEADS // parts)
        )
        grads = (qkv_grad, out_grad, up_grad, down_grad, small_sum[: tall[4].shape[0]])
        return lamb_split(*update, grads, (output, input_grad))

    head_cols = D // parts
    ff_rows = down_master.shape[0] // parts
    qkv_own = sliced(qkv_master, part, parts, 3).astype(jnp.bfloat16)
    up_own = sliced(up_master, part, parts, shards).astype(jnp.bfloat16)
    down_own = lax.dynamic_slice_in_dim(down_master, part * ff_rows, ff_rows).astype(jnp.bfloat16)
    out_own = out_master.astype(jnp.bfloat16)
    small_own = small_master.astype(jnp.bfloat16)

    def small_vectors(small_all):
        vectors = split_small(small_all)
        vectors[4] = sliced(vectors[4][None], part, parts, 3)[0]
        vectors[6] = sliced(vectors[6][None], part, parts, shards)[0]
        return vectors

    def over_shards(own):
        return lax.all_gather(own, "fsdp", axis=0, tiled=True)

    x_all = lax.all_gather(tokens_in, "dp", axis=0, tiled=True)
    cotangent_all = lax.all_gather(cotangent, "dp", axis=0, tiled=True)
    lengths_all = lax.all_gather(lengths, "dp", axis=0, tiled=True)
    qkv_weight, up_weight, down_weight = (over_shards(w) for w in (qkv_own, up_own, down_own))
    out_weight = lax.dynamic_slice_in_dim(over_shards(out_own), part * head_cols, head_cols)
    gain_one, shift_one, gain_two, shift_two, qkv_bias, out_bias, up_bias, down_bias = (
        small_vectors(over_shards(small_own).astype(jnp.float32))
    )
    out_part, scaled_part, terms, sums = layer(
        x_all,
        cotangent_all,
        lengths_all,
        (qkv_weight, out_weight, up_weight, down_weight),
        (gain_one, shift_one, gain_two, shift_two, qkv_bias, up_bias),
        part,
    )
    norm_sums, d_qkv_bias, d_up_bias = sums
    out_sum = lax.psum_scatter(out_part, "dp", scatter_dimension=0, tiled=True)
    scaled = lax.psum_scatter(scaled_part, "dp", scatter_dimension=0, tiled=True)
    out_sum, scaled = out_sum.astype(jnp.float32), scaled.astype(jnp.float32)

    inputs = tokens_in[0].astype(jnp.float32)
    live = (jnp.arange(length) < lengths[0]).astype(jnp.float32)[:, None]
    back = cotangent[0].astype(jnp.float32) * live
    back_total = jnp.sum(back, axis=0)

    def spread(values, pieces):
        wide = jnp.zeros((pieces, parts, values.shape[0] // pieces), jnp.float32)
        return lax.dynamic_update_index_in_dim(
            wide, values.reshape(pieces, -1), part, axis=1
        ).reshape(-1)

    small_grad = jnp.concatenate(
        [
            norm_sums.reshape(4 * D),
            spread(d_qkv_bias, 3),
            back_total,
            spread(d_up_bias, shards),
            back_total,
        ]
    )
    small_sum = lax.psum(small_grad, ("dp", "fsdp"))
    small_rows = small_master.shape[0]
    small_sum = lax.dynamic_slice_in_dim(small_sum, shard * small_rows, small_rows)
    qkv_term, out_term, up_term, down_term = terms
    out_wide = lax.dynamic_update_slice_in_dim(
        jnp.zeros((D, D), jnp.bfloat16), out_term, part * head_cols, axis=0
    )

    def to_owner(term):
        own = lax.psum_scatter(term, "fsdp", scatter_dimension=0, tiled=True)
        return lax.all_gather(own, "dp", axis=0, tiled=False).astype(jnp.float32)

    reduced = (
        joined(to_owner(qkv_term), 3),
        lax.psum(
            lax.psum_scatter(out_wide, "fsdp", scatter_dimension=0, tiled=True), "dp"
        ).astype(jnp.float32),
        joined(to_owner(up_term), shards),
        to_owner(down_term).reshape(down_master.shape),
        small_sum,
    )

    unit_rows, inverse_rows = normalize(inputs)
    output = ((inputs + out_sum + out_bias + down_bias) * live).astype(jnp.bfloat16)
    input_grad = back + inverse_rows * (
        scaled
        - jnp.mean(scaled, axis=-1, keepdims=True)
        - unit_rows * jnp.mean(scaled * unit_rows, axis=-1, keepdims=True)
    )
    return (output[None], input_grad.astype(jnp.bfloat16)[None]) + lamb(*update, reduced)


def lamb_rows(first_old, second_old, master, grad):
    first_new = BETA_ONE * first_old + (1.0 - BETA_ONE) * grad
    second_new = BETA_TWO * second_old + (1.0 - BETA_TWO) * grad * grad
    root = second_new * lax.rsqrt(second_new)
    update = first_new / (root + ADAM_EPSILON) + DECAY * master
    return first_new, second_new, update


def lane_sums(values):
    squares = jnp.sum(values * values, axis=0, keepdims=True)
    total = squares[:, 0:128]
    for n in range(1, squares.shape[1] // 128):
        total = total + squares[:, n * 128 : (n + 1) * 128]
    return total


def moments_kernel(*refs):
    qkv_grad, out_grad, up_grad, down_grad, small_grad = refs[0:5]
    masters, firsts, seconds = refs[5:10], refs[10:15], refs[15:20]
    first_news, second_news, updates, squares = refs[20:25], refs[25:30], refs[30:35], refs[35]
    step = pl.program_id(0)

    @pl.when(step == 0)
    def _():
        squares[...] = jnp.zeros_like(squares)

    def one(number, span, grad):
        index = (slice(None), span)
        rows = firsts[number].shape[0]
        place = (pl.ds(pl.multiple_of(step * rows, rows), rows), span)
        master = masters[number][place]
        first_new, second_new, update = lamb_rows(
            firsts[number][index], seconds[number][index], master, grad
        )
        first_news[number][index] = first_new
        second_news[number][index] = second_new
        updates[number][place] = update
        return lane_sums(master), lane_sums(update)

    def add(number, pairs):
        weight, update = pairs[0]
        for more_weight, more_update in pairs[1:]:
            weight, update = weight + more_weight, update + more_update
        squares[number : number + 1] += weight
        squares[8 + number : 9 + number] += update

    f32 = jnp.float32
    parts = qkv_grad.shape[0]
    width = qkv_grad.shape[2] // 3
    add(
        0,
        [
            one(
                0,
                slice((c * parts + d) * width, (c * parts + d + 1) * width),
                qkv_grad[d, :, c * width : (c + 1) * width].astype(f32),
            )
            for c in range(3)
            for d in range(parts)
        ],
    )
    add(1, [one(1, slice(None), out_grad[...].astype(f32))])
    pieces = up_grad.shape[2] // 128
    add(
        2,
        [
            one(
                2,
                slice((g * parts + d) * 128, (g * parts + d + 1) * 128),
                up_grad[d, :, g * 128 : (g + 1) * 128].astype(f32),
            )
            for g in range(pieces)
            for d in range(parts)
        ],
    )
    add(3, [one(3, slice(None), down_grad[0].astype(f32))])

    @pl.when(step == 0)
    def _():
        first_new, second_new, update = lamb_rows(
            firsts[4][...], seconds[4][...], masters[4][...], small_grad[...]
        )
        first_news[4][...] = first_new
        second_news[4][...] = second_new
        updates[4][...] = update
        squares[4:5] += lane_sums(masters[4][...])
        squares[12:13] += lane_sums(update)


def lamb_specs(masters, steps):
    specs = [pl.BlockSpec((m.shape[0] // steps, m.shape[1]), lambda i: (i, 0)) for m in masters[:4]]
    return specs + [pl.BlockSpec(masters[4].shape, lambda i: (0, 0))]


def moments(grads, masters, firsts, seconds, steps=4):
    qkv_grad, out_grad, up_grad, down_grad, small_grad = grads
    shape = jax.ShapeDtypeStruct
    each = lamb_specs(masters, steps)
    rows = qkv_grad.shape[1]
    halves = steps // qkv_grad.shape[0]
    grad_specs = [
        pl.BlockSpec((qkv_grad.shape[0], rows // steps, qkv_grad.shape[2]), lambda i: (0, i, 0)),
        each[1],
        pl.BlockSpec((up_grad.shape[0], rows // steps, up_grad.shape[2]), lambda i: (0, i, 0)),
        pl.BlockSpec(
            (1, rows // halves, down_grad.shape[2]), lambda i: (i // halves, i % halves, 0)
        ),
        each[4],
    ]
    out = [shape(m.shape, jnp.float32) for m in masters]
    near = [pltpu.VMEM(m.shape, jnp.float32) for m in masters]
    results = pl.pallas_call(
        moments_kernel,
        grid=(steps,),
        in_specs=grad_specs + [VMEM_SPEC] * 5 + each * 2,
        out_specs=each * 2 + [VMEM_SPEC] * 5 + [pl.BlockSpec((16, 128), lambda i: (0, 0))],
        out_shape=out * 2 + near + [shape((16, 128), jnp.float32)],
        compiler_params=pltpu.CompilerParams(vmem_limit_bytes=24 << 20),
        name="moments",
    )(*grads, *masters, *firsts, *seconds)
    return results[0:5], results[5:10], results[10:15], results[15]


def norms_kernel(squares, total, everyone, send_sem, recv_sem):
    shard, part = lax.axis_index("fsdp"), lax.axis_index("dp")
    peers = [(part, (shard + k) % 8) for k in range(1, 8)]
    barrier = pltpu.get_barrier_semaphore()
    for peer in peers:
        pl.semaphore_signal(barrier, inc=1, device_id=peer, device_id_type=MESH_ID)
    pl.semaphore_wait(barrier, 7)
    for k in range(1, 8):
        send(
            squares, everyone.at[shard], send_sem.at[k - 1], recv_sem.at[k - 1], peers[k - 1]
        ).start()
    everyone[shard] = squares[...]
    for k in range(1, 8):
        arrived(everyone.at[(shard + 8 - k) % 8], recv_sem.at[k - 1], peers[7 - k])
    summed = everyone[0]
    for k in range(1, 8):
        summed = summed + everyone[k]
    norms = jnp.sqrt(jnp.sum(summed, axis=1, keepdims=True))
    total[...] = jnp.broadcast_to(norms, (16, 128))
    for k in range(1, 8):
        sent(squares, send_sem.at[k - 1], peers[k - 1])


def norms(squares):
    dma = pltpu.SemaphoreType.DMA
    return pl.pallas_call(
        norms_kernel,
        out_shape=jax.ShapeDtypeStruct((16, 128), jnp.float32),
        in_specs=[VMEM_SPEC],
        out_specs=VMEM_SPEC,
        scratch_shapes=[pltpu.VMEM((8, 16, 128), jnp.float32), dma((7,)), dma((7,))],
        compiler_params=pltpu.CompilerParams(
            collective_id=1, has_side_effects=True, vmem_limit_bytes=2 << 20
        ),
        name="norms",
    )(squares)


def step_kernel(*refs):
    total, masters, updates, layer_outs = refs[0], refs[1:6], refs[6:11], refs[11:13]
    news, outs, lamb_norms = refs[13:18], refs[18:20], refs[20]
    step = pl.program_id(0)
    for number in range(5):
        weight_norm = total[number : number + 1, 0:1]
        update_norm = total[8 + number : 9 + number, 0:1]
        scale = RATE * (weight_norm / update_norm)
        rows = news[number].shape[0]
        place = slice(None)
        if rows < masters[number].shape[0]:
            place = pl.ds(pl.multiple_of(step * rows, rows), rows)
        news[number][...] = masters[number][place] - scale * updates[number][place]
    for source, target in zip(layer_outs, outs):
        target[...] = source[...]

    @pl.when(step == 0)
    def _():
        row = lax.broadcasted_iota(jnp.int32, (8, 128), 0)
        lane = lax.broadcasted_iota(jnp.int32, (8, 128), 1)
        for n in range(2):
            half = jnp.where(row == lane, total[8 * n : 8 * n + 8], 0.0)
            lamb_norms[n : n + 1] = jnp.sum(half, axis=0, keepdims=True)[:, 0:5]


def step_masters(total, masters, updates, layer_outs, steps=4):
    shape = jax.ShapeDtypeStruct
    out_specs = [
        pl.BlockSpec((o.shape[0] // steps, o.shape[1]), lambda i: (i, 0)) for o in layer_outs
    ]
    results = pl.pallas_call(
        step_kernel,
        grid=(steps,),
        in_specs=[pl.BlockSpec((16, 128), lambda i: (0, 0))] + [VMEM_SPEC] * 10 + out_specs,
        out_specs=lamb_specs(masters, steps)
        + out_specs
        + [pl.BlockSpec((2, 5), lambda i: (0, 0))],
        out_shape=[shape(m.shape, jnp.float32) for m in masters]
        + [shape(o.shape, o.dtype) for o in layer_outs]
        + [shape((2, 5), jnp.float32)],
        compiler_params=pltpu.CompilerParams(vmem_limit_bytes=12 << 20),
        name="step_masters",
    )(total, *masters, *updates, *layer_outs)
    return results[0:5], results[5:7], results[7]


def lamb_split(masters, firsts, seconds, grads, layer_outs):
    def tall(arrays):
        return tuple(arrays[:4]) + (arrays[4].reshape(-1, 128),)

    def flat_small(arrays):
        return tuple(arrays[:4]) + (arrays[4].reshape(-1),)

    def placed(arrays, space):
        return tuple(pltpu.with_memory_space_constraint(a, space) for a in arrays)

    masters = placed(tall(masters), pltpu.VMEM)
    firsts, seconds = placed(tall(firsts), pltpu.HBM), placed(tall(seconds), pltpu.HBM)
    grads = placed(grads[:4], pltpu.HBM) + (grads[4],)
    first_news, second_news, updates, squares = moments(grads, masters, firsts, seconds)
    news, outs, lamb_norms = step_masters(norms(squares), masters, updates, layer_outs)
    return (
        tuple(out[None] for out in outs)
        + flat_small(news)
        + flat_small(first_news)
        + flat_small(second_news)
        + (lamb_norms,)
    )


def lamb(masters, firsts, seconds, reduced):
    updates = []
    first_news = []
    second_news = []
    for first_old, second_old, master, grad_sum in zip(firsts, seconds, masters, reduced):
        first_new = BETA_ONE * first_old + (1.0 - BETA_ONE) * grad_sum
        second_new = BETA_TWO * second_old + (1.0 - BETA_TWO) * grad_sum * grad_sum
        updates.append(first_new / (jnp.sqrt(second_new) + ADAM_EPSILON) + DECAY * master)
        first_news.append(first_new)
        second_news.append(second_new)
    weight_squares, update_squares = lax.psum(
        (local_squares(masters), local_squares(updates)), "fsdp"
    )
    weight_norms = jnp.sqrt(weight_squares)
    update_norms = jnp.sqrt(update_squares)
    new_masters = [
        masters[number] - RATE * (weight_norms[number] / update_norms[number]) * updates[number]
        for number in range(5)
    ]
    lamb_norms = jnp.stack([weight_norms, update_norms])
    return tuple(new_masters) + tuple(first_news) + tuple(second_news) + (lamb_norms,)


def solution(mesh):
    in_specs = (
        P(("dp", "fsdp"), None, None),
        P(("dp", "fsdp"), None, None),
        P(("dp", "fsdp")),
        P("fsdp", None),
        P("fsdp", None),
        P("fsdp", None),
        P("fsdp", None),
        P("fsdp"),
        P("fsdp", None),
        P("fsdp", None),
        P("fsdp", None),
        P("fsdp", None),
        P("fsdp"),
        P("fsdp", None),
        P("fsdp", None),
        P("fsdp", None),
        P("fsdp", None),
        P("fsdp"),
    )
    out_specs = (
        P(("dp", "fsdp"), None, None),
        P(("dp", "fsdp"), None, None),
        P("fsdp", None),
        P("fsdp", None),
        P("fsdp", None),
        P("fsdp", None),
        P("fsdp"),
        P("fsdp", None),
        P("fsdp", None),
        P("fsdp", None),
        P("fsdp", None),
        P("fsdp"),
        P("fsdp", None),
        P("fsdp", None),
        P("fsdp", None),
        P("fsdp", None),
        P("fsdp"),
        P(),
    )
    return jax.shard_map(local_split, mesh=mesh, in_specs=in_specs, out_specs=out_specs, check_vma=False)
```

```python
import math

import jax
import jax.numpy as jnp
import numpy as np
from jax import lax
from jax.experimental import pallas as pl
from jax.experimental.pallas import tpu as pltpu
from jax.sharding import PartitionSpec as P

D = 1024
HEADS = 16
HD = 64
FF = 4096
ROT = 16
SMALL = 13312


NORM_EPSILON = 1e-05
ADAM_EPSILON = 1e-06
ROPE_BASE = 10000.0
RATE = 0.5
DECAY = 0.01
BETA_ONE = 0.5
BETA_TWO = 0.5


def split_small(small_vector):
    bounds = [0, D, 2 * D, 3 * D, 4 * D, 7 * D, 8 * D, 8 * D + FF, 9 * D + FF]
    return [small_vector[bounds[number] : bounds[number + 1]] for number in range(8)]


def normalize(values):
    average = jnp.mean(values, axis=-1, keepdims=True)
    centred = values - average
    variance = jnp.mean(centred * centred, axis=-1, keepdims=True)
    inverse = lax.rsqrt(variance + NORM_EPSILON)
    return (centred * inverse, inverse)


def rotary_tables(length):
    half_dims = ROT // 2
    position = jnp.arange(length, dtype=jnp.float32)[:, None]
    number = jnp.arange(half_dims, dtype=jnp.float32)[None, :]
    angle = position * jnp.exp(number * (-2.0 * math.log(ROPE_BASE) / ROT))
    return (jnp.cos(angle)[:, None, :], jnp.sin(angle)[:, None, :])


def rotate(heads_in, cosine_table, sine_table):
    half_dims = ROT // 2
    first_half = heads_in[..., :half_dims]
    second_half = heads_in[..., half_dims:ROT]
    return jnp.concatenate(
        [
            first_half * cosine_table - second_half * sine_table,
            second_half * cosine_table + first_half * sine_table,
            heads_in[..., ROT:],
        ],
        axis=-1,
    )


def rotate_back(grads_in, cosine_table, sine_table):
    half_dims = ROT // 2
    first_half = grads_in[..., :half_dims]
    second_half = grads_in[..., half_dims:ROT]
    return jnp.concatenate(
        [
            first_half * cosine_table + second_half * sine_table,
            second_half * cosine_table - first_half * sine_table,
            grads_in[..., ROT:],
        ],
        axis=-1,
    )


def gelu_slope(values):
    return 0.5 * (1.0 + lax.erf(values * 2.0 ** (-0.5))) + values * jnp.exp(
        -0.5 * values * values
    ) * (2.0 * math.pi) ** (-0.5)


def against(left, right):
    return lax.dot_general(
        left, right, (((1,), (1,)), ((), ())), preferred_element_type=jnp.float32
    )


def outer_sum(columns, right):
    return lax.dot_general(
        columns, right, (((0,), (0,)), ((), ())), preferred_element_type=jnp.float32
    )


def local_squares(arrays):
    return jnp.stack([jnp.sum(array_in * array_in) for array_in in arrays])


def sliced(master, part, parts, pieces):
    rows, columns = master.shape
    width = columns // (pieces * parts)
    return lax.dynamic_index_in_dim(
        master.reshape(rows, pieces, parts, width), part, axis=2, keepdims=False
    ).reshape(rows, pieces * width)


def joined(slices, pieces):
    parts, rows, columns = slices.shape
    width = columns // pieces
    return (
        slices.reshape(parts, rows, pieces, width)
        .transpose(1, 2, 0, 3)
        .reshape(rows, pieces * parts * width)
    )


def layer(x_all, cotangent_all, lengths_all, weights, small_all, part):
    qkv_weight, out_weight, up_weight, down_weight = weights
    group, length, _ = x_all.shape
    tokens = group * length
    head_cols = out_weight.shape[0]
    heads = head_cols // HD
    gain_one, shift_one, gain_two, shift_two, qkv_bias, up_bias = small_all
    inputs = x_all.reshape(tokens, D).astype(jnp.float32)
    position = jnp.arange(length)
    live = (position[None, :] < lengths_all[:, None]).astype(jnp.float32).reshape(tokens, 1)
    allowed = (position[None, None, :] <= position[None, :, None]) & (
        position[None, None, :] < lengths_all[:, None, None]
    )
    unit_rows, _ = normalize(inputs)
    normed_one = (unit_rows * gain_one + shift_one).astype(jnp.bfloat16)
    normed_two = (unit_rows * gain_two + shift_two).astype(jnp.bfloat16)
    projected = jnp.dot(normed_one, qkv_weight, preferred_element_type=jnp.float32) + qkv_bias
    projected = projected.reshape(group, length, 3, heads, HD)
    cosine_table, sine_table = rotary_tables(length)
    query_heads = rotate(projected[:, :, 0], cosine_table, sine_table).astype(jnp.bfloat16)
    key_heads = rotate(projected[:, :, 1], cosine_table, sine_table).astype(jnp.bfloat16)
    value_heads = projected[:, :, 2].astype(jnp.bfloat16)
    scores = jnp.einsum(
        "gqhd,gkhd->ghqk", query_heads, key_heads, preferred_element_type=jnp.float32
    ) * HD ** (-0.5)
    scores = jnp.where(allowed[:, None], scores, -1e30)
    row_top = jnp.max(scores, axis=-1, keepdims=True)
    raised = jnp.exp(scores - row_top)
    attend = raised / jnp.sum(raised, axis=-1, keepdims=True)
    attend_low = attend.astype(jnp.bfloat16)
    mixed = jnp.einsum(
        "ghqk,gkhd->gqhd", attend_low, value_heads, preferred_element_type=jnp.float32
    )
    mixed = mixed.reshape(tokens, head_cols).astype(jnp.bfloat16)
    hidden = jnp.dot(normed_two, up_weight, preferred_element_type=jnp.float32) + up_bias
    activated = jax.nn.gelu(hidden, approximate=False).astype(jnp.bfloat16)
    out_part = jnp.dot(mixed, out_weight, preferred_element_type=jnp.float32) + jnp.dot(
        activated, down_weight, preferred_element_type=jnp.float32
    )

    back = (cotangent_all.reshape(tokens, D).astype(jnp.float32) * live).astype(jnp.bfloat16)
    d_hidden = (against(back, down_weight) * gelu_slope(hidden)).astype(jnp.bfloat16)
    d_mixed = against(back, out_weight).astype(jnp.bfloat16).reshape(group, length, heads, HD)
    d_attend = jnp.einsum(
        "gqhd,gkhd->ghqk", d_mixed, value_heads, preferred_element_type=jnp.float32
    )
    row_inner = jnp.sum(attend * d_attend, axis=-1, keepdims=True)
    d_scores = (attend * (d_attend - row_inner)).astype(jnp.bfloat16)
    d_queries = jnp.einsum(
        "ghqk,gkhd->gqhd", d_scores, key_heads, preferred_element_type=jnp.float32
    ) * HD ** (-0.5)
    d_keys = jnp.einsum(
        "ghqk,gqhd->gkhd", d_scores, query_heads, preferred_element_type=jnp.float32
    ) * HD ** (-0.5)
    d_values = jnp.einsum(
        "ghqk,gqhd->gkhd", attend_low, d_mixed, preferred_element_type=jnp.float32
    )
    d_projected = jnp.stack(
        [
            rotate_back(d_queries, cosine_table, sine_table),
            rotate_back(d_keys, cosine_table, sine_table),
            d_values,
        ],
        axis=2,
    )
    d_projected = d_projected.reshape(tokens, 3 * head_cols).astype(jnp.bfloat16)
    d_normed_one = against(d_projected, qkv_weight)
    d_normed_two = against(d_hidden, up_weight)
    scaled_part = d_normed_one * gain_one + d_normed_two * gain_two
    norm_sums = jnp.stack(
        [
            jnp.sum(d_normed_one * unit_rows, axis=0),
            jnp.sum(d_normed_one, axis=0),
            jnp.sum(d_normed_two * unit_rows, axis=0),
            jnp.sum(d_normed_two, axis=0),
        ]
    )
    d_qkv_bias = jnp.sum(d_projected, axis=0, dtype=jnp.float32)
    d_up_bias = jnp.sum(d_hidden, axis=0, dtype=jnp.float32)
    terms = (
        outer_sum(normed_one, d_projected),
        outer_sum(mixed, back),
        outer_sum(normed_two, d_hidden),
        outer_sum(activated, back),
    )
    return (
        out_part.astype(jnp.bfloat16),
        scaled_part.astype(jnp.bfloat16),
        tuple(term.astype(jnp.bfloat16) for term in terms),
        (norm_sums, d_qkv_bias, d_up_bias),
    )


MESH_ID = pl.DeviceIdType.MESH
HALF = 128


class Place:
    def __init__(self):
        self.part = lax.axis_index("dp")
        self.shard = lax.axis_index("fsdp")
        self.z = self.shard // 2
        self.core = self.shard % 2
        self.x_part = 2 * (self.part // 2) + 1 - self.part % 2
        self.y_part = (self.part + 2) % 4
        self.far_part = 3 - self.part
        self.across_x = (self.x_part, self.shard)
        self.across_y = (self.y_part, self.shard)
        self.across_far = (self.far_part, self.shard)
        self.other_core = (self.part, 2 * self.z + 1 - self.core)
        self.up = (self.part, jnp.minimum(self.shard + 2, 7))
        self.down = (self.part, jnp.maximum(self.shard - 2, 0))

    def shard_after(self, k):
        return (self.part, (self.shard + k) % 8)


def send(source, target, send_sem, recv_sem, device):
    return pltpu.make_async_remote_copy(
        src_ref=source,
        dst_ref=target,
        send_sem=send_sem,
        recv_sem=recv_sem,
        device_id=device,
        device_id_type=MESH_ID,
    )


def arrived(target, recv_sem, device):
    send(target, target, recv_sem, recv_sem, device).wait_recv()


def sent(source, send_sem, device):
    send(source, source, send_sem, send_sem, device).wait_send()


def greet(at):
    barrier = pltpu.get_barrier_semaphore()
    peers = [at.across_x, at.across_y, at.across_far] + [at.shard_after(k) for k in range(1, 8)]
    for peer in peers:
        pl.semaphore_signal(barrier, inc=1, device_id=peer, device_id_type=MESH_ID)
    return lambda: pl.semaphore_wait(barrier, len(peers))


SPANS = ((0, 768), (768, 1792), (1792, 2816))
Q, U, N = 0, 1, 2


def nt(left, right):
    return lax.dot_general(
        left, right, (((1,), (1,)), ((), ())), preferred_element_type=jnp.float32
    )


def tn(left, right):
    return lax.dot_general(
        left, right, (((0,), (0,)), ((), ())), preferred_element_type=jnp.float32
    )


def nn(left, right):
    return jnp.dot(left, right, preferred_element_type=jnp.float32)


def flat(value):
    return value.reshape(value.shape[0] * value.shape[1], value.shape[2])


def layer_kernel(
    length_own,
    x_own,
    cot_own,
    qkv_master,
    out_master,
    up_master,
    down_master,
    small_master,
    tables_in,
    output_out,
    input_grad_out,
    qkv_all,
    up_all,
    down_all,
    out_grad,
    small_sum,
    tables,
    output,
    input_grad,
    x_all,
    cot_all,
    len_all,
    w_all,
    out_all,
    small_own,
    small_all,
    vectors,
    qkv_bias,
    up_bias,
    stats,
    normed_one,
    normed_two,
    back,
    heads_qkv,
    mixed,
    d_projected,
    hidden,
    d_hidden,
    out_part,
    dx_part,
    terms,
    out_term,
    sums,
    d_qkv_bias,
    d_up_bias,
    small_part,
    plane_one,
    plane_two,
    plane_turn,
    core_in,
    line_in,
    out_core_in,
    out_line,
    out_line_in,
    small_in,
    small_total,
    small_plane,
    load_sem,
    plane_send,
    plane_recv,
    early_send,
    early_recv,
    len_send,
    len_recv,
    w_send,
    w_recv,
    out_send,
    out_recv,
    small_send,
    small_recv,
    part_send,
    part_recv,
    core_send,
    core_recv,
    line_send,
    line_recv,
    rows_send,
    rows_recv,
    all_send,
    all_recv,
    keep_sem,
    total_send,
    total_recv,
    store_sem,
):
    f32, bf16 = jnp.float32, jnp.bfloat16
    at = Place()
    z, core, part, shard = at.z, at.core, at.part, at.shard
    all_are_in = greet(at)
    length = x_own.shape[0]
    head_cols = mixed.shape[2]
    activated = normed_one
    place_x, place_y = part % 2, part // 2

    def near_first(i):
        return 2 * ((place_y + i // 2) % 2) + (place_x + i % 2) % 2

    def far_first(i):
        return 2 * ((place_y + 1 - i % 2) % 2) + (place_x + 1 - i // 2) % 2

    def piece(ref, slot, n):
        return ref.at[slot, :, SPANS[n][0] : SPANS[n][1]]

    plane_peers = (
        (at.across_x, at.x_part),
        (at.across_y, at.y_part),
        (at.across_far, at.far_part),
    )

    stage = [hidden.at[n, 0:128] for n in range(4)]
    loads = []
    for c in range(3):
        columns = pl.ds(pl.multiple_of(c * D + part * head_cols, 128), head_cols)
        target = stage[0].at[:, c * head_cols : (c + 1) * head_cols]
        loads.append((qkv_master.at[:, columns], target))
    loads.append((out_master, stage[1]))
    for g in range(8):
        columns = pl.ds(pl.multiple_of(g * (FF // 8) + part * 128, 128), 128)
        loads.append((up_master.at[:, columns], stage[2].at[:, g * 128 : (g + 1) * 128]))
    rows = pl.ds(pl.multiple_of(part * 128, 128), 128)
    loads.append((down_master.at[rows], stage[3]))
    loads.append((x_own, x_all.at[part]))
    loads.append((cot_own, cot_all.at[part]))
    loads.append((tables_in, tables))

    def load(n):
        return pltpu.make_async_copy(loads[n][0], loads[n][1], load_sem.at[n])

    for n in range(len(loads)):
        load(n).start()
    len_all[part] = jnp.full((8, 128), length_own[0], jnp.int32).astype(f32)
    small_own[...] = jnp.zeros_like(small_own)
    small_own[0:13] = small_master[...].astype(bf16).astype(f32)
    small_all[shard] = small_own[...]
    all_are_in()

    halves = (slice(0, HALF), slice(HALF, 2 * HALF))
    quarters = (slice(0, HALF // 2), slice(HALF // 2, HALF))
    activations = ((x_own, x_all), (cot_own, cot_all))
    neighbours = ((at.across_x, at.x_part), (at.across_y, at.y_part))

    def send_activations():
        for r, (peer, _) in enumerate(neighbours):
            send(
                x_own, x_all.at[part], plane_send.at[0, r], plane_recv.at[0, r], peer
            ).start()
        for r, (peer, _) in enumerate(neighbours):
            send(
                cot_own.at[halves[0]],
                cot_all.at[part, halves[0]],
                early_send.at[r],
                early_recv.at[r],
                peer,
            ).start()

    def send_rest():
        for r, (peer, _) in enumerate(neighbours):
            send(
                cot_own.at[halves[1]],
                cot_all.at[part, halves[1]],
                plane_send.at[1, r],
                plane_recv.at[1, r],
                peer,
            ).start()

    def cast(n, first, last):
        for m in range(first, last):
            load(m).wait()
        low, high = SPANS[n]
        w_all[shard, :, low:high] = stage[(0, 2, 3)[n]][:, 0 : high - low].astype(bf16)

    def send_own(n):
        cast(n, *((0, 3), (4, 12), (12, 13))[n])
        block = piece(w_all, shard, n)

        @pl.when(z < 3)
        def _():
            send(block, block, w_send.at[0, n, z], w_recv.at[n, shard], at.up).start()

        @pl.when(z > 0)
        def _():
            send(block, block, w_send.at[1, n, z], w_recv.at[n, shard], at.down).start()

        send(block, block, w_send.at[2, n, z], w_recv.at[n, shard], at.other_core).start()

    def forward(k, n):
        @pl.when(z >= k)
        def _():
            source = 2 * (z - k) + core
            block = piece(w_all, source, n)
            arrived(block, w_recv.at[n, source], at.down)

            @pl.when(z < 3)
            def _():
                send(block, block, w_send.at[0, n, z - k], w_recv.at[n, source], at.up).start()

            send(
                block, block, w_send.at[2, n, z - k], w_recv.at[n, source], at.other_core
            ).start()

        @pl.when(z + k <= 3)
        def _():
            source = 2 * (z + k) + core
            block = piece(w_all, source, n)
            arrived(block, w_recv.at[n, source], at.up)

            @pl.when(z > 0)
            def _():
                send(block, block, w_send.at[1, n, z + k], w_recv.at[n, source], at.down).start()

            send(
                block, block, w_send.at[2, n, z + k], w_recv.at[n, source], at.other_core
            ).start()

    def from_core(n):
        for other in range(4):
            source = 2 * other + 1 - core
            arrived(piece(w_all, source, n), w_recv.at[n, source], at.other_core)

    def send_out_rows():
        load(3).wait()

        @pl.when(z == part)
        def _():
            out_all[core] = stage[1][...].astype(bf16)
            block = out_all.at[core]

            @pl.when(z < 3)
            def _():
                send(block, block, out_send.at[0], out_recv.at[core], at.up).start()

            @pl.when(z > 0)
            def _():
                send(block, block, out_send.at[1], out_recv.at[core], at.down).start()

            send(block, block, out_send.at[2], out_recv.at[core], at.other_core).start()

    def out_from_core():
        arrived(out_all.at[1 - core], out_recv.at[1 - core], at.other_core)

    def forward_out(k):
        @pl.when((z - k == part) | (z + k == part))
        def _():
            block = out_all.at[core]
            arrived(block, out_recv.at[core], at.up)

            @pl.when((z > part) & (z < 3))
            def _():
                send(block, block, out_send.at[0], out_recv.at[core], at.up).start()

            @pl.when((z < part) & (z > 0))
            def _():
                send(block, block, out_send.at[1], out_recv.at[core], at.down).start()

            send(block, block, out_send.at[2], out_recv.at[core], at.other_core).start()

    def forward_neighbour(n, r):
        peer, source = neighbours[r]
        whole = activations[n][1]
        if n == 0:
            arrived(whole.at[source], plane_recv.at[0, r], peer)
        else:
            arrived(whole.at[source, halves[0]], early_recv.at[r], peer)
            arrived(whole.at[source, halves[1]], plane_recv.at[1, r], peer)
        block = whole.at[source, halves[r]]
        onward = neighbours[1 - r][0]
        send(block, block, plane_send.at[n, 2 + r], plane_recv.at[n, 2 + r], onward).start()

    def forward_x(n):
        forward_neighbour(n, 0)

    def forward_y(n):
        forward_neighbour(n, 1)

    def far_halves(n):
        whole = activations[n][1]
        arrived(whole.at[at.far_part, 0:HALF], plane_recv.at[n, 2], at.across_y)
        arrived(whole.at[at.far_part, HALF : 2 * HALF], plane_recv.at[n, 3], at.across_x)

    def send_small():
        for n, (peer, _) in enumerate(plane_peers):
            send(len_all.at[part], len_all.at[part], len_send.at[n], len_recv.at[n], peer).start()
        for k in range(1, 8):
            send(
                small_own,
                small_all.at[shard],
                small_send.at[k - 1],
                small_recv.at[k - 1],
                at.shard_after(k),
            ).start()

    def unpack_small():
        for n in (13, 14, 15):
            load(n).wait()
        for n, (peer, other) in enumerate(plane_peers):
            arrived(len_all.at[other], len_recv.at[n], peer)
        for k in range(1, 8):
            arrived(
                small_all.at[(shard + 8 - k) % 8], small_recv.at[k - 1], at.shard_after(8 - k)
            )
        for number, row in enumerate((0, 8, 16, 24, 56, 96)):
            for n in range(8):
                source = row + n
                vectors[number : number + 1, n * 128 : (n + 1) * 128] = small_all[
                    source // 13, source % 13 : source % 13 + 1
                ]
        for c in range(3):
            for n in range(2):
                source = 32 + 8 * c + 2 * part + n
                columns = slice((2 * c + n) * 128, (2 * c + n + 1) * 128)
                qkv_bias[:, columns] = small_all[source // 13, pl.ds(source % 13, 1)]
        for g in range(8):
            source = 64 + 4 * g + part
            up_bias[:, g * 128 : (g + 1) * 128] = small_all[source // 13, pl.ds(source % 13, 1)]

    sums[...] = jnp.zeros_like(sums)
    d_qkv_bias[...] = jnp.zeros_like(d_qkv_bias)
    d_up_bias[...] = jnp.zeros_like(d_up_bias)
    block_rows = 64

    def norm_rows(s):
        @pl.loop(0, length // block_rows)
        def _(i):
            r = pl.ds(pl.multiple_of(i * block_rows, block_rows), block_rows)
            values = x_all[s, r, :].astype(f32)
            mean = jnp.mean(values, axis=-1, keepdims=True)
            centred = values - mean
            inverse = lax.rsqrt(
                jnp.mean(centred * centred, axis=-1, keepdims=True) + NORM_EPSILON
            )
            stats[s, r, 0:1] = mean
            stats[s, r, 1:2] = inverse
            unit = centred * inverse
            normed_one[s, r, :] = (unit * vectors[0:1] + vectors[1:2]).astype(bf16)
            normed_two[s, r, :] = (unit * vectors[2:3] + vectors[3:4]).astype(bf16)

    def live_rows(s):
        index = lax.broadcasted_iota(jnp.int32, (length, 1), 0)
        return index.astype(f32) < len_all[s][0:1, 0:1]

    def rotate(value, sign):
        return (
            value * tables[0]
            + sign * pltpu.roll(value, head_cols - ROT // 2, 1) * tables[1]
            + sign * pltpu.roll(value, ROT // 2, 1) * tables[2]
        )

    def project(s):
        norm_rows(s)
        low, high = SPANS[Q]
        value = nn(normed_one[s], flat(w_all[:, :, low:high])) + qkv_bias[...]
        heads_qkv[s, :, 0:head_cols] = rotate(value[:, 0:head_cols], 1.0).astype(bf16)
        heads_qkv[s, :, head_cols : 2 * head_cols] = rotate(
            value[:, head_cols : 2 * head_cols], 1.0
        ).astype(bf16)
        heads_qkv[s, :, 2 * head_cols :] = value[:, 2 * head_cols :].astype(bf16)

    def attend(s):
        cot = cot_all[s]
        back[s] = jnp.where(live_rows(s), cot, jnp.zeros_like(cot))
        queries = heads_qkv[s, :, 0:head_cols]
        keys = heads_qkv[s, :, head_cols : 2 * head_cols]
        values = heads_qkv[s, :, 2 * head_cols :]
        d_mixed = nt(back[s], flat(out_all[...])).astype(bf16)
        row = lax.broadcasted_iota(jnp.int32, (length, length), 0)
        column = lax.broadcasted_iota(jnp.int32, (length, length), 1)
        allowed = (column <= row) & (column.astype(f32) < len_all[s][0:1, 0:1])
        lane = lax.broadcasted_iota(jnp.int32, (length, head_cols), 1)
        zero = jnp.zeros((), bf16)
        mixed_sum = jnp.zeros((length, head_cols), f32)
        d_queries = d_keys = d_values = mixed_sum
        for h in range(head_cols // HD):
            of_head = (lane >= h * HD) & (lane < (h + 1) * HD)
            q_h, k_h, v_h, d_h = (
                jnp.where(of_head, t, zero) for t in (queries, keys, values, d_mixed)
            )
            scores = jnp.where(allowed, nt(q_h, keys) * HD**-0.5, -1e30)
            raised = jnp.exp(scores - jnp.max(scores, axis=-1, keepdims=True))
            weights = raised * (1.0 / jnp.sum(raised, axis=-1, keepdims=True))
            low = weights.astype(bf16)
            mixed_sum = mixed_sum + nn(low, v_h)
            d_weights = nt(d_h, values)
            inner = jnp.sum(weights * d_weights, axis=-1, keepdims=True)
            d_scores = (weights * (d_weights - inner)).astype(bf16)
            d_queries = d_queries + nn(d_scores, k_h)
            d_keys = d_keys + tn(d_scores, q_h)
            d_values = d_values + tn(low, d_h)
        mixed[s] = mixed_sum.astype(bf16)
        for n, value in enumerate(
            (rotate(d_queries * HD**-0.5, -1.0), rotate(d_keys * HD**-0.5, -1.0), d_values)
        ):
            rounded = value.astype(bf16)
            columns = slice(n * head_cols, (n + 1) * head_cols)
            d_projected[s, :, columns] = rounded
            d_qkv_bias[:, columns] += jnp.sum(rounded.astype(f32), axis=0, keepdims=True)

    def gradient(left, right, n):
        low, high = SPANS[n]

        @pl.loop(0, 8)
        def _(f):
            columns = pl.ds(pl.multiple_of(f * 128, 128), 128)
            terms[f, :, low:high] = tn(flat(left[:, :, columns]), flat(right[...])).astype(bf16)

    def to_core(n):
        for other in range(4):
            send(
                piece(terms, 2 * other + 1 - core, n),
                piece(core_in, other, n),
                core_send.at[n, other],
                core_recv.at[n, other],
                at.other_core,
            ).start()

    def add_core(n):
        low, high = SPANS[n]
        for other in (3, 0, 2, 1):
            arrived(piece(core_in, other, n), core_recv.at[n, other], at.other_core)
            terms[2 * other + core, :, low:high] = (
                terms[2 * other + core, :, low:high].astype(f32)
                + core_in[other, :, low:high].astype(f32)
            ).astype(bf16)

    def pass_on(n, me, target):
        low, high = SPANS[n]

        @pl.when(z == me)
        def _():
            own = piece(terms, 2 * target + core, n)
            if me not in (0, 3):
                source = at.down if me < target else at.up
                arrived(piece(line_in, target, n), line_recv.at[n, target], source)
                terms[2 * target + core, :, low:high] = (
                    terms[2 * target + core, :, low:high].astype(f32)
                    + line_in[target, :, low:high].astype(f32)
                ).astype(bf16)
            slot = 4 if me == target + 1 else target
            send(
                own,
                piece(line_in, slot, n),
                line_send.at[n, target],
                line_recv.at[n, slot],
                at.up if me < target else at.down,
            ).start()

    def line_starts(n):
        for target in (3, 2, 1):
            pass_on(n, 0, target)
        for target in (0, 1, 2):
            pass_on(n, 3, target)

    def line_step(n, step):
        for me, target in (((1, 3), (2, 0)), ((1, 2), (2, 1)), ((2, 3), (1, 0)))[step]:
            pass_on(n, me, target)

    wholes = (qkv_all, up_all, down_all)

    def line_ends(n):
        low, high = SPANS[n]
        total = 2 * z + core

        def add(slot, source):
            arrived(piece(line_in, slot, n), line_recv.at[n, slot], source)
            terms[total, :, low:high] = (
                terms[total, :, low:high].astype(f32) + line_in[slot, :, low:high].astype(f32)
            ).astype(bf16)

        @pl.when(z > 0)
        def _():
            add(z, at.down)

        @pl.when(z < 3)
        def _():
            add(4, at.up)

        own = piece(terms, total, n)
        target = wholes[n].at[part]
        send(own, target, all_send.at[n, 0], all_recv.at[n, 0], at.across_x).start()
        send(own, target, all_send.at[n, 1], all_recv.at[n, 1], at.across_y).start()
        pltpu.make_async_copy(own, target, keep_sem.at[n]).start()

    def share(n):
        whole = wholes[n]
        arrived(whole.at[at.x_part], all_recv.at[n, 0], at.across_x)
        block = whole.at[at.x_part, 0:64]
        send(block, block, all_send.at[n, 2], all_recv.at[n, 2], at.across_y).start()
        arrived(whole.at[at.y_part], all_recv.at[n, 1], at.across_y)
        block = whole.at[at.y_part, 64:128]
        send(block, block, all_send.at[n, 3], all_recv.at[n, 3], at.across_x).start()

    def out_to_core():
        send(
            out_term.at[1 - core], out_core_in, rows_send.at[0], rows_recv.at[0], at.other_core
        ).start()

    def out_add(block):
        out_line[...] = (out_line[...].astype(f32) + block.astype(f32)).astype(bf16)

    def out_add_core():
        arrived(out_core_in, rows_recv.at[0], at.other_core)
        out_line[...] = out_term[core]
        out_add(out_core_in[...])

    def out_step(step):
        @pl.when((z == step) & (z < part))
        def _():
            if step > 0:
                arrived(out_line_in.at[0], rows_recv.at[1], at.down)
                out_add(out_line_in[0])
            send(out_line, out_line_in.at[0], rows_send.at[1], rows_recv.at[1], at.up).start()

        @pl.when((z == 3 - step) & (z > part))
        def _():
            if step > 0:
                arrived(out_line_in.at[1], rows_recv.at[2], at.up)
                out_add(out_line_in[1])
            send(out_line, out_line_in.at[1], rows_send.at[1], rows_recv.at[2], at.down).start()

    def out_ends():
        @pl.when(z == part)
        def _():
            @pl.when(z > 0)
            def _():
                arrived(out_line_in.at[0], rows_recv.at[1], at.down)
                out_add(out_line_in[0])

            @pl.when(z < 3)
            def _():
                arrived(out_line_in.at[1], rows_recv.at[2], at.up)
                out_add(out_line_in[1])

            for r, (peer, _) in enumerate(neighbours):
                send(
                    out_line.at[quarters[r]],
                    out_grad.at[quarters[r]],
                    rows_send.at[2 + r],
                    rows_recv.at[3],
                    peer,
                ).start()
            pltpu.make_async_copy(out_line, out_grad, keep_sem.at[3]).start()

    def out_share():
        for r, (peer, source) in enumerate(neighbours):

            @pl.when(z == source)
            def _():
                block = out_grad.at[quarters[r]]
                arrived(block, rows_recv.at[3], peer)
                onward = neighbours[1 - r][0]
                send(block, block, rows_send.at[4], rows_recv.at[4 + r], onward).start()

    def out_far():
        @pl.when(z == at.far_part)
        def _():
            for r, (peer, _) in enumerate(neighbours):
                block = out_grad.at[quarters[r]]
                arrived(block, rows_recv.at[4 + r], neighbours[1 - r][0])
                send(block, block, rows_send.at[2 + r], rows_recv.at[4 + r], peer).start()

    def out_gradient():
        for n in range(2):
            columns = slice(n * 128, (n + 1) * 128)
            out_term[n] = tn(flat(mixed[:, :, columns]), flat(back[...])).astype(bf16)

    part_refs = (out_part, dx_part)
    routes = (
        (halves[0], at.across_x, at.x_part, at.across_y, at.y_part),
        (halves[1], at.across_y, at.y_part, at.across_x, at.x_part),
    )

    def send_part(n, r, m):
        half, peer, peer_part, _, _ = routes[r]
        target = (at.far_part, peer_part)[m]
        send(
            part_refs[n].at[target, half],
            plane_one.at[n, r, m],
            part_send.at[n, r, m],
            part_recv.at[n, r, m],
            peer,
        ).start()

    def turn_part(n, r):
        half, peer, _, turn, turned = routes[r]
        arrived(plane_one.at[n, r, 0], part_recv.at[n, r, 0], peer)
        plane_turn[n, r] = (
            part_refs[n][turned, half].astype(f32) + plane_one[n, r, 0].astype(f32)
        ).astype(bf16)
        send(
            plane_turn.at[n, r],
            plane_two.at[n, r],
            part_send.at[n, r, 2],
            part_recv.at[n, r, 2],
            turn,
        ).start()

    def whole_part(n, r):
        half, peer, _, turn, _ = routes[r]
        arrived(plane_one.at[n, r, 1], part_recv.at[n, r, 1], peer)
        arrived(plane_two.at[n, r], part_recv.at[n, r, 2], turn)
        return (
            part_refs[n][part, half].astype(f32)
            + plane_one[n, r, 1].astype(f32)
            + plane_two[n, r].astype(f32)
        )

    up_low, up_high = SPANS[U]
    down_low, down_high = SPANS[N]

    def feed_in(s):
        value = nn(normed_two[s], flat(w_all[:, :, up_low:up_high])) + up_bias[...]
        hidden[s] = value
        activated[s] = (value * (0.5 * (1.0 + lax.erf(value * 2.0**-0.5)))).astype(bf16)

    def feed_out(s):
        out_part[s] = (
            nn(activated[s], flat(w_all[:, :, down_low:down_high]))
            + nn(mixed[s], flat(out_all[...]))
        ).astype(bf16)

    def feed_back(s):
        slope = gelu_slope(hidden[s])
        low = (nt(back[s], flat(w_all[:, :, down_low:down_high])) * slope).astype(bf16)
        d_hidden[s] = low
        d_up_bias[...] += jnp.sum(low.astype(f32), axis=0, keepdims=True)

    def norm_back(s):
        d_two = nt(d_hidden[s], flat(w_all[:, :, up_low:up_high]))
        d_one = nt(d_projected[s], flat(w_all[:, :, SPANS[Q][0] : SPANS[Q][1]]))
        unit = (x_all[s].astype(f32) - stats[s][:, 0:1]) * stats[s][:, 1:2]
        sums[0:1] += jnp.sum(d_one * unit, axis=0, keepdims=True)
        sums[1:2] += jnp.sum(d_one, axis=0, keepdims=True)
        sums[2:3] += jnp.sum(d_two * unit, axis=0, keepdims=True)
        sums[3:4] += jnp.sum(d_two, axis=0, keepdims=True)
        dx_part[s] = (d_one * vectors[0:1] + d_two * vectors[2:3]).astype(bf16)

    def place(row, value):
        small_part[row // 13, pl.ds(row % 13, 1)] = value

    def small_start():
        small_part[...] = jnp.zeros_like(small_part)
        back_total = jnp.sum(back[part].astype(f32), axis=0, keepdims=True)
        for n in range(8):
            columns = slice(n * 128, (n + 1) * 128)
            for number in range(4):
                place(8 * number + n, sums[number : number + 1, columns])
            place(56 + n, back_total[:, columns])
            place(96 + n, back_total[:, columns])
            place(64 + 4 * n + part, d_up_bias[:, columns])
        for c in range(3):
            for n in range(2):
                columns = slice((2 * c + n) * 128, (2 * c + n + 1) * 128)
                place(32 + 8 * c + 2 * part + n, d_qkv_bias[:, columns])
        for k in range(1, 8):
            send(
                small_part.at[(shard + k) % 8],
                small_in.at[k - 1],
                total_send.at[k - 1],
                total_recv.at[k - 1],
                at.shard_after(k),
            ).start()

    def small_turn():
        total = small_part[shard]
        for k in range(1, 8):
            arrived(small_in.at[k - 1], total_recv.at[k - 1], at.shard_after(8 - k))
            total = total + small_in[k - 1]
        small_total[...] = total
        for n, (peer, _) in enumerate(plane_peers):
            send(
                small_total, small_plane.at[part], total_send.at[7 + n], total_recv.at[7 + n], peer
            ).start()
        small_plane[part] = total

    def small_end():
        for n, (peer, other) in enumerate(plane_peers):
            arrived(small_plane.at[other], total_recv.at[7 + n], peer)
        small_sum[...] = (small_plane[0] + small_plane[1]) + (small_plane[2] + small_plane[3])

    def write_output(r):
        half = halves[r]
        values = x_all[part, half].astype(f32)
        summed = values + whole_part(0, r) + vectors[4:5] + vectors[5:6]
        output[half] = jnp.where(live_rows(part)[half], summed, 0.0).astype(bf16)
        pltpu.make_async_copy(output.at[half], output_out.at[half], store_sem.at[0, r]).start()

    def write_input_grad(r):
        half = halves[r]
        scaled = whole_part(1, r)
        inverse = stats[part, half, 1:2]
        unit = (x_all[part, half].astype(f32) - stats[part, half, 0:1]) * inverse
        result = back[part, half].astype(f32) + inverse * (
            scaled
            - jnp.mean(scaled, axis=-1, keepdims=True)
            - unit * jnp.mean(scaled * unit, axis=-1, keepdims=True)
        )
        input_grad[half] = result.astype(bf16)
        pltpu.make_async_copy(
            input_grad.at[half], input_grad_out.at[half], store_sem.at[1, r]
        ).start()

    at_end = (z == 0) | (z == 3)
    middle = (z == 1) | (z == 2)
    send_activations()
    send_own(Q)
    send_out_rows()
    send_small()

    @pl.when(middle)
    def _():
        send_rest()
        forward(1, Q)
        forward_out(1)
        forward(2, Q)
        forward_y(0)

    send_own(U)

    @pl.when(at_end)
    def _():
        forward_y(0)
        forward(1, Q)
        forward(2, Q)

    @pl.when(middle)
    def _():
        forward_out(2)
        forward(1, U)

    forward_x(0)

    @pl.when(middle)
    def _():
        from_core(Q)

    send_own(N)

    @pl.when(at_end)
    def _():
        send_rest()
        forward(3, Q)
        from_core(Q)

    unpack_small()

    @pl.loop(0, 4)
    def _(i):
        project(near_first(i))

        @pl.when((i == 0) & at_end)
        def _():
            forward_out(1)
            far_halves(0)

        @pl.when((i == 1) & at_end)
        def _():
            forward_out(2)

        @pl.when((i == 2) & at_end)
        def _():
            forward_out(3)

        @pl.when((i == 2) & middle)
        def _():
            far_halves(0)
            forward_x(1)
            forward(2, U)
            out_from_core()

    @pl.when(at_end)
    def _():
        out_from_core()

    forward_y(1)

    @pl.when(at_end)
    def _():
        forward_x(1)

    @pl.when(middle)
    def _():
        forward(1, N)

    @pl.loop(0, 4)
    def _(i):
        attend(near_first(i))

        @pl.when((i == 2) & middle)
        def _():
            forward(2, N)

        @pl.when(i == 2)
        def _():
            far_halves(1)

        @pl.when((i == 2) & at_end)
        def _():
            forward(1, U)

    @pl.when(at_end)
    def _():
        forward(2, U)

    @pl.when(middle)
    def _():
        from_core(N)

    gradient(normed_one, d_projected, Q)

    @pl.when(at_end)
    def _():
        to_core(Q)

    @pl.when(middle)
    def _():
        from_core(U)

    out_gradient()

    @pl.when(at_end)
    def _():
        forward(3, U)
        add_core(Q)
        out_to_core()
        line_starts(Q)
        forward(1, N)
        from_core(U)

    @pl.when(middle)
    def _():
        to_core(Q)

    @pl.loop(0, 4)
    def _(i):
        feed_in(i)

        @pl.when((i == 2) & at_end)
        def _():
            forward(2, N)

    @pl.when(at_end)
    def _():
        out_add_core()

    gradient(activated, back, N)

    @pl.when(at_end)
    def _():
        out_step(0)
        forward(3, N)
        from_core(N)

    @pl.loop(0, 4)
    def _(i):
        feed_out(far_first(i))

        @pl.when(i == 0)
        def _():
            send_part(0, 0, 0)
            send_part(0, 1, 0)

        @pl.when((i == 0) & at_end)
        def _():
            to_core(N)

        @pl.when((i == 1) & at_end)
        def _():
            send_part(0, 0, 1)
            add_core(N)

        @pl.when((i == 2) & at_end)
        def _():
            send_part(0, 1, 1)

    @pl.when(middle)
    def _():
        out_to_core()

    @pl.loop(0, 4)
    def _(i):
        feed_back(far_first(i))

        @pl.when((i == 0) & middle)
        def _():
            send_part(0, 1, 1)
            add_core(Q)

        @pl.when((i == 1) & middle)
        def _():
            out_add_core()

        @pl.when(i == 2)
        def _():
            send_part(1, 0, 0)
            send_part(1, 1, 0)

        @pl.when((i == 2) & middle)
        def _():
            turn_part(0, 0)
            turn_part(0, 1)
            line_step(Q, 1)
            out_step(1)
            add_core(N)

        @pl.when((i == 3) & middle)
        def _():
            send_part(1, 1, 1)
            line_step(N, 0)

        norm_back(far_first(i))

        @pl.when((i == 0) & at_end)
        def _():
            line_starts(N)

        @pl.when((i == 0) & middle)
        def _():
            send_part(0, 0, 1)
            line_step(Q, 0)

        @pl.when((i == 1) & middle)
        def _():
            to_core(N)

        @pl.when((i == 2) & at_end)
        def _():
            turn_part(0, 0)
            send_part(1, 1, 1)

        @pl.when((i == 2) & middle)
        def _():
            line_step(Q, 2)

    @pl.when(at_end)
    def _():
        turn_part(0, 1)

    @pl.when(middle)
    def _():
        send_part(1, 0, 1)

    gradient(normed_two, d_hidden, U)

    @pl.when(at_end)
    def _():
        send_part(1, 0, 1)

    @pl.when(middle)
    def _():
        small_start()

    to_core(U)

    @pl.when(at_end)
    def _():
        small_start()

    line_ends(Q)

    @pl.when(middle)
    def _():
        line_step(N, 1)
        line_step(N, 2)

    add_core(U)

    @pl.when(middle)
    def _():
        out_step(2)
        out_ends()
        line_ends(N)
        turn_part(1, 1)
        line_step(U, 0)
        small_turn()
        out_share()

    turn_part(1, 0)

    @pl.when(at_end)
    def _():
        line_starts(U)
        turn_part(1, 1)
        line_ends(N)
        out_ends()

    share(Q)

    @pl.when(middle)
    def _():
        line_step(U, 1)
        line_step(U, 2)
        write_input_grad(1)
        line_ends(U)
        write_output(0)
        share(N)

    write_output(1)

    @pl.when(at_end)
    def _():
        write_output(0)
        out_share()
        write_input_grad(1)
        share(N)
        line_ends(U)

    @pl.when(middle)
    def _():
        share(U)
        write_input_grad(0)

    out_far()

    @pl.when(at_end)
    def _():
        small_turn()
        write_input_grad(0)
        share(U)

    small_end()
    for r, half in enumerate(halves):
        pltpu.make_async_copy(output.at[half], output_out.at[half], store_sem.at[0, r]).wait()
        pltpu.make_async_copy(
            input_grad.at[half], input_grad_out.at[half], store_sem.at[1, r]
        ).wait()
    for r, (peer, source) in enumerate(neighbours):

        @pl.when(z == source)
        def _():
            arrived(out_grad.at[quarters[1 - r]], rows_recv.at[5 - r], neighbours[1 - r][0])
            sent(out_grad.at[quarters[r]], rows_send.at[4], neighbours[1 - r][0])

        @pl.when((z == part) | (z == at.far_part))
        def _():
            sent(out_grad.at[quarters[r]], rows_send.at[2 + r], peer)

    @pl.when(z != part)
    def _():
        sent(out_line, rows_send.at[1], at.up)

    @pl.when(z == part)
    def _():
        pltpu.make_async_copy(out_line, out_grad, keep_sem.at[3]).wait()

    sent(out_line, rows_send.at[0], at.other_core)
    for r, (peer, _) in enumerate(neighbours):
        sent(x_own, plane_send.at[0, r], peer)
        sent(cot_own.at[halves[0]], early_send.at[r], peer)
        sent(cot_own.at[halves[1]], plane_send.at[1, r], peer)
        for n in range(2):
            sent(x_all.at[part, halves[0]], plane_send.at[n, 2 + r], peer)
    for n, (peer, _) in enumerate(plane_peers):
        sent(len_all.at[part], len_send.at[n], peer)
        sent(small_total, total_send.at[7 + n], peer)
    for k in range(1, 8):
        sent(small_own, small_send.at[k - 1], at.shard_after(k))
        sent(small_total, total_send.at[k - 1], at.shard_after(k))
    for n in range(3):
        for other in range(4):
            block = piece(w_all, 2 * other + core, n)
            sent(block, w_send.at[2, n, other], at.other_core)
            sent(block, core_send.at[n, other], at.other_core)

            @pl.when((other <= z) & (z < 3))
            def _():
                sent(block, w_send.at[0, n, other], at.up)

            @pl.when((other >= z) & (z > 0))
            def _():
                sent(block, w_send.at[1, n, other], at.down)

            @pl.when(z != other)
            def _():
                sent(block, line_send.at[n, other], at.up)

    block = out_all.at[core]
    sent(block, out_send.at[2], at.other_core)

    @pl.when((z >= part) & (z < 3))
    def _():
        sent(block, out_send.at[0], at.up)

    @pl.when((z <= part) & (z > 0))
    def _():
        sent(block, out_send.at[1], at.down)

    for n in range(2):
        for r in range(2):
            for m in range(3):
                sent(plane_turn.at[n, r], part_send.at[n, r, m], at.across_x)
    for n, whole in enumerate(wholes):
        arrived(whole.at[at.far_part, 0:64], all_recv.at[n, 2], at.across_y)
        arrived(whole.at[at.far_part, 64:128], all_recv.at[n, 3], at.across_x)
        own = piece(terms, shard, n)
        sent(own, all_send.at[n, 0], at.across_x)
        sent(own, all_send.at[n, 1], at.across_y)
        sent(whole.at[part, 0:64], all_send.at[n, 2], at.across_y)
        sent(whole.at[part, 64:128], all_send.at[n, 3], at.across_x)
        pltpu.make_async_copy(own, whole.at[part], keep_sem.at[n]).wait()


VMEM_SPEC = pl.BlockSpec(memory_space=pltpu.VMEM)
HBM_SPEC = pl.BlockSpec(memory_space=pl.ANY)


def whole_layer(lengths, x_own, cot_own, masters, tables):
    shape = jax.ShapeDtypeStruct
    vmem, dma = pltpu.VMEM, pltpu.SemaphoreType.DMA
    bf16, f32 = jnp.bfloat16, jnp.float32
    length = x_own.shape[0]
    group = 4
    head_cols, wide, rows = D // group, 2816, 128

    def by_sequence(width, kind=bf16):
        return vmem((group, length, width), kind)

    return pl.pallas_call(
        layer_kernel,
        out_shape=(
            shape(x_own.shape, bf16),
            shape(x_own.shape, bf16),
            shape((group, rows, 3 * head_cols), bf16),
            shape((group, rows, FF // group), bf16),
            shape((group, rows, D), bf16),
            shape((rows, D), bf16),
            shape((16, 128), f32),
        ),
        in_specs=[pl.BlockSpec(memory_space=pltpu.SMEM)]
        + [HBM_SPEC] * 6
        + [VMEM_SPEC, HBM_SPEC],
        out_specs=(HBM_SPEC,) * 6 + (VMEM_SPEC,),
        scratch_shapes=[
            vmem(tables.shape, f32),
            vmem(x_own.shape, bf16),
            vmem(x_own.shape, bf16),
            by_sequence(D),
            by_sequence(D),
            vmem((group, 8, 128), f32),
            vmem((8, rows, wide), bf16),
            vmem((2, rows, D), bf16),
            vmem((16, 128), f32),
            vmem((8, 16, 128), f32),
            vmem((8, D), f32),
            vmem((1, 3 * head_cols), f32),
            vmem((1, FF // group), f32),
            by_sequence(128, f32),
            by_sequence(D),
            by_sequence(D),
            by_sequence(D),
            by_sequence(3 * head_cols),
            by_sequence(head_cols),
            by_sequence(3 * head_cols),
            by_sequence(FF // group, f32),
            by_sequence(FF // group),
            by_sequence(D),
            by_sequence(D),
            vmem((8, rows, wide), bf16),
            vmem((2, rows, D), bf16),
            vmem((8, D), f32),
            vmem((1, 3 * head_cols), f32),
            vmem((1, FF // group), f32),
            vmem((8, 16, 128), f32),
            vmem((2, 2, 2, HALF, D), bf16),
            vmem((2, 2, HALF, D), bf16),
            vmem((2, 2, HALF, D), bf16),
            vmem((4, rows, wide), bf16),
            vmem((5, rows, wide), bf16),
            vmem((rows, D), bf16),
            vmem((rows, D), bf16),
            vmem((2, rows, D), bf16),
            vmem((7, 16, 128), f32),
            vmem((16, 128), f32),
            vmem((4, 16, 128), f32),
            dma((16,)),
            dma((2, 4)),
            dma((2, 4)),
            dma((2,)),
            dma((2,)),
            dma((3,)),
            dma((3,)),
            dma((3, 3, 4)),
            dma((3, 8)),
            dma((3,)),
            dma((2,)),
            dma((7,)),
            dma((7,)),
            dma((2, 2, 3)),
            dma((2, 2, 3)),
            dma((3, 4)),
            dma((3, 4)),
            dma((3, 4)),
            dma((3, 5)),
            dma((5,)),
            dma((6,)),
            dma((3, 4)),
            dma((3, 4)),
            dma((4,)),
            dma((10,)),
            dma((10,)),
            dma((2, 2)),
        ],
        compiler_params=pltpu.CompilerParams(
            collective_id=0, has_side_effects=True, vmem_limit_bytes=56 << 20
        ),
        name="layer",
    )(lengths, x_own, cot_own, *masters, tables)


def rope_tables(length, heads):
    half = ROT // 2
    angle = np.arange(length)[:, None] * ROPE_BASE ** (-2.0 * np.arange(half) / ROT)[None]
    table = np.zeros((3, length, HD), np.float32)
    table[0] = 1.0
    table[0, :, :half] = table[0, :, half:ROT] = np.cos(angle)
    table[1, :, :half] = -np.sin(angle)
    table[2, :, half:ROT] = np.sin(angle)
    return jnp.asarray(np.tile(table, (1, 1, heads)))


def local_split(
    tokens_in,
    cotangent,
    lengths,
    qkv_master,
    out_master,
    up_master,
    down_master,
    small_master,
    qkv_first,
    out_first,
    up_first,
    down_first,
    small_first,
    qkv_second,
    out_second,
    up_second,
    down_second,
    small_second,
):
    masters = (qkv_master, out_master, up_master, down_master, small_master)
    firsts = (qkv_first, out_first, up_first, down_first, small_first)
    seconds = (qkv_second, out_second, up_second, down_second, small_second)
    parts, shards = lax.axis_size("dp"), lax.axis_size("fsdp")
    part, shard = lax.axis_index("dp"), lax.axis_index("fsdp")
    length = tokens_in.shape[1]
    update = (masters, firsts, seconds)
    if (parts, shards) == (4, 8):
        tall = tuple(masters[:4]) + (small_master.reshape(-1, 128),)
        output, input_grad, qkv_grad, up_grad, down_grad, out_grad, small_sum = whole_layer(
            lengths, tokens_in[0], cotangent[0], tall, rope_tables(length, HEADS // parts)
        )
        grads = (qkv_grad, out_grad, up_grad, down_grad, small_sum[: tall[4].shape[0]])
        return lamb_split(*update, grads, (output, input_grad))

    head_cols = D // parts
    ff_rows = down_master.shape[0] // parts
    qkv_own = sliced(qkv_master, part, parts, 3).astype(jnp.bfloat16)
    up_own = sliced(up_master, part, parts, shards).astype(jnp.bfloat16)
    down_own = lax.dynamic_slice_in_dim(down_master, part * ff_rows, ff_rows).astype(jnp.bfloat16)
    out_own = out_master.astype(jnp.bfloat16)
    small_own = small_master.astype(jnp.bfloat16)

    def small_vectors(small_all):
        vectors = split_small(small_all)
        vectors[4] = sliced(vectors[4][None], part, parts, 3)[0]
        vectors[6] = sliced(vectors[6][None], part, parts, shards)[0]
        return vectors

    def over_shards(own):
        return lax.all_gather(own, "fsdp", axis=0, tiled=True)

    x_all = lax.all_gather(tokens_in, "dp", axis=0, tiled=True)
    cotangent_all = lax.all_gather(cotangent, "dp", axis=0, tiled=True)
    lengths_all = lax.all_gather(lengths, "dp", axis=0, tiled=True)
    qkv_weight, up_weight, down_weight = (over_shards(w) for w in (qkv_own, up_own, down_own))
    out_weight = lax.dynamic_slice_in_dim(over_shards(out_own), part * head_cols, head_cols)
    gain_one, shift_one, gain_two, shift_two, qkv_bias, out_bias, up_bias, down_bias = (
        small_vectors(over_shards(small_own).astype(jnp.float32))
    )
    out_part, scaled_part, terms, sums = layer(
        x_all,
        cotangent_all,
        lengths_all,
        (qkv_weight, out_weight, up_weight, down_weight),
        (gain_one, shift_one, gain_two, shift_two, qkv_bias, up_bias),
        part,
    )
    norm_sums, d_qkv_bias, d_up_bias = sums
    out_sum = lax.psum_scatter(out_part, "dp", scatter_dimension=0, tiled=True)
    scaled = lax.psum_scatter(scaled_part, "dp", scatter_dimension=0, tiled=True)
    out_sum, scaled = out_sum.astype(jnp.float32), scaled.astype(jnp.float32)

    inputs = tokens_in[0].astype(jnp.float32)
    live = (jnp.arange(length) < lengths[0]).astype(jnp.float32)[:, None]
    back = cotangent[0].astype(jnp.float32) * live
    back_total = jnp.sum(back, axis=0)

    def spread(values, pieces):
        wide = jnp.zeros((pieces, parts, values.shape[0] // pieces), jnp.float32)
        return lax.dynamic_update_index_in_dim(
            wide, values.reshape(pieces, -1), part, axis=1
        ).reshape(-1)

    small_grad = jnp.concatenate(
        [
            norm_sums.reshape(4 * D),
            spread(d_qkv_bias, 3),
            back_total,
            spread(d_up_bias, shards),
            back_total,
        ]
    )
    small_sum = lax.psum(small_grad, ("dp", "fsdp"))
    small_rows = small_master.shape[0]
    small_sum = lax.dynamic_slice_in_dim(small_sum, shard * small_rows, small_rows)
    qkv_term, out_term, up_term, down_term = terms
    out_wide = lax.dynamic_update_slice_in_dim(
        jnp.zeros((D, D), jnp.bfloat16), out_term, part * head_cols, axis=0
    )

    def to_owner(term):
        own = lax.psum_scatter(term, "fsdp", scatter_dimension=0, tiled=True)
        return lax.all_gather(own, "dp", axis=0, tiled=False).astype(jnp.float32)

    reduced = (
        joined(to_owner(qkv_term), 3),
        lax.psum(
            lax.psum_scatter(out_wide, "fsdp", scatter_dimension=0, tiled=True), "dp"
        ).astype(jnp.float32),
        joined(to_owner(up_term), shards),
        to_owner(down_term).reshape(down_master.shape),
        small_sum,
    )

    unit_rows, inverse_rows = normalize(inputs)
    output = ((inputs + out_sum + out_bias + down_bias) * live).astype(jnp.bfloat16)
    input_grad = back + inverse_rows * (
        scaled
        - jnp.mean(scaled, axis=-1, keepdims=True)
        - unit_rows * jnp.mean(scaled * unit_rows, axis=-1, keepdims=True)
    )
    return (output[None], input_grad.astype(jnp.bfloat16)[None]) + lamb(*update, reduced)


def lamb_rows(first_old, second_old, master, grad):
    first_new = BETA_ONE * first_old + (1.0 - BETA_ONE) * grad
    second_new = BETA_TWO * second_old + (1.0 - BETA_TWO) * grad * grad
    root = second_new * lax.rsqrt(second_new)
    update = first_new / (root + ADAM_EPSILON) + DECAY * master
    return first_new, second_new, update


def lane_sums(values):
    squares = jnp.sum(values * values, axis=0, keepdims=True)
    total = squares[:, 0:128]
    for n in range(1, squares.shape[1] // 128):
        total = total + squares[:, n * 128 : (n + 1) * 128]
    return total


def moments_kernel(*refs):
    qkv_grad, out_grad, up_grad, down_grad, small_grad = refs[0:5]
    masters, firsts, seconds = refs[5:10], refs[10:15], refs[15:20]
    first_news, second_news, updates, squares = refs[20:25], refs[25:30], refs[30:35], refs[35]
    step = pl.program_id(0)

    @pl.when(step == 0)
    def _():
        squares[...] = jnp.zeros_like(squares)

    def one(number, span, grad):
        index = (slice(None), span)
        rows = firsts[number].shape[0]
        place = (pl.ds(pl.multiple_of(step * rows, rows), rows), span)
        master = masters[number][place]
        first_new, second_new, update = lamb_rows(
            firsts[number][index], seconds[number][index], master, grad
        )
        first_news[number][index] = first_new
        second_news[number][index] = second_new
        updates[number][place] = update
        return lane_sums(master), lane_sums(update)

    def add(number, pairs):
        weight, update = pairs[0]
        for more_weight, more_update in pairs[1:]:
            weight, update = weight + more_weight, update + more_update
        squares[number : number + 1] += weight
        squares[8 + number : 9 + number] += update

    f32 = jnp.float32
    parts = qkv_grad.shape[0]
    width = qkv_grad.shape[2] // 3
    add(
        0,
        [
            one(
                0,
                slice((c * parts + d) * width, (c * parts + d + 1) * width),
                qkv_grad[d, :, c * width : (c + 1) * width].astype(f32),
            )
            for c in range(3)
            for d in range(parts)
        ],
    )
    add(1, [one(1, slice(None), out_grad[...].astype(f32))])
    pieces = up_grad.shape[2] // 128
    add(
        2,
        [
            one(
                2,
                slice((g * parts + d) * 128, (g * parts + d + 1) * 128),
                up_grad[d, :, g * 128 : (g + 1) * 128].astype(f32),
            )
            for g in range(pieces)
            for d in range(parts)
        ],
    )
    add(3, [one(3, slice(None), down_grad[0].astype(f32))])

    @pl.when(step == 0)
    def _():
        first_new, second_new, update = lamb_rows(
            firsts[4][...], seconds[4][...], masters[4][...], small_grad[...]
        )
        first_news[4][...] = first_new
        second_news[4][...] = second_new
        updates[4][...] = update
        squares[4:5] += lane_sums(masters[4][...])
        squares[12:13] += lane_sums(update)


def lamb_specs(masters, steps):
    specs = [pl.BlockSpec((m.shape[0] // steps, m.shape[1]), lambda i: (i, 0)) for m in masters[:4]]
    return specs + [pl.BlockSpec(masters[4].shape, lambda i: (0, 0))]


def moments(grads, masters, firsts, seconds, steps=4):
    qkv_grad, out_grad, up_grad, down_grad, small_grad = grads
    shape = jax.ShapeDtypeStruct
    each = lamb_specs(masters, steps)
    rows = qkv_grad.shape[1]
    halves = steps // qkv_grad.shape[0]
    grad_specs = [
        pl.BlockSpec((qkv_grad.shape[0], rows // steps, qkv_grad.shape[2]), lambda i: (0, i, 0)),
        each[1],
        pl.BlockSpec((up_grad.shape[0], rows // steps, up_grad.shape[2]), lambda i: (0, i, 0)),
        pl.BlockSpec(
            (1, rows // halves, down_grad.shape[2]), lambda i: (i // halves, i % halves, 0)
        ),
        each[4],
    ]
    out = [shape(m.shape, jnp.float32) for m in masters]
    near = [pltpu.VMEM(m.shape, jnp.float32) for m in masters]
    results = pl.pallas_call(
        moments_kernel,
        grid=(steps,),
        in_specs=grad_specs + [VMEM_SPEC] * 5 + each * 2,
        out_specs=each * 2 + [VMEM_SPEC] * 5 + [pl.BlockSpec((16, 128), lambda i: (0, 0))],
        out_shape=out * 2 + near + [shape((16, 128), jnp.float32)],
        compiler_params=pltpu.CompilerParams(vmem_limit_bytes=24 << 20),
        name="moments",
    )(*grads, *masters, *firsts, *seconds)
    return results[0:5], results[5:10], results[10:15], results[15]


def norms_kernel(squares, total, everyone, send_sem, recv_sem):
    shard, part = lax.axis_index("fsdp"), lax.axis_index("dp")
    peers = [(part, (shard + k) % 8) for k in range(1, 8)]
    barrier = pltpu.get_barrier_semaphore()
    for peer in peers:
        pl.semaphore_signal(barrier, inc=1, device_id=peer, device_id_type=MESH_ID)
    pl.semaphore_wait(barrier, 7)
    for k in range(1, 8):
        send(
            squares, everyone.at[shard], send_sem.at[k - 1], recv_sem.at[k - 1], peers[k - 1]
        ).start()
    everyone[shard] = squares[...]
    for k in range(1, 8):
        arrived(everyone.at[(shard + 8 - k) % 8], recv_sem.at[k - 1], peers[7 - k])
    summed = everyone[0]
    for k in range(1, 8):
        summed = summed + everyone[k]
    norms = jnp.sqrt(jnp.sum(summed, axis=1, keepdims=True))
    total[...] = jnp.broadcast_to(norms, (16, 128))
    for k in range(1, 8):
        sent(squares, send_sem.at[k - 1], peers[k - 1])


def norms(squares):
    dma = pltpu.SemaphoreType.DMA
    return pl.pallas_call(
        norms_kernel,
        out_shape=jax.ShapeDtypeStruct((16, 128), jnp.float32),
        in_specs=[VMEM_SPEC],
        out_specs=VMEM_SPEC,
        scratch_shapes=[pltpu.VMEM((8, 16, 128), jnp.float32), dma((7,)), dma((7,))],
        compiler_params=pltpu.CompilerParams(
            collective_id=1, has_side_effects=True, vmem_limit_bytes=2 << 20
        ),
        name="norms",
    )(squares)


def step_kernel(*refs):
    total, masters, updates, layer_outs = refs[0], refs[1:6], refs[6:11], refs[11:13]
    news, outs, lamb_norms = refs[13:18], refs[18:20], refs[20]
    step = pl.program_id(0)
    for number in range(5):
        weight_norm = total[number : number + 1, 0:1]
        update_norm = total[8 + number : 9 + number, 0:1]
        scale = RATE * (weight_norm / update_norm)
        rows = news[number].shape[0]
        place = slice(None)
        if rows < masters[number].shape[0]:
            place = pl.ds(pl.multiple_of(step * rows, rows), rows)
        news[number][...] = masters[number][place] - scale * updates[number][place]
    for source, target in zip(layer_outs, outs):
        target[...] = source[...]

    @pl.when(step == 0)
    def _():
        row = lax.broadcasted_iota(jnp.int32, (8, 128), 0)
        lane = lax.broadcasted_iota(jnp.int32, (8, 128), 1)
        for n in range(2):
            half = jnp.where(row == lane, total[8 * n : 8 * n + 8], 0.0)
            lamb_norms[n : n + 1] = jnp.sum(half, axis=0, keepdims=True)[:, 0:5]


def step_masters(total, masters, updates, layer_outs, steps=4):
    shape = jax.ShapeDtypeStruct
    out_specs = [
        pl.BlockSpec((o.shape[0] // steps, o.shape[1]), lambda i: (i, 0)) for o in layer_outs
    ]
    results = pl.pallas_call(
        step_kernel,
        grid=(steps,),
        in_specs=[pl.BlockSpec((16, 128), lambda i: (0, 0))] + [VMEM_SPEC] * 10 + out_specs,
        out_specs=lamb_specs(masters, steps)
        + out_specs
        + [pl.BlockSpec((2, 5), lambda i: (0, 0))],
        out_shape=[shape(m.shape, jnp.float32) for m in masters]
        + [shape(o.shape, o.dtype) for o in layer_outs]
        + [shape((2, 5), jnp.float32)],
        compiler_params=pltpu.CompilerParams(vmem_limit_bytes=12 << 20),
        name="step_masters",
    )(total, *masters, *updates, *layer_outs)
    return results[0:5], results[5:7], results[7]


def lamb_split(masters, firsts, seconds, grads, layer_outs):
    def tall(arrays):
        return tuple(arrays[:4]) + (arrays[4].reshape(-1, 128),)

    def flat_small(arrays):
        return tuple(arrays[:4]) + (arrays[4].reshape(-1),)

    def placed(arrays, space):
        return tuple(pltpu.with_memory_space_constraint(a, space) for a in arrays)

    masters = placed(tall(masters), pltpu.VMEM)
    firsts, seconds = placed(tall(firsts), pltpu.HBM), placed(tall(seconds), pltpu.HBM)
    grads = placed(grads, pltpu.HBM)
    first_news, second_news, updates, squares = moments(grads, masters, firsts, seconds)
    news, outs, lamb_norms = step_masters(norms(squares), masters, updates, layer_outs)
    return (
        tuple(out[None] for out in outs)
        + flat_small(news)
        + flat_small(first_news)
        + flat_small(second_news)
        + (lamb_norms,)
    )


def lamb(masters, firsts, seconds, reduced):
    updates = []
    first_news = []
    second_news = []
    for first_old, second_old, master, grad_sum in zip(firsts, seconds, masters, reduced):
        first_new = BETA_ONE * first_old + (1.0 - BETA_ONE) * grad_sum
        second_new = BETA_TWO * second_old + (1.0 - BETA_TWO) * grad_sum * grad_sum
        updates.append(first_new / (jnp.sqrt(second_new) + ADAM_EPSILON) + DECAY * master)
        first_news.append(first_new)
        second_news.append(second_new)
    weight_squares, update_squares = lax.psum(
        (local_squares(masters), local_squares(updates)), "fsdp"
    )
    weight_norms = jnp.sqrt(weight_squares)
    update_norms = jnp.sqrt(update_squares)
    new_masters = [
        masters[number] - RATE * (weight_norms[number] / update_norms[number]) * updates[number]
        for number in range(5)
    ]
    lamb_norms = jnp.stack([weight_norms, update_norms])
    return tuple(new_masters) + tuple(first_news) + tuple(second_news) + (lamb_norms,)


def solution(mesh):
    in_specs = (
        P(("dp", "fsdp"), None, None),
        P(("dp", "fsdp"), None, None),
        P(("dp", "fsdp")),
        P("fsdp", None),
        P("fsdp", None),
        P("fsdp", None),
        P("fsdp", None),
        P("fsdp"),
        P("fsdp", None),
        P("fsdp", None),
        P("fsdp", None),
        P("fsdp", None),
        P("fsdp"),
        P("fsdp", None),
        P("fsdp", None),
        P("fsdp", None),
        P("fsdp", None),
        P("fsdp"),
    )
    out_specs = (
        P(("dp", "fsdp"), None, None),
        P(("dp", "fsdp"), None, None),
        P("fsdp", None),
        P("fsdp", None),
        P("fsdp", None),
        P("fsdp", None),
        P("fsdp"),
        P("fsdp", None),
        P("fsdp", None),
        P("fsdp", None),
        P("fsdp", None),
        P("fsdp"),
        P("fsdp", None),
        P("fsdp", None),
        P("fsdp", None),
        P("fsdp", None),
        P("fsdp"),
        P(),
    )
    return jax.shard_map(local_split, mesh=mesh, in_specs=in_specs, out_specs=out_specs, check_vma=False)
```

```python
import math

import jax
import jax.numpy as jnp
import numpy as np
from jax import lax
from jax.experimental import pallas as pl
from jax.experimental.pallas import tpu as pltpu
from jax.sharding import PartitionSpec as P

D = 1024
HEADS = 16
HD = 64
FF = 4096
ROT = 16
SMALL = 13312


NORM_EPSILON = 1e-05
ADAM_EPSILON = 1e-06
ROPE_BASE = 10000.0
RATE = 0.5
DECAY = 0.01
BETA_ONE = 0.5
BETA_TWO = 0.5


def split_small(small_vector):
    bounds = [0, D, 2 * D, 3 * D, 4 * D, 7 * D, 8 * D, 8 * D + FF, 9 * D + FF]
    return [small_vector[bounds[number] : bounds[number + 1]] for number in range(8)]


def normalize(values):
    average = jnp.mean(values, axis=-1, keepdims=True)
    centred = values - average
    variance = jnp.mean(centred * centred, axis=-1, keepdims=True)
    inverse = lax.rsqrt(variance + NORM_EPSILON)
    return (centred * inverse, inverse)


def rotary_tables(length):
    half_dims = ROT // 2
    position = jnp.arange(length, dtype=jnp.float32)[:, None]
    number = jnp.arange(half_dims, dtype=jnp.float32)[None, :]
    angle = position * jnp.exp(number * (-2.0 * math.log(ROPE_BASE) / ROT))
    return (jnp.cos(angle)[:, None, :], jnp.sin(angle)[:, None, :])


def rotate(heads_in, cosine_table, sine_table):
    half_dims = ROT // 2
    first_half = heads_in[..., :half_dims]
    second_half = heads_in[..., half_dims:ROT]
    return jnp.concatenate(
        [
            first_half * cosine_table - second_half * sine_table,
            second_half * cosine_table + first_half * sine_table,
            heads_in[..., ROT:],
        ],
        axis=-1,
    )


def rotate_back(grads_in, cosine_table, sine_table):
    half_dims = ROT // 2
    first_half = grads_in[..., :half_dims]
    second_half = grads_in[..., half_dims:ROT]
    return jnp.concatenate(
        [
            first_half * cosine_table + second_half * sine_table,
            second_half * cosine_table - first_half * sine_table,
            grads_in[..., ROT:],
        ],
        axis=-1,
    )


def gelu_slope(values):
    return 0.5 * (1.0 + lax.erf(values * 2.0 ** (-0.5))) + values * jnp.exp(
        -0.5 * values * values
    ) * (2.0 * math.pi) ** (-0.5)


def against(left, right):
    return lax.dot_general(
        left, right, (((1,), (1,)), ((), ())), preferred_element_type=jnp.float32
    )


def outer_sum(columns, right):
    return lax.dot_general(
        columns, right, (((0,), (0,)), ((), ())), preferred_element_type=jnp.float32
    )


def local_squares(arrays):
    return jnp.stack([jnp.sum(array_in * array_in) for array_in in arrays])


def sliced(master, part, parts, pieces):
    rows, columns = master.shape
    width = columns // (pieces * parts)
    return lax.dynamic_index_in_dim(
        master.reshape(rows, pieces, parts, width), part, axis=2, keepdims=False
    ).reshape(rows, pieces * width)


def joined(slices, pieces):
    parts, rows, columns = slices.shape
    width = columns // pieces
    return (
        slices.reshape(parts, rows, pieces, width)
        .transpose(1, 2, 0, 3)
        .reshape(rows, pieces * parts * width)
    )


def layer(x_all, cotangent_all, lengths_all, weights, small_all, part):
    qkv_weight, out_weight, up_weight, down_weight = weights
    group, length, _ = x_all.shape
    tokens = group * length
    head_cols = out_weight.shape[0]
    heads = head_cols // HD
    gain_one, shift_one, gain_two, shift_two, qkv_bias, up_bias = small_all
    inputs = x_all.reshape(tokens, D).astype(jnp.float32)
    position = jnp.arange(length)
    live = (position[None, :] < lengths_all[:, None]).astype(jnp.float32).reshape(tokens, 1)
    allowed = (position[None, None, :] <= position[None, :, None]) & (
        position[None, None, :] < lengths_all[:, None, None]
    )
    unit_rows, _ = normalize(inputs)
    normed_one = (unit_rows * gain_one + shift_one).astype(jnp.bfloat16)
    normed_two = (unit_rows * gain_two + shift_two).astype(jnp.bfloat16)
    projected = jnp.dot(normed_one, qkv_weight, preferred_element_type=jnp.float32) + qkv_bias
    projected = projected.reshape(group, length, 3, heads, HD)
    cosine_table, sine_table = rotary_tables(length)
    query_heads = rotate(projected[:, :, 0], cosine_table, sine_table).astype(jnp.bfloat16)
    key_heads = rotate(projected[:, :, 1], cosine_table, sine_table).astype(jnp.bfloat16)
    value_heads = projected[:, :, 2].astype(jnp.bfloat16)
    scores = jnp.einsum(
        "gqhd,gkhd->ghqk", query_heads, key_heads, preferred_element_type=jnp.float32
    ) * HD ** (-0.5)
    scores = jnp.where(allowed[:, None], scores, -1e30)
    row_top = jnp.max(scores, axis=-1, keepdims=True)
    raised = jnp.exp(scores - row_top)
    attend = raised / jnp.sum(raised, axis=-1, keepdims=True)
    attend_low = attend.astype(jnp.bfloat16)
    mixed = jnp.einsum(
        "ghqk,gkhd->gqhd", attend_low, value_heads, preferred_element_type=jnp.float32
    )
    mixed = mixed.reshape(tokens, head_cols).astype(jnp.bfloat16)
    hidden = jnp.dot(normed_two, up_weight, preferred_element_type=jnp.float32) + up_bias
    activated = jax.nn.gelu(hidden, approximate=False).astype(jnp.bfloat16)
    out_part = jnp.dot(mixed, out_weight, preferred_element_type=jnp.float32) + jnp.dot(
        activated, down_weight, preferred_element_type=jnp.float32
    )

    back = (cotangent_all.reshape(tokens, D).astype(jnp.float32) * live).astype(jnp.bfloat16)
    d_hidden = (against(back, down_weight) * gelu_slope(hidden)).astype(jnp.bfloat16)
    d_mixed = against(back, out_weight).astype(jnp.bfloat16).reshape(group, length, heads, HD)
    d_attend = jnp.einsum(
        "gqhd,gkhd->ghqk", d_mixed, value_heads, preferred_element_type=jnp.float32
    )
    row_inner = jnp.sum(attend * d_attend, axis=-1, keepdims=True)
    d_scores = (attend * (d_attend - row_inner)).astype(jnp.bfloat16)
    d_queries = jnp.einsum(
        "ghqk,gkhd->gqhd", d_scores, key_heads, preferred_element_type=jnp.float32
    ) * HD ** (-0.5)
    d_keys = jnp.einsum(
        "ghqk,gqhd->gkhd", d_scores, query_heads, preferred_element_type=jnp.float32
    ) * HD ** (-0.5)
    d_values = jnp.einsum(
        "ghqk,gqhd->gkhd", attend_low, d_mixed, preferred_element_type=jnp.float32
    )
    d_projected = jnp.stack(
        [
            rotate_back(d_queries, cosine_table, sine_table),
            rotate_back(d_keys, cosine_table, sine_table),
            d_values,
        ],
        axis=2,
    )
    d_projected = d_projected.reshape(tokens, 3 * head_cols).astype(jnp.bfloat16)
    d_normed_one = against(d_projected, qkv_weight)
    d_normed_two = against(d_hidden, up_weight)
    scaled_part = d_normed_one * gain_one + d_normed_two * gain_two
    norm_sums = jnp.stack(
        [
            jnp.sum(d_normed_one * unit_rows, axis=0),
            jnp.sum(d_normed_one, axis=0),
            jnp.sum(d_normed_two * unit_rows, axis=0),
            jnp.sum(d_normed_two, axis=0),
        ]
    )
    d_qkv_bias = jnp.sum(d_projected, axis=0, dtype=jnp.float32)
    d_up_bias = jnp.sum(d_hidden, axis=0, dtype=jnp.float32)
    terms = (
        outer_sum(normed_one, d_projected),
        outer_sum(mixed, back),
        outer_sum(normed_two, d_hidden),
        outer_sum(activated, back),
    )
    return (
        out_part.astype(jnp.bfloat16),
        scaled_part.astype(jnp.bfloat16),
        tuple(term.astype(jnp.bfloat16) for term in terms),
        (norm_sums, d_qkv_bias, d_up_bias),
    )


MESH_ID = pl.DeviceIdType.MESH
HALF = 128


class Place:
    def __init__(self):
        self.part = lax.axis_index("dp")
        self.shard = lax.axis_index("fsdp")
        self.z = self.shard // 2
        self.core = self.shard % 2
        self.x_part = 2 * (self.part // 2) + 1 - self.part % 2
        self.y_part = (self.part + 2) % 4
        self.far_part = 3 - self.part
        self.across_x = (self.x_part, self.shard)
        self.across_y = (self.y_part, self.shard)
        self.across_far = (self.far_part, self.shard)
        self.other_core = (self.part, 2 * self.z + 1 - self.core)
        self.up = (self.part, jnp.minimum(self.shard + 2, 7))
        self.down = (self.part, jnp.maximum(self.shard - 2, 0))

    def shard_after(self, k):
        return (self.part, (self.shard + k) % 8)


def send(source, target, send_sem, recv_sem, device):
    return pltpu.make_async_remote_copy(
        src_ref=source,
        dst_ref=target,
        send_sem=send_sem,
        recv_sem=recv_sem,
        device_id=device,
        device_id_type=MESH_ID,
    )


def arrived(target, recv_sem, device):
    send(target, target, recv_sem, recv_sem, device).wait_recv()


def sent(source, send_sem, device):
    send(source, source, send_sem, send_sem, device).wait_send()


def greet(at):
    barrier = pltpu.get_barrier_semaphore()
    peers = [at.across_x, at.across_y, at.across_far] + [at.shard_after(k) for k in range(1, 8)]
    for peer in peers:
        pl.semaphore_signal(barrier, inc=1, device_id=peer, device_id_type=MESH_ID)
    return lambda: pl.semaphore_wait(barrier, len(peers))


SPANS = ((0, 768), (768, 1792), (1792, 2816))
Q, U, N = 0, 1, 2


def nt(left, right):
    return lax.dot_general(
        left, right, (((1,), (1,)), ((), ())), preferred_element_type=jnp.float32
    )


def tn(left, right):
    return lax.dot_general(
        left, right, (((0,), (0,)), ((), ())), preferred_element_type=jnp.float32
    )


def nn(left, right):
    return jnp.dot(left, right, preferred_element_type=jnp.float32)


def flat(value):
    return value.reshape(value.shape[0] * value.shape[1], value.shape[2])


def layer_kernel(
    length_own,
    x_own,
    cot_own,
    qkv_master,
    out_master,
    up_master,
    down_master,
    small_master,
    tables_in,
    output_out,
    input_grad_out,
    qkv_all,
    up_all,
    down_all,
    out_grad,
    small_sum,
    tables,
    x_all,
    cot_all,
    len_all,
    w_all,
    out_all,
    small_own,
    small_all,
    vectors,
    qkv_bias,
    up_bias,
    stats,
    normed_one,
    normed_two,
    back,
    heads_qkv,
    mixed,
    d_projected,
    hidden,
    d_hidden,
    out_part,
    dx_part,
    terms,
    out_term,
    sums,
    d_qkv_bias,
    d_up_bias,
    small_part,
    plane_one,
    plane_two,
    core_in,
    line_in,
    out_core_in,
    out_line,
    out_line_in,
    small_in,
    small_total,
    small_plane,
    load_sem,
    plane_send,
    plane_recv,
    early_send,
    early_recv,
    len_send,
    len_recv,
    w_send,
    w_recv,
    out_send,
    out_recv,
    small_send,
    small_recv,
    part_send,
    part_recv,
    core_send,
    core_recv,
    line_send,
    line_recv,
    rows_send,
    rows_recv,
    all_send,
    all_recv,
    keep_sem,
    total_send,
    total_recv,
    store_sem,
):
    f32, bf16 = jnp.float32, jnp.bfloat16
    at = Place()
    z, core, part, shard = at.z, at.core, at.part, at.shard
    all_are_in = greet(at)
    length = x_own.shape[0]
    head_cols = mixed.shape[2]
    activated = normed_one
    place_x, place_y = part % 2, part // 2

    def near_first(i):
        return 2 * ((place_y + i // 2) % 2) + (place_x + i % 2) % 2

    def far_first(i):
        return 2 * ((place_y + 1 - i % 2) % 2) + (place_x + 1 - i // 2) % 2

    def piece(ref, slot, n):
        return ref.at[slot, :, SPANS[n][0] : SPANS[n][1]]

    plane_peers = (
        (at.across_x, at.x_part),
        (at.across_y, at.y_part),
        (at.across_far, at.far_part),
    )

    stage = [hidden.at[n, 0:128] for n in range(4)]
    loads = []
    for c in range(3):
        columns = pl.ds(pl.multiple_of(c * D + part * head_cols, 128), head_cols)
        target = stage[0].at[:, c * head_cols : (c + 1) * head_cols]
        loads.append((qkv_master.at[:, columns], target))
    loads.append((out_master, stage[1]))
    for g in range(8):
        columns = pl.ds(pl.multiple_of(g * (FF // 8) + part * 128, 128), 128)
        loads.append((up_master.at[:, columns], stage[2].at[:, g * 128 : (g + 1) * 128]))
    rows = pl.ds(pl.multiple_of(part * 128, 128), 128)
    loads.append((down_master.at[rows], stage[3]))
    loads.append((x_own, x_all.at[part]))
    loads.append((cot_own, cot_all.at[part]))
    loads.append((tables_in, tables))

    def load(n):
        return pltpu.make_async_copy(loads[n][0], loads[n][1], load_sem.at[n])

    for n in range(len(loads)):
        load(n).start()
    len_all[part] = jnp.full((8, 128), length_own[0], jnp.int32).astype(f32)
    small_own[...] = jnp.zeros_like(small_own)
    small_own[0:13] = small_master[...].astype(bf16).astype(f32)
    small_all[shard] = small_own[...]
    all_are_in()

    halves = (slice(0, HALF), slice(HALF, 2 * HALF))
    quarters = (slice(0, HALF // 2), slice(HALF // 2, HALF))
    activations = ((x_own, x_all), (cot_own, cot_all))
    neighbours = ((at.across_x, at.x_part), (at.across_y, at.y_part))

    def send_activations():
        for r, (peer, _) in enumerate(neighbours):
            send(
                x_own, x_all.at[part], plane_send.at[0, r], plane_recv.at[0, r], peer
            ).start()
        for r, (peer, _) in enumerate(neighbours):
            send(
                cot_own.at[halves[0]],
                cot_all.at[part, halves[0]],
                early_send.at[r],
                early_recv.at[r],
                peer,
            ).start()

    def send_rest():
        for r, (peer, _) in enumerate(neighbours):
            send(
                cot_own.at[halves[1]],
                cot_all.at[part, halves[1]],
                plane_send.at[1, r],
                plane_recv.at[1, r],
                peer,
            ).start()

    def cast(n, first, last):
        for m in range(first, last):
            load(m).wait()
        low, high = SPANS[n]
        w_all[shard, :, low:high] = stage[(0, 2, 3)[n]][:, 0 : high - low].astype(bf16)

    def send_own(n):
        cast(n, *((0, 3), (4, 12), (12, 13))[n])
        block = piece(w_all, shard, n)

        @pl.when(z < 3)
        def _():
            send(block, block, w_send.at[0, n, z], w_recv.at[n, shard], at.up).start()

        @pl.when(z > 0)
        def _():
            send(block, block, w_send.at[1, n, z], w_recv.at[n, shard], at.down).start()

        send(block, block, w_send.at[2, n, z], w_recv.at[n, shard], at.other_core).start()

    def forward(k, n):
        @pl.when(z >= k)
        def _():
            source = 2 * (z - k) + core
            block = piece(w_all, source, n)
            arrived(block, w_recv.at[n, source], at.down)

            @pl.when(z < 3)
            def _():
                send(block, block, w_send.at[0, n, z - k], w_recv.at[n, source], at.up).start()

            send(
                block, block, w_send.at[2, n, z - k], w_recv.at[n, source], at.other_core
            ).start()

        @pl.when(z + k <= 3)
        def _():
            source = 2 * (z + k) + core
            block = piece(w_all, source, n)
            arrived(block, w_recv.at[n, source], at.up)

            @pl.when(z > 0)
            def _():
                send(block, block, w_send.at[1, n, z + k], w_recv.at[n, source], at.down).start()

            send(
                block, block, w_send.at[2, n, z + k], w_recv.at[n, source], at.other_core
            ).start()

    def from_core(n):
        for other in range(4):
            source = 2 * other + 1 - core
            arrived(piece(w_all, source, n), w_recv.at[n, source], at.other_core)

    def send_out_rows():
        load(3).wait()

        @pl.when(z == part)
        def _():
            out_all[core] = stage[1][...].astype(bf16)
            block = out_all.at[core]

            @pl.when(z < 3)
            def _():
                send(block, block, out_send.at[0], out_recv.at[core], at.up).start()

            @pl.when(z > 0)
            def _():
                send(block, block, out_send.at[1], out_recv.at[core], at.down).start()

            send(block, block, out_send.at[2], out_recv.at[core], at.other_core).start()

    def out_from_core():
        arrived(out_all.at[1 - core], out_recv.at[1 - core], at.other_core)

    def forward_out(k):
        @pl.when((z - k == part) | (z + k == part))
        def _():
            block = out_all.at[core]
            arrived(block, out_recv.at[core], at.up)

            @pl.when((z > part) & (z < 3))
            def _():
                send(block, block, out_send.at[0], out_recv.at[core], at.up).start()

            @pl.when((z < part) & (z > 0))
            def _():
                send(block, block, out_send.at[1], out_recv.at[core], at.down).start()

            send(block, block, out_send.at[2], out_recv.at[core], at.other_core).start()

    def forward_neighbour(n, r):
        peer, source = neighbours[r]
        whole = activations[n][1]
        if n == 0:
            arrived(whole.at[source], plane_recv.at[0, r], peer)
        else:
            arrived(whole.at[source, halves[0]], early_recv.at[r], peer)
            arrived(whole.at[source, halves[1]], plane_recv.at[1, r], peer)
        block = whole.at[source, halves[r]]
        onward = neighbours[1 - r][0]
        send(block, block, plane_send.at[n, 2 + r], plane_recv.at[n, 2 + r], onward).start()

    def forward_x(n):
        forward_neighbour(n, 0)

    def forward_y(n):
        forward_neighbour(n, 1)

    def far_halves(n):
        whole = activations[n][1]
        arrived(whole.at[at.far_part, 0:HALF], plane_recv.at[n, 2], at.across_y)
        arrived(whole.at[at.far_part, HALF : 2 * HALF], plane_recv.at[n, 3], at.across_x)

    def send_small():
        for n, (peer, _) in enumerate(plane_peers):
            send(len_all.at[part], len_all.at[part], len_send.at[n], len_recv.at[n], peer).start()
        for k in range(1, 8):
            send(
                small_own,
                small_all.at[shard],
                small_send.at[k - 1],
                small_recv.at[k - 1],
                at.shard_after(k),
            ).start()

    def unpack_small():
        for n in (13, 14, 15):
            load(n).wait()
        for n, (peer, other) in enumerate(plane_peers):
            arrived(len_all.at[other], len_recv.at[n], peer)
        for k in range(1, 8):
            arrived(
                small_all.at[(shard + 8 - k) % 8], small_recv.at[k - 1], at.shard_after(8 - k)
            )
        for number, row in enumerate((0, 8, 16, 24, 56, 96)):
            for n in range(8):
                source = row + n
                vectors[number : number + 1, n * 128 : (n + 1) * 128] = small_all[
                    source // 13, source % 13 : source % 13 + 1
                ]
        for c in range(3):
            for n in range(2):
                source = 32 + 8 * c + 2 * part + n
                columns = slice((2 * c + n) * 128, (2 * c + n + 1) * 128)
                qkv_bias[:, columns] = small_all[source // 13, pl.ds(source % 13, 1)]
        for g in range(8):
            source = 64 + 4 * g + part
            up_bias[:, g * 128 : (g + 1) * 128] = small_all[source // 13, pl.ds(source % 13, 1)]

    sums[...] = jnp.zeros_like(sums)
    d_qkv_bias[...] = jnp.zeros_like(d_qkv_bias)
    d_up_bias[...] = jnp.zeros_like(d_up_bias)
    block_rows = 64

    def norm_rows(s):
        @pl.loop(0, length // block_rows)
        def _(i):
            r = pl.ds(pl.multiple_of(i * block_rows, block_rows), block_rows)
            values = x_all[s, r, :].astype(f32)
            mean = jnp.mean(values, axis=-1, keepdims=True)
            centred = values - mean
            inverse = lax.rsqrt(
                jnp.mean(centred * centred, axis=-1, keepdims=True) + NORM_EPSILON
            )
            stats[s, r, 0:1] = mean
            stats[s, r, 1:2] = inverse
            unit = centred * inverse
            normed_one[s, r, :] = (unit * vectors[0:1] + vectors[1:2]).astype(bf16)
            normed_two[s, r, :] = (unit * vectors[2:3] + vectors[3:4]).astype(bf16)

    def live_rows(s):
        index = lax.broadcasted_iota(jnp.int32, (length, 1), 0)
        return index.astype(f32) < len_all[s][0:1, 0:1]

    def rotate(value, sign):
        return (
            value * tables[0]
            + sign * pltpu.roll(value, head_cols - ROT // 2, 1) * tables[1]
            + sign * pltpu.roll(value, ROT // 2, 1) * tables[2]
        )

    def project(s):
        norm_rows(s)
        low, high = SPANS[Q]
        value = nn(normed_one[s], flat(w_all[:, :, low:high])) + qkv_bias[...]
        heads_qkv[s, :, 0:head_cols] = rotate(value[:, 0:head_cols], 1.0).astype(bf16)
        heads_qkv[s, :, head_cols : 2 * head_cols] = rotate(
            value[:, head_cols : 2 * head_cols], 1.0
        ).astype(bf16)
        heads_qkv[s, :, 2 * head_cols :] = value[:, 2 * head_cols :].astype(bf16)

    def attend(s):
        cot = cot_all[s]
        back[s] = jnp.where(live_rows(s), cot, jnp.zeros_like(cot))
        queries = heads_qkv[s, :, 0:head_cols]
        keys = heads_qkv[s, :, head_cols : 2 * head_cols]
        values = heads_qkv[s, :, 2 * head_cols :]
        d_mixed = nt(back[s], flat(out_all[...])).astype(bf16)
        row = lax.broadcasted_iota(jnp.int32, (length, length), 0)
        column = lax.broadcasted_iota(jnp.int32, (length, length), 1)
        allowed = (column <= row) & (column.astype(f32) < len_all[s][0:1, 0:1])
        lane = lax.broadcasted_iota(jnp.int32, (length, head_cols), 1)
        zero = jnp.zeros((), bf16)
        mixed_sum = jnp.zeros((length, head_cols), f32)
        d_queries = d_keys = d_values = mixed_sum
        for h in range(head_cols // HD):
            of_head = (lane >= h * HD) & (lane < (h + 1) * HD)
            q_h, k_h, v_h, d_h = (
                jnp.where(of_head, t, zero) for t in (queries, keys, values, d_mixed)
            )
            scores = jnp.where(allowed, nt(q_h, keys) * HD**-0.5, -1e30)
            raised = jnp.exp(scores - jnp.max(scores, axis=-1, keepdims=True))
            weights = raised * (1.0 / jnp.sum(raised, axis=-1, keepdims=True))
            low = weights.astype(bf16)
            mixed_sum = mixed_sum + nn(low, v_h)
            d_weights = nt(d_h, values)
            inner = jnp.sum(weights * d_weights, axis=-1, keepdims=True)
            d_scores = (weights * (d_weights - inner)).astype(bf16)
            d_queries = d_queries + nn(d_scores, k_h)
            d_keys = d_keys + tn(d_scores, q_h)
            d_values = d_values + tn(low, d_h)
        mixed[s] = mixed_sum.astype(bf16)
        for n, value in enumerate(
            (rotate(d_queries * HD**-0.5, -1.0), rotate(d_keys * HD**-0.5, -1.0), d_values)
        ):
            rounded = value.astype(bf16)
            columns = slice(n * head_cols, (n + 1) * head_cols)
            d_projected[s, :, columns] = rounded
            d_qkv_bias[:, columns] += jnp.sum(rounded.astype(f32), axis=0, keepdims=True)

    def gradient(left, right, n):
        low, high = SPANS[n]

        @pl.loop(0, 8)
        def _(f):
            columns = pl.ds(pl.multiple_of(f * 128, 128), 128)
            terms[f, :, low:high] = tn(flat(left[:, :, columns]), flat(right[...])).astype(bf16)

    def to_core(n):
        for other in range(4):
            send(
                piece(terms, 2 * other + 1 - core, n),
                piece(core_in, other, n),
                core_send.at[n, other],
                core_recv.at[n, other],
                at.other_core,
            ).start()

    def add_core(n):
        low, high = SPANS[n]
        for other in (3, 0, 2, 1):
            arrived(piece(core_in, other, n), core_recv.at[n, other], at.other_core)
            terms[2 * other + core, :, low:high] = (
                terms[2 * other + core, :, low:high].astype(f32)
                + core_in[other, :, low:high].astype(f32)
            ).astype(bf16)

    def pass_on(n, me, target):
        low, high = SPANS[n]

        @pl.when(z == me)
        def _():
            own = piece(terms, 2 * target + core, n)
            if me not in (0, 3):
                source = at.down if me < target else at.up
                arrived(piece(line_in, target, n), line_recv.at[n, target], source)
                terms[2 * target + core, :, low:high] = (
                    terms[2 * target + core, :, low:high].astype(f32)
                    + line_in[target, :, low:high].astype(f32)
                ).astype(bf16)
            slot = 4 if me == target + 1 else target
            send(
                own,
                piece(line_in, slot, n),
                line_send.at[n, target],
                line_recv.at[n, slot],
                at.up if me < target else at.down,
            ).start()

    def line_starts(n):
        for target in (3, 2, 1):
            pass_on(n, 0, target)
        for target in (0, 1, 2):
            pass_on(n, 3, target)

    def line_step(n, step):
        for me, target in (((1, 3), (2, 0)), ((1, 2), (2, 1)), ((2, 3), (1, 0)))[step]:
            pass_on(n, me, target)

    wholes = (qkv_all, up_all, down_all)

    def line_ends(n):
        low, high = SPANS[n]
        total = 2 * z + core

        def add(slot, source):
            arrived(piece(line_in, slot, n), line_recv.at[n, slot], source)
            terms[total, :, low:high] = (
                terms[total, :, low:high].astype(f32) + line_in[slot, :, low:high].astype(f32)
            ).astype(bf16)

        @pl.when(z > 0)
        def _():
            add(z, at.down)

        @pl.when(z < 3)
        def _():
            add(4, at.up)

        own = piece(terms, total, n)
        target = wholes[n].at[part]
        send(own, target, all_send.at[n, 0], all_recv.at[n, 0], at.across_x).start()
        send(own, target, all_send.at[n, 1], all_recv.at[n, 1], at.across_y).start()
        pltpu.make_async_copy(own, target, keep_sem.at[n]).start()

    def share(n):
        whole = wholes[n]
        arrived(whole.at[at.x_part], all_recv.at[n, 0], at.across_x)
        block = whole.at[at.x_part, 0:64]
        send(block, block, all_send.at[n, 2], all_recv.at[n, 2], at.across_y).start()
        arrived(whole.at[at.y_part], all_recv.at[n, 1], at.across_y)
        block = whole.at[at.y_part, 64:128]
        send(block, block, all_send.at[n, 3], all_recv.at[n, 3], at.across_x).start()

    def out_to_core():
        send(
            out_term.at[1 - core], out_core_in, rows_send.at[0], rows_recv.at[0], at.other_core
        ).start()

    def out_add(block):
        out_line[...] = (out_line[...].astype(f32) + block.astype(f32)).astype(bf16)

    def out_add_core():
        arrived(out_core_in, rows_recv.at[0], at.other_core)
        out_line[...] = out_term[core]
        out_add(out_core_in[...])

    def out_step(step):
        @pl.when((z == step) & (z < part))
        def _():
            if step > 0:
                arrived(out_line_in.at[0], rows_recv.at[1], at.down)
                out_add(out_line_in[0])
            send(out_line, out_line_in.at[0], rows_send.at[1], rows_recv.at[1], at.up).start()

        @pl.when((z == 3 - step) & (z > part))
        def _():
            if step > 0:
                arrived(out_line_in.at[1], rows_recv.at[2], at.up)
                out_add(out_line_in[1])
            send(out_line, out_line_in.at[1], rows_send.at[1], rows_recv.at[2], at.down).start()

    def out_ends():
        @pl.when(z == part)
        def _():
            @pl.when(z > 0)
            def _():
                arrived(out_line_in.at[0], rows_recv.at[1], at.down)
                out_add(out_line_in[0])

            @pl.when(z < 3)
            def _():
                arrived(out_line_in.at[1], rows_recv.at[2], at.up)
                out_add(out_line_in[1])

            for r, (peer, _) in enumerate(neighbours):
                send(
                    out_line.at[quarters[r]],
                    out_grad.at[quarters[r]],
                    rows_send.at[2 + r],
                    rows_recv.at[3],
                    peer,
                ).start()
            pltpu.make_async_copy(out_line, out_grad, keep_sem.at[3]).start()

    def out_share():
        for r, (peer, source) in enumerate(neighbours):

            @pl.when(z == source)
            def _():
                block = out_grad.at[quarters[r]]
                arrived(block, rows_recv.at[3], peer)
                onward = neighbours[1 - r][0]
                send(block, block, rows_send.at[4], rows_recv.at[4 + r], onward).start()

    def out_far():
        @pl.when(z == at.far_part)
        def _():
            for r, (peer, _) in enumerate(neighbours):
                block = out_grad.at[quarters[r]]
                arrived(block, rows_recv.at[4 + r], neighbours[1 - r][0])
                send(block, block, rows_send.at[2 + r], rows_recv.at[4 + r], peer).start()

    def out_gradient():
        for n in range(2):
            columns = slice(n * 128, (n + 1) * 128)
            out_term[n] = tn(flat(mixed[:, :, columns]), flat(back[...])).astype(bf16)

    part_refs = (out_part, dx_part)
    routes = (
        (halves[0], at.across_x, at.x_part, at.across_y, at.y_part),
        (halves[1], at.across_y, at.y_part, at.across_x, at.x_part),
    )

    def send_part(n, r, m):
        half, peer, peer_part, _, _ = routes[r]
        target = (at.far_part, peer_part)[m]
        send(
            part_refs[n].at[target, half],
            plane_one.at[n, r, m],
            part_send.at[n, r, m],
            part_recv.at[n, r, m],
            peer,
        ).start()

    def turn_part(n, r):
        half, peer, _, turn, turned = routes[r]
        arrived(plane_one.at[n, r, 0], part_recv.at[n, r, 0], peer)
        part_refs[n][turned, half] = (
            part_refs[n][turned, half].astype(f32) + plane_one[n, r, 0].astype(f32)
        ).astype(bf16)
        send(
            part_refs[n].at[turned, half],
            plane_two.at[n, r],
            part_send.at[n, r, 2],
            part_recv.at[n, r, 2],
            turn,
        ).start()

    def whole_part(n, r):
        half, peer, _, turn, _ = routes[r]
        arrived(plane_one.at[n, r, 1], part_recv.at[n, r, 1], peer)
        arrived(plane_two.at[n, r], part_recv.at[n, r, 2], turn)
        return (
            part_refs[n][part, half].astype(f32)
            + plane_one[n, r, 1].astype(f32)
            + plane_two[n, r].astype(f32)
        )

    up_low, up_high = SPANS[U]
    down_low, down_high = SPANS[N]

    def feed_in(s):
        value = nn(normed_two[s], flat(w_all[:, :, up_low:up_high])) + up_bias[...]
        hidden[s] = value
        activated[s] = (value * (0.5 * (1.0 + lax.erf(value * 2.0**-0.5)))).astype(bf16)

    def feed_out(s):
        out_part[s] = (
            nn(activated[s], flat(w_all[:, :, down_low:down_high]))
            + nn(mixed[s], flat(out_all[...]))
        ).astype(bf16)

    def feed_back(s):
        slope = gelu_slope(hidden[s])
        low = (nt(back[s], flat(w_all[:, :, down_low:down_high])) * slope).astype(bf16)
        d_hidden[s] = low
        d_up_bias[...] += jnp.sum(low.astype(f32), axis=0, keepdims=True)

    def norm_back(s):
        d_two = nt(d_hidden[s], flat(w_all[:, :, up_low:up_high]))
        d_one = nt(d_projected[s], flat(w_all[:, :, SPANS[Q][0] : SPANS[Q][1]]))
        unit = (x_all[s].astype(f32) - stats[s][:, 0:1]) * stats[s][:, 1:2]
        sums[0:1] += jnp.sum(d_one * unit, axis=0, keepdims=True)
        sums[1:2] += jnp.sum(d_one, axis=0, keepdims=True)
        sums[2:3] += jnp.sum(d_two * unit, axis=0, keepdims=True)
        sums[3:4] += jnp.sum(d_two, axis=0, keepdims=True)
        dx_part[s] = (d_one * vectors[0:1] + d_two * vectors[2:3]).astype(bf16)

    def place(row, value):
        small_part[row // 13, pl.ds(row % 13, 1)] = value

    def small_start():
        small_part[...] = jnp.zeros_like(small_part)
        back_total = jnp.sum(back[part].astype(f32), axis=0, keepdims=True)
        for n in range(8):
            columns = slice(n * 128, (n + 1) * 128)
            for number in range(4):
                place(8 * number + n, sums[number : number + 1, columns])
            place(56 + n, back_total[:, columns])
            place(96 + n, back_total[:, columns])
            place(64 + 4 * n + part, d_up_bias[:, columns])
        for c in range(3):
            for n in range(2):
                columns = slice((2 * c + n) * 128, (2 * c + n + 1) * 128)
                place(32 + 8 * c + 2 * part + n, d_qkv_bias[:, columns])
        for k in range(1, 8):
            send(
                small_part.at[(shard + k) % 8],
                small_in.at[k - 1],
                total_send.at[k - 1],
                total_recv.at[k - 1],
                at.shard_after(k),
            ).start()

    def small_turn():
        total = small_part[shard]
        for k in range(1, 8):
            arrived(small_in.at[k - 1], total_recv.at[k - 1], at.shard_after(8 - k))
            total = total + small_in[k - 1]
        small_total[...] = total
        for n, (peer, _) in enumerate(plane_peers):
            send(
                small_total, small_plane.at[part], total_send.at[7 + n], total_recv.at[7 + n], peer
            ).start()
        small_plane[part] = total

    def small_end():
        for n, (peer, other) in enumerate(plane_peers):
            arrived(small_plane.at[other], total_recv.at[7 + n], peer)
        small_sum[...] = (small_plane[0] + small_plane[1]) + (small_plane[2] + small_plane[3])

    def write_output(r):
        half = halves[r]
        values = x_all[part, half].astype(f32)
        summed = values + whole_part(0, r) + vectors[4:5] + vectors[5:6]
        output = out_part.at[part]
        output[half] = jnp.where(live_rows(part)[half], summed, 0.0).astype(bf16)
        pltpu.make_async_copy(output.at[half], output_out.at[half], store_sem.at[0, r]).start()

    def write_input_grad(r):
        half = halves[r]
        scaled = whole_part(1, r)
        inverse = stats[part, half, 1:2]
        unit = (x_all[part, half].astype(f32) - stats[part, half, 0:1]) * inverse
        result = back[part, half].astype(f32) + inverse * (
            scaled
            - jnp.mean(scaled, axis=-1, keepdims=True)
            - unit * jnp.mean(scaled * unit, axis=-1, keepdims=True)
        )
        input_grad = dx_part.at[part]
        input_grad[half] = result.astype(bf16)
        pltpu.make_async_copy(
            input_grad.at[half], input_grad_out.at[half], store_sem.at[1, r]
        ).start()

    at_end = (z == 0) | (z == 3)
    middle = (z == 1) | (z == 2)
    send_activations()
    send_own(Q)
    send_out_rows()
    send_small()

    @pl.when(middle)
    def _():
        send_rest()
        forward(1, Q)
        forward_out(1)
        forward(2, Q)
        forward_y(0)

    send_own(U)

    @pl.when(at_end)
    def _():
        forward_y(0)
        forward(1, Q)
        forward(2, Q)

    @pl.when(middle)
    def _():
        forward_out(2)
        forward(1, U)

    forward_x(0)

    @pl.when(middle)
    def _():
        from_core(Q)

    send_own(N)

    @pl.when(at_end)
    def _():
        send_rest()
        forward(3, Q)
        from_core(Q)

    unpack_small()

    @pl.loop(0, 4)
    def _(i):
        project(near_first(i))

        @pl.when((i == 0) & at_end)
        def _():
            forward_out(1)
            far_halves(0)

        @pl.when((i == 1) & at_end)
        def _():
            forward_out(2)

        @pl.when((i == 2) & at_end)
        def _():
            forward_out(3)

        @pl.when((i == 2) & middle)
        def _():
            far_halves(0)
            forward_x(1)
            forward(2, U)
            out_from_core()

    @pl.when(at_end)
    def _():
        out_from_core()

    forward_y(1)

    @pl.when(at_end)
    def _():
        forward_x(1)

    @pl.when(middle)
    def _():
        forward(1, N)

    @pl.loop(0, 4)
    def _(i):
        attend(near_first(i))

        @pl.when((i == 2) & middle)
        def _():
            forward(2, N)

        @pl.when(i == 2)
        def _():
            far_halves(1)

        @pl.when((i == 2) & at_end)
        def _():
            forward(1, U)

    @pl.when(at_end)
    def _():
        forward(2, U)

    @pl.when(middle)
    def _():
        from_core(N)

    gradient(normed_one, d_projected, Q)

    @pl.when(at_end)
    def _():
        to_core(Q)

    @pl.when(middle)
    def _():
        from_core(U)

    out_gradient()

    @pl.when(at_end)
    def _():
        forward(3, U)
        add_core(Q)
        out_to_core()
        line_starts(Q)
        forward(1, N)
        from_core(U)

    @pl.when(middle)
    def _():
        to_core(Q)

    @pl.loop(0, 4)
    def _(i):
        feed_in(i)

        @pl.when((i == 2) & at_end)
        def _():
            forward(2, N)

    @pl.when(at_end)
    def _():
        out_add_core()

    gradient(activated, back, N)

    @pl.when(at_end)
    def _():
        out_step(0)
        forward(3, N)
        from_core(N)

    @pl.loop(0, 4)
    def _(i):
        feed_out(far_first(i))

        @pl.when(i == 0)
        def _():
            send_part(0, 0, 0)
            send_part(0, 1, 0)

        @pl.when((i == 0) & at_end)
        def _():
            to_core(N)

        @pl.when((i == 1) & at_end)
        def _():
            send_part(0, 0, 1)
            add_core(N)

        @pl.when((i == 2) & at_end)
        def _():
            send_part(0, 1, 1)

    @pl.when(middle)
    def _():
        out_to_core()

    @pl.loop(0, 4)
    def _(i):
        feed_back(far_first(i))

        @pl.when((i == 0) & middle)
        def _():
            send_part(0, 1, 1)
            add_core(Q)

        @pl.when((i == 1) & middle)
        def _():
            out_add_core()

        @pl.when(i == 2)
        def _():
            send_part(1, 0, 0)
            send_part(1, 1, 0)

        @pl.when((i == 2) & middle)
        def _():
            turn_part(0, 0)
            turn_part(0, 1)
            line_step(Q, 1)
            out_step(1)
            add_core(N)

        @pl.when((i == 3) & middle)
        def _():
            send_part(1, 1, 1)
            line_step(N, 0)

        norm_back(far_first(i))

        @pl.when((i == 0) & at_end)
        def _():
            line_starts(N)

        @pl.when((i == 0) & middle)
        def _():
            send_part(0, 0, 1)
            line_step(Q, 0)

        @pl.when((i == 1) & middle)
        def _():
            to_core(N)

        @pl.when((i == 2) & at_end)
        def _():
            turn_part(0, 0)
            send_part(1, 1, 1)

        @pl.when((i == 2) & middle)
        def _():
            line_step(Q, 2)

    @pl.when(at_end)
    def _():
        turn_part(0, 1)

    @pl.when(middle)
    def _():
        send_part(1, 0, 1)

    gradient(normed_two, d_hidden, U)

    @pl.when(at_end)
    def _():
        send_part(1, 0, 1)

    @pl.when(middle)
    def _():
        small_start()

    to_core(U)

    @pl.when(at_end)
    def _():
        small_start()

    line_ends(Q)

    @pl.when(middle)
    def _():
        line_step(N, 1)
        line_step(N, 2)

    add_core(U)

    @pl.when(middle)
    def _():
        out_step(2)
        out_ends()
        line_ends(N)
        turn_part(1, 1)
        line_step(U, 0)
        small_turn()
        out_share()

    turn_part(1, 0)

    @pl.when(at_end)
    def _():
        line_starts(U)
        turn_part(1, 1)
        line_ends(N)
        out_ends()

    share(Q)

    @pl.when(middle)
    def _():
        line_step(U, 1)
        line_step(U, 2)
        write_input_grad(1)
        line_ends(U)
        write_output(0)
        share(N)

    write_output(1)

    @pl.when(at_end)
    def _():
        write_output(0)
        out_share()
        write_input_grad(1)
        share(N)
        line_ends(U)

    @pl.when(middle)
    def _():
        share(U)
        write_input_grad(0)

    out_far()

    @pl.when(at_end)
    def _():
        small_turn()
        write_input_grad(0)
        share(U)

    small_end()
    output, input_grad = out_part.at[part], dx_part.at[part]
    for r, half in enumerate(halves):
        pltpu.make_async_copy(output.at[half], output_out.at[half], store_sem.at[0, r]).wait()
        pltpu.make_async_copy(
            input_grad.at[half], input_grad_out.at[half], store_sem.at[1, r]
        ).wait()
    for r, (peer, source) in enumerate(neighbours):

        @pl.when(z == source)
        def _():
            arrived(out_grad.at[quarters[1 - r]], rows_recv.at[5 - r], neighbours[1 - r][0])
            sent(out_grad.at[quarters[r]], rows_send.at[4], neighbours[1 - r][0])

        @pl.when((z == part) | (z == at.far_part))
        def _():
            sent(out_grad.at[quarters[r]], rows_send.at[2 + r], peer)

    @pl.when(z != part)
    def _():
        sent(out_line, rows_send.at[1], at.up)

    @pl.when(z == part)
    def _():
        pltpu.make_async_copy(out_line, out_grad, keep_sem.at[3]).wait()

    sent(out_line, rows_send.at[0], at.other_core)
    for r, (peer, _) in enumerate(neighbours):
        sent(x_own, plane_send.at[0, r], peer)
        sent(cot_own.at[halves[0]], early_send.at[r], peer)
        sent(cot_own.at[halves[1]], plane_send.at[1, r], peer)
        for n in range(2):
            sent(x_all.at[part, halves[0]], plane_send.at[n, 2 + r], peer)
    for n, (peer, _) in enumerate(plane_peers):
        sent(len_all.at[part], len_send.at[n], peer)
        sent(small_total, total_send.at[7 + n], peer)
    for k in range(1, 8):
        sent(small_own, small_send.at[k - 1], at.shard_after(k))
        sent(small_total, total_send.at[k - 1], at.shard_after(k))
    for n in range(3):
        for other in range(4):
            block = piece(w_all, 2 * other + core, n)
            sent(block, w_send.at[2, n, other], at.other_core)
            sent(block, core_send.at[n, other], at.other_core)

            @pl.when((other <= z) & (z < 3))
            def _():
                sent(block, w_send.at[0, n, other], at.up)

            @pl.when((other >= z) & (z > 0))
            def _():
                sent(block, w_send.at[1, n, other], at.down)

            @pl.when(z != other)
            def _():
                sent(block, line_send.at[n, other], at.up)

    block = out_all.at[core]
    sent(block, out_send.at[2], at.other_core)

    @pl.when((z >= part) & (z < 3))
    def _():
        sent(block, out_send.at[0], at.up)

    @pl.when((z <= part) & (z > 0))
    def _():
        sent(block, out_send.at[1], at.down)

    for n in range(2):
        for r in range(2):
            for m in range(3):
                sent(plane_two.at[n, r], part_send.at[n, r, m], at.across_x)
    for n, whole in enumerate(wholes):
        arrived(whole.at[at.far_part, 0:64], all_recv.at[n, 2], at.across_y)
        arrived(whole.at[at.far_part, 64:128], all_recv.at[n, 3], at.across_x)
        own = piece(terms, shard, n)
        sent(own, all_send.at[n, 0], at.across_x)
        sent(own, all_send.at[n, 1], at.across_y)
        sent(whole.at[part, 0:64], all_send.at[n, 2], at.across_y)
        sent(whole.at[part, 64:128], all_send.at[n, 3], at.across_x)
        pltpu.make_async_copy(own, whole.at[part], keep_sem.at[n]).wait()


VMEM_SPEC = pl.BlockSpec(memory_space=pltpu.VMEM)
HBM_SPEC = pl.BlockSpec(memory_space=pl.ANY)


def whole_layer(lengths, x_own, cot_own, masters, tables):
    shape = jax.ShapeDtypeStruct
    vmem, dma = pltpu.VMEM, pltpu.SemaphoreType.DMA
    bf16, f32 = jnp.bfloat16, jnp.float32
    length = x_own.shape[0]
    group = 4
    head_cols, wide, rows = D // group, 2816, 128

    def by_sequence(width, kind=bf16):
        return vmem((group, length, width), kind)

    return pl.pallas_call(
        layer_kernel,
        out_shape=(
            shape(x_own.shape, bf16),
            shape(x_own.shape, bf16),
            shape((group, rows, 3 * head_cols), bf16),
            shape((group, rows, FF // group), bf16),
            shape((group, rows, D), bf16),
            shape((rows, D), bf16),
            shape((16, 128), f32),
        ),
        in_specs=[pl.BlockSpec(memory_space=pltpu.SMEM)]
        + [HBM_SPEC] * 6
        + [VMEM_SPEC, HBM_SPEC],
        out_specs=(HBM_SPEC,) * 6 + (VMEM_SPEC,),
        scratch_shapes=[
            vmem(tables.shape, f32),
            by_sequence(D),
            by_sequence(D),
            vmem((group, 8, 128), f32),
            vmem((8, rows, wide), bf16),
            vmem((2, rows, D), bf16),
            vmem((16, 128), f32),
            vmem((8, 16, 128), f32),
            vmem((8, D), f32),
            vmem((1, 3 * head_cols), f32),
            vmem((1, FF // group), f32),
            by_sequence(128, f32),
            by_sequence(D),
            by_sequence(D),
            by_sequence(D),
            by_sequence(3 * head_cols),
            by_sequence(head_cols),
            by_sequence(3 * head_cols),
            by_sequence(FF // group, f32),
            by_sequence(FF // group),
            by_sequence(D),
            by_sequence(D),
            vmem((8, rows, wide), bf16),
            vmem((2, rows, D), bf16),
            vmem((8, D), f32),
            vmem((1, 3 * head_cols), f32),
            vmem((1, FF // group), f32),
            vmem((8, 16, 128), f32),
            vmem((2, 2, 2, HALF, D), bf16),
            vmem((2, 2, HALF, D), bf16),
            vmem((4, rows, wide), bf16),
            vmem((5, rows, wide), bf16),
            vmem((rows, D), bf16),
            vmem((rows, D), bf16),
            vmem((2, rows, D), bf16),
            vmem((7, 16, 128), f32),
            vmem((16, 128), f32),
            vmem((4, 16, 128), f32),
            dma((16,)),
            dma((2, 4)),
            dma((2, 4)),
            dma((2,)),
            dma((2,)),
            dma((3,)),
            dma((3,)),
            dma((3, 3, 4)),
            dma((3, 8)),
            dma((3,)),
            dma((2,)),
            dma((7,)),
            dma((7,)),
            dma((2, 2, 3)),
            dma((2, 2, 3)),
            dma((3, 4)),
            dma((3, 4)),
            dma((3, 4)),
            dma((3, 5)),
            dma((5,)),
            dma((6,)),
            dma((3, 4)),
            dma((3, 4)),
            dma((4,)),
            dma((10,)),
            dma((10,)),
            dma((2, 2)),
        ],
        compiler_params=pltpu.CompilerParams(
            collective_id=0, has_side_effects=True, vmem_limit_bytes=54 << 20
        ),
        name="layer",
    )(lengths, x_own, cot_own, *masters, tables)


def rope_tables(length, heads):
    half = ROT // 2
    angle = np.arange(length)[:, None] * ROPE_BASE ** (-2.0 * np.arange(half) / ROT)[None]
    table = np.zeros((3, length, HD), np.float32)
    table[0] = 1.0
    table[0, :, :half] = table[0, :, half:ROT] = np.cos(angle)
    table[1, :, :half] = -np.sin(angle)
    table[2, :, half:ROT] = np.sin(angle)
    return jnp.asarray(np.tile(table, (1, 1, heads)))


def local_split(
    tokens_in,
    cotangent,
    lengths,
    qkv_master,
    out_master,
    up_master,
    down_master,
    small_master,
    qkv_first,
    out_first,
    up_first,
    down_first,
    small_first,
    qkv_second,
    out_second,
    up_second,
    down_second,
    small_second,
):
    masters = (qkv_master, out_master, up_master, down_master, small_master)
    firsts = (qkv_first, out_first, up_first, down_first, small_first)
    seconds = (qkv_second, out_second, up_second, down_second, small_second)
    parts, shards = lax.axis_size("dp"), lax.axis_size("fsdp")
    part, shard = lax.axis_index("dp"), lax.axis_index("fsdp")
    length = tokens_in.shape[1]
    update = (masters, firsts, seconds)
    if (parts, shards) == (4, 8):
        tall = tuple(masters[:4]) + (small_master.reshape(-1, 128),)
        output, input_grad, qkv_grad, up_grad, down_grad, out_grad, small_sum = whole_layer(
            lengths, tokens_in[0], cotangent[0], tall, rope_tables(length, HEADS // parts)
        )
        grads = (qkv_grad, out_grad, up_grad, down_grad, small_sum[: tall[4].shape[0]])
        return lamb_split(*update, grads, (output, input_grad))

    head_cols = D // parts
    ff_rows = down_master.shape[0] // parts
    qkv_own = sliced(qkv_master, part, parts, 3).astype(jnp.bfloat16)
    up_own = sliced(up_master, part, parts, shards).astype(jnp.bfloat16)
    down_own = lax.dynamic_slice_in_dim(down_master, part * ff_rows, ff_rows).astype(jnp.bfloat16)
    out_own = out_master.astype(jnp.bfloat16)
    small_own = small_master.astype(jnp.bfloat16)

    def small_vectors(small_all):
        vectors = split_small(small_all)
        vectors[4] = sliced(vectors[4][None], part, parts, 3)[0]
        vectors[6] = sliced(vectors[6][None], part, parts, shards)[0]
        return vectors

    def over_shards(own):
        return lax.all_gather(own, "fsdp", axis=0, tiled=True)

    x_all = lax.all_gather(tokens_in, "dp", axis=0, tiled=True)
    cotangent_all = lax.all_gather(cotangent, "dp", axis=0, tiled=True)
    lengths_all = lax.all_gather(lengths, "dp", axis=0, tiled=True)
    qkv_weight, up_weight, down_weight = (over_shards(w) for w in (qkv_own, up_own, down_own))
    out_weight = lax.dynamic_slice_in_dim(over_shards(out_own), part * head_cols, head_cols)
    gain_one, shift_one, gain_two, shift_two, qkv_bias, out_bias, up_bias, down_bias = (
        small_vectors(over_shards(small_own).astype(jnp.float32))
    )
    out_part, scaled_part, terms, sums = layer(
        x_all,
        cotangent_all,
        lengths_all,
        (qkv_weight, out_weight, up_weight, down_weight),
        (gain_one, shift_one, gain_two, shift_two, qkv_bias, up_bias),
        part,
    )
    norm_sums, d_qkv_bias, d_up_bias = sums
    out_sum = lax.psum_scatter(out_part, "dp", scatter_dimension=0, tiled=True)
    scaled = lax.psum_scatter(scaled_part, "dp", scatter_dimension=0, tiled=True)
    out_sum, scaled = out_sum.astype(jnp.float32), scaled.astype(jnp.float32)

    inputs = tokens_in[0].astype(jnp.float32)
    live = (jnp.arange(length) < lengths[0]).astype(jnp.float32)[:, None]
    back = cotangent[0].astype(jnp.float32) * live
    back_total = jnp.sum(back, axis=0)

    def spread(values, pieces):
        wide = jnp.zeros((pieces, parts, values.shape[0] // pieces), jnp.float32)
        return lax.dynamic_update_index_in_dim(
            wide, values.reshape(pieces, -1), part, axis=1
        ).reshape(-1)

    small_grad = jnp.concatenate(
        [
            norm_sums.reshape(4 * D),
            spread(d_qkv_bias, 3),
            back_total,
            spread(d_up_bias, shards),
            back_total,
        ]
    )
    small_sum = lax.psum(small_grad, ("dp", "fsdp"))
    small_rows = small_master.shape[0]
    small_sum = lax.dynamic_slice_in_dim(small_sum, shard * small_rows, small_rows)
    qkv_term, out_term, up_term, down_term = terms
    out_wide = lax.dynamic_update_slice_in_dim(
        jnp.zeros((D, D), jnp.bfloat16), out_term, part * head_cols, axis=0
    )

    def to_owner(term):
        own = lax.psum_scatter(term, "fsdp", scatter_dimension=0, tiled=True)
        return lax.all_gather(own, "dp", axis=0, tiled=False).astype(jnp.float32)

    reduced = (
        joined(to_owner(qkv_term), 3),
        lax.psum(
            lax.psum_scatter(out_wide, "fsdp", scatter_dimension=0, tiled=True), "dp"
        ).astype(jnp.float32),
        joined(to_owner(up_term), shards),
        to_owner(down_term).reshape(down_master.shape),
        small_sum,
    )

    unit_rows, inverse_rows = normalize(inputs)
    output = ((inputs + out_sum + out_bias + down_bias) * live).astype(jnp.bfloat16)
    input_grad = back + inverse_rows * (
        scaled
        - jnp.mean(scaled, axis=-1, keepdims=True)
        - unit_rows * jnp.mean(scaled * unit_rows, axis=-1, keepdims=True)
    )
    return (output[None], input_grad.astype(jnp.bfloat16)[None]) + lamb(*update, reduced)


def lamb_rows(first_old, second_old, master, grad):
    first_new = BETA_ONE * first_old + (1.0 - BETA_ONE) * grad
    second_new = BETA_TWO * second_old + (1.0 - BETA_TWO) * grad * grad
    root = second_new * lax.rsqrt(second_new)
    update = first_new / (root + ADAM_EPSILON) + DECAY * master
    return first_new, second_new, update


def lane_sums(values):
    squares = jnp.sum(values * values, axis=0, keepdims=True)
    total = squares[:, 0:128]
    for n in range(1, squares.shape[1] // 128):
        total = total + squares[:, n * 128 : (n + 1) * 128]
    return total


def moments_kernel(*refs):
    qkv_grad, out_grad, up_grad, down_grad, small_grad = refs[0:5]
    masters, firsts, seconds = refs[5:10], refs[10:15], refs[15:20]
    first_news, second_news, updates, squares = refs[20:25], refs[25:30], refs[30:35], refs[35]
    step = pl.program_id(0)

    @pl.when(step == 0)
    def _():
        squares[...] = jnp.zeros_like(squares)

    def one(number, span, grad):
        index = (slice(None), span)
        rows = firsts[number].shape[0]
        place = (pl.ds(pl.multiple_of(step * rows, rows), rows), span)
        master = masters[number][place]
        first_new, second_new, update = lamb_rows(
            firsts[number][index], seconds[number][index], master, grad
        )
        first_news[number][index] = first_new
        second_news[number][index] = second_new
        updates[number][place] = update
        return lane_sums(master), lane_sums(update)

    def add(number, pairs):
        weight, update = pairs[0]
        for more_weight, more_update in pairs[1:]:
            weight, update = weight + more_weight, update + more_update
        squares[number : number + 1] += weight
        squares[8 + number : 9 + number] += update

    f32 = jnp.float32
    parts = qkv_grad.shape[0]
    width = qkv_grad.shape[2] // 3
    add(
        0,
        [
            one(
                0,
                slice((c * parts + d) * width, (c * parts + d + 1) * width),
                qkv_grad[d, :, c * width : (c + 1) * width].astype(f32),
            )
            for c in range(3)
            for d in range(parts)
        ],
    )
    add(1, [one(1, slice(None), out_grad[...].astype(f32))])
    pieces = up_grad.shape[2] // 128
    add(
        2,
        [
            one(
                2,
                slice((g * parts + d) * 128, (g * parts + d + 1) * 128),
                up_grad[d, :, g * 128 : (g + 1) * 128].astype(f32),
            )
            for g in range(pieces)
            for d in range(parts)
        ],
    )
    add(3, [one(3, slice(None), down_grad[0].astype(f32))])

    @pl.when(step == 0)
    def _():
        first_new, second_new, update = lamb_rows(
            firsts[4][...], seconds[4][...], masters[4][...], small_grad[...]
        )
        first_news[4][...] = first_new
        second_news[4][...] = second_new
        updates[4][...] = update
        squares[4:5] += lane_sums(masters[4][...])
        squares[12:13] += lane_sums(update)


def lamb_specs(masters, steps):
    specs = [pl.BlockSpec((m.shape[0] // steps, m.shape[1]), lambda i: (i, 0)) for m in masters[:4]]
    return specs + [pl.BlockSpec(masters[4].shape, lambda i: (0, 0))]


def moments(grads, masters, firsts, seconds, steps=4):
    qkv_grad, out_grad, up_grad, down_grad, small_grad = grads
    shape = jax.ShapeDtypeStruct
    each = lamb_specs(masters, steps)
    rows = qkv_grad.shape[1]
    halves = steps // qkv_grad.shape[0]
    grad_specs = [
        pl.BlockSpec((qkv_grad.shape[0], rows // steps, qkv_grad.shape[2]), lambda i: (0, i, 0)),
        each[1],
        pl.BlockSpec((up_grad.shape[0], rows // steps, up_grad.shape[2]), lambda i: (0, i, 0)),
        pl.BlockSpec(
            (1, rows // halves, down_grad.shape[2]), lambda i: (i // halves, i % halves, 0)
        ),
        each[4],
    ]
    out = [shape(m.shape, jnp.float32) for m in masters]
    near = [pltpu.VMEM(m.shape, jnp.float32) for m in masters]
    results = pl.pallas_call(
        moments_kernel,
        grid=(steps,),
        in_specs=grad_specs + [VMEM_SPEC] * 5 + each * 2,
        out_specs=each * 2 + [VMEM_SPEC] * 5 + [pl.BlockSpec((16, 128), lambda i: (0, 0))],
        out_shape=out * 2 + near + [shape((16, 128), jnp.float32)],
        compiler_params=pltpu.CompilerParams(vmem_limit_bytes=24 << 20),
        name="moments",
    )(*grads, *masters, *firsts, *seconds)
    return results[0:5], results[5:10], results[10:15], results[15]


def norms_kernel(squares, total, everyone, send_sem, recv_sem):
    shard, part = lax.axis_index("fsdp"), lax.axis_index("dp")
    peers = [(part, (shard + k) % 8) for k in range(1, 8)]
    barrier = pltpu.get_barrier_semaphore()
    for peer in peers:
        pl.semaphore_signal(barrier, inc=1, device_id=peer, device_id_type=MESH_ID)
    pl.semaphore_wait(barrier, 7)
    for k in range(1, 8):
        send(
            squares, everyone.at[shard], send_sem.at[k - 1], recv_sem.at[k - 1], peers[k - 1]
        ).start()
    everyone[shard] = squares[...]
    for k in range(1, 8):
        arrived(everyone.at[(shard + 8 - k) % 8], recv_sem.at[k - 1], peers[7 - k])
    summed = everyone[0]
    for k in range(1, 8):
        summed = summed + everyone[k]
    norms = jnp.sqrt(jnp.sum(summed, axis=1, keepdims=True))
    total[...] = jnp.broadcast_to(norms, (16, 128))
    for k in range(1, 8):
        sent(squares, send_sem.at[k - 1], peers[k - 1])


def norms(squares):
    dma = pltpu.SemaphoreType.DMA
    return pl.pallas_call(
        norms_kernel,
        out_shape=jax.ShapeDtypeStruct((16, 128), jnp.float32),
        in_specs=[VMEM_SPEC],
        out_specs=VMEM_SPEC,
        scratch_shapes=[pltpu.VMEM((8, 16, 128), jnp.float32), dma((7,)), dma((7,))],
        compiler_params=pltpu.CompilerParams(
            collective_id=1, has_side_effects=True, vmem_limit_bytes=2 << 20
        ),
        name="norms",
    )(squares)


def step_kernel(*refs):
    total, masters, updates, layer_outs = refs[0], refs[1:6], refs[6:11], refs[11:13]
    news, outs, lamb_norms = refs[13:18], refs[18:20], refs[20]
    step = pl.program_id(0)
    for number in range(5):
        weight_norm = total[number : number + 1, 0:1]
        update_norm = total[8 + number : 9 + number, 0:1]
        scale = RATE * (weight_norm / update_norm)
        rows = news[number].shape[0]
        place = slice(None)
        if rows < masters[number].shape[0]:
            place = pl.ds(pl.multiple_of(step * rows, rows), rows)
        news[number][...] = masters[number][place] - scale * updates[number][place]
    for source, target in zip(layer_outs, outs):
        target[...] = source[...]

    @pl.when(step == 0)
    def _():
        row = lax.broadcasted_iota(jnp.int32, (8, 128), 0)
        lane = lax.broadcasted_iota(jnp.int32, (8, 128), 1)
        for n in range(2):
            half = jnp.where(row == lane, total[8 * n : 8 * n + 8], 0.0)
            lamb_norms[n : n + 1] = jnp.sum(half, axis=0, keepdims=True)[:, 0:5]


def step_masters(total, masters, updates, layer_outs, steps=4):
    shape = jax.ShapeDtypeStruct
    out_specs = [
        pl.BlockSpec((o.shape[0] // steps, o.shape[1]), lambda i: (i, 0)) for o in layer_outs
    ]
    results = pl.pallas_call(
        step_kernel,
        grid=(steps,),
        in_specs=[pl.BlockSpec((16, 128), lambda i: (0, 0))] + [VMEM_SPEC] * 10 + out_specs,
        out_specs=lamb_specs(masters, steps)
        + out_specs
        + [pl.BlockSpec((2, 5), lambda i: (0, 0))],
        out_shape=[shape(m.shape, jnp.float32) for m in masters]
        + [shape(o.shape, o.dtype) for o in layer_outs]
        + [shape((2, 5), jnp.float32)],
        compiler_params=pltpu.CompilerParams(vmem_limit_bytes=12 << 20),
        name="step_masters",
    )(total, *masters, *updates, *layer_outs)
    return results[0:5], results[5:7], results[7]


def lamb_split(masters, firsts, seconds, grads, layer_outs):
    def tall(arrays):
        return tuple(arrays[:4]) + (arrays[4].reshape(-1, 128),)

    def flat_small(arrays):
        return tuple(arrays[:4]) + (arrays[4].reshape(-1),)

    def placed(arrays, space):
        return tuple(pltpu.with_memory_space_constraint(a, space) for a in arrays)

    masters = placed(tall(masters), pltpu.VMEM)
    firsts, seconds = tall(firsts), tall(seconds)
    firsts = placed(firsts[:1], pltpu.VMEM) + placed(firsts[1:], pltpu.HBM)
    seconds = placed(seconds, pltpu.HBM)
    grads = placed(grads, pltpu.HBM)
    first_news, second_news, updates, squares = moments(grads, masters, firsts, seconds)
    news, outs, lamb_norms = step_masters(norms(squares), masters, updates, layer_outs)
    return (
        tuple(out[None] for out in outs)
        + flat_small(news)
        + flat_small(first_news)
        + flat_small(second_news)
        + (lamb_norms,)
    )


def lamb(masters, firsts, seconds, reduced):
    updates = []
    first_news = []
    second_news = []
    for first_old, second_old, master, grad_sum in zip(firsts, seconds, masters, reduced):
        first_new = BETA_ONE * first_old + (1.0 - BETA_ONE) * grad_sum
        second_new = BETA_TWO * second_old + (1.0 - BETA_TWO) * grad_sum * grad_sum
        updates.append(first_new / (jnp.sqrt(second_new) + ADAM_EPSILON) + DECAY * master)
        first_news.append(first_new)
        second_news.append(second_new)
    weight_squares, update_squares = lax.psum(
        (local_squares(masters), local_squares(updates)), "fsdp"
    )
    weight_norms = jnp.sqrt(weight_squares)
    update_norms = jnp.sqrt(update_squares)
    new_masters = [
        masters[number] - RATE * (weight_norms[number] / update_norms[number]) * updates[number]
        for number in range(5)
    ]
    lamb_norms = jnp.stack([weight_norms, update_norms])
    return tuple(new_masters) + tuple(first_news) + tuple(second_news) + (lamb_norms,)


def solution(mesh):
    in_specs = (
        P(("dp", "fsdp"), None, None),
        P(("dp", "fsdp"), None, None),
        P(("dp", "fsdp")),
        P("fsdp", None),
        P("fsdp", None),
        P("fsdp", None),
        P("fsdp", None),
        P("fsdp"),
        P("fsdp", None),
        P("fsdp", None),
        P("fsdp", None),
        P("fsdp", None),
        P("fsdp"),
        P("fsdp", None),
        P("fsdp", None),
        P("fsdp", None),
        P("fsdp", None),
        P("fsdp"),
    )
    out_specs = (
        P(("dp", "fsdp"), None, None),
        P(("dp", "fsdp"), None, None),
        P("fsdp", None),
        P("fsdp", None),
        P("fsdp", None),
        P("fsdp", None),
        P("fsdp"),
        P("fsdp", None),
        P("fsdp", None),
        P("fsdp", None),
        P("fsdp", None),
        P("fsdp"),
        P("fsdp", None),
        P("fsdp", None),
        P("fsdp", None),
        P("fsdp", None),
        P("fsdp"),
        P(),
    )
    return jax.shard_map(local_split, mesh=mesh, in_specs=in_specs, out_specs=out_specs, check_vma=False)
```
